256 devices in a mesh: inl: 8 (over z_lo, core), xln: 8 (over x, z_hi), section: 4 (over y).
Axes of the slice: x: 4, y: 4, z: 8 (z_hi: 2, z_lo: 4; z = z_hi * 4 + z_lo), core: 2. Of those that a mesh axis runs over, the one named last changes fastest.
Arguments:
- skips: bfloat16 [4, 8192, 1024], P('section', ('inl', 'xln')), may hold values from -6 to 6
- deconv_weight: bfloat16 [4, 1024, 1024], P('section'), may hold values from -0.1875 to 0.1875
- norm_gain: float32 [4, 2, 128], P('section'), may hold values from 0.5 to 2
- conv_in: bfloat16 [4, 27, 128, 128], P('section'), may hold values from -0.109375 to 0.109375
- conv_out: bfloat16 [4, 27, 32, 128], P('section'), may hold values from -0.109375 to 0.109375
Outputs:
- features: bfloat16 [32, 32, 2048], P('section', 'inl', 'xln')
The draws below stay inside these ranges and needn't reach their ends.
All inputs are finite; a program needn't handle non-finite values.
Results may differ from the reference program's by a relative error of at most 0.012.
Values may be sent and summed in bfloat16 or wider, within the bound.
A program may use at most 64 MiB of HBM per device.

```python
import math
import jax
import jax.numpy as jnp
from jax import lax

D = 1024
CH = 128
OUTCH = 32
GZ = 8
SKIPS = 4
GX = 16
GY = 64
SEQ = 8192
NXC = 32
NYC = 128
NZC = 16


def level_of(key, dims, split, low, top_value):
    gain = 1.0
    for dim, shards_of in split:
        draws = jax.random.uniform(jax.random.fold_in(jax.random.fold_in(key, 6), dim), (shards_of,), jnp.float32, low / len(split), top_value / len(split))
        gain = gain * jnp.repeat(jnp.exp(draws), dims[dim] // shards_of).reshape((-1,) + (1,) * (len(dims) - 1 - dim))
    return gain


def noise(key, extent, width, reach, cuts=(), kind=jnp.bfloat16):
    array = width * jax.random.normal(key, extent, jnp.float32)
    if cuts:
        array = array * level_of(key, extent, cuts, -0.22, 0.18)
    return jnp.clip(array, -reach, reach).astype(kind)


def setup_inputs(seed: int = 0) -> dict:
    key_of = jax.random.split(jax.random.key(seed), 6)
    skips = noise(key_of[0], (SKIPS, SEQ, D), 1.0, 6.0, ((0, 4), (1, 64)))
    deconv_weight = noise(key_of[1], (SKIPS, D, 8 * CH), D ** -0.5, 0.1875, ((0, 4),))
    norm_gain = jnp.clip(jnp.exp(math.log(2.0) - 1.3862944 * jax.random.uniform(key_of[2], (SKIPS, 2, CH), jnp.float32) ** level_of(key_of[2], (SKIPS, 2, CH), ((0, 4),), -0.2, 0.2)), 0.5, 2.0)
    conv_in = noise(key_of[3], (SKIPS, 27, CH, CH), (27 * CH) ** -0.5, 0.109375, ((0, 4),))
    conv_out = noise(key_of[4], (SKIPS, 27, OUTCH, CH), (27 * CH) ** -0.5, 0.109375, ((0, 4),))
    return dict(skips=skips, deconv_weight=deconv_weight, norm_gain=norm_gain, conv_in=conv_in, conv_out=conv_out)


epsilon = 1e-05

def normalize(values, scale):
    mean_square = lax.optimization_barrier(jnp.mean(values * values, axis=-1, keepdims=True))
    return values * lax.rsqrt(mean_square + epsilon) * scale

def convolve(field, kernel):
    shaped = kernel.reshape(3, 3, 3, kernel.shape[1], kernel.shape[2])
    result = lax.conv_general_dilated(field[None], shaped, (1, 1, 1), ((1, 1), (1, 1), (1, 1)), dimension_numbers=('NDHWC', 'DHWIO', 'NDHWC'), precision=lax.Precision.HIGHEST)
    return result[0]

def branch(operands):
    tokens_one, weight, gains, kernel_in, kernel_out = operands
    upsampled = jnp.dot(tokens_one, weight, preferred_element_type=jnp.float32).reshape(GY, GX, GZ, 8, CH)
    field = jax.nn.gelu(normalize(upsampled, gains[0]), approximate=True).astype(jnp.bfloat16)
    field = field.reshape(GY, GX, GZ, 2, 2, 2, CH).transpose(1, 3, 0, 4, 2, 5, 6).reshape(NXC, NYC, NZC, CH)
    inner = convolve(field.astype(jnp.float32), kernel_in.astype(jnp.float32))
    mixed = jax.nn.gelu(normalize(inner, gains[1]) + field.astype(jnp.float32), approximate=True).astype(jnp.bfloat16)
    return convolve(mixed.astype(jnp.float32), kernel_out.astype(jnp.float32).transpose(0, 2, 1))

def reference(skips, deconv_weight, norm_gain, conv_in, conv_out):
    terms = lax.map(branch, (skips, deconv_weight, norm_gain, conv_in, conv_out))
    total = lax.optimization_barrier(jnp.sum(terms, axis=0))
    return total.transpose(3, 0, 1, 2).reshape(OUTCH, NXC, NYC * NZC).astype(jnp.bfloat16)
```

```python
import functools

import jax
import jax.numpy as jnp
from jax import lax
from jax.experimental import pallas as pl
from jax.experimental.pallas import tpu as pltpu
from jax.sharding import PartitionSpec as P

MESH = pl.DeviceIdType.MESH

PXD = 2
GZ = 8


epsilon = 1e-05


def with_halo(block, sides, width):
    for axis, dim in sides:
        count = lax.axis_size(axis)
        forward = [(i, i + 1) for i in range(count - 1)]
        backward = [(target, source) for source, target in forward]
        low = lax.ppermute(
            lax.slice_in_dim(block, block.shape[dim] - width, None, axis=dim), axis, forward
        )
        high = lax.ppermute(lax.slice_in_dim(block, 0, width, axis=dim), axis, backward)
        block = jnp.concatenate([low, block, high], axis=dim)
    return block


def normalize(values, scale):
    mean_square = jnp.mean(values * values, axis=-1, keepdims=True)
    return values * lax.rsqrt(mean_square + epsilon) * scale


def activate(upsampled, gains):
    width = gains.shape[1]
    shaped = upsampled.reshape(upsampled.shape[:-1] + (upsampled.shape[-1] // width, width))
    result = jax.nn.gelu(normalize(shaped, gains[0]), approximate=True).astype(jnp.bfloat16)
    return result.reshape(upsampled.shape)


def finish(inner, residual_part, gains):
    return jax.nn.gelu(
        normalize(inner, gains[1]) + residual_part.astype(jnp.float32), approximate=True
    ).astype(jnp.bfloat16)


def conv_taps(padded, kernel, out_x, out_y):
    depth = padded.shape[2]
    channels = padded.shape[3]
    deeper = jnp.pad(padded, ((0, 0), (0, 0), (1, 1), (0, 0)))
    total = jnp.zeros((out_x * out_y * depth, kernel.shape[2]), jnp.float32)
    for offset_x in range(3):
        for offset_y in range(3):
            for offset_z in range(3):
                window = deeper[
                    offset_x : offset_x + out_x,
                    offset_y : offset_y + out_y,
                    offset_z : offset_z + depth,
                ]
                total = total + jnp.dot(
                    window.reshape(-1, channels),
                    kernel[(offset_x * 3 + offset_y) * 3 + offset_z],
                    preferred_element_type=jnp.float32,
                )
    return total.reshape(out_x, out_y, depth, kernel.shape[2])


def conv_rows(padded, kernel_rows, out_x, out_y):
    depth = padded.shape[2]
    channels = padded.shape[3]
    deeper = jnp.pad(padded, ((0, 0), (0, 0), (1, 1), (0, 0)))
    total = jnp.zeros((kernel_rows.shape[1], out_x * out_y * depth), jnp.float32)
    for offset_x in range(3):
        for offset_y in range(3):
            for offset_z in range(3):
                window = deeper[
                    offset_x : offset_x + out_x,
                    offset_y : offset_y + out_y,
                    offset_z : offset_z + depth,
                ]
                total = total + lax.dot_general(
                    kernel_rows[(offset_x * 3 + offset_y) * 3 + offset_z],
                    window.reshape(-1, channels),
                    (((1,), (1,)), ((), ())),
                    preferred_element_type=jnp.float32,
                )
    return total.reshape(kernel_rows.shape[1], out_x, out_y * depth)


def reduce_scatter_kernel(count, parts_ref, out_ref, held, send_sem, recv_sem):
    me = lax.axis_index("section")
    barrier = pltpu.get_barrier_semaphore()
    for step in range(1, count):
        peer = lax.rem(me + step, count)
        pl.semaphore_signal(barrier, inc=1, device_id={"section": peer}, device_id_type=MESH)
    pl.semaphore_wait(barrier, count - 1)
    sends = []
    for step in range(1, count):
        peer = lax.rem(me + step, count)
        copy = pltpu.make_async_remote_copy(
            src_ref=parts_ref.at[peer],
            dst_ref=held.at[step],
            send_sem=send_sem.at[step],
            recv_sem=recv_sem.at[step],
            device_id={"section": peer},
            device_id_type=MESH,
        )
        copy.start()
        sends.append(copy)
    total = parts_ref[me]
    for step in range(1, count):
        sends[step - 1].wait_recv()
        total = total + held[step]
    for copy in sends:
        copy.wait_send()
    out_ref[...] = total.astype(out_ref.dtype)


def reduce_scatter(parts):
    count = lax.axis_size("section")
    shaped = parts.reshape((count, parts.shape[0] // count) + parts.shape[1:])
    return pl.pallas_call(
        functools.partial(reduce_scatter_kernel, count),
        out_shape=jax.ShapeDtypeStruct(shaped.shape[1:], jnp.bfloat16),
        in_specs=[pl.BlockSpec(memory_space=pltpu.VMEM)],
        out_specs=pl.BlockSpec(memory_space=pltpu.VMEM),
        scratch_shapes=[
            pltpu.VMEM(shaped.shape, jnp.float32),
            pltpu.SemaphoreType.DMA((count,)),
            pltpu.SemaphoreType.DMA((count,)),
        ],
        compiler_params=pltpu.CompilerParams(collective_id=0, has_side_effects=True),
    )(shaped)


def local(skips, deconv_weight, norm_gain, conv_in, conv_out):
    inl_size = lax.axis_size("inl")
    tokens_here = skips[0]
    weight = deconv_weight[0]
    gains = norm_gain[0]
    channels = gains.shape[1]
    lines = tokens_here.shape[0] // (inl_size * PXD * GZ)
    cell_x = 2 * PXD
    cell_y = 2 * inl_size * lines
    cell_z = 2 * GZ
    ready = tokens_here.reshape(1, 1, lines, inl_size, PXD * GZ, tokens_here.shape[1])
    moved = lax.all_to_all(
        lax.all_to_all(ready, "inl", split_axis=3, concat_axis=0, tiled=True),
        "xln",
        split_axis=0,
        concat_axis=1,
        tiled=True,
    )
    upsampled = jnp.dot(
        moved.reshape(-1, tokens_here.shape[1]), weight, preferred_element_type=jnp.float32
    )
    brick = activate(upsampled, gains)
    field = (
        brick.reshape(cell_y // 2, PXD, GZ, 2, 2, 2, channels)
        .transpose(1, 3, 0, 4, 2, 5, 6)
        .reshape(cell_x, cell_y, cell_z, channels)
    )
    edged = with_halo(field, (("inl", 0), ("xln", 1)), 1)
    inner = conv_taps(edged, conv_in[0], cell_x, cell_y)
    merged = finish(inner, field, gains)
    padded = with_halo(merged, (("inl", 0), ("xln", 1)), 1)
    kernel_out = conv_out[0]
    return reduce_scatter(conv_rows(padded, kernel_out, cell_x, cell_y))


def solution(mesh):
    return jax.shard_map(
        local,
        mesh=mesh,
        in_specs=(
            P("section", ("inl", "xln"), None),
            P("section", None, None),
            P("section", None, None),
            P("section", None, None, None),
            P("section", None, None, None),
        ),
        out_specs=P("section", "inl", "xln"),
        check_vma=False,
    )
```

```python
import functools

import jax
import jax.numpy as jnp
from jax import lax
from jax.experimental import pallas as pl
from jax.experimental.pallas import tpu as pltpu
from jax.sharding import PartitionSpec as P

MESH = pl.DeviceIdType.MESH

PXD = 2
GZ = 8


epsilon = 1e-05


def with_halo(block, sides, width):
    for axis, dim in sides:
        count = lax.axis_size(axis)
        forward = [(i, i + 1) for i in range(count - 1)]
        backward = [(target, source) for source, target in forward]
        low = lax.ppermute(
            lax.slice_in_dim(block, block.shape[dim] - width, None, axis=dim), axis, forward
        )
        high = lax.ppermute(lax.slice_in_dim(block, 0, width, axis=dim), axis, backward)
        block = jnp.concatenate([low, block, high], axis=dim)
    return block


def normalize(values, scale):
    mean_square = jnp.mean(values * values, axis=-1, keepdims=True)
    return values * lax.rsqrt(mean_square + epsilon) * scale


def activate(upsampled, gains):
    width = gains.shape[1]
    shaped = upsampled.reshape(upsampled.shape[:-1] + (upsampled.shape[-1] // width, width))
    result = jax.nn.gelu(normalize(shaped, gains[0]), approximate=True).astype(jnp.bfloat16)
    return result.reshape(upsampled.shape)


def finish(inner, residual_part, gains):
    return jax.nn.gelu(
        normalize(inner, gains[1]) + residual_part.astype(jnp.float32), approximate=True
    ).astype(jnp.bfloat16)


def conv_taps(padded, kernel, out_x, out_y):
    depth = padded.shape[2]
    channels = padded.shape[3]
    deeper = jnp.pad(padded, ((0, 0), (0, 0), (1, 1), (0, 0)))
    total = jnp.zeros((out_x * out_y * depth, kernel.shape[2]), jnp.float32)
    for offset_x in range(3):
        for offset_y in range(3):
            for offset_z in range(3):
                window = deeper[
                    offset_x : offset_x + out_x,
                    offset_y : offset_y + out_y,
                    offset_z : offset_z + depth,
                ]
                total = total + jnp.dot(
                    window.reshape(-1, channels),
                    kernel[(offset_x * 3 + offset_y) * 3 + offset_z],
                    preferred_element_type=jnp.float32,
                )
    return total.reshape(out_x, out_y, depth, kernel.shape[2])


def conv_rows(padded, kernel_rows, out_x, out_y):
    depth = padded.shape[2]
    channels = padded.shape[3]
    deeper = jnp.pad(padded, ((0, 0), (0, 0), (1, 1), (0, 0)))
    total = jnp.zeros((kernel_rows.shape[1], out_x * out_y * depth), jnp.float32)
    for offset_x in range(3):
        for offset_y in range(3):
            for offset_z in range(3):
                window = deeper[
                    offset_x : offset_x + out_x,
                    offset_y : offset_y + out_y,
                    offset_z : offset_z + depth,
                ]
                total = total + lax.dot_general(
                    kernel_rows[(offset_x * 3 + offset_y) * 3 + offset_z],
                    window.reshape(-1, channels),
                    (((1,), (1,)), ((), ())),
                    preferred_element_type=jnp.float32,
                )
    return total.reshape(kernel_rows.shape[1], out_x, out_y * depth)


def reduce_scatter_kernel(count, parts_ref, out_ref, held, send_sem, recv_sem):
    me = lax.axis_index("section")
    barrier = pltpu.get_barrier_semaphore()
    for step in range(1, count):
        peer = lax.rem(me + step, count)
        pl.semaphore_signal(barrier, inc=1, device_id={"section": peer}, device_id_type=MESH)
    pl.semaphore_wait(barrier, count - 1)
    sends = []
    for step in range(1, count):
        peer = lax.rem(me + step, count)
        copy = pltpu.make_async_remote_copy(
            src_ref=parts_ref.at[peer],
            dst_ref=held.at[step],
            send_sem=send_sem.at[step],
            recv_sem=recv_sem.at[step],
            device_id={"section": peer},
            device_id_type=MESH,
        )
        copy.start()
        sends.append(copy)
    total = parts_ref[me]
    for step in range(1, count):
        sends[step - 1].wait_recv()
        total = total + held[step]
    for copy in sends:
        copy.wait_send()
    out_ref[...] = total.astype(out_ref.dtype)


def reduce_scatter(parts):
    count = lax.axis_size("section")
    shaped = parts.reshape((count, parts.shape[0] // count) + parts.shape[1:])
    return pl.pallas_call(
        functools.partial(reduce_scatter_kernel, count),
        out_shape=jax.ShapeDtypeStruct(shaped.shape[1:], jnp.bfloat16),
        in_specs=[pl.BlockSpec(memory_space=pltpu.VMEM)],
        out_specs=pl.BlockSpec(memory_space=pltpu.VMEM),
        scratch_shapes=[
            pltpu.VMEM(shaped.shape, jnp.float32),
            pltpu.SemaphoreType.DMA((count,)),
            pltpu.SemaphoreType.DMA((count,)),
        ],
        compiler_params=pltpu.CompilerParams(collective_id=0, has_side_effects=True),
    )(shaped)


DIRECTIONS = [(dx, dy) for dx in (-1, 0, 1) for dy in (-1, 0, 1) if (dx, dy) != (0, 0)]


def halo_span(step, size):
    if step < 0:
        return (0, 1), (size + 1, size + 2)
    if step > 0:
        return (size - 1, size), (0, 1)
    return (0, size), (1, size + 1)


def halo_kernel(field_ref, out_ref, held, send_sem, recv_sem):
    nx, ny = field_ref.shape[0], field_ref.shape[1]
    count_x, count_y = lax.axis_size("inl"), lax.axis_size("xln")
    me_x, me_y = lax.axis_index("inl"), lax.axis_index("xln")
    barrier = pltpu.get_barrier_semaphore()
    for dx, dy in DIRECTIONS:
        pl.semaphore_signal(
            barrier,
            inc=1,
            device_id={"inl": lax.rem(me_x + dx + count_x, count_x), "xln": lax.rem(me_y + dy + count_y, count_y)},
            device_id_type=MESH,
        )
    pl.semaphore_wait(barrier, len(DIRECTIONS))
    copies = []
    for index, (dx, dy) in enumerate(DIRECTIONS):
        (sx0, sx1), (tx0, tx1) = halo_span(dx, nx)
        (sy0, sy1), (ty0, ty1) = halo_span(dy, ny)
        to_x, to_y = me_x + dx, me_y + dy
        copy = pltpu.make_async_remote_copy(
            src_ref=field_ref.at[sx0:sx1, sy0:sy1],
            dst_ref=held.at[tx0:tx1, ty0:ty1],
            send_sem=send_sem.at[index],
            recv_sem=recv_sem.at[index],
            device_id={"inl": to_x, "xln": to_y},
            device_id_type=MESH,
        )
        sends = (to_x >= 0) & (to_x < count_x) & (to_y >= 0) & (to_y < count_y)
        from_x, from_y = me_x - dx, me_y - dy
        gets = (from_x >= 0) & (from_x < count_x) & (from_y >= 0) & (from_y < count_y)

        @pl.when(sends)
        def _():
            copy.start()

        @pl.when(jnp.logical_not(gets))
        def _():
            held[tx0:tx1, ty0:ty1] = jnp.zeros((tx1 - tx0, ty1 - ty0) + held.shape[2:], held.dtype)

        copies.append((copy, sends, gets))
    held[1 : nx + 1, 1 : ny + 1] = field_ref[...]
    for copy, sends, gets in copies:

        @pl.when(gets)
        def _():
            copy.wait_recv()

        @pl.when(sends)
        def _():
            copy.wait_send()

    out_ref[...] = held[...]


def exchange_halo(field, collective):
    nx, ny = field.shape[0], field.shape[1]
    shape = (nx + 2, ny + 2) + field.shape[2:]
    return pl.pallas_call(
        halo_kernel,
        out_shape=jax.ShapeDtypeStruct(shape, field.dtype),
        in_specs=[pl.BlockSpec(memory_space=pltpu.VMEM)],
        out_specs=pl.BlockSpec(memory_space=pltpu.VMEM),
        scratch_shapes=[
            pltpu.VMEM(shape, field.dtype),
            pltpu.SemaphoreType.DMA((len(DIRECTIONS),)),
            pltpu.SemaphoreType.DMA((len(DIRECTIONS),)),
        ],
        compiler_params=pltpu.CompilerParams(collective_id=collective, has_side_effects=True),
    )(field)


def local(skips, deconv_weight, norm_gain, conv_in, conv_out):
    inl_size = lax.axis_size("inl")
    tokens_here = skips[0]
    weight = deconv_weight[0]
    gains = norm_gain[0]
    channels = gains.shape[1]
    lines = tokens_here.shape[0] // (inl_size * PXD * GZ)
    cell_x = 2 * PXD
    cell_y = 2 * inl_size * lines
    cell_z = 2 * GZ
    ready = tokens_here.reshape(1, 1, lines, inl_size, PXD * GZ, tokens_here.shape[1])
    moved = lax.all_to_all(
        lax.all_to_all(ready, "inl", split_axis=3, concat_axis=0, tiled=True),
        "xln",
        split_axis=0,
        concat_axis=1,
        tiled=True,
    )
    upsampled = jnp.dot(
        moved.reshape(-1, tokens_here.shape[1]), weight, preferred_element_type=jnp.float32
    )
    brick = activate(upsampled, gains)
    field = (
        brick.reshape(cell_y // 2, PXD, GZ, 2, 2, 2, channels)
        .transpose(1, 3, 0, 4, 2, 5, 6)
        .reshape(cell_x, cell_y, cell_z, channels)
    )
    edged = exchange_halo(field, 1)
    inner = conv_taps(edged, conv_in[0], cell_x, cell_y)
    merged = finish(inner, field, gains)
    padded = exchange_halo(merged, 2)
    kernel_out = conv_out[0]
    return reduce_scatter(conv_rows(padded, kernel_out, cell_x, cell_y))


def solution(mesh):
    return jax.shard_map(
        local,
        mesh=mesh,
        in_specs=(
            P("section", ("inl", "xln"), None),
            P("section", None, None),
            P("section", None, None),
            P("section", None, None, None),
            P("section", None, None, None),
        ),
        out_specs=P("section", "inl", "xln"),
        check_vma=False,
    )
```

```python
import functools

import jax
import jax.numpy as jnp
from jax import lax
from jax.experimental import pallas as pl
from jax.experimental.pallas import tpu as pltpu
from jax.sharding import PartitionSpec as P

MESH = pl.DeviceIdType.MESH

PXD = 2
GZ = 8


epsilon = 1e-05


def with_halo(block, sides, width):
    for axis, dim in sides:
        count = lax.axis_size(axis)
        forward = [(i, i + 1) for i in range(count - 1)]
        backward = [(target, source) for source, target in forward]
        low = lax.ppermute(
            lax.slice_in_dim(block, block.shape[dim] - width, None, axis=dim), axis, forward
        )
        high = lax.ppermute(lax.slice_in_dim(block, 0, width, axis=dim), axis, backward)
        block = jnp.concatenate([low, block, high], axis=dim)
    return block


def normalize(values, scale):
    mean_square = jnp.mean(values * values, axis=-1, keepdims=True)
    return values * lax.rsqrt(mean_square + epsilon) * scale


def activate(upsampled, gains):
    width = gains.shape[1]
    shaped = upsampled.reshape(upsampled.shape[:-1] + (upsampled.shape[-1] // width, width))
    result = jax.nn.gelu(normalize(shaped, gains[0]), approximate=True).astype(jnp.bfloat16)
    return result.reshape(upsampled.shape)


def finish(inner, residual_part, gains):
    return jax.nn.gelu(
        normalize(inner, gains[1]) + residual_part.astype(jnp.float32), approximate=True
    ).astype(jnp.bfloat16)


def conv_taps(padded, kernel, out_x, out_y):
    depth = padded.shape[2]
    channels = padded.shape[3]
    deeper = jnp.pad(padded, ((0, 0), (0, 0), (1, 1), (0, 0)))
    total = jnp.zeros((out_x * out_y * depth, kernel.shape[2]), jnp.float32)
    for offset_x in range(3):
        for offset_y in range(3):
            for offset_z in range(3):
                window = deeper[
                    offset_x : offset_x + out_x,
                    offset_y : offset_y + out_y,
                    offset_z : offset_z + depth,
                ]
                total = total + jnp.dot(
                    window.reshape(-1, channels),
                    kernel[(offset_x * 3 + offset_y) * 3 + offset_z],
                    preferred_element_type=jnp.float32,
                )
    return total.reshape(out_x, out_y, depth, kernel.shape[2])


def conv_rows(padded, kernel_rows, out_x, out_y):
    depth = padded.shape[2]
    channels = padded.shape[3]
    deeper = jnp.pad(padded, ((0, 0), (0, 0), (1, 1), (0, 0)))
    total = jnp.zeros((kernel_rows.shape[1], out_x * out_y * depth), jnp.float32)
    for offset_x in range(3):
        for offset_y in range(3):
            for offset_z in range(3):
                window = deeper[
                    offset_x : offset_x + out_x,
                    offset_y : offset_y + out_y,
                    offset_z : offset_z + depth,
                ]
                total = total + lax.dot_general(
                    kernel_rows[(offset_x * 3 + offset_y) * 3 + offset_z],
                    window.reshape(-1, channels),
                    (((1,), (1,)), ((), ())),
                    preferred_element_type=jnp.float32,
                )
    return total.reshape(kernel_rows.shape[1], out_x, out_y * depth)


def reduce_scatter_kernel(count, parts_ref, out_ref, held, send_sem, recv_sem):
    me = lax.axis_index("section")
    barrier = pltpu.get_barrier_semaphore()
    for step in range(1, count):
        peer = lax.rem(me + step, count)
        pl.semaphore_signal(barrier, inc=1, device_id={"section": peer}, device_id_type=MESH)
    pl.semaphore_wait(barrier, count - 1)
    sends = []
    for step in range(1, count):
        peer = lax.rem(me + step, count)
        copy = pltpu.make_async_remote_copy(
            src_ref=parts_ref.at[peer],
            dst_ref=held.at[step],
            send_sem=send_sem.at[step],
            recv_sem=recv_sem.at[step],
            device_id={"section": peer},
            device_id_type=MESH,
        )
        copy.start()
        sends.append(copy)
    total = parts_ref[me]
    for step in range(1, count):
        sends[step - 1].wait_recv()
        total = total + held[step]
    for copy in sends:
        copy.wait_send()
    out_ref[...] = total.astype(out_ref.dtype)


def reduce_scatter(parts):
    count = lax.axis_size("section")
    shaped = parts.reshape((count, parts.shape[0] // count) + parts.shape[1:])
    return pl.pallas_call(
        functools.partial(reduce_scatter_kernel, count),
        out_shape=jax.ShapeDtypeStruct(shaped.shape[1:], jnp.bfloat16),
        in_specs=[pl.BlockSpec(memory_space=pltpu.VMEM)],
        out_specs=pl.BlockSpec(memory_space=pltpu.VMEM),
        scratch_shapes=[
            pltpu.VMEM(shaped.shape, jnp.float32),
            pltpu.SemaphoreType.DMA((count,)),
            pltpu.SemaphoreType.DMA((count,)),
        ],
        compiler_params=pltpu.CompilerParams(collective_id=0, has_side_effects=True),
    )(shaped)


DIRECTIONS = [(dx, dy) for dx in (-1, 0, 1) for dy in (-1, 0, 1) if (dx, dy) != (0, 0)]


def halo_span(step, size):
    if step < 0:
        return (0, 1), (size + 1, size + 2)
    if step > 0:
        return (size - 1, size), (0, 1)
    return (0, size), (1, size + 1)


def halo_kernel(field_ref, out_ref, held, send_sem, recv_sem):
    nx, ny = field_ref.shape[0], field_ref.shape[1]
    count_x, count_y = lax.axis_size("inl"), lax.axis_size("xln")
    me_x, me_y = lax.axis_index("inl"), lax.axis_index("xln")
    barrier = pltpu.get_barrier_semaphore()
    for dx, dy in DIRECTIONS:
        pl.semaphore_signal(
            barrier,
            inc=1,
            device_id={"inl": lax.rem(me_x + dx + count_x, count_x), "xln": lax.rem(me_y + dy + count_y, count_y)},
            device_id_type=MESH,
        )
    pl.semaphore_wait(barrier, len(DIRECTIONS))
    copies = []
    for index, (dx, dy) in enumerate(DIRECTIONS):
        (sx0, sx1), (tx0, tx1) = halo_span(dx, nx)
        (sy0, sy1), (ty0, ty1) = halo_span(dy, ny)
        to_x, to_y = me_x + dx, me_y + dy
        copy = pltpu.make_async_remote_copy(
            src_ref=field_ref.at[sx0:sx1, sy0:sy1],
            dst_ref=held.at[tx0:tx1, ty0:ty1],
            send_sem=send_sem.at[index],
            recv_sem=recv_sem.at[index],
            device_id={"inl": to_x, "xln": to_y},
            device_id_type=MESH,
        )
        sends = (to_x >= 0) & (to_x < count_x) & (to_y >= 0) & (to_y < count_y)
        from_x, from_y = me_x - dx, me_y - dy
        gets = (from_x >= 0) & (from_x < count_x) & (from_y >= 0) & (from_y < count_y)

        @pl.when(sends)
        def _():
            copy.start()

        @pl.when(jnp.logical_not(gets))
        def _():
            held[tx0:tx1, ty0:ty1] = jnp.zeros((tx1 - tx0, ty1 - ty0) + held.shape[2:], held.dtype)

        copies.append((copy, sends, gets))
    held[1 : nx + 1, 1 : ny + 1] = field_ref[...]
    for copy, sends, gets in copies:

        @pl.when(gets)
        def _():
            copy.wait_recv()

        @pl.when(sends)
        def _():
            copy.wait_send()

    out_ref[...] = held[...]


def exchange_halo(field, collective):
    nx, ny = field.shape[0], field.shape[1]
    shape = (nx + 2, ny + 2) + field.shape[2:]
    return pl.pallas_call(
        halo_kernel,
        out_shape=jax.ShapeDtypeStruct(shape, field.dtype),
        in_specs=[pl.BlockSpec(memory_space=pltpu.VMEM)],
        out_specs=pl.BlockSpec(memory_space=pltpu.VMEM),
        scratch_shapes=[
            pltpu.VMEM(shape, field.dtype),
            pltpu.SemaphoreType.DMA((len(DIRECTIONS),)),
            pltpu.SemaphoreType.DMA((len(DIRECTIONS),)),
        ],
        compiler_params=pltpu.CompilerParams(collective_id=collective, has_side_effects=True),
    )(field)


def gather_kernel(tokens_ref, out_ref, held, send_sem, recv_sem):
    count = lax.axis_size("inl")
    me_x, me_y = lax.axis_index("inl"), lax.axis_index("xln")
    rows = tokens_ref.shape[0] // count
    diagonal = me_x == me_y
    barrier = pltpu.get_barrier_semaphore()
    for other in range(count):
        for target in ({"inl": other, "xln": me_x}, {"inl": me_y, "xln": other}):

            @pl.when((target["inl"] != me_x) | (target["xln"] != me_y))
            def _():
                pl.semaphore_signal(barrier, inc=1, device_id=target, device_id_type=MESH)

    pl.semaphore_wait(barrier, 2 * count - 2 * diagonal.astype(jnp.int32))
    copies = []
    for other in range(count):
        copy = pltpu.make_async_remote_copy(
            src_ref=tokens_ref.at[pl.ds(other * rows, rows)],
            dst_ref=held.at[me_y],
            send_sem=send_sem.at[other],
            recv_sem=recv_sem.at[me_y],
            device_id={"inl": other, "xln": me_x},
            device_id_type=MESH,
        )
        to_self = (other == me_x) & diagonal

        @pl.when(jnp.logical_not(to_self))
        def _():
            copy.start()

        copies.append((copy, to_self))
    for source in range(count):
        incoming = pltpu.make_async_remote_copy(
            src_ref=tokens_ref.at[pl.ds(0, rows)],
            dst_ref=held.at[source],
            send_sem=send_sem.at[source],
            recv_sem=recv_sem.at[source],
            device_id={"inl": me_y, "xln": source},
            device_id_type=MESH,
        )
        from_self = (source == me_y) & diagonal

        @pl.when(jnp.logical_not(from_self))
        def _():
            incoming.wait_recv()

        @pl.when(from_self)
        def _():
            out_ref[source] = tokens_ref[pl.ds(pl.multiple_of(me_x * rows, rows), rows)]

        @pl.when(jnp.logical_not(from_self))
        def _():
            out_ref[source] = held[source]

    for copy, to_self in copies:

        @pl.when(jnp.logical_not(to_self))
        def _():
            copy.wait_send()


def gather_bricks(tokens):
    count = lax.axis_size("inl")
    rows = tokens.shape[0] // count
    shape = (lax.axis_size("xln"), rows, tokens.shape[1])
    return pl.pallas_call(
        gather_kernel,
        out_shape=jax.ShapeDtypeStruct(shape, tokens.dtype),
        in_specs=[pl.BlockSpec(memory_space=pltpu.VMEM)],
        out_specs=pl.BlockSpec(memory_space=pltpu.VMEM),
        scratch_shapes=[
            pltpu.VMEM(shape, tokens.dtype),
            pltpu.SemaphoreType.DMA((count,)),
            pltpu.SemaphoreType.DMA((count,)),
        ],
        compiler_params=pltpu.CompilerParams(collective_id=3, has_side_effects=True),
    )(tokens)


def local(skips, deconv_weight, norm_gain, conv_in, conv_out):
    inl_size = lax.axis_size("inl")
    tokens_here = skips[0]
    weight = deconv_weight[0]
    gains = norm_gain[0]
    channels = gains.shape[1]
    lines = tokens_here.shape[0] // (inl_size * PXD * GZ)
    cell_x = 2 * PXD
    cell_y = 2 * inl_size * lines
    cell_z = 2 * GZ
    moved = gather_bricks(tokens_here)
    upsampled = jnp.dot(
        moved.reshape(-1, tokens_here.shape[1]), weight, preferred_element_type=jnp.float32
    )
    brick = activate(upsampled, gains)
    field = (
        brick.reshape(cell_y // 2, PXD, GZ, 2, 2, 2, channels)
        .transpose(1, 3, 0, 4, 2, 5, 6)
        .reshape(cell_x, cell_y, cell_z, channels)
    )
    edged = exchange_halo(field, 1)
    inner = conv_taps(edged, conv_in[0], cell_x, cell_y)
    merged = finish(inner, field, gains)
    padded = exchange_halo(merged, 2)
    kernel_out = conv_out[0]
    return reduce_scatter(conv_rows(padded, kernel_out, cell_x, cell_y))


def solution(mesh):
    return jax.shard_map(
        local,
        mesh=mesh,
        in_specs=(
            P("section", ("inl", "xln"), None),
            P("section", None, None),
            P("section", None, None),
            P("section", None, None, None),
            P("section", None, None, None),
        ),
        out_specs=P("section", "inl", "xln"),
        check_vma=False,
    )
```

```python
import functools

import jax
import jax.numpy as jnp
from jax import lax
from jax.experimental import pallas as pl
from jax.experimental.pallas import tpu as pltpu
from jax.sharding import PartitionSpec as P

MESH = pl.DeviceIdType.MESH

PXD = 2
GZ = 8


epsilon = 1e-05


def with_halo(block, sides, width):
    for axis, dim in sides:
        count = lax.axis_size(axis)
        forward = [(i, i + 1) for i in range(count - 1)]
        backward = [(target, source) for source, target in forward]
        low = lax.ppermute(
            lax.slice_in_dim(block, block.shape[dim] - width, None, axis=dim), axis, forward
        )
        high = lax.ppermute(lax.slice_in_dim(block, 0, width, axis=dim), axis, backward)
        block = jnp.concatenate([low, block, high], axis=dim)
    return block


def normalize(values, scale):
    mean_square = jnp.mean(values * values, axis=-1, keepdims=True)
    return values * lax.rsqrt(mean_square + epsilon) * scale


def activate(upsampled, gains):
    width = gains.shape[1]
    shaped = upsampled.reshape(upsampled.shape[:-1] + (upsampled.shape[-1] // width, width))
    result = jax.nn.gelu(normalize(shaped, gains[0]), approximate=True).astype(jnp.bfloat16)
    return result.reshape(upsampled.shape)


def finish(inner, residual_part, gains):
    return jax.nn.gelu(
        normalize(inner, gains[1]) + residual_part.astype(jnp.float32), approximate=True
    ).astype(jnp.bfloat16)


def conv_taps(padded, kernel, out_x, out_y):
    depth = padded.shape[2]
    channels = padded.shape[3]
    deeper = jnp.pad(padded, ((0, 0), (0, 0), (1, 1), (0, 0)))
    total = jnp.zeros((out_x * out_y * depth, kernel.shape[2]), jnp.float32)
    for offset_x in range(3):
        for offset_y in range(3):
            for offset_z in range(3):
                window = deeper[
                    offset_x : offset_x + out_x,
                    offset_y : offset_y + out_y,
                    offset_z : offset_z + depth,
                ]
                total = total + jnp.dot(
                    window.reshape(-1, channels),
                    kernel[(offset_x * 3 + offset_y) * 3 + offset_z],
                    preferred_element_type=jnp.float32,
                )
    return total.reshape(out_x, out_y, depth, kernel.shape[2])


def conv_rows(padded, kernel_rows, out_x, out_y):
    depth = padded.shape[2]
    channels = padded.shape[3]
    deeper = jnp.pad(padded, ((0, 0), (0, 0), (1, 1), (0, 0)))
    total = jnp.zeros((kernel_rows.shape[1], out_x * out_y * depth), jnp.float32)
    for offset_x in range(3):
        for offset_y in range(3):
            for offset_z in range(3):
                window = deeper[
                    offset_x : offset_x + out_x,
                    offset_y : offset_y + out_y,
                    offset_z : offset_z + depth,
                ]
                total = total + lax.dot_general(
                    kernel_rows[(offset_x * 3 + offset_y) * 3 + offset_z],
                    window.reshape(-1, channels),
                    (((1,), (1,)), ((), ())),
                    preferred_element_type=jnp.float32,
                )
    return total.reshape(kernel_rows.shape[1], out_x, out_y * depth)


def reduce_scatter_kernel(count, parts_ref, out_ref, held, send_sem, recv_sem):
    me = lax.axis_index("section")
    barrier = pltpu.get_barrier_semaphore()
    for step in range(1, count):
        peer = lax.rem(me + step, count)
        pl.semaphore_signal(barrier, inc=1, device_id={"section": peer}, device_id_type=MESH)
    pl.semaphore_wait(barrier, count - 1)
    sends = []
    for step in range(1, count):
        peer = lax.rem(me + step, count)
        copy = pltpu.make_async_remote_copy(
            src_ref=parts_ref.at[peer],
            dst_ref=held.at[step],
            send_sem=send_sem.at[step],
            recv_sem=recv_sem.at[step],
            device_id={"section": peer},
            device_id_type=MESH,
        )
        copy.start()
        sends.append(copy)
    total = parts_ref[me]
    for step in range(1, count):
        sends[step - 1].wait_recv()
        total = total + held[step]
    for copy in sends:
        copy.wait_send()
    out_ref[...] = total.astype(out_ref.dtype)


def reduce_scatter(parts):
    count = lax.axis_size("section")
    shaped = parts.reshape((count, parts.shape[0] // count) + parts.shape[1:])
    return pl.pallas_call(
        functools.partial(reduce_scatter_kernel, count),
        out_shape=jax.ShapeDtypeStruct(shaped.shape[1:], jnp.bfloat16),
        in_specs=[pl.BlockSpec(memory_space=pltpu.VMEM)],
        out_specs=pl.BlockSpec(memory_space=pltpu.VMEM),
        scratch_shapes=[
            pltpu.VMEM(shaped.shape, jnp.float32),
            pltpu.SemaphoreType.DMA((count,)),
            pltpu.SemaphoreType.DMA((count,)),
        ],
        compiler_params=pltpu.CompilerParams(collective_id=0, has_side_effects=True),
    )(shaped)


DIRECTIONS = [(dx, dy) for dx in (-1, 0, 1) for dy in (-1, 0, 1) if (dx, dy) != (0, 0)]


def halo_span(step, size):
    if step < 0:
        return (0, 1), (size + 1, size + 2)
    if step > 0:
        return (size - 1, size), (0, 1)
    return (0, size), (1, size + 1)


def halo_kernel(field_ref, out_ref, held, send_sem, recv_sem):
    nx, ny = field_ref.shape[0], field_ref.shape[1]
    count_x, count_y = lax.axis_size("inl"), lax.axis_size("xln")
    me_x, me_y = lax.axis_index("inl"), lax.axis_index("xln")
    barrier = pltpu.get_barrier_semaphore()
    for dx, dy in DIRECTIONS:
        pl.semaphore_signal(
            barrier,
            inc=1,
            device_id={"inl": lax.rem(me_x + dx + count_x, count_x), "xln": lax.rem(me_y + dy + count_y, count_y)},
            device_id_type=MESH,
        )
    pl.semaphore_wait(barrier, len(DIRECTIONS))
    copies = []
    for index, (dx, dy) in enumerate(DIRECTIONS):
        (sx0, sx1), (tx0, tx1) = halo_span(dx, nx)
        (sy0, sy1), (ty0, ty1) = halo_span(dy, ny)
        to_x, to_y = me_x + dx, me_y + dy
        copy = pltpu.make_async_remote_copy(
            src_ref=field_ref.at[sx0:sx1, sy0:sy1],
            dst_ref=held.at[tx0:tx1, ty0:ty1],
            send_sem=send_sem.at[index],
            recv_sem=recv_sem.at[index],
            device_id={"inl": to_x, "xln": to_y},
            device_id_type=MESH,
        )
        sends = (to_x >= 0) & (to_x < count_x) & (to_y >= 0) & (to_y < count_y)
        from_x, from_y = me_x - dx, me_y - dy
        gets = (from_x >= 0) & (from_x < count_x) & (from_y >= 0) & (from_y < count_y)

        @pl.when(sends)
        def _():
            copy.start()

        @pl.when(jnp.logical_not(gets))
        def _():
            held[tx0:tx1, ty0:ty1] = jnp.zeros((tx1 - tx0, ty1 - ty0) + held.shape[2:], held.dtype)

        copies.append((copy, sends, gets))
    held[1 : nx + 1, 1 : ny + 1] = field_ref[...]
    for copy, sends, gets in copies:

        @pl.when(gets)
        def _():
            copy.wait_recv()

        @pl.when(sends)
        def _():
            copy.wait_send()

    if out_ref is not None:
        out_ref[...] = held[...]


def gelu_tanh(values):
    return 0.5 * values * (1.0 + jnp.tanh(0.7978845608028654 * (values + 0.044715 * (values * values * values))))


def conv_kernel(
    residual, field_ref, kernel_ref, gains_ref, out_ref, held, shifted, send_sem, recv_sem
):
    halo_kernel(field_ref, None, held, send_sem, recv_sem)
    nx, ny, nz, channels = field_ref.shape
    cells = nx * ny * nz
    width = shifted.shape[2]
    parts = []
    for offset_z in range(3):
        part = jnp.zeros((cells, width), jnp.float32)
        for offset_x in range(3):
            for offset_y in range(3):
                window = held[offset_x : offset_x + nx, offset_y : offset_y + ny].reshape(cells, channels)
                tap = kernel_ref[(offset_x * 3 + offset_y) * 3 + offset_z]
                if residual:
                    part = part + jnp.dot(window, tap, preferred_element_type=jnp.float32)
                else:
                    part = part + lax.dot_general(
                        window, tap, (((1,), (1,)), ((), ())), preferred_element_type=jnp.float32
                    )
        parts.append(part.reshape(nx * ny, nz, width))
    edge = jnp.zeros((nx * ny, 1, width), jnp.float32)
    shifted[:, 0:1] = edge
    shifted[:, nz + 1 : nz + 2] = edge
    shifted[:, 1 : nz + 1] = parts[0]
    total = parts[1] + shifted[:, 0:nz]
    shifted[:, 1 : nz + 1] = parts[2]
    total = total + shifted[:, 2 : nz + 2]
    if residual:
        mean_square = jnp.mean(total * total, axis=-1, keepdims=True)
        normed = total * lax.rsqrt(mean_square + epsilon) * gains_ref[1:2, :]
        base = field_ref[...].reshape(nx * ny, nz, channels).astype(jnp.float32)
        out_ref[...] = gelu_tanh(normed + base).astype(out_ref.dtype).reshape(out_ref.shape)
    else:
        out_ref[...] = total.reshape(out_ref.shape)


def conv_stage(field, kernel, gains, residual, collective):
    nx, ny, nz, channels = field.shape
    width = kernel.shape[2] if residual else kernel.shape[1]
    padded = (nx + 2, ny + 2, nz, channels)
    dtype = jnp.bfloat16 if residual else jnp.float32
    return pl.pallas_call(
        functools.partial(conv_kernel, residual),
        out_shape=jax.ShapeDtypeStruct((nx, ny, nz, width), dtype),
        in_specs=[pl.BlockSpec(memory_space=pltpu.VMEM)] * 3,
        out_specs=pl.BlockSpec(memory_space=pltpu.VMEM),
        scratch_shapes=[
            pltpu.VMEM(padded, field.dtype),
            pltpu.VMEM((nx * ny, nz + 2, width), jnp.float32),
            pltpu.SemaphoreType.DMA((len(DIRECTIONS),)),
            pltpu.SemaphoreType.DMA((len(DIRECTIONS),)),
        ],
        compiler_params=pltpu.CompilerParams(collective_id=collective, has_side_effects=True),
    )(field, kernel, gains)


def exchange_halo(field, collective):
    nx, ny = field.shape[0], field.shape[1]
    shape = (nx + 2, ny + 2) + field.shape[2:]
    return pl.pallas_call(
        halo_kernel,
        out_shape=jax.ShapeDtypeStruct(shape, field.dtype),
        in_specs=[pl.BlockSpec(memory_space=pltpu.VMEM)],
        out_specs=pl.BlockSpec(memory_space=pltpu.VMEM),
        scratch_shapes=[
            pltpu.VMEM(shape, field.dtype),
            pltpu.SemaphoreType.DMA((len(DIRECTIONS),)),
            pltpu.SemaphoreType.DMA((len(DIRECTIONS),)),
        ],
        compiler_params=pltpu.CompilerParams(collective_id=collective, has_side_effects=True),
    )(field)


def gather_kernel(tokens_ref, out_ref, held, send_sem, recv_sem):
    count = lax.axis_size("inl")
    me_x, me_y = lax.axis_index("inl"), lax.axis_index("xln")
    rows = tokens_ref.shape[0] // count
    diagonal = me_x == me_y
    barrier = pltpu.get_barrier_semaphore()
    for other in range(count):
        for target in ({"inl": other, "xln": me_x}, {"inl": me_y, "xln": other}):

            @pl.when((target["inl"] != me_x) | (target["xln"] != me_y))
            def _():
                pl.semaphore_signal(barrier, inc=1, device_id=target, device_id_type=MESH)

    pl.semaphore_wait(barrier, 2 * count - 2 * diagonal.astype(jnp.int32))
    copies = []
    for other in range(count):
        copy = pltpu.make_async_remote_copy(
            src_ref=tokens_ref.at[pl.ds(other * rows, rows)],
            dst_ref=held.at[me_y],
            send_sem=send_sem.at[other],
            recv_sem=recv_sem.at[me_y],
            device_id={"inl": other, "xln": me_x},
            device_id_type=MESH,
        )
        to_self = (other == me_x) & diagonal

        @pl.when(jnp.logical_not(to_self))
        def _():
            copy.start()

        copies.append((copy, to_self))
    for source in range(count):
        incoming = pltpu.make_async_remote_copy(
            src_ref=tokens_ref.at[pl.ds(0, rows)],
            dst_ref=held.at[source],
            send_sem=send_sem.at[source],
            recv_sem=recv_sem.at[source],
            device_id={"inl": me_y, "xln": source},
            device_id_type=MESH,
        )
        from_self = (source == me_y) & diagonal

        @pl.when(jnp.logical_not(from_self))
        def _():
            incoming.wait_recv()

        @pl.when(from_self)
        def _():
            out_ref[source] = tokens_ref[pl.ds(pl.multiple_of(me_x * rows, rows), rows)]

        @pl.when(jnp.logical_not(from_self))
        def _():
            out_ref[source] = held[source]

    for copy, to_self in copies:

        @pl.when(jnp.logical_not(to_self))
        def _():
            copy.wait_send()


def gather_bricks(tokens):
    count = lax.axis_size("inl")
    rows = tokens.shape[0] // count
    shape = (lax.axis_size("xln"), rows, tokens.shape[1])
    return pl.pallas_call(
        gather_kernel,
        out_shape=jax.ShapeDtypeStruct(shape, tokens.dtype),
        in_specs=[pl.BlockSpec(memory_space=pltpu.VMEM)],
        out_specs=pl.BlockSpec(memory_space=pltpu.VMEM),
        scratch_shapes=[
            pltpu.VMEM(shape, tokens.dtype),
            pltpu.SemaphoreType.DMA((count,)),
            pltpu.SemaphoreType.DMA((count,)),
        ],
        compiler_params=pltpu.CompilerParams(collective_id=3, has_side_effects=True),
    )(tokens)


def local(skips, deconv_weight, norm_gain, conv_in, conv_out):
    inl_size = lax.axis_size("inl")
    tokens_here = skips[0]
    weight = deconv_weight[0]
    gains = norm_gain[0]
    channels = gains.shape[1]
    lines = tokens_here.shape[0] // (inl_size * PXD * GZ)
    cell_x = 2 * PXD
    cell_y = 2 * inl_size * lines
    cell_z = 2 * GZ
    moved = gather_bricks(tokens_here)
    upsampled = jnp.dot(
        moved.reshape(-1, tokens_here.shape[1]), weight, preferred_element_type=jnp.float32
    )
    brick = activate(upsampled, gains)
    field = (
        brick.reshape(cell_y // 2, PXD, GZ, 2, 2, 2, channels)
        .transpose(1, 3, 0, 4, 2, 5, 6)
        .reshape(cell_x, cell_y, cell_z, channels)
    )
    merged = conv_stage(field, conv_in[0], gains, True, 1)
    partial = conv_stage(merged, conv_out[0], gains, False, 2)
    outch = partial.shape[-1]
    rows = partial.reshape(-1, outch).T.reshape(outch, cell_x, cell_y * cell_z)
    return reduce_scatter(rows)


def solution(mesh):
    return jax.shard_map(
        local,
        mesh=mesh,
        in_specs=(
            P("section", ("inl", "xln"), None),
            P("section", None, None),
            P("section", None, None),
            P("section", None, None, None),
            P("section", None, None, None),
        ),
        out_specs=P("section", "inl", "xln"),
        check_vma=False,
    )
```

```python
import functools

import jax
import jax.numpy as jnp
from jax import lax
from jax.experimental import pallas as pl
from jax.experimental.pallas import tpu as pltpu
from jax.sharding import PartitionSpec as P

MESH = pl.DeviceIdType.MESH
PXD = 2
GZ = 8


epsilon = 1e-05


def normalize(values, scale):
    mean_square = jnp.mean(values * values, axis=-1, keepdims=True)
    return values * lax.rsqrt(mean_square + epsilon) * scale


def activate(upsampled, gains):
    width = gains.shape[1]
    shaped = upsampled.reshape(upsampled.shape[:-1] + (upsampled.shape[-1] // width, width))
    result = jax.nn.gelu(normalize(shaped, gains[0]), approximate=True).astype(jnp.bfloat16)
    return result.reshape(upsampled.shape)


def gelu_tanh(values):
    return 0.5 * values * (1.0 + jnp.tanh(0.7978845608028654 * (values + 0.044715 * (values * values * values))))


def reduce_scatter_kernel(count, parts_ref, out_ref, held, send_sem, recv_sem):
    me = lax.axis_index("section")
    barrier = pltpu.get_barrier_semaphore()
    for step in range(1, count):
        peer = lax.rem(me + step, count)
        pl.semaphore_signal(barrier, inc=1, device_id={"section": peer}, device_id_type=MESH)
    pl.semaphore_wait(barrier, count - 1)
    sends = []
    for step in range(1, count):
        peer = lax.rem(me + step, count)
        copy = pltpu.make_async_remote_copy(
            src_ref=parts_ref.at[peer],
            dst_ref=held.at[step],
            send_sem=send_sem.at[step],
            recv_sem=recv_sem.at[step],
            device_id={"section": peer},
            device_id_type=MESH,
        )
        copy.start()
        sends.append(copy)
    total = parts_ref[me]
    for step in range(1, count):
        sends[step - 1].wait_recv()
        total = total + held[step]
    for copy in sends:
        copy.wait_send()
    out_ref[...] = total.astype(out_ref.dtype)


def reduce_scatter(parts):
    count = lax.axis_size("section")
    shaped = parts.reshape((count, parts.shape[0] // count) + parts.shape[1:])
    return pl.pallas_call(
        functools.partial(reduce_scatter_kernel, count),
        out_shape=jax.ShapeDtypeStruct(shaped.shape[1:], jnp.bfloat16),
        in_specs=[pl.BlockSpec(memory_space=pltpu.VMEM)],
        out_specs=pl.BlockSpec(memory_space=pltpu.VMEM),
        scratch_shapes=[
            pltpu.VMEM(shaped.shape, jnp.float32),
            pltpu.SemaphoreType.DMA((count,)),
            pltpu.SemaphoreType.DMA((count,)),
        ],
        compiler_params=pltpu.CompilerParams(collective_id=0, has_side_effects=True),
    )(shaped)


def send_groups(me_x, me_y, count):
    return [
        (me_x, me_y + 1, None),
        (me_x + 1, 0, (me_y == count - 1) & (me_x + 1 < count)),
        (me_x - 1, count + 1, (me_y == 0) & (me_x > 0)),
    ]


def gather_kernel(tokens_ref, out_ref, held, send_sem, recv_sem):
    count = lax.axis_size("inl")
    me_x, me_y = lax.axis_index("inl"), lax.axis_index("xln")
    rows = tokens_ref.shape[0] // count
    slots = out_ref.shape[0]
    one = jnp.int32(1)
    groups = send_groups(me_x, me_y, count)
    sources = [(me_y - 1, count - 1, me_y >= 1)]
    sources += [(me_y, other, None) for other in range(count)]
    sources += [(me_y + 1, 0, me_y + 1 < count)]

    def is_me(x, y):
        return (x == me_x) & (y == me_y)

    barrier = pltpu.get_barrier_semaphore()
    expected = jnp.int32(0)
    for column, _, exists in groups:
        live = True if exists is None else exists
        expected = expected + jnp.where(live, count, 0)
        for other in range(count):

            @pl.when(jnp.logical_and(live, jnp.logical_not(is_me(other, column))))
            def _():
                pl.semaphore_signal(barrier, inc=1, device_id={"inl": other, "xln": column}, device_id_type=MESH)

            expected = expected - jnp.where(jnp.logical_and(live, is_me(other, column)), one, 0)
    for source_x, source_y, exists in sources:
        live = True if exists is None else exists
        mine = jnp.logical_and(live, is_me(source_x, source_y))
        expected = expected + jnp.where(jnp.logical_and(live, jnp.logical_not(mine)), one, 0)

        @pl.when(jnp.logical_and(live, jnp.logical_not(mine)))
        def _():
            pl.semaphore_signal(barrier, inc=1, device_id={"inl": source_x, "xln": source_y}, device_id_type=MESH)

    pl.semaphore_wait(barrier, expected)
    copies = []
    for index, (column, slot, exists) in enumerate(groups):
        live = True if exists is None else exists
        for other in range(count):
            copy = pltpu.make_async_remote_copy(
                src_ref=tokens_ref.at[pl.ds(other * rows, rows)],
                dst_ref=held.at[slot],
                send_sem=send_sem.at[index * count + other],
                recv_sem=recv_sem.at[slot],
                device_id={"inl": other, "xln": column},
                device_id_type=MESH,
            )
            remote = jnp.logical_and(live, jnp.logical_not(is_me(other, column)))

            @pl.when(remote)
            def _():
                copy.start()

            copies.append((copy, remote))
    for slot, (source_x, source_y, exists) in enumerate(sources):
        live = True if exists is None else exists
        mine = jnp.logical_and(live, is_me(source_x, source_y))
        remote = jnp.logical_and(live, jnp.logical_not(mine))
        incoming = pltpu.make_async_remote_copy(
            src_ref=tokens_ref.at[pl.ds(0, rows)],
            dst_ref=held.at[slot],
            send_sem=send_sem.at[0],
            recv_sem=recv_sem.at[slot],
            device_id={"inl": source_x, "xln": source_y},
            device_id_type=MESH,
        )

        @pl.when(remote)
        def _():
            incoming.wait_recv()
            out_ref[slot] = held[slot]

        @pl.when(mine)
        def _():
            out_ref[slot] = tokens_ref[pl.ds(pl.multiple_of(me_x * rows, rows), rows)]

        @pl.when(jnp.logical_not(live))
        def _():
            out_ref[slot] = jnp.zeros(out_ref.shape[1:], out_ref.dtype)

    for copy, remote in copies:

        @pl.when(remote)
        def _():
            copy.wait_send()


def gather_bricks(tokens):
    count = lax.axis_size("inl")
    rows = tokens.shape[0] // count
    shape = (lax.axis_size("xln") + 2, rows, tokens.shape[1])
    return pl.pallas_call(
        gather_kernel,
        out_shape=jax.ShapeDtypeStruct(shape, tokens.dtype),
        in_specs=[pl.BlockSpec(memory_space=pltpu.VMEM)],
        out_specs=pl.BlockSpec(memory_space=pltpu.VMEM),
        scratch_shapes=[
            pltpu.VMEM(shape, tokens.dtype),
            pltpu.SemaphoreType.DMA((3 * count,)),
            pltpu.SemaphoreType.DMA((shape[0],)),
        ],
        compiler_params=pltpu.CompilerParams(collective_id=3, has_side_effects=True),
    )(tokens)


def halo_x(field_ref, held, send_sem, recv_sem):
    nx = field_ref.shape[0]
    count = lax.axis_size("inl")
    me = lax.axis_index("inl")
    barrier = pltpu.get_barrier_semaphore()
    for step in (-1, 1):
        pl.semaphore_signal(
            barrier, inc=1, device_id={"inl": lax.rem(me + step + count, count)}, device_id_type=MESH
        )
    pl.semaphore_wait(barrier, 2)
    copies = []
    for index, step in enumerate((-1, 1)):
        source, target = (0, nx + 1) if step < 0 else (nx - 1, 0)
        copy = pltpu.make_async_remote_copy(
            src_ref=field_ref.at[source : source + 1],
            dst_ref=held.at[target : target + 1],
            send_sem=send_sem.at[index],
            recv_sem=recv_sem.at[index],
            device_id={"inl": me + step},
            device_id_type=MESH,
        )
        sends = (me + step >= 0) & (me + step < count)
        gets = (me - step >= 0) & (me - step < count)

        @pl.when(sends)
        def _():
            copy.start()

        @pl.when(jnp.logical_not(gets))
        def _():
            held[target : target + 1] = jnp.zeros((1,) + held.shape[1:], held.dtype)

        copies.append((copy, sends, gets))
    held[1 : nx + 1] = field_ref[...]
    for copy, sends, gets in copies:

        @pl.when(gets)
        def _():
            copy.wait_recv()

        @pl.when(sends)
        def _():
            copy.wait_send()


def conv_kernel(
    residual, field_ref, kernel_ref, gains_ref, out_ref, held, shifted, send_sem, recv_sem
):
    halo_x(field_ref, held, send_sem, recv_sem)
    nx, ny_in, nz, channels = field_ref.shape
    ny = ny_in - 2
    cells = nx * ny * nz
    width = shifted.shape[2]
    parts = []
    for offset_z in range(3):
        part = jnp.zeros((cells, width), jnp.float32)
        for offset_x in range(3):
            for offset_y in range(3):
                window = held[offset_x : offset_x + nx, offset_y : offset_y + ny].reshape(cells, channels)
                tap = kernel_ref[(offset_x * 3 + offset_y) * 3 + offset_z]
                if residual:
                    part = part + jnp.dot(window, tap, preferred_element_type=jnp.float32)
                else:
                    part = part + lax.dot_general(
                        window, tap, (((1,), (1,)), ((), ())), preferred_element_type=jnp.float32
                    )
        parts.append(part.reshape(nx * ny, nz, width))
    edge = jnp.zeros((nx * ny, 1, width), jnp.float32)
    shifted[:, 0:1] = edge
    shifted[:, nz + 1 : nz + 2] = edge
    shifted[:, 1 : nz + 1] = parts[0]
    total = parts[1] + shifted[:, 0:nz]
    shifted[:, 1 : nz + 1] = parts[2]
    total = total + shifted[:, 2 : nz + 2]
    if residual:
        mean_square = jnp.mean(total * total, axis=-1, keepdims=True)
        normed = total * lax.rsqrt(mean_square + epsilon) * gains_ref[1:2, :]
        base = field_ref[:, 1 : ny + 1].reshape(nx * ny, nz, channels).astype(jnp.float32)
        mixed = gelu_tanh(normed + base).reshape(nx, ny, nz, channels)
        me_y, count_y = lax.axis_index("xln"), lax.axis_size("xln")
        row = lax.broadcasted_iota(jnp.int32, mixed.shape, 1)
        outside = ((row == 0) & (me_y == 0)) | ((row == ny - 1) & (me_y == count_y - 1))
        out_ref[...] = jnp.where(outside, 0.0, mixed).astype(out_ref.dtype)
    else:
        out_ref[...] = total.reshape(out_ref.shape)


def conv_stage(field, kernel, gains, residual, collective):
    nx, ny_in, nz, channels = field.shape
    width = kernel.shape[2] if residual else kernel.shape[1]
    padded = (nx + 2, ny_in, nz, channels)
    ny = ny_in - 2
    dtype = jnp.bfloat16 if residual else jnp.float32
    return pl.pallas_call(
        functools.partial(conv_kernel, residual),
        out_shape=jax.ShapeDtypeStruct((nx, ny, nz, width), dtype),
        in_specs=[pl.BlockSpec(memory_space=pltpu.VMEM)] * 3,
        out_specs=pl.BlockSpec(memory_space=pltpu.VMEM),
        scratch_shapes=[
            pltpu.VMEM(padded, field.dtype),
            pltpu.VMEM((nx * ny, nz + 2, width), jnp.float32),
            pltpu.SemaphoreType.DMA((2,)),
            pltpu.SemaphoreType.DMA((2,)),
        ],
        compiler_params=pltpu.CompilerParams(collective_id=collective, has_side_effects=True),
    )(field, kernel, gains)


def local(skips, deconv_weight, norm_gain, conv_in, conv_out):
    inl_size = lax.axis_size("inl")
    tokens_here = skips[0]
    weight = deconv_weight[0]
    gains = norm_gain[0]
    channels = gains.shape[1]
    cell_x = 2 * PXD
    cell_y = 2 * lax.axis_size("xln")
    cell_z = 2 * GZ
    assert tokens_here.shape[0] == inl_size * PXD * GZ
    moved = gather_bricks(tokens_here)
    lines = moved.shape[0]
    upsampled = jnp.dot(
        moved.reshape(-1, tokens_here.shape[1]), weight, preferred_element_type=jnp.float32
    )
    brick = activate(upsampled, gains)
    field = (
        brick.reshape(lines, PXD, GZ, 2, 2, 2, channels)
        .transpose(1, 3, 0, 4, 2, 5, 6)
        .reshape(cell_x, 2 * lines, cell_z, channels)
    )
    merged = conv_stage(field, conv_in[0], gains, True, 1)
    partial = conv_stage(merged, conv_out[0], gains, False, 2)
    outch = partial.shape[-1]
    rows = partial.reshape(-1, outch).T.reshape(outch, cell_x, cell_y * cell_z)
    return reduce_scatter(rows)


def solution(mesh):
    return jax.shard_map(
        local,
        mesh=mesh,
        in_specs=(
            P("section", ("inl", "xln"), None),
            P("section", None, None),
            P("section", None, None),
            P("section", None, None, None),
            P("section", None, None, None),
        ),
        out_specs=P("section", "inl", "xln"),
        check_vma=False,
    )
```

```python
import functools

import jax
import jax.numpy as jnp
from jax import lax
from jax.experimental import pallas as pl
from jax.experimental.pallas import tpu as pltpu
from jax.sharding import PartitionSpec as P

MESH = pl.DeviceIdType.MESH
PXD = 2
GZ = 8


epsilon = 1e-05


def normalize(values, scale):
    mean_square = jnp.mean(values * values, axis=-1, keepdims=True)
    return values * lax.rsqrt(mean_square + epsilon) * scale


def activate(upsampled, gains):
    width = gains.shape[1]
    shaped = upsampled.reshape(upsampled.shape[:-1] + (upsampled.shape[-1] // width, width))
    result = jax.nn.gelu(normalize(shaped, gains[0]), approximate=True).astype(jnp.bfloat16)
    return result.reshape(upsampled.shape)


def gelu_tanh(values):
    return 0.5 * values * (1.0 + jnp.tanh(0.7978845608028654 * (values + 0.044715 * (values * values * values))))


def reduce_scatter_kernel(count, parts_ref, out_ref, held, send_sem, recv_sem):
    me = lax.axis_index("section")
    barrier = pltpu.get_barrier_semaphore()
    for step in range(1, count):
        peer = lax.rem(me + step, count)
        pl.semaphore_signal(barrier, inc=1, device_id={"section": peer}, device_id_type=MESH)
    pl.semaphore_wait(barrier, count - 1)
    sends = []
    for step in range(1, count):
        peer = lax.rem(me + step, count)
        copy = pltpu.make_async_remote_copy(
            src_ref=parts_ref.at[peer],
            dst_ref=held.at[step],
            send_sem=send_sem.at[step],
            recv_sem=recv_sem.at[step],
            device_id={"section": peer},
            device_id_type=MESH,
        )
        copy.start()
        sends.append(copy)
    total = parts_ref[me]
    for step in range(1, count):
        sends[step - 1].wait_recv()
        total = total + held[step]
    for copy in sends:
        copy.wait_send()
    out_ref[...] = total.astype(out_ref.dtype)


def reduce_scatter(parts):
    count = lax.axis_size("section")
    shaped = parts.reshape((count, parts.shape[0] // count) + parts.shape[1:])
    return pl.pallas_call(
        functools.partial(reduce_scatter_kernel, count),
        out_shape=jax.ShapeDtypeStruct(shaped.shape[1:], jnp.bfloat16),
        in_specs=[pl.BlockSpec(memory_space=pltpu.VMEM)],
        out_specs=pl.BlockSpec(memory_space=pltpu.VMEM),
        scratch_shapes=[
            pltpu.VMEM(shaped.shape, jnp.float32),
            pltpu.SemaphoreType.DMA((count,)),
            pltpu.SemaphoreType.DMA((count,)),
        ],
        compiler_params=pltpu.CompilerParams(collective_id=0, has_side_effects=True),
    )(shaped)


def send_groups(me_x, me_y, count):
    return [
        (me_x, me_y + 1, None),
        (me_x + 1, 0, (me_y == count - 1) & (me_x + 1 < count)),
        (me_x - 1, count + 1, (me_y == 0) & (me_x > 0)),
    ]


def gather_kernel(tokens_ref, weight_hbm, gains_ref, out_ref, weight, field, held, send_sem, recv_sem, weight_sem):
    count = lax.axis_size("inl")
    me_x, me_y = lax.axis_index("inl"), lax.axis_index("xln")
    rows = tokens_ref.shape[0] // count
    width = gains_ref.shape[1]
    one = jnp.int32(1)
    loading = pltpu.make_async_copy(weight_hbm, weight, weight_sem)
    loading.start()
    groups = send_groups(me_x, me_y, count)
    sources = [(me_y - 1, count - 1, me_y >= 1)]
    sources += [(me_y, other, None) for other in range(count)]
    sources += [(me_y + 1, 0, me_y + 1 < count)]

    def is_me(x, y):
        return (x == me_x) & (y == me_y)

    barrier = pltpu.get_barrier_semaphore()
    expected = jnp.int32(0)
    for column, _, exists in groups:
        live = True if exists is None else exists
        expected = expected + jnp.where(live, count, 0)
        for other in range(count):

            @pl.when(jnp.logical_and(live, jnp.logical_not(is_me(other, column))))
            def _():
                pl.semaphore_signal(barrier, inc=1, device_id={"inl": other, "xln": column}, device_id_type=MESH)

            expected = expected - jnp.where(jnp.logical_and(live, is_me(other, column)), one, 0)
    for source_x, source_y, exists in sources:
        live = True if exists is None else exists
        mine = jnp.logical_and(live, is_me(source_x, source_y))
        expected = expected + jnp.where(jnp.logical_and(live, jnp.logical_not(mine)), one, 0)

        @pl.when(jnp.logical_and(live, jnp.logical_not(mine)))
        def _():
            pl.semaphore_signal(barrier, inc=1, device_id={"inl": source_x, "xln": source_y}, device_id_type=MESH)

    loading.wait()
    upsampled = jnp.dot(tokens_ref[...], weight[...], preferred_element_type=jnp.float32)
    for group in range(upsampled.shape[1] // width):
        part = upsampled[:, group * width : (group + 1) * width]
        mean_square = jnp.mean(part * part, axis=-1, keepdims=True)
        normed = part * lax.rsqrt(mean_square + epsilon) * gains_ref[0:1, :]
        field[:, group * width : (group + 1) * width] = gelu_tanh(normed).astype(field.dtype)
    pl.semaphore_wait(barrier, expected)
    copies = []
    for index, (column, slot, exists) in enumerate(groups):
        live = True if exists is None else exists
        for other in range(count):
            copy = pltpu.make_async_remote_copy(
                src_ref=field.at[pl.ds(other * rows, rows)],
                dst_ref=held.at[slot],
                send_sem=send_sem.at[index * count + other],
                recv_sem=recv_sem.at[slot],
                device_id={"inl": other, "xln": column},
                device_id_type=MESH,
            )
            remote = jnp.logical_and(live, jnp.logical_not(is_me(other, column)))

            @pl.when(remote)
            def _():
                copy.start()

            copies.append((copy, remote))
    for slot, (source_x, source_y, exists) in enumerate(sources):
        live = True if exists is None else exists
        mine = jnp.logical_and(live, is_me(source_x, source_y))
        remote = jnp.logical_and(live, jnp.logical_not(mine))
        incoming = pltpu.make_async_remote_copy(
            src_ref=field.at[pl.ds(0, rows)],
            dst_ref=held.at[slot],
            send_sem=send_sem.at[0],
            recv_sem=recv_sem.at[slot],
            device_id={"inl": source_x, "xln": source_y},
            device_id_type=MESH,
        )

        @pl.when(remote)
        def _():
            incoming.wait_recv()
            out_ref[slot] = held[slot]

        @pl.when(mine)
        def _():
            out_ref[slot] = field[pl.ds(pl.multiple_of(me_x * rows, rows), rows)]

        @pl.when(jnp.logical_not(live))
        def _():
            out_ref[slot] = jnp.zeros(out_ref.shape[1:], out_ref.dtype)

    for copy, remote in copies:

        @pl.when(remote)
        def _():
            copy.wait_send()


def gather_bricks(tokens, weight, gains):
    count = lax.axis_size("inl")
    rows = tokens.shape[0] // count
    shape = (lax.axis_size("xln") + 2, rows, weight.shape[1])
    return pl.pallas_call(
        gather_kernel,
        out_shape=jax.ShapeDtypeStruct(shape, jnp.bfloat16),
        in_specs=[
            pl.BlockSpec(memory_space=pltpu.VMEM),
            pl.BlockSpec(memory_space=pl.ANY),
            pl.BlockSpec(memory_space=pltpu.VMEM),
        ],
        out_specs=pl.BlockSpec(memory_space=pltpu.VMEM),
        scratch_shapes=[
            pltpu.VMEM(weight.shape, weight.dtype),
            pltpu.VMEM((tokens.shape[0], weight.shape[1]), jnp.bfloat16),
            pltpu.VMEM(shape, jnp.bfloat16),
            pltpu.SemaphoreType.DMA((3 * count,)),
            pltpu.SemaphoreType.DMA((shape[0],)),
            pltpu.SemaphoreType.DMA(()),
        ],
        compiler_params=pltpu.CompilerParams(collective_id=3, has_side_effects=True),
    )(tokens, weight, gains)


def halo_x(field_ref, held, send_sem, recv_sem):
    nx = field_ref.shape[0]
    count = lax.axis_size("inl")
    me = lax.axis_index("inl")
    barrier = pltpu.get_barrier_semaphore()
    for step in (-1, 1):
        pl.semaphore_signal(
            barrier, inc=1, device_id={"inl": lax.rem(me + step + count, count)}, device_id_type=MESH
        )
    pl.semaphore_wait(barrier, 2)
    copies = []
    for index, step in enumerate((-1, 1)):
        source, target = (0, nx + 1) if step < 0 else (nx - 1, 0)
        copy = pltpu.make_async_remote_copy(
            src_ref=field_ref.at[source : source + 1],
            dst_ref=held.at[target : target + 1],
            send_sem=send_sem.at[index],
            recv_sem=recv_sem.at[index],
            device_id={"inl": me + step},
            device_id_type=MESH,
        )
        sends = (me + step >= 0) & (me + step < count)
        gets = (me - step >= 0) & (me - step < count)

        @pl.when(sends)
        def _():
            copy.start()

        @pl.when(jnp.logical_not(gets))
        def _():
            held[target : target + 1] = jnp.zeros((1,) + held.shape[1:], held.dtype)

        copies.append((copy, sends, gets))
    held[1 : nx + 1] = field_ref[...]
    for copy, sends, gets in copies:

        @pl.when(gets)
        def _():
            copy.wait_recv()

        @pl.when(sends)
        def _():
            copy.wait_send()


def conv_kernel(
    residual, field_ref, kernel_ref, gains_ref, out_ref, held, shifted, send_sem, recv_sem
):
    halo_x(field_ref, held, send_sem, recv_sem)
    nx, ny_in, nz, channels = field_ref.shape
    ny = ny_in - 2
    cells = nx * ny * nz
    width = shifted.shape[2]
    parts = []
    for offset_z in range(3):
        part = jnp.zeros((cells, width), jnp.float32)
        for offset_x in range(3):
            for offset_y in range(3):
                window = held[offset_x : offset_x + nx, offset_y : offset_y + ny].reshape(cells, channels)
                tap = kernel_ref[(offset_x * 3 + offset_y) * 3 + offset_z]
                if residual:
                    part = part + jnp.dot(window, tap, preferred_element_type=jnp.float32)
                else:
                    part = part + lax.dot_general(
                        window, tap, (((1,), (1,)), ((), ())), preferred_element_type=jnp.float32
                    )
        parts.append(part.reshape(nx * ny, nz, width))
    edge = jnp.zeros((nx * ny, 1, width), jnp.float32)
    shifted[:, 0:1] = edge
    shifted[:, nz + 1 : nz + 2] = edge
    shifted[:, 1 : nz + 1] = parts[0]
    total = parts[1] + shifted[:, 0:nz]
    shifted[:, 1 : nz + 1] = parts[2]
    total = total + shifted[:, 2 : nz + 2]
    if residual:
        mean_square = jnp.mean(total * total, axis=-1, keepdims=True)
        normed = total * lax.rsqrt(mean_square + epsilon) * gains_ref[1:2, :]
        base = field_ref[:, 1 : ny + 1].reshape(nx * ny, nz, channels).astype(jnp.float32)
        mixed = gelu_tanh(normed + base).reshape(nx, ny, nz, channels)
        me_y, count_y = lax.axis_index("xln"), lax.axis_size("xln")
        row = lax.broadcasted_iota(jnp.int32, mixed.shape, 1)
        outside = ((row == 0) & (me_y == 0)) | ((row == ny - 1) & (me_y == count_y - 1))
        out_ref[...] = jnp.where(outside, 0.0, mixed).astype(out_ref.dtype)
    else:
        out_ref[...] = total.reshape(out_ref.shape)


def conv_stage(field, kernel, gains, residual, collective):
    nx, ny_in, nz, channels = field.shape
    width = kernel.shape[2] if residual else kernel.shape[1]
    padded = (nx + 2, ny_in, nz, channels)
    ny = ny_in - 2
    dtype = jnp.bfloat16 if residual else jnp.float32
    return pl.pallas_call(
        functools.partial(conv_kernel, residual),
        out_shape=jax.ShapeDtypeStruct((nx, ny, nz, width), dtype),
        in_specs=[pl.BlockSpec(memory_space=pltpu.VMEM)] * 3,
        out_specs=pl.BlockSpec(memory_space=pltpu.VMEM),
        scratch_shapes=[
            pltpu.VMEM(padded, field.dtype),
            pltpu.VMEM((nx * ny, nz + 2, width), jnp.float32),
            pltpu.SemaphoreType.DMA((2,)),
            pltpu.SemaphoreType.DMA((2,)),
        ],
        compiler_params=pltpu.CompilerParams(collective_id=collective, has_side_effects=True),
    )(field, kernel, gains)


def local(skips, deconv_weight, norm_gain, conv_in, conv_out):
    inl_size = lax.axis_size("inl")
    tokens_here = skips[0]
    weight = deconv_weight[0]
    gains = norm_gain[0]
    channels = gains.shape[1]
    cell_x = 2 * PXD
    cell_y = 2 * lax.axis_size("xln")
    cell_z = 2 * GZ
    assert tokens_here.shape[0] == inl_size * PXD * GZ
    brick = gather_bricks(tokens_here, weight, gains)
    lines = brick.shape[0]
    field = (
        brick.reshape(lines, PXD, GZ, 2, 2, 2, channels)
        .transpose(1, 3, 0, 4, 2, 5, 6)
        .reshape(cell_x, 2 * lines, cell_z, channels)
    )
    merged = conv_stage(field, conv_in[0], gains, True, 1)
    partial = conv_stage(merged, conv_out[0], gains, False, 2)
    outch = partial.shape[-1]
    rows = partial.reshape(-1, outch).T.reshape(outch, cell_x, cell_y * cell_z)
    return reduce_scatter(rows)


def solution(mesh):
    return jax.shard_map(
        local,
        mesh=mesh,
        in_specs=(
            P("section", ("inl", "xln"), None),
            P("section", None, None),
            P("section", None, None),
            P("section", None, None, None),
            P("section", None, None, None),
        ),
        out_specs=P("section", "inl", "xln"),
        check_vma=False,
    )
```

```python
import functools

import jax
import jax.numpy as jnp
from jax import lax
from jax.experimental import pallas as pl
from jax.experimental.pallas import tpu as pltpu
from jax.sharding import PartitionSpec as P

MESH = pl.DeviceIdType.MESH
PXD = 2
GZ = 8


epsilon = 1e-05


def normalize(values, scale):
    mean_square = jnp.mean(values * values, axis=-1, keepdims=True)
    return values * lax.rsqrt(mean_square + epsilon) * scale


def activate(upsampled, gains):
    width = gains.shape[1]
    shaped = upsampled.reshape(upsampled.shape[:-1] + (upsampled.shape[-1] // width, width))
    result = jax.nn.gelu(normalize(shaped, gains[0]), approximate=True).astype(jnp.bfloat16)
    return result.reshape(upsampled.shape)


def gelu_tanh(values):
    return 0.5 * values * (1.0 + jnp.tanh(0.7978845608028654 * (values + 0.044715 * (values * values * values))))


def reduce_scatter_kernel(count, parts_ref, out_ref, held, send_sem, recv_sem):
    me = lax.axis_index("section")
    barrier = pltpu.get_barrier_semaphore()
    for step in range(1, count):
        peer = lax.rem(me + step, count)
        pl.semaphore_signal(barrier, inc=1, device_id={"section": peer}, device_id_type=MESH)
    pl.semaphore_wait(barrier, count - 1)
    sends = []
    for step in range(1, count):
        peer = lax.rem(me + step, count)
        copy = pltpu.make_async_remote_copy(
            src_ref=parts_ref.at[peer],
            dst_ref=held.at[step],
            send_sem=send_sem.at[step],
            recv_sem=recv_sem.at[step],
            device_id={"section": peer},
            device_id_type=MESH,
        )
        copy.start()
        sends.append(copy)
    total = parts_ref[me]
    for step in range(1, count):
        sends[step - 1].wait_recv()
        total = total + held[step]
    for copy in sends:
        copy.wait_send()
    out_ref[...] = total.astype(out_ref.dtype)


def reduce_scatter(parts):
    count = lax.axis_size("section")
    shaped = parts.reshape((count, parts.shape[0] // count) + parts.shape[1:])
    return pl.pallas_call(
        functools.partial(reduce_scatter_kernel, count),
        out_shape=jax.ShapeDtypeStruct(shaped.shape[1:], jnp.bfloat16),
        in_specs=[pl.BlockSpec(memory_space=pltpu.VMEM)],
        out_specs=pl.BlockSpec(memory_space=pltpu.VMEM),
        scratch_shapes=[
            pltpu.VMEM(shaped.shape, jnp.float32),
            pltpu.SemaphoreType.DMA((count,)),
            pltpu.SemaphoreType.DMA((count,)),
        ],
        compiler_params=pltpu.CompilerParams(collective_id=0, has_side_effects=True),
    )(shaped)


def send_groups(me_x, me_y, count):
    return [
        (me_x, me_y + 1, None),
        (me_x + 1, 0, (me_y == count - 1) & (me_x + 1 < count)),
        (me_x - 1, count + 1, (me_y == 0) & (me_x > 0)),
    ]


def gather_kernel(tokens_ref, weight_hbm, gains_ref, out_ref, weight, field, held, send_sem, recv_sem, weight_sem):
    count = lax.axis_size("inl")
    me_x, me_y = lax.axis_index("inl"), lax.axis_index("xln")
    rows = tokens_ref.shape[0] // count
    width = gains_ref.shape[1]
    one = jnp.int32(1)
    loading = pltpu.make_async_copy(weight_hbm, weight, weight_sem)
    loading.start()
    groups = send_groups(me_x, me_y, count)
    sources = [(me_y - 1, count - 1, me_y >= 1)]
    sources += [(me_y, other, None) for other in range(count)]
    sources += [(me_y + 1, 0, me_y + 1 < count)]

    def is_me(x, y):
        return (x == me_x) & (y == me_y)

    barrier = pltpu.get_barrier_semaphore()
    expected = jnp.int32(0)
    for column, _, exists in groups:
        live = True if exists is None else exists
        expected = expected + jnp.where(live, count, 0)
        for other in range(count):

            @pl.when(jnp.logical_and(live, jnp.logical_not(is_me(other, column))))
            def _():
                pl.semaphore_signal(barrier, inc=1, device_id={"inl": other, "xln": column}, device_id_type=MESH)

            expected = expected - jnp.where(jnp.logical_and(live, is_me(other, column)), one, 0)
    for source_x, source_y, exists in sources:
        live = True if exists is None else exists
        mine = jnp.logical_and(live, is_me(source_x, source_y))
        expected = expected + jnp.where(jnp.logical_and(live, jnp.logical_not(mine)), one, 0)

        @pl.when(jnp.logical_and(live, jnp.logical_not(mine)))
        def _():
            pl.semaphore_signal(barrier, inc=1, device_id={"inl": source_x, "xln": source_y}, device_id_type=MESH)

    loading.wait()
    upsampled = jnp.dot(tokens_ref[...], weight[...], preferred_element_type=jnp.float32)
    for group in range(upsampled.shape[1] // width):
        part = upsampled[:, group * width : (group + 1) * width]
        mean_square = jnp.mean(part * part, axis=-1, keepdims=True)
        normed = part * lax.rsqrt(mean_square + epsilon) * gains_ref[0:1, :]
        field[:, group * width : (group + 1) * width] = gelu_tanh(normed).astype(field.dtype)
    pl.semaphore_wait(barrier, expected)
    copies = []
    for index, (column, slot, exists) in enumerate(groups):
        live = True if exists is None else exists
        for other in range(count):
            copy = pltpu.make_async_remote_copy(
                src_ref=field.at[pl.ds(other * rows, rows)],
                dst_ref=held.at[slot],
                send_sem=send_sem.at[index * count + other],
                recv_sem=recv_sem.at[slot],
                device_id={"inl": other, "xln": column},
                device_id_type=MESH,
            )
            remote = jnp.logical_and(live, jnp.logical_not(is_me(other, column)))

            @pl.when(remote)
            def _():
                copy.start()

            copies.append((copy, remote))
    for slot, (source_x, source_y, exists) in enumerate(sources):
        live = True if exists is None else exists
        mine = jnp.logical_and(live, is_me(source_x, source_y))
        remote = jnp.logical_and(live, jnp.logical_not(mine))
        incoming = pltpu.make_async_remote_copy(
            src_ref=field.at[pl.ds(0, rows)],
            dst_ref=held.at[slot],
            send_sem=send_sem.at[0],
            recv_sem=recv_sem.at[slot],
            device_id={"inl": source_x, "xln": source_y},
            device_id_type=MESH,
        )

        @pl.when(remote)
        def _():
            incoming.wait_recv()
            out_ref[slot] = held[slot]

        @pl.when(mine)
        def _():
            out_ref[slot] = field[pl.ds(pl.multiple_of(me_x * rows, rows), rows)]

        @pl.when(jnp.logical_not(live))
        def _():
            out_ref[slot] = jnp.zeros(out_ref.shape[1:], out_ref.dtype)

    for copy, remote in copies:

        @pl.when(remote)
        def _():
            copy.wait_send()


def gather_bricks(tokens, weight, gains):
    count = lax.axis_size("inl")
    rows = tokens.shape[0] // count
    shape = (lax.axis_size("xln") + 2, rows, weight.shape[1])
    return pl.pallas_call(
        gather_kernel,
        out_shape=jax.ShapeDtypeStruct(shape, jnp.bfloat16),
        in_specs=[
            pl.BlockSpec(memory_space=pltpu.VMEM),
            pl.BlockSpec(memory_space=pl.ANY),
            pl.BlockSpec(memory_space=pltpu.VMEM),
        ],
        out_specs=pl.BlockSpec(memory_space=pltpu.VMEM),
        scratch_shapes=[
            pltpu.VMEM(weight.shape, weight.dtype),
            pltpu.VMEM((tokens.shape[0], weight.shape[1]), jnp.bfloat16),
            pltpu.VMEM(shape, jnp.bfloat16),
            pltpu.SemaphoreType.DMA((3 * count,)),
            pltpu.SemaphoreType.DMA((shape[0],)),
            pltpu.SemaphoreType.DMA(()),
        ],
        compiler_params=pltpu.CompilerParams(collective_id=3, has_side_effects=True),
    )(tokens, weight, gains)


def halo_x(field_ref, held, send_sem, recv_sem, others=0):
    nx = field_ref.shape[0]
    count = lax.axis_size("inl")
    me = lax.axis_index("inl")
    barrier = pltpu.get_barrier_semaphore()
    for step in (-1, 1):
        pl.semaphore_signal(
            barrier, inc=1, device_id={"inl": lax.rem(me + step + count, count)}, device_id_type=MESH
        )
    pl.semaphore_wait(barrier, 2 + others)
    copies = []
    for index, step in enumerate((-1, 1)):
        source, target = (0, nx + 1) if step < 0 else (nx - 1, 0)
        copy = pltpu.make_async_remote_copy(
            src_ref=field_ref.at[source : source + 1],
            dst_ref=held.at[target : target + 1],
            send_sem=send_sem.at[index],
            recv_sem=recv_sem.at[index],
            device_id={"inl": me + step},
            device_id_type=MESH,
        )
        sends = (me + step >= 0) & (me + step < count)
        gets = (me - step >= 0) & (me - step < count)

        @pl.when(sends)
        def _():
            copy.start()

        @pl.when(jnp.logical_not(gets))
        def _():
            held[target : target + 1] = jnp.zeros((1,) + held.shape[1:], held.dtype)

        copies.append((copy, sends, gets))
    held[1 : nx + 1] = field_ref[...]
    for copy, sends, gets in copies:

        @pl.when(gets)
        def _():
            copy.wait_recv()

        @pl.when(sends)
        def _():
            copy.wait_send()


def conv_kernel(
    residual, field_ref, kernel_ref, gains_ref, out_ref, held, shifted, send_sem, recv_sem
):
    halo_x(field_ref, held, send_sem, recv_sem)
    nx, ny_in, nz, channels = field_ref.shape
    ny = ny_in - 2
    cells = nx * ny * nz
    width = shifted.shape[2]
    parts = []
    for offset_z in range(3):
        part = jnp.zeros((cells, width), jnp.float32)
        for offset_x in range(3):
            for offset_y in range(3):
                window = held[offset_x : offset_x + nx, offset_y : offset_y + ny].reshape(cells, channels)
                tap = kernel_ref[(offset_x * 3 + offset_y) * 3 + offset_z]
                if residual:
                    part = part + jnp.dot(window, tap, preferred_element_type=jnp.float32)
                else:
                    part = part + lax.dot_general(
                        window, tap, (((1,), (1,)), ((), ())), preferred_element_type=jnp.float32
                    )
        parts.append(part.reshape(nx * ny, nz, width))
    edge = jnp.zeros((nx * ny, 1, width), jnp.float32)
    shifted[:, 0:1] = edge
    shifted[:, nz + 1 : nz + 2] = edge
    shifted[:, 1 : nz + 1] = parts[0]
    total = parts[1] + shifted[:, 0:nz]
    shifted[:, 1 : nz + 1] = parts[2]
    total = total + shifted[:, 2 : nz + 2]
    if residual:
        mean_square = jnp.mean(total * total, axis=-1, keepdims=True)
        normed = total * lax.rsqrt(mean_square + epsilon) * gains_ref[1:2, :]
        base = field_ref[:, 1 : ny + 1].reshape(nx * ny, nz, channels).astype(jnp.float32)
        mixed = gelu_tanh(normed + base).reshape(nx, ny, nz, channels)
        me_y, count_y = lax.axis_index("xln"), lax.axis_size("xln")
        row = lax.broadcasted_iota(jnp.int32, mixed.shape, 1)
        outside = ((row == 0) & (me_y == 0)) | ((row == ny - 1) & (me_y == count_y - 1))
        out_ref[...] = jnp.where(outside, 0.0, mixed).astype(out_ref.dtype)
    else:
        out_ref[...] = total.reshape(out_ref.shape)


def conv_stage(field, kernel, gains, residual, collective):
    nx, ny_in, nz, channels = field.shape
    width = kernel.shape[2] if residual else kernel.shape[1]
    padded = (nx + 2, ny_in, nz, channels)
    ny = ny_in - 2
    dtype = jnp.bfloat16 if residual else jnp.float32
    return pl.pallas_call(
        functools.partial(conv_kernel, residual),
        out_shape=jax.ShapeDtypeStruct((nx, ny, nz, width), dtype),
        in_specs=[pl.BlockSpec(memory_space=pltpu.VMEM)] * 3,
        out_specs=pl.BlockSpec(memory_space=pltpu.VMEM),
        scratch_shapes=[
            pltpu.VMEM(padded, field.dtype),
            pltpu.VMEM((nx * ny, nz + 2, width), jnp.float32),
            pltpu.SemaphoreType.DMA((2,)),
            pltpu.SemaphoreType.DMA((2,)),
        ],
        compiler_params=pltpu.CompilerParams(collective_id=collective, has_side_effects=True),
    )(field, kernel, gains)


def final_kernel(field_ref, kernel_ref, out_ref, held, spread, shifted, parts, inbox, send_sem, recv_sem, sum_send, sum_recv):
    count = lax.axis_size("section")
    me = lax.axis_index("section")
    for step in range(1, count):
        pl.semaphore_signal(
            pltpu.get_barrier_semaphore(),
            inc=1,
            device_id={"section": lax.rem(me + step, count)},
            device_id_type=MESH,
        )
    halo_x(field_ref, held, send_sem, recv_sem, count - 1)
    nx, ny_in, nz, channels = field_ref.shape
    ny = ny_in - 2
    cells = nx * ny * nz
    outch = kernel_ref.shape[1]
    planes = (nx + 2) * ny_in
    edge = jnp.zeros((planes, 1, channels), jnp.float32)
    shifted[:, 0:1] = edge
    shifted[:, nz + 1 : nz + 2] = edge
    shifted[:, 1 : nz + 1] = held[...].reshape(planes, nz, channels).astype(jnp.float32)
    spread[0] = shifted[:, 0:nz].astype(spread.dtype).reshape(held.shape)
    spread[1] = held[...]
    spread[2] = shifted[:, 2 : nz + 2].astype(spread.dtype).reshape(held.shape)
    total = jnp.zeros((outch, cells), jnp.float32)
    for offset_x in range(3):
        for offset_y in range(3):
            for offset_z in range(3):
                window = spread[offset_z, offset_x : offset_x + nx, offset_y : offset_y + ny].reshape(cells, channels)
                total = total + lax.dot_general(
                    kernel_ref[(offset_x * 3 + offset_y) * 3 + offset_z],
                    window,
                    (((1,), (1,)), ((), ())),
                    preferred_element_type=jnp.float32,
                )
    block = outch // count
    for peer in range(count):
        parts[peer] = total[peer * block : (peer + 1) * block]
    sends = []
    for step in range(1, count):
        peer = lax.rem(me + step, count)
        copy = pltpu.make_async_remote_copy(
            src_ref=parts.at[peer],
            dst_ref=inbox.at[step],
            send_sem=sum_send.at[step],
            recv_sem=sum_recv.at[step],
            device_id={"section": peer},
            device_id_type=MESH,
        )
        copy.start()
        sends.append(copy)
    result = parts[me]
    for step in range(1, count):
        sends[step - 1].wait_recv()
        result = result + inbox[step]
    for copy in sends:
        copy.wait_send()
    out_ref[...] = result.reshape(out_ref.shape).astype(out_ref.dtype)


def final_stage(field, kernel, collective):
    nx, ny_in, nz, channels = field.shape
    ny = ny_in - 2
    count = lax.axis_size("section")
    outch = kernel.shape[1]
    padded = (nx + 2, ny_in, nz, channels)
    block = outch // count
    return pl.pallas_call(
        final_kernel,
        out_shape=jax.ShapeDtypeStruct((block, nx, ny * nz), jnp.bfloat16),
        in_specs=[pl.BlockSpec(memory_space=pltpu.VMEM)] * 2,
        out_specs=pl.BlockSpec(memory_space=pltpu.VMEM),
        scratch_shapes=[
            pltpu.VMEM(padded, field.dtype),
            pltpu.VMEM((3,) + padded, field.dtype),
            pltpu.VMEM(((nx + 2) * ny_in, nz + 2, channels), jnp.float32),
            pltpu.VMEM((count, block, nx * ny * nz), jnp.float32),
            pltpu.VMEM((count, block, nx * ny * nz), jnp.float32),
            pltpu.SemaphoreType.DMA((2,)),
            pltpu.SemaphoreType.DMA((2,)),
            pltpu.SemaphoreType.DMA((count,)),
            pltpu.SemaphoreType.DMA((count,)),
        ],
        compiler_params=pltpu.CompilerParams(collective_id=collective, has_side_effects=True),
    )(field, kernel)


def local(skips, deconv_weight, norm_gain, conv_in, conv_out):
    inl_size = lax.axis_size("inl")
    tokens_here = skips[0]
    weight = deconv_weight[0]
    gains = norm_gain[0]
    channels = gains.shape[1]
    cell_x = 2 * PXD
    cell_y = 2 * lax.axis_size("xln")
    cell_z = 2 * GZ
    assert tokens_here.shape[0] == inl_size * PXD * GZ
    brick = gather_bricks(tokens_here, weight, gains)
    lines = brick.shape[0]
    field = (
        brick.reshape(lines, PXD, GZ, 2, 2, 2, channels)
        .transpose(1, 3, 0, 4, 2, 5, 6)
        .reshape(cell_x, 2 * lines, cell_z, channels)
    )
    merged = conv_stage(field, conv_in[0], gains, True, 1)
    return final_stage(merged, conv_out[0], 2)


def solution(mesh):
    return jax.shard_map(
        local,
        mesh=mesh,
        in_specs=(
            P("section", ("inl", "xln"), None),
            P("section", None, None),
            P("section", None, None),
            P("section", None, None, None),
            P("section", None, None, None),
        ),
        out_specs=P("section", "inl", "xln"),
        check_vma=False,
    )
```

```python
import functools

import jax
import jax.numpy as jnp
from jax import lax
from jax.experimental import pallas as pl
from jax.experimental.pallas import tpu as pltpu
from jax.sharding import PartitionSpec as P

MESH = pl.DeviceIdType.MESH
PXD = 2
GZ = 8


epsilon = 1e-05


def normalize(values, scale):
    mean_square = jnp.mean(values * values, axis=-1, keepdims=True)
    return values * lax.rsqrt(mean_square + epsilon) * scale


def activate(upsampled, gains):
    width = gains.shape[1]
    shaped = upsampled.reshape(upsampled.shape[:-1] + (upsampled.shape[-1] // width, width))
    result = jax.nn.gelu(normalize(shaped, gains[0]), approximate=True).astype(jnp.bfloat16)
    return result.reshape(upsampled.shape)


def gelu_tanh(values):
    return 0.5 * values * (1.0 + jnp.tanh(0.7978845608028654 * (values + 0.044715 * (values * values * values))))


def reduce_scatter_kernel(count, parts_ref, out_ref, held, send_sem, recv_sem):
    me = lax.axis_index("section")
    barrier = pltpu.get_barrier_semaphore()
    for step in range(1, count):
        peer = lax.rem(me + step, count)
        pl.semaphore_signal(barrier, inc=1, device_id={"section": peer}, device_id_type=MESH)
    pl.semaphore_wait(barrier, count - 1)
    sends = []
    for step in range(1, count):
        peer = lax.rem(me + step, count)
        copy = pltpu.make_async_remote_copy(
            src_ref=parts_ref.at[peer],
            dst_ref=held.at[step],
            send_sem=send_sem.at[step],
            recv_sem=recv_sem.at[step],
            device_id={"section": peer},
            device_id_type=MESH,
        )
        copy.start()
        sends.append(copy)
    total = parts_ref[me]
    for step in range(1, count):
        sends[step - 1].wait_recv()
        total = total + held[step]
    for copy in sends:
        copy.wait_send()
    out_ref[...] = total.astype(out_ref.dtype)


def reduce_scatter(parts):
    count = lax.axis_size("section")
    shaped = parts.reshape((count, parts.shape[0] // count) + parts.shape[1:])
    return pl.pallas_call(
        functools.partial(reduce_scatter_kernel, count),
        out_shape=jax.ShapeDtypeStruct(shaped.shape[1:], jnp.bfloat16),
        in_specs=[pl.BlockSpec(memory_space=pltpu.VMEM)],
        out_specs=pl.BlockSpec(memory_space=pltpu.VMEM),
        scratch_shapes=[
            pltpu.VMEM(shaped.shape, jnp.float32),
            pltpu.SemaphoreType.DMA((count,)),
            pltpu.SemaphoreType.DMA((count,)),
        ],
        compiler_params=pltpu.CompilerParams(collective_id=0, has_side_effects=True),
    )(shaped)


def send_groups(me_x, me_y, count):
    return [
        (me_x, me_y + 1, None),
        (me_x + 1, 0, (me_y == count - 1) & (me_x + 1 < count)),
        (me_x - 1, count + 1, (me_y == 0) & (me_x > 0)),
    ]


def gather_kernel(tokens_ref, weight_hbm, gains_ref, out_ref, weight, field, held, send_sem, recv_sem, weight_sem):
    count = lax.axis_size("inl")
    me_x, me_y = lax.axis_index("inl"), lax.axis_index("xln")
    rows = tokens_ref.shape[0] // count
    width = gains_ref.shape[1]
    one = jnp.int32(1)
    loading = pltpu.make_async_copy(weight_hbm, weight, weight_sem)
    loading.start()
    groups = send_groups(me_x, me_y, count)
    sources = [(me_y - 1, count - 1, me_y >= 1)]
    sources += [(me_y, other, None) for other in range(count)]
    sources += [(me_y + 1, 0, me_y + 1 < count)]

    def is_me(x, y):
        return (x == me_x) & (y == me_y)

    barrier = pltpu.get_barrier_semaphore()
    expected = jnp.int32(0)
    for column, _, exists in groups:
        live = True if exists is None else exists
        expected = expected + jnp.where(live, count, 0)
        for other in range(count):

            @pl.when(jnp.logical_and(live, jnp.logical_not(is_me(other, column))))
            def _():
                pl.semaphore_signal(barrier, inc=1, device_id={"inl": other, "xln": column}, device_id_type=MESH)

            expected = expected - jnp.where(jnp.logical_and(live, is_me(other, column)), one, 0)
    for source_x, source_y, exists in sources:
        live = True if exists is None else exists
        mine = jnp.logical_and(live, is_me(source_x, source_y))
        expected = expected + jnp.where(jnp.logical_and(live, jnp.logical_not(mine)), one, 0)

        @pl.when(jnp.logical_and(live, jnp.logical_not(mine)))
        def _():
            pl.semaphore_signal(barrier, inc=1, device_id={"inl": source_x, "xln": source_y}, device_id_type=MESH)

    loading.wait()
    upsampled = jnp.dot(tokens_ref[...], weight[...], preferred_element_type=jnp.float32)
    for group in range(upsampled.shape[1] // width):
        part = upsampled[:, group * width : (group + 1) * width]
        mean_square = jnp.mean(part * part, axis=-1, keepdims=True)
        normed = part * lax.rsqrt(mean_square + epsilon) * gains_ref[0:1, :]
        field[:, group * width : (group + 1) * width] = gelu_tanh(normed).astype(field.dtype)
    pl.semaphore_wait(barrier, expected)
    copies = []
    for index, (column, slot, exists) in enumerate(groups):
        live = True if exists is None else exists
        for other in range(count):
            copy = pltpu.make_async_remote_copy(
                src_ref=field.at[pl.ds(other * rows, rows)],
                dst_ref=held.at[slot],
                send_sem=send_sem.at[index * count + other],
                recv_sem=recv_sem.at[slot],
                device_id={"inl": other, "xln": column},
                device_id_type=MESH,
            )
            remote = jnp.logical_and(live, jnp.logical_not(is_me(other, column)))

            @pl.when(remote)
            def _():
                copy.start()

            copies.append((copy, remote))
    for slot, (source_x, source_y, exists) in enumerate(sources):
        live = True if exists is None else exists
        mine = jnp.logical_and(live, is_me(source_x, source_y))
        remote = jnp.logical_and(live, jnp.logical_not(mine))
        incoming = pltpu.make_async_remote_copy(
            src_ref=field.at[pl.ds(0, rows)],
            dst_ref=held.at[slot],
            send_sem=send_sem.at[0],
            recv_sem=recv_sem.at[slot],
            device_id={"inl": source_x, "xln": source_y},
            device_id_type=MESH,
        )

        @pl.when(remote)
        def _():
            incoming.wait_recv()
            out_ref[slot] = held[slot]

        @pl.when(mine)
        def _():
            out_ref[slot] = field[pl.ds(pl.multiple_of(me_x * rows, rows), rows)]

        @pl.when(jnp.logical_not(live))
        def _():
            out_ref[slot] = jnp.zeros(out_ref.shape[1:], out_ref.dtype)

    for copy, remote in copies:

        @pl.when(remote)
        def _():
            copy.wait_send()


def gather_bricks(tokens, weight, gains):
    count = lax.axis_size("inl")
    rows = tokens.shape[0] // count
    shape = (lax.axis_size("xln") + 2, rows, weight.shape[1])
    return pl.pallas_call(
        gather_kernel,
        out_shape=jax.ShapeDtypeStruct(shape, jnp.bfloat16),
        in_specs=[
            pl.BlockSpec(memory_space=pltpu.VMEM),
            pl.BlockSpec(memory_space=pl.ANY),
            pl.BlockSpec(memory_space=pltpu.VMEM),
        ],
        out_specs=pl.BlockSpec(memory_space=pltpu.VMEM),
        scratch_shapes=[
            pltpu.VMEM(weight.shape, weight.dtype),
            pltpu.VMEM((tokens.shape[0], weight.shape[1]), jnp.bfloat16),
            pltpu.VMEM(shape, jnp.bfloat16),
            pltpu.SemaphoreType.DMA((3 * count,)),
            pltpu.SemaphoreType.DMA((shape[0],)),
            pltpu.SemaphoreType.DMA(()),
        ],
        compiler_params=pltpu.CompilerParams(collective_id=3, has_side_effects=True),
    )(tokens, weight, gains)


def halo_x(field_ref, held, send_sem, recv_sem, others=0):
    nx = field_ref.shape[0]
    count = lax.axis_size("inl")
    me = lax.axis_index("inl")
    if others is not None:
        barrier = pltpu.get_barrier_semaphore()
        for step in (-1, 1):
            pl.semaphore_signal(
                barrier, inc=1, device_id={"inl": lax.rem(me + step + count, count)}, device_id_type=MESH
            )
        pl.semaphore_wait(barrier, 2 + others)
    copies = []
    for index, step in enumerate((-1, 1)):
        source, target = (0, nx + 1) if step < 0 else (nx - 1, 0)
        copy = pltpu.make_async_remote_copy(
            src_ref=field_ref.at[source : source + 1],
            dst_ref=held.at[target : target + 1],
            send_sem=send_sem.at[index],
            recv_sem=recv_sem.at[index],
            device_id={"inl": me + step},
            device_id_type=MESH,
        )
        sends = (me + step >= 0) & (me + step < count)
        gets = (me - step >= 0) & (me - step < count)

        @pl.when(sends)
        def _():
            copy.start()

        @pl.when(jnp.logical_not(gets))
        def _():
            held[target : target + 1] = jnp.zeros((1,) + held.shape[1:], held.dtype)

        copies.append((copy, sends, gets))
    held[1 : nx + 1] = field_ref[...]
    for copy, sends, gets in copies:

        @pl.when(gets)
        def _():
            copy.wait_recv()

        @pl.when(sends)
        def _():
            copy.wait_send()


def conv_kernel(
    residual, field_ref, kernel_ref, gains_ref, out_ref, held, shifted, send_sem, recv_sem
):
    halo_x(field_ref, held, send_sem, recv_sem)
    nx, ny_in, nz, channels = field_ref.shape
    ny = ny_in - 2
    cells = nx * ny * nz
    width = shifted.shape[2]
    parts = []
    for offset_z in range(3):
        part = jnp.zeros((cells, width), jnp.float32)
        for offset_x in range(3):
            for offset_y in range(3):
                window = held[offset_x : offset_x + nx, offset_y : offset_y + ny].reshape(cells, channels)
                tap = kernel_ref[(offset_x * 3 + offset_y) * 3 + offset_z]
                if residual:
                    part = part + jnp.dot(window, tap, preferred_element_type=jnp.float32)
                else:
                    part = part + lax.dot_general(
                        window, tap, (((1,), (1,)), ((), ())), preferred_element_type=jnp.float32
                    )
        parts.append(part.reshape(nx * ny, nz, width))
    edge = jnp.zeros((nx * ny, 1, width), jnp.float32)
    shifted[:, 0:1] = edge
    shifted[:, nz + 1 : nz + 2] = edge
    shifted[:, 1 : nz + 1] = parts[0]
    total = parts[1] + shifted[:, 0:nz]
    shifted[:, 1 : nz + 1] = parts[2]
    total = total + shifted[:, 2 : nz + 2]
    if residual:
        mean_square = jnp.mean(total * total, axis=-1, keepdims=True)
        normed = total * lax.rsqrt(mean_square + epsilon) * gains_ref[1:2, :]
        base = field_ref[:, 1 : ny + 1].reshape(nx * ny, nz, channels).astype(jnp.float32)
        mixed = gelu_tanh(normed + base).reshape(nx, ny, nz, channels)
        me_y, count_y = lax.axis_index("xln"), lax.axis_size("xln")
        row = lax.broadcasted_iota(jnp.int32, mixed.shape, 1)
        outside = ((row == 0) & (me_y == 0)) | ((row == ny - 1) & (me_y == count_y - 1))
        out_ref[...] = jnp.where(outside, 0.0, mixed).astype(out_ref.dtype)
    else:
        out_ref[...] = total.reshape(out_ref.shape)


def conv_stage(field, kernel, gains, residual, collective):
    nx, ny_in, nz, channels = field.shape
    width = kernel.shape[2] if residual else kernel.shape[1]
    padded = (nx + 2, ny_in, nz, channels)
    ny = ny_in - 2
    dtype = jnp.bfloat16 if residual else jnp.float32
    return pl.pallas_call(
        functools.partial(conv_kernel, residual),
        out_shape=jax.ShapeDtypeStruct((nx, ny, nz, width), dtype),
        in_specs=[pl.BlockSpec(memory_space=pltpu.VMEM)] * 3,
        out_specs=pl.BlockSpec(memory_space=pltpu.VMEM),
        scratch_shapes=[
            pltpu.VMEM(padded, field.dtype),
            pltpu.VMEM((nx * ny, nz + 2, width), jnp.float32),
            pltpu.SemaphoreType.DMA((2,)),
            pltpu.SemaphoreType.DMA((2,)),
        ],
        compiler_params=pltpu.CompilerParams(collective_id=collective, has_side_effects=True),
    )(field, kernel, gains)


def final_kernel(field_ref, kernel_ref, out_ref, held, spread, shifted, parts, inbox, send_sem, recv_sem, sum_send, sum_recv):
    count = lax.axis_size("section")
    me = lax.axis_index("section")
    for step in range(1, count):
        pl.semaphore_signal(
            pltpu.get_barrier_semaphore(),
            inc=1,
            device_id={"section": lax.rem(me + step, count)},
            device_id_type=MESH,
        )
    halo_x(field_ref, held, send_sem, recv_sem, count - 1)
    nx, ny_in, nz, channels = field_ref.shape
    ny = ny_in - 2
    cells = nx * ny * nz
    outch = kernel_ref.shape[1]
    planes = (nx + 2) * ny_in
    edge = jnp.zeros((planes, 1, channels), jnp.float32)
    shifted[:, 0:1] = edge
    shifted[:, nz + 1 : nz + 2] = edge
    shifted[:, 1 : nz + 1] = held[...].reshape(planes, nz, channels).astype(jnp.float32)
    spread[0] = shifted[:, 0:nz].astype(spread.dtype).reshape(held.shape)
    spread[1] = held[...]
    spread[2] = shifted[:, 2 : nz + 2].astype(spread.dtype).reshape(held.shape)
    total = jnp.zeros((outch, cells), jnp.float32)
    for offset_x in range(3):
        for offset_y in range(3):
            for offset_z in range(3):
                window = spread[offset_z, offset_x : offset_x + nx, offset_y : offset_y + ny].reshape(cells, channels)
                total = total + lax.dot_general(
                    kernel_ref[(offset_x * 3 + offset_y) * 3 + offset_z],
                    window,
                    (((1,), (1,)), ((), ())),
                    preferred_element_type=jnp.float32,
                )
    block = outch // count
    for peer in range(count):
        parts[peer] = total[peer * block : (peer + 1) * block]
    sends = []
    for step in range(1, count):
        peer = lax.rem(me + step, count)
        copy = pltpu.make_async_remote_copy(
            src_ref=parts.at[peer],
            dst_ref=inbox.at[step],
            send_sem=sum_send.at[step],
            recv_sem=sum_recv.at[step],
            device_id={"section": peer},
            device_id_type=MESH,
        )
        copy.start()
        sends.append(copy)
    result = parts[me]
    for step in range(1, count):
        sends[step - 1].wait_recv()
        result = result + inbox[step]
    for copy in sends:
        copy.wait_send()
    out_ref[...] = result.reshape(out_ref.shape).astype(out_ref.dtype)


def final_stage(field, kernel, collective):
    nx, ny_in, nz, channels = field.shape
    ny = ny_in - 2
    count = lax.axis_size("section")
    outch = kernel.shape[1]
    padded = (nx + 2, ny_in, nz, channels)
    block = outch // count
    return pl.pallas_call(
        final_kernel,
        out_shape=jax.ShapeDtypeStruct((block, nx, ny * nz), jnp.bfloat16),
        in_specs=[pl.BlockSpec(memory_space=pltpu.VMEM)] * 2,
        out_specs=pl.BlockSpec(memory_space=pltpu.VMEM),
        scratch_shapes=[
            pltpu.VMEM(padded, field.dtype),
            pltpu.VMEM((3,) + padded, field.dtype),
            pltpu.VMEM(((nx + 2) * ny_in, nz + 2, channels), jnp.float32),
            pltpu.VMEM((count, block, nx * ny * nz), jnp.float32),
            pltpu.VMEM((count, block, nx * ny * nz), jnp.float32),
            pltpu.SemaphoreType.DMA((2,)),
            pltpu.SemaphoreType.DMA((2,)),
            pltpu.SemaphoreType.DMA((count,)),
            pltpu.SemaphoreType.DMA((count,)),
        ],
        compiler_params=pltpu.CompilerParams(collective_id=collective, has_side_effects=True),
    )(field, kernel)


def block_kernel(
    field_ref, kernel_in_ref, gains_ref, kernel_out_ref, out_ref,
    held, shifted, mixed, held_out, spread, shifted_out, parts, inbox,
    send_sem, recv_sem, send_out, recv_out, sum_send, sum_recv,
):
    count = lax.axis_size("section")
    me = lax.axis_index("section")
    for step in range(1, count):
        pl.semaphore_signal(
            pltpu.get_barrier_semaphore(),
            inc=1,
            device_id={"section": lax.rem(me + step, count)},
            device_id_type=MESH,
        )
    halo_x(field_ref, held, send_sem, recv_sem, count - 1)
    nx, ny_in, nz, channels = field_ref.shape
    ny = ny_in - 2
    cells = nx * ny * nz
    width = channels
    parts_in = []
    for offset_z in range(3):
        part = jnp.zeros((cells, width), jnp.float32)
        for offset_x in range(3):
            for offset_y in range(3):
                window = held[offset_x : offset_x + nx, offset_y : offset_y + ny].reshape(cells, channels)
                tap = kernel_in_ref[(offset_x * 3 + offset_y) * 3 + offset_z]
                part = part + jnp.dot(window, tap, preferred_element_type=jnp.float32)
        parts_in.append(part.reshape(nx * ny, nz, width))
    edge = jnp.zeros((nx * ny, 1, width), jnp.float32)
    shifted[:, 0:1] = edge
    shifted[:, nz + 1 : nz + 2] = edge
    shifted[:, 1 : nz + 1] = parts_in[0]
    total = parts_in[1] + shifted[:, 0:nz]
    shifted[:, 1 : nz + 1] = parts_in[2]
    total = total + shifted[:, 2 : nz + 2]
    mean_square = jnp.mean(total * total, axis=-1, keepdims=True)
    normed = total * lax.rsqrt(mean_square + epsilon) * gains_ref[1:2, :]
    base = field_ref[:, 1 : ny + 1].reshape(nx * ny, nz, channels).astype(jnp.float32)
    activated = gelu_tanh(normed + base).reshape(nx, ny, nz, channels)
    me_y, count_y = lax.axis_index("xln"), lax.axis_size("xln")
    row = lax.broadcasted_iota(jnp.int32, activated.shape, 1)
    outside = ((row == 0) & (me_y == 0)) | ((row == ny - 1) & (me_y == count_y - 1))
    mixed[...] = jnp.where(outside, 0.0, activated).astype(mixed.dtype)

    halo_x(mixed, held_out, send_out, recv_out, None)
    ny_out = ny - 2
    cells_out = nx * ny_out * nz
    outch = kernel_out_ref.shape[1]
    planes = (nx + 2) * ny
    edge = jnp.zeros((planes, 1, channels), jnp.float32)
    shifted_out[:, 0:1] = edge
    shifted_out[:, nz + 1 : nz + 2] = edge
    shifted_out[:, 1 : nz + 1] = held_out[...].reshape(planes, nz, channels).astype(jnp.float32)
    spread[0] = shifted_out[:, 0:nz].astype(spread.dtype).reshape(held_out.shape)
    spread[1] = held_out[...]
    spread[2] = shifted_out[:, 2 : nz + 2].astype(spread.dtype).reshape(held_out.shape)
    result_t = jnp.zeros((outch, cells_out), jnp.float32)
    for offset_x in range(3):
        for offset_y in range(3):
            for offset_z in range(3):
                window = spread[offset_z, offset_x : offset_x + nx, offset_y : offset_y + ny_out].reshape(
                    cells_out, channels
                )
                result_t = result_t + lax.dot_general(
                    kernel_out_ref[(offset_x * 3 + offset_y) * 3 + offset_z],
                    window,
                    (((1,), (1,)), ((), ())),
                    preferred_element_type=jnp.float32,
                )
    block = outch // count
    for peer in range(count):
        parts[peer] = result_t[peer * block : (peer + 1) * block]
    sends = []
    for step in range(1, count):
        peer = lax.rem(me + step, count)
        copy = pltpu.make_async_remote_copy(
            src_ref=parts.at[peer],
            dst_ref=inbox.at[step],
            send_sem=sum_send.at[step],
            recv_sem=sum_recv.at[step],
            device_id={"section": peer},
            device_id_type=MESH,
        )
        copy.start()
        sends.append(copy)
    result = parts[me]
    for step in range(1, count):
        sends[step - 1].wait_recv()
        result = result + inbox[step]
    for copy in sends:
        copy.wait_send()
    out_ref[...] = result.reshape(out_ref.shape).astype(out_ref.dtype)


def decoder_block(field, kernel_in, gains, kernel_out, collective):
    nx, ny_in, nz, channels = field.shape
    ny = ny_in - 2
    ny_out = ny - 2
    count = lax.axis_size("section")
    outch = kernel_out.shape[1]
    block = outch // count
    return pl.pallas_call(
        block_kernel,
        out_shape=jax.ShapeDtypeStruct((block, nx, ny_out * nz), jnp.bfloat16),
        in_specs=[pl.BlockSpec(memory_space=pltpu.VMEM)] * 4,
        out_specs=pl.BlockSpec(memory_space=pltpu.VMEM),
        scratch_shapes=[
            pltpu.VMEM((nx + 2, ny_in, nz, channels), field.dtype),
            pltpu.VMEM((nx * ny, nz + 2, channels), jnp.float32),
            pltpu.VMEM((nx, ny, nz, channels), field.dtype),
            pltpu.VMEM((nx + 2, ny, nz, channels), field.dtype),
            pltpu.VMEM((3, nx + 2, ny, nz, channels), field.dtype),
            pltpu.VMEM(((nx + 2) * ny, nz + 2, channels), jnp.float32),
            pltpu.VMEM((count, block, nx * ny_out * nz), jnp.float32),
            pltpu.VMEM((count, block, nx * ny_out * nz), jnp.float32),
            pltpu.SemaphoreType.DMA((2,)),
            pltpu.SemaphoreType.DMA((2,)),
            pltpu.SemaphoreType.DMA((2,)),
            pltpu.SemaphoreType.DMA((2,)),
            pltpu.SemaphoreType.DMA((count,)),
            pltpu.SemaphoreType.DMA((count,)),
        ],
        compiler_params=pltpu.CompilerParams(collective_id=collective, has_side_effects=True),
    )(field, kernel_in, gains, kernel_out)


def local(skips, deconv_weight, norm_gain, conv_in, conv_out):
    inl_size = lax.axis_size("inl")
    tokens_here = skips[0]
    weight = deconv_weight[0]
    gains = norm_gain[0]
    channels = gains.shape[1]
    cell_x = 2 * PXD
    cell_y = 2 * lax.axis_size("xln")
    cell_z = 2 * GZ
    assert tokens_here.shape[0] == inl_size * PXD * GZ
    brick = gather_bricks(tokens_here, weight, gains)
    lines = brick.shape[0]
    field = (
        brick.reshape(lines, PXD, GZ, 2, 2, 2, channels)
        .transpose(1, 3, 0, 4, 2, 5, 6)
        .reshape(cell_x, 2 * lines, cell_z, channels)
    )
    return decoder_block(field, conv_in[0], gains, conv_out[0], 1)


def solution(mesh):
    return jax.shard_map(
        local,
        mesh=mesh,
        in_specs=(
            P("section", ("inl", "xln"), None),
            P("section", None, None),
            P("section", None, None),
            P("section", None, None, None),
            P("section", None, None, None),
        ),
        out_specs=P("section", "inl", "xln"),
        check_vma=False,
    )
```

```python
import functools

import jax
import jax.numpy as jnp
from jax import lax
from jax.experimental import pallas as pl
from jax.experimental.pallas import tpu as pltpu
from jax.sharding import PartitionSpec as P

MESH = pl.DeviceIdType.MESH
PXD = 2
GZ = 8


epsilon = 1e-05


def normalize(values, scale):
    mean_square = jnp.mean(values * values, axis=-1, keepdims=True)
    return values * lax.rsqrt(mean_square + epsilon) * scale


def activate(upsampled, gains):
    width = gains.shape[1]
    shaped = upsampled.reshape(upsampled.shape[:-1] + (upsampled.shape[-1] // width, width))
    result = jax.nn.gelu(normalize(shaped, gains[0]), approximate=True).astype(jnp.bfloat16)
    return result.reshape(upsampled.shape)


def gelu_tanh(values):
    return 0.5 * values * (1.0 + jnp.tanh(0.7978845608028654 * (values + 0.044715 * (values * values * values))))


def reduce_scatter_kernel(count, parts_ref, out_ref, held, send_sem, recv_sem):
    me = lax.axis_index("section")
    barrier = pltpu.get_barrier_semaphore()
    for step in range(1, count):
        peer = lax.rem(me + step, count)
        pl.semaphore_signal(barrier, inc=1, device_id={"section": peer}, device_id_type=MESH)
    pl.semaphore_wait(barrier, count - 1)
    sends = []
    for step in range(1, count):
        peer = lax.rem(me + step, count)
        copy = pltpu.make_async_remote_copy(
            src_ref=parts_ref.at[peer],
            dst_ref=held.at[step],
            send_sem=send_sem.at[step],
            recv_sem=recv_sem.at[step],
            device_id={"section": peer},
            device_id_type=MESH,
        )
        copy.start()
        sends.append(copy)
    total = parts_ref[me]
    for step in range(1, count):
        sends[step - 1].wait_recv()
        total = total + held[step]
    for copy in sends:
        copy.wait_send()
    out_ref[...] = total.astype(out_ref.dtype)


def reduce_scatter(parts):
    count = lax.axis_size("section")
    shaped = parts.reshape((count, parts.shape[0] // count) + parts.shape[1:])
    return pl.pallas_call(
        functools.partial(reduce_scatter_kernel, count),
        out_shape=jax.ShapeDtypeStruct(shaped.shape[1:], jnp.bfloat16),
        in_specs=[pl.BlockSpec(memory_space=pltpu.VMEM)],
        out_specs=pl.BlockSpec(memory_space=pltpu.VMEM),
        scratch_shapes=[
            pltpu.VMEM(shaped.shape, jnp.float32),
            pltpu.SemaphoreType.DMA((count,)),
            pltpu.SemaphoreType.DMA((count,)),
        ],
        compiler_params=pltpu.CompilerParams(collective_id=0, has_side_effects=True),
    )(shaped)


def send_groups(me_x, me_y, count):
    return [
        (me_x, me_y + 1, None),
        (me_x + 1, 0, (me_y == count - 1) & (me_x + 1 < count)),
        (me_x - 1, count + 1, (me_y == 0) & (me_x > 0)),
    ]


def gather_kernel(tokens_ref, weight_hbm, gains_ref, out_ref, weight, field, held, send_sem, recv_sem, weight_sem):
    count = lax.axis_size("inl")
    me_x, me_y = lax.axis_index("inl"), lax.axis_index("xln")
    rows = tokens_ref.shape[0] // count
    width = gains_ref.shape[1]
    one = jnp.int32(1)
    loading = pltpu.make_async_copy(weight_hbm, weight, weight_sem)
    loading.start()
    groups = send_groups(me_x, me_y, count)
    sources = [(me_y - 1, count - 1, me_y >= 1)]
    sources += [(me_y, other, None) for other in range(count)]
    sources += [(me_y + 1, 0, me_y + 1 < count)]

    def is_me(x, y):
        return (x == me_x) & (y == me_y)

    barrier = pltpu.get_barrier_semaphore()
    expected = jnp.int32(0)
    for column, _, exists in groups:
        live = True if exists is None else exists
        expected = expected + jnp.where(live, count, 0)
        for other in range(count):

            @pl.when(jnp.logical_and(live, jnp.logical_not(is_me(other, column))))
            def _():
                pl.semaphore_signal(barrier, inc=1, device_id={"inl": other, "xln": column}, device_id_type=MESH)

            expected = expected - jnp.where(jnp.logical_and(live, is_me(other, column)), one, 0)
    for source_x, source_y, exists in sources:
        live = True if exists is None else exists
        mine = jnp.logical_and(live, is_me(source_x, source_y))
        expected = expected + jnp.where(jnp.logical_and(live, jnp.logical_not(mine)), one, 0)

        @pl.when(jnp.logical_and(live, jnp.logical_not(mine)))
        def _():
            pl.semaphore_signal(barrier, inc=1, device_id={"inl": source_x, "xln": source_y}, device_id_type=MESH)

    loading.wait()
    upsampled = jnp.dot(tokens_ref[...], weight[...], preferred_element_type=jnp.float32)
    for group in range(upsampled.shape[1] // width):
        part = upsampled[:, group * width : (group + 1) * width]
        mean_square = jnp.mean(part * part, axis=-1, keepdims=True)
        normed = part * lax.rsqrt(mean_square + epsilon) * gains_ref[0:1, :]
        field[:, group * width : (group + 1) * width] = gelu_tanh(normed).astype(field.dtype)
    pl.semaphore_wait(barrier, expected)
    copies = []
    for index, (column, slot, exists) in enumerate(groups):
        live = True if exists is None else exists
        for turn in range(count):
            other = lax.rem(me_y + turn, count)
            copy = pltpu.make_async_remote_copy(
                src_ref=field.at[pl.ds(pl.multiple_of(other * rows, rows), rows)],
                dst_ref=held.at[slot],
                send_sem=send_sem.at[index * count + turn],
                recv_sem=recv_sem.at[slot],
                device_id={"inl": other, "xln": column},
                device_id_type=MESH,
            )
            remote = jnp.logical_and(live, jnp.logical_not(is_me(other, column)))

            @pl.when(remote)
            def _():
                copy.start()

            copies.append((copy, remote))
    for slot, (source_x, source_y, exists) in enumerate(sources):
        live = True if exists is None else exists
        mine = jnp.logical_and(live, is_me(source_x, source_y))
        remote = jnp.logical_and(live, jnp.logical_not(mine))
        incoming = pltpu.make_async_remote_copy(
            src_ref=field.at[pl.ds(0, rows)],
            dst_ref=held.at[slot],
            send_sem=send_sem.at[0],
            recv_sem=recv_sem.at[slot],
            device_id={"inl": source_x, "xln": source_y},
            device_id_type=MESH,
        )

        @pl.when(remote)
        def _():
            incoming.wait_recv()
            out_ref[slot] = held[slot]

        @pl.when(mine)
        def _():
            out_ref[slot] = field[pl.ds(pl.multiple_of(me_x * rows, rows), rows)]

        @pl.when(jnp.logical_not(live))
        def _():
            out_ref[slot] = jnp.zeros(out_ref.shape[1:], out_ref.dtype)

    for copy, remote in copies:

        @pl.when(remote)
        def _():
            copy.wait_send()


def gather_bricks(tokens, weight, gains):
    count = lax.axis_size("inl")
    rows = tokens.shape[0] // count
    shape = (lax.axis_size("xln") + 2, rows, weight.shape[1])
    return pl.pallas_call(
        gather_kernel,
        out_shape=jax.ShapeDtypeStruct(shape, jnp.bfloat16),
        in_specs=[
            pl.BlockSpec(memory_space=pltpu.VMEM),
            pl.BlockSpec(memory_space=pl.ANY),
            pl.BlockSpec(memory_space=pltpu.VMEM),
        ],
        out_specs=pl.BlockSpec(memory_space=pltpu.VMEM),
        scratch_shapes=[
            pltpu.VMEM(weight.shape, weight.dtype),
            pltpu.VMEM((tokens.shape[0], weight.shape[1]), jnp.bfloat16),
            pltpu.VMEM(shape, jnp.bfloat16),
            pltpu.SemaphoreType.DMA((3 * count,)),
            pltpu.SemaphoreType.DMA((shape[0],)),
            pltpu.SemaphoreType.DMA(()),
        ],
        compiler_params=pltpu.CompilerParams(collective_id=3, has_side_effects=True),
    )(tokens, weight, gains)


def halo_x(field_ref, held, send_sem, recv_sem, others=0):
    nx = field_ref.shape[0]
    count = lax.axis_size("inl")
    me = lax.axis_index("inl")
    if others is not None:
        barrier = pltpu.get_barrier_semaphore()
        for step in (-1, 1):
            pl.semaphore_signal(
                barrier, inc=1, device_id={"inl": lax.rem(me + step + count, count)}, device_id_type=MESH
            )
        pl.semaphore_wait(barrier, 2 + others)
    copies = []
    for index, step in enumerate((-1, 1)):
        source, target = (0, nx + 1) if step < 0 else (nx - 1, 0)
        copy = pltpu.make_async_remote_copy(
            src_ref=field_ref.at[source : source + 1],
            dst_ref=held.at[target : target + 1],
            send_sem=send_sem.at[index],
            recv_sem=recv_sem.at[index],
            device_id={"inl": me + step},
            device_id_type=MESH,
        )
        sends = (me + step >= 0) & (me + step < count)
        gets = (me - step >= 0) & (me - step < count)

        @pl.when(sends)
        def _():
            copy.start()

        @pl.when(jnp.logical_not(gets))
        def _():
            held[target : target + 1] = jnp.zeros((1,) + held.shape[1:], held.dtype)

        copies.append((copy, sends, gets))
    held[1 : nx + 1] = field_ref[...]
    for copy, sends, gets in copies:

        @pl.when(gets)
        def _():
            copy.wait_recv()

        @pl.when(sends)
        def _():
            copy.wait_send()


def conv_kernel(
    residual, field_ref, kernel_ref, gains_ref, out_ref, held, shifted, send_sem, recv_sem
):
    halo_x(field_ref, held, send_sem, recv_sem)
    nx, ny_in, nz, channels = field_ref.shape
    ny = ny_in - 2
    cells = nx * ny * nz
    width = shifted.shape[2]
    parts = []
    for offset_z in range(3):
        part = jnp.zeros((cells, width), jnp.float32)
        for offset_x in range(3):
            for offset_y in range(3):
                window = held[offset_x : offset_x + nx, offset_y : offset_y + ny].reshape(cells, channels)
                tap = kernel_ref[(offset_x * 3 + offset_y) * 3 + offset_z]
                if residual:
                    part = part + jnp.dot(window, tap, preferred_element_type=jnp.float32)
                else:
                    part = part + lax.dot_general(
                        window, tap, (((1,), (1,)), ((), ())), preferred_element_type=jnp.float32
                    )
        parts.append(part.reshape(nx * ny, nz, width))
    edge = jnp.zeros((nx * ny, 1, width), jnp.float32)
    shifted[:, 0:1] = edge
    shifted[:, nz + 1 : nz + 2] = edge
    shifted[:, 1 : nz + 1] = parts[0]
    total = parts[1] + shifted[:, 0:nz]
    shifted[:, 1 : nz + 1] = parts[2]
    total = total + shifted[:, 2 : nz + 2]
    if residual:
        mean_square = jnp.mean(total * total, axis=-1, keepdims=True)
        normed = total * lax.rsqrt(mean_square + epsilon) * gains_ref[1:2, :]
        base = field_ref[:, 1 : ny + 1].reshape(nx * ny, nz, channels).astype(jnp.float32)
        mixed = gelu_tanh(normed + base).reshape(nx, ny, nz, channels)
        me_y, count_y = lax.axis_index("xln"), lax.axis_size("xln")
        row = lax.broadcasted_iota(jnp.int32, mixed.shape, 1)
        outside = ((row == 0) & (me_y == 0)) | ((row == ny - 1) & (me_y == count_y - 1))
        out_ref[...] = jnp.where(outside, 0.0, mixed).astype(out_ref.dtype)
    else:
        out_ref[...] = total.reshape(out_ref.shape)


def conv_stage(field, kernel, gains, residual, collective):
    nx, ny_in, nz, channels = field.shape
    width = kernel.shape[2] if residual else kernel.shape[1]
    padded = (nx + 2, ny_in, nz, channels)
    ny = ny_in - 2
    dtype = jnp.bfloat16 if residual else jnp.float32
    return pl.pallas_call(
        functools.partial(conv_kernel, residual),
        out_shape=jax.ShapeDtypeStruct((nx, ny, nz, width), dtype),
        in_specs=[pl.BlockSpec(memory_space=pltpu.VMEM)] * 3,
        out_specs=pl.BlockSpec(memory_space=pltpu.VMEM),
        scratch_shapes=[
            pltpu.VMEM(padded, field.dtype),
            pltpu.VMEM((nx * ny, nz + 2, width), jnp.float32),
            pltpu.SemaphoreType.DMA((2,)),
            pltpu.SemaphoreType.DMA((2,)),
        ],
        compiler_params=pltpu.CompilerParams(collective_id=collective, has_side_effects=True),
    )(field, kernel, gains)


def final_kernel(field_ref, kernel_ref, out_ref, held, spread, shifted, parts, inbox, send_sem, recv_sem, sum_send, sum_recv):
    count = lax.axis_size("section")
    me = lax.axis_index("section")
    for step in range(1, count):
        pl.semaphore_signal(
            pltpu.get_barrier_semaphore(),
            inc=1,
            device_id={"section": lax.rem(me + step, count)},
            device_id_type=MESH,
        )
    halo_x(field_ref, held, send_sem, recv_sem, count - 1)
    nx, ny_in, nz, channels = field_ref.shape
    ny = ny_in - 2
    cells = nx * ny * nz
    outch = kernel_ref.shape[1]
    planes = (nx + 2) * ny_in
    edge = jnp.zeros((planes, 1, channels), jnp.float32)
    shifted[:, 0:1] = edge
    shifted[:, nz + 1 : nz + 2] = edge
    shifted[:, 1 : nz + 1] = held[...].reshape(planes, nz, channels).astype(jnp.float32)
    spread[0] = shifted[:, 0:nz].astype(spread.dtype).reshape(held.shape)
    spread[1] = held[...]
    spread[2] = shifted[:, 2 : nz + 2].astype(spread.dtype).reshape(held.shape)
    total = jnp.zeros((outch, cells), jnp.float32)
    for offset_x in range(3):
        for offset_y in range(3):
            for offset_z in range(3):
                window = spread[offset_z, offset_x : offset_x + nx, offset_y : offset_y + ny].reshape(cells, channels)
                total = total + lax.dot_general(
                    kernel_ref[(offset_x * 3 + offset_y) * 3 + offset_z],
                    window,
                    (((1,), (1,)), ((), ())),
                    preferred_element_type=jnp.float32,
                )
    block = outch // count
    for peer in range(count):
        parts[peer] = total[peer * block : (peer + 1) * block]
    sends = []
    for step in range(1, count):
        peer = lax.rem(me + step, count)
        copy = pltpu.make_async_remote_copy(
            src_ref=parts.at[peer],
            dst_ref=inbox.at[step],
            send_sem=sum_send.at[step],
            recv_sem=sum_recv.at[step],
            device_id={"section": peer},
            device_id_type=MESH,
        )
        copy.start()
        sends.append(copy)
    result = parts[me]
    for step in range(1, count):
        sends[step - 1].wait_recv()
        result = result + inbox[step]
    for copy in sends:
        copy.wait_send()
    out_ref[...] = result.reshape(out_ref.shape).astype(out_ref.dtype)


def final_stage(field, kernel, collective):
    nx, ny_in, nz, channels = field.shape
    ny = ny_in - 2
    count = lax.axis_size("section")
    outch = kernel.shape[1]
    padded = (nx + 2, ny_in, nz, channels)
    block = outch // count
    return pl.pallas_call(
        final_kernel,
        out_shape=jax.ShapeDtypeStruct((block, nx, ny * nz), jnp.bfloat16),
        in_specs=[pl.BlockSpec(memory_space=pltpu.VMEM)] * 2,
        out_specs=pl.BlockSpec(memory_space=pltpu.VMEM),
        scratch_shapes=[
            pltpu.VMEM(padded, field.dtype),
            pltpu.VMEM((3,) + padded, field.dtype),
            pltpu.VMEM(((nx + 2) * ny_in, nz + 2, channels), jnp.float32),
            pltpu.VMEM((count, block, nx * ny * nz), jnp.float32),
            pltpu.VMEM((count, block, nx * ny * nz), jnp.float32),
            pltpu.SemaphoreType.DMA((2,)),
            pltpu.SemaphoreType.DMA((2,)),
            pltpu.SemaphoreType.DMA((count,)),
            pltpu.SemaphoreType.DMA((count,)),
        ],
        compiler_params=pltpu.CompilerParams(collective_id=collective, has_side_effects=True),
    )(field, kernel)


def block_kernel(
    field_ref, kernel_in_ref, gains_ref, kernel_out_ref, out_ref,
    held, shifted, mixed, held_out, spread, shifted_out, parts, inbox,
    send_sem, recv_sem, send_out, recv_out, sum_send, sum_recv,
):
    count = lax.axis_size("section")
    me = lax.axis_index("section")
    for step in range(1, count):
        pl.semaphore_signal(
            pltpu.get_barrier_semaphore(),
            inc=1,
            device_id={"section": lax.rem(me + step, count)},
            device_id_type=MESH,
        )
    halo_x(field_ref, held, send_sem, recv_sem, count - 1)
    nx, ny_in, nz, channels = field_ref.shape
    ny = ny_in - 2
    cells = nx * ny * nz
    width = channels
    parts_in = []
    for offset_z in range(3):
        part = jnp.zeros((cells, width), jnp.float32)
        for offset_x in range(3):
            for offset_y in range(3):
                window = held[offset_x : offset_x + nx, offset_y : offset_y + ny].reshape(cells, channels)
                tap = kernel_in_ref[(offset_x * 3 + offset_y) * 3 + offset_z]
                part = part + jnp.dot(window, tap, preferred_element_type=jnp.float32)
        parts_in.append(part.reshape(nx * ny, nz, width))
    edge = jnp.zeros((nx * ny, 1, width), jnp.float32)
    shifted[:, 0:1] = edge
    shifted[:, nz + 1 : nz + 2] = edge
    shifted[:, 1 : nz + 1] = parts_in[0]
    total = parts_in[1] + shifted[:, 0:nz]
    shifted[:, 1 : nz + 1] = parts_in[2]
    total = total + shifted[:, 2 : nz + 2]
    mean_square = jnp.mean(total * total, axis=-1, keepdims=True)
    normed = total * lax.rsqrt(mean_square + epsilon) * gains_ref[1:2, :]
    base = field_ref[:, 1 : ny + 1].reshape(nx * ny, nz, channels).astype(jnp.float32)
    activated = gelu_tanh(normed + base).reshape(nx, ny, nz, channels)
    me_y, count_y = lax.axis_index("xln"), lax.axis_size("xln")
    row = lax.broadcasted_iota(jnp.int32, activated.shape, 1)
    outside = ((row == 0) & (me_y == 0)) | ((row == ny - 1) & (me_y == count_y - 1))
    mixed[...] = jnp.where(outside, 0.0, activated).astype(mixed.dtype)

    halo_x(mixed, held_out, send_out, recv_out, None)
    ny_out = ny - 2
    cells_out = nx * ny_out * nz
    outch = kernel_out_ref.shape[1]
    planes = (nx + 2) * ny
    edge = jnp.zeros((planes, 1, channels), jnp.float32)
    shifted_out[:, 0:1] = edge
    shifted_out[:, nz + 1 : nz + 2] = edge
    shifted_out[:, 1 : nz + 1] = held_out[...].reshape(planes, nz, channels).astype(jnp.float32)
    spread[0] = shifted_out[:, 0:nz].astype(spread.dtype).reshape(held_out.shape)
    spread[1] = held_out[...]
    spread[2] = shifted_out[:, 2 : nz + 2].astype(spread.dtype).reshape(held_out.shape)
    result_t = jnp.zeros((outch, cells_out), jnp.float32)
    for offset_x in range(3):
        for offset_y in range(3):
            for offset_z in range(3):
                window = spread[offset_z, offset_x : offset_x + nx, offset_y : offset_y + ny_out].reshape(
                    cells_out, channels
                )
                result_t = result_t + lax.dot_general(
                    kernel_out_ref[(offset_x * 3 + offset_y) * 3 + offset_z],
                    window,
                    (((1,), (1,)), ((), ())),
                    preferred_element_type=jnp.float32,
                )
    block = outch // count
    for peer in range(count):
        parts[peer] = result_t[peer * block : (peer + 1) * block]
    sends = []
    for step in range(1, count):
        peer = lax.rem(me + step, count)
        copy = pltpu.make_async_remote_copy(
            src_ref=parts.at[peer],
            dst_ref=inbox.at[step],
            send_sem=sum_send.at[step],
            recv_sem=sum_recv.at[step],
            device_id={"section": peer},
            device_id_type=MESH,
        )
        copy.start()
        sends.append(copy)
    result = parts[me]
    for step in range(1, count):
        sends[step - 1].wait_recv()
        result = result + inbox[step]
    for copy in sends:
        copy.wait_send()
    out_ref[...] = result.reshape(out_ref.shape).astype(out_ref.dtype)


def decoder_block(field, kernel_in, gains, kernel_out, collective):
    nx, ny_in, nz, channels = field.shape
    ny = ny_in - 2
    ny_out = ny - 2
    count = lax.axis_size("section")
    outch = kernel_out.shape[1]
    block = outch // count
    return pl.pallas_call(
        block_kernel,
        out_shape=jax.ShapeDtypeStruct((block, nx, ny_out * nz), jnp.bfloat16),
        in_specs=[pl.BlockSpec(memory_space=pltpu.VMEM)] * 4,
        out_specs=pl.BlockSpec(memory_space=pltpu.VMEM),
        scratch_shapes=[
            pltpu.VMEM((nx + 2, ny_in, nz, channels), field.dtype),
            pltpu.VMEM((nx * ny, nz + 2, channels), jnp.float32),
            pltpu.VMEM((nx, ny, nz, channels), field.dtype),
            pltpu.VMEM((nx + 2, ny, nz, channels), field.dtype),
            pltpu.VMEM((3, nx + 2, ny, nz, channels), field.dtype),
            pltpu.VMEM(((nx + 2) * ny, nz + 2, channels), jnp.float32),
            pltpu.VMEM((count, block, nx * ny_out * nz), jnp.float32),
            pltpu.VMEM((count, block, nx * ny_out * nz), jnp.float32),
            pltpu.SemaphoreType.DMA((2,)),
            pltpu.SemaphoreType.DMA((2,)),
            pltpu.SemaphoreType.DMA((2,)),
            pltpu.SemaphoreType.DMA((2,)),
            pltpu.SemaphoreType.DMA((count,)),
            pltpu.SemaphoreType.DMA((count,)),
        ],
        compiler_params=pltpu.CompilerParams(collective_id=collective, has_side_effects=True),
    )(field, kernel_in, gains, kernel_out)


def local(skips, deconv_weight, norm_gain, conv_in, conv_out):
    inl_size = lax.axis_size("inl")
    tokens_here = skips[0]
    weight = deconv_weight[0]
    gains = norm_gain[0]
    channels = gains.shape[1]
    cell_x = 2 * PXD
    cell_y = 2 * lax.axis_size("xln")
    cell_z = 2 * GZ
    assert tokens_here.shape[0] == inl_size * PXD * GZ
    brick = gather_bricks(tokens_here, weight, gains)
    lines = brick.shape[0]
    field = (
        brick.reshape(lines, PXD, GZ, 2, 2, 2, channels)
        .transpose(1, 3, 0, 4, 2, 5, 6)
        .reshape(cell_x, 2 * lines, cell_z, channels)
    )
    return decoder_block(field, conv_in[0], gains, conv_out[0], 1)


def solution(mesh):
    return jax.shard_map(
        local,
        mesh=mesh,
        in_specs=(
            P("section", ("inl", "xln"), None),
            P("section", None, None),
            P("section", None, None),
            P("section", None, None, None),
            P("section", None, None, None),
        ),
        out_specs=P("section", "inl", "xln"),
        check_vma=False,
    )
```

```python
import functools

import jax
import jax.numpy as jnp
from jax import lax
from jax.experimental import pallas as pl
from jax.experimental.pallas import tpu as pltpu
from jax.sharding import PartitionSpec as P

MESH = pl.DeviceIdType.MESH
PXD = 2
GZ = 8


epsilon = 1e-05


def normalize(values, scale):
    mean_square = jnp.mean(values * values, axis=-1, keepdims=True)
    return values * lax.rsqrt(mean_square + epsilon) * scale


def activate(upsampled, gains):
    width = gains.shape[1]
    shaped = upsampled.reshape(upsampled.shape[:-1] + (upsampled.shape[-1] // width, width))
    result = jax.nn.gelu(normalize(shaped, gains[0]), approximate=True).astype(jnp.bfloat16)
    return result.reshape(upsampled.shape)


def gelu_tanh(values):
    return 0.5 * values * (1.0 + jnp.tanh(0.7978845608028654 * (values + 0.044715 * (values * values * values))))


def reduce_scatter_kernel(count, parts_ref, out_ref, held, send_sem, recv_sem):
    me = lax.axis_index("section")
    barrier = pltpu.get_barrier_semaphore()
    for step in range(1, count):
        peer = lax.rem(me + step, count)
        pl.semaphore_signal(barrier, inc=1, device_id={"section": peer}, device_id_type=MESH)
    pl.semaphore_wait(barrier, count - 1)
    sends = []
    for step in range(1, count):
        peer = lax.rem(me + step, count)
        copy = pltpu.make_async_remote_copy(
            src_ref=parts_ref.at[peer],
            dst_ref=held.at[step],
            send_sem=send_sem.at[step],
            recv_sem=recv_sem.at[step],
            device_id={"section": peer},
            device_id_type=MESH,
        )
        copy.start()
        sends.append(copy)
    total = parts_ref[me]
    for step in range(1, count):
        sends[step - 1].wait_recv()
        total = total + held[step]
    for copy in sends:
        copy.wait_send()
    out_ref[...] = total.astype(out_ref.dtype)


def reduce_scatter(parts):
    count = lax.axis_size("section")
    shaped = parts.reshape((count, parts.shape[0] // count) + parts.shape[1:])
    return pl.pallas_call(
        functools.partial(reduce_scatter_kernel, count),
        out_shape=jax.ShapeDtypeStruct(shaped.shape[1:], jnp.bfloat16),
        in_specs=[pl.BlockSpec(memory_space=pltpu.VMEM)],
        out_specs=pl.BlockSpec(memory_space=pltpu.VMEM),
        scratch_shapes=[
            pltpu.VMEM(shaped.shape, jnp.float32),
            pltpu.SemaphoreType.DMA((count,)),
            pltpu.SemaphoreType.DMA((count,)),
        ],
        compiler_params=pltpu.CompilerParams(collective_id=0, has_side_effects=True),
    )(shaped)


def send_groups(me_x, me_y, count):
    return [
        (me_x, me_y + 1, None),
        (me_x + 1, 0, (me_y == count - 1) & (me_x + 1 < count)),
        (me_x - 1, count + 1, (me_y == 0) & (me_x > 0)),
    ]


def gather_kernel(tokens_ref, weight_hbm, gains_ref, out_ref, weight, field, held, send_sem, recv_sem, weight_sem):
    count = lax.axis_size("inl")
    me_x, me_y = lax.axis_index("inl"), lax.axis_index("xln")
    rows = tokens_ref.shape[0] // count
    width = gains_ref.shape[1]
    one = jnp.int32(1)
    loading = pltpu.make_async_copy(weight_hbm, weight, weight_sem)
    loading.start()
    groups = send_groups(me_x, me_y, count)
    sources = [(me_y - 1, count - 1, me_y >= 1)]
    sources += [(me_y, other, None) for other in range(count)]
    sources += [(me_y + 1, 0, me_y + 1 < count)]

    def is_me(x, y):
        return (x == me_x) & (y == me_y)

    barrier = pltpu.get_barrier_semaphore()
    expected = jnp.int32(0)
    for column, _, exists in groups:
        live = True if exists is None else exists
        expected = expected + jnp.where(live, count, 0)
        for other in range(count):

            @pl.when(jnp.logical_and(live, jnp.logical_not(is_me(other, column))))
            def _():
                pl.semaphore_signal(barrier, inc=1, device_id={"inl": other, "xln": column}, device_id_type=MESH)

            expected = expected - jnp.where(jnp.logical_and(live, is_me(other, column)), one, 0)
    for source_x, source_y, exists in sources:
        live = True if exists is None else exists
        mine = jnp.logical_and(live, is_me(source_x, source_y))
        expected = expected + jnp.where(jnp.logical_and(live, jnp.logical_not(mine)), one, 0)

        @pl.when(jnp.logical_and(live, jnp.logical_not(mine)))
        def _():
            pl.semaphore_signal(barrier, inc=1, device_id={"inl": source_x, "xln": source_y}, device_id_type=MESH)

    loading.wait()
    upsampled = jnp.dot(tokens_ref[...], weight[...], preferred_element_type=jnp.float32)
    for group in range(upsampled.shape[1] // width):
        part = upsampled[:, group * width : (group + 1) * width]
        mean_square = jnp.mean(part * part, axis=-1, keepdims=True)
        normed = part * lax.rsqrt(mean_square + epsilon) * gains_ref[0:1, :]
        field[:, group * width : (group + 1) * width] = gelu_tanh(normed).astype(field.dtype)
    pl.semaphore_wait(barrier, expected)
    copies = []
    for index, (column, slot, exists) in enumerate(groups):
        live = True if exists is None else exists
        for turn in range(count):
            other = lax.rem(me_y + turn, count)
            copy = pltpu.make_async_remote_copy(
                src_ref=field.at[pl.ds(pl.multiple_of(other * rows, rows), rows)],
                dst_ref=held.at[slot],
                send_sem=send_sem.at[index * count + turn],
                recv_sem=recv_sem.at[slot],
                device_id={"inl": other, "xln": column},
                device_id_type=MESH,
            )
            remote = jnp.logical_and(live, jnp.logical_not(is_me(other, column)))

            @pl.when(remote)
            def _():
                copy.start()

            copies.append((copy, remote))
    for slot, (source_x, source_y, exists) in enumerate(sources):
        live = True if exists is None else exists
        mine = jnp.logical_and(live, is_me(source_x, source_y))
        remote = jnp.logical_and(live, jnp.logical_not(mine))
        incoming = pltpu.make_async_remote_copy(
            src_ref=field.at[pl.ds(0, rows)],
            dst_ref=held.at[slot],
            send_sem=send_sem.at[0],
            recv_sem=recv_sem.at[slot],
            device_id={"inl": source_x, "xln": source_y},
            device_id_type=MESH,
        )

        @pl.when(remote)
        def _():
            incoming.wait_recv()
            out_ref[slot] = held[slot]

        @pl.when(mine)
        def _():
            out_ref[slot] = field[pl.ds(pl.multiple_of(me_x * rows, rows), rows)]

        @pl.when(jnp.logical_not(live))
        def _():
            out_ref[slot] = jnp.zeros(out_ref.shape[1:], out_ref.dtype)

    for copy, remote in copies:

        @pl.when(remote)
        def _():
            copy.wait_send()


def gather_bricks(tokens, weight, gains):
    count = lax.axis_size("inl")
    rows = tokens.shape[0] // count
    shape = (lax.axis_size("xln") + 2, rows, weight.shape[1])
    return pl.pallas_call(
        gather_kernel,
        out_shape=jax.ShapeDtypeStruct(shape, jnp.bfloat16),
        in_specs=[
            pl.BlockSpec(memory_space=pltpu.VMEM),
            pl.BlockSpec(memory_space=pl.ANY),
            pl.BlockSpec(memory_space=pltpu.VMEM),
        ],
        out_specs=pl.BlockSpec(memory_space=pltpu.VMEM),
        scratch_shapes=[
            pltpu.VMEM(weight.shape, weight.dtype),
            pltpu.VMEM((tokens.shape[0], weight.shape[1]), jnp.bfloat16),
            pltpu.VMEM(shape, jnp.bfloat16),
            pltpu.SemaphoreType.DMA((3 * count,)),
            pltpu.SemaphoreType.DMA((shape[0],)),
            pltpu.SemaphoreType.DMA(()),
        ],
        compiler_params=pltpu.CompilerParams(collective_id=3, has_side_effects=True),
    )(tokens, weight, gains)


def halo_x(field_ref, held, send_sem, recv_sem, others=0):
    nx = field_ref.shape[0]
    count = lax.axis_size("inl")
    me = lax.axis_index("inl")
    if others is not None:
        barrier = pltpu.get_barrier_semaphore()
        for step in (-1, 1):

            @pl.when((me + step >= 0) & (me + step < count))
            def _():
                pl.semaphore_signal(barrier, inc=1, device_id={"inl": me + step}, device_id_type=MESH)

        present = (me > 0).astype(jnp.int32) + (me < count - 1).astype(jnp.int32)
        pl.semaphore_wait(barrier, present + others)
    copies = []
    for index, step in enumerate((-1, 1)):
        source, target = (0, nx + 1) if step < 0 else (nx - 1, 0)
        copy = pltpu.make_async_remote_copy(
            src_ref=field_ref.at[source : source + 1],
            dst_ref=held.at[target : target + 1],
            send_sem=send_sem.at[index],
            recv_sem=recv_sem.at[index],
            device_id={"inl": me + step},
            device_id_type=MESH,
        )
        sends = (me + step >= 0) & (me + step < count)
        gets = (me - step >= 0) & (me - step < count)

        @pl.when(sends)
        def _():
            copy.start()

        @pl.when(jnp.logical_not(gets))
        def _():
            held[target : target + 1] = jnp.zeros((1,) + held.shape[1:], held.dtype)

        copies.append((copy, sends, gets))
    held[1 : nx + 1] = field_ref[...]
    for copy, sends, gets in copies:

        @pl.when(gets)
        def _():
            copy.wait_recv()

        @pl.when(sends)
        def _():
            copy.wait_send()


def conv_kernel(
    residual, field_ref, kernel_ref, gains_ref, out_ref, held, shifted, send_sem, recv_sem
):
    halo_x(field_ref, held, send_sem, recv_sem)
    nx, ny_in, nz, channels = field_ref.shape
    ny = ny_in - 2
    cells = nx * ny * nz
    width = shifted.shape[2]
    parts = []
    for offset_z in range(3):
        part = jnp.zeros((cells, width), jnp.float32)
        for offset_x in range(3):
            for offset_y in range(3):
                window = held[offset_x : offset_x + nx, offset_y : offset_y + ny].reshape(cells, channels)
                tap = kernel_ref[(offset_x * 3 + offset_y) * 3 + offset_z]
                if residual:
                    part = part + jnp.dot(window, tap, preferred_element_type=jnp.float32)
                else:
                    part = part + lax.dot_general(
                        window, tap, (((1,), (1,)), ((), ())), preferred_element_type=jnp.float32
                    )
        parts.append(part.reshape(nx * ny, nz, width))
    edge = jnp.zeros((nx * ny, 1, width), jnp.float32)
    shifted[:, 0:1] = edge
    shifted[:, nz + 1 : nz + 2] = edge
    shifted[:, 1 : nz + 1] = parts[0]
    total = parts[1] + shifted[:, 0:nz]
    shifted[:, 1 : nz + 1] = parts[2]
    total = total + shifted[:, 2 : nz + 2]
    if residual:
        mean_square = jnp.mean(total * total, axis=-1, keepdims=True)
        normed = total * lax.rsqrt(mean_square + epsilon) * gains_ref[1:2, :]
        base = field_ref[:, 1 : ny + 1].reshape(nx * ny, nz, channels).astype(jnp.float32)
        mixed = gelu_tanh(normed + base).reshape(nx, ny, nz, channels)
        me_y, count_y = lax.axis_index("xln"), lax.axis_size("xln")
        row = lax.broadcasted_iota(jnp.int32, mixed.shape, 1)
        outside = ((row == 0) & (me_y == 0)) | ((row == ny - 1) & (me_y == count_y - 1))
        out_ref[...] = jnp.where(outside, 0.0, mixed).astype(out_ref.dtype)
    else:
        out_ref[...] = total.reshape(out_ref.shape)


def conv_stage(field, kernel, gains, residual, collective):
    nx, ny_in, nz, channels = field.shape
    width = kernel.shape[2] if residual else kernel.shape[1]
    padded = (nx + 2, ny_in, nz, channels)
    ny = ny_in - 2
    dtype = jnp.bfloat16 if residual else jnp.float32
    return pl.pallas_call(
        functools.partial(conv_kernel, residual),
        out_shape=jax.ShapeDtypeStruct((nx, ny, nz, width), dtype),
        in_specs=[pl.BlockSpec(memory_space=pltpu.VMEM)] * 3,
        out_specs=pl.BlockSpec(memory_space=pltpu.VMEM),
        scratch_shapes=[
            pltpu.VMEM(padded, field.dtype),
            pltpu.VMEM((nx * ny, nz + 2, width), jnp.float32),
            pltpu.SemaphoreType.DMA((2,)),
            pltpu.SemaphoreType.DMA((2,)),
        ],
        compiler_params=pltpu.CompilerParams(collective_id=collective, has_side_effects=True),
    )(field, kernel, gains)


def final_kernel(field_ref, kernel_ref, out_ref, held, spread, shifted, parts, inbox, send_sem, recv_sem, sum_send, sum_recv):
    count = lax.axis_size("section")
    me = lax.axis_index("section")
    for step in range(1, count):
        pl.semaphore_signal(
            pltpu.get_barrier_semaphore(),
            inc=1,
            device_id={"section": lax.rem(me + step, count)},
            device_id_type=MESH,
        )
    halo_x(field_ref, held, send_sem, recv_sem, count - 1)
    nx, ny_in, nz, channels = field_ref.shape
    ny = ny_in - 2
    cells = nx * ny * nz
    outch = kernel_ref.shape[1]
    planes = (nx + 2) * ny_in
    edge = jnp.zeros((planes, 1, channels), jnp.float32)
    shifted[:, 0:1] = edge
    shifted[:, nz + 1 : nz + 2] = edge
    shifted[:, 1 : nz + 1] = held[...].reshape(planes, nz, channels).astype(jnp.float32)
    spread[0] = shifted[:, 0:nz].astype(spread.dtype).reshape(held.shape)
    spread[1] = held[...]
    spread[2] = shifted[:, 2 : nz + 2].astype(spread.dtype).reshape(held.shape)
    total = jnp.zeros((outch, cells), jnp.float32)
    for offset_x in range(3):
        for offset_y in range(3):
            for offset_z in range(3):
                window = spread[offset_z, offset_x : offset_x + nx, offset_y : offset_y + ny].reshape(cells, channels)
                total = total + lax.dot_general(
                    kernel_ref[(offset_x * 3 + offset_y) * 3 + offset_z],
                    window,
                    (((1,), (1,)), ((), ())),
                    preferred_element_type=jnp.float32,
                )
    block = outch // count
    for peer in range(count):
        parts[peer] = total[peer * block : (peer + 1) * block]
    sends = []
    for step in range(1, count):
        peer = lax.rem(me + step, count)
        copy = pltpu.make_async_remote_copy(
            src_ref=parts.at[peer],
            dst_ref=inbox.at[step],
            send_sem=sum_send.at[step],
            recv_sem=sum_recv.at[step],
            device_id={"section": peer},
            device_id_type=MESH,
        )
        copy.start()
        sends.append(copy)
    result = parts[me]
    for step in range(1, count):
        sends[step - 1].wait_recv()
        result = result + inbox[step]
    for copy in sends:
        copy.wait_send()
    out_ref[...] = result.reshape(out_ref.shape).astype(out_ref.dtype)


def final_stage(field, kernel, collective):
    nx, ny_in, nz, channels = field.shape
    ny = ny_in - 2
    count = lax.axis_size("section")
    outch = kernel.shape[1]
    padded = (nx + 2, ny_in, nz, channels)
    block = outch // count
    return pl.pallas_call(
        final_kernel,
        out_shape=jax.ShapeDtypeStruct((block, nx, ny * nz), jnp.bfloat16),
        in_specs=[pl.BlockSpec(memory_space=pltpu.VMEM)] * 2,
        out_specs=pl.BlockSpec(memory_space=pltpu.VMEM),
        scratch_shapes=[
            pltpu.VMEM(padded, field.dtype),
            pltpu.VMEM((3,) + padded, field.dtype),
            pltpu.VMEM(((nx + 2) * ny_in, nz + 2, channels), jnp.float32),
            pltpu.VMEM((count, block, nx * ny * nz), jnp.float32),
            pltpu.VMEM((count, block, nx * ny * nz), jnp.float32),
            pltpu.SemaphoreType.DMA((2,)),
            pltpu.SemaphoreType.DMA((2,)),
            pltpu.SemaphoreType.DMA((count,)),
            pltpu.SemaphoreType.DMA((count,)),
        ],
        compiler_params=pltpu.CompilerParams(collective_id=collective, has_side_effects=True),
    )(field, kernel)


def block_kernel(
    field_ref, kernel_in_ref, gains_ref, kernel_out_ref, out_ref,
    held, shifted, mixed, held_out, spread, shifted_out, parts, inbox,
    send_sem, recv_sem, send_out, recv_out, sum_send, sum_recv,
):
    count = lax.axis_size("section")
    me = lax.axis_index("section")
    for step in range(1, count):
        pl.semaphore_signal(
            pltpu.get_barrier_semaphore(),
            inc=1,
            device_id={"section": lax.rem(me + step, count)},
            device_id_type=MESH,
        )
    halo_x(field_ref, held, send_sem, recv_sem, count - 1)
    nx, ny_in, nz, channels = field_ref.shape
    ny = ny_in - 2
    cells = nx * ny * nz
    width = channels
    parts_in = []
    for offset_z in range(3):
        part = jnp.zeros((cells, width), jnp.float32)
        for offset_x in range(3):
            for offset_y in range(3):
                window = held[offset_x : offset_x + nx, offset_y : offset_y + ny].reshape(cells, channels)
                tap = kernel_in_ref[(offset_x * 3 + offset_y) * 3 + offset_z]
                part = part + jnp.dot(window, tap, preferred_element_type=jnp.float32)
        parts_in.append(part.reshape(nx * ny, nz, width))
    edge = jnp.zeros((nx * ny, 1, width), jnp.float32)
    shifted[:, 0:1] = edge
    shifted[:, nz + 1 : nz + 2] = edge
    shifted[:, 1 : nz + 1] = parts_in[0]
    total = parts_in[1] + shifted[:, 0:nz]
    shifted[:, 1 : nz + 1] = parts_in[2]
    total = total + shifted[:, 2 : nz + 2]
    mean_square = jnp.mean(total * total, axis=-1, keepdims=True)
    normed = total * lax.rsqrt(mean_square + epsilon) * gains_ref[1:2, :]
    base = field_ref[:, 1 : ny + 1].reshape(nx * ny, nz, channels).astype(jnp.float32)
    activated = gelu_tanh(normed + base).reshape(nx, ny, nz, channels)
    me_y, count_y = lax.axis_index("xln"), lax.axis_size("xln")
    row = lax.broadcasted_iota(jnp.int32, activated.shape, 1)
    outside = ((row == 0) & (me_y == 0)) | ((row == ny - 1) & (me_y == count_y - 1))
    mixed[...] = jnp.where(outside, 0.0, activated).astype(mixed.dtype)

    halo_x(mixed, held_out, send_out, recv_out, None)
    ny_out = ny - 2
    cells_out = nx * ny_out * nz
    outch = kernel_out_ref.shape[1]
    planes = (nx + 2) * ny
    edge = jnp.zeros((planes, 1, channels), jnp.float32)
    shifted_out[:, 0:1] = edge
    shifted_out[:, nz + 1 : nz + 2] = edge
    shifted_out[:, 1 : nz + 1] = held_out[...].reshape(planes, nz, channels).astype(jnp.float32)
    spread[0] = shifted_out[:, 0:nz].astype(spread.dtype).reshape(held_out.shape)
    spread[1] = held_out[...]
    spread[2] = shifted_out[:, 2 : nz + 2].astype(spread.dtype).reshape(held_out.shape)
    result_t = jnp.zeros((outch, cells_out), jnp.float32)
    for offset_x in range(3):
        for offset_y in range(3):
            for offset_z in range(3):
                window = spread[offset_z, offset_x : offset_x + nx, offset_y : offset_y + ny_out].reshape(
                    cells_out, channels
                )
                result_t = result_t + lax.dot_general(
                    kernel_out_ref[(offset_x * 3 + offset_y) * 3 + offset_z],
                    window,
                    (((1,), (1,)), ((), ())),
                    preferred_element_type=jnp.float32,
                )
    block = outch // count
    for peer in range(count):
        parts[peer] = result_t[peer * block : (peer + 1) * block]
    sends = []
    for step in range(1, count):
        peer = lax.rem(me + step, count)
        copy = pltpu.make_async_remote_copy(
            src_ref=parts.at[peer],
            dst_ref=inbox.at[step],
            send_sem=sum_send.at[step],
            recv_sem=sum_recv.at[step],
            device_id={"section": peer},
            device_id_type=MESH,
        )
        copy.start()
        sends.append(copy)
    result = parts[me]
    for step in range(1, count):
        sends[step - 1].wait_recv()
        result = result + inbox[step]
    for copy in sends:
        copy.wait_send()
    out_ref[...] = result.reshape(out_ref.shape).astype(out_ref.dtype)


def decoder_block(field, kernel_in, gains, kernel_out, collective):
    nx, ny_in, nz, channels = field.shape
    ny = ny_in - 2
    ny_out = ny - 2
    count = lax.axis_size("section")
    outch = kernel_out.shape[1]
    block = outch // count
    return pl.pallas_call(
        block_kernel,
        out_shape=jax.ShapeDtypeStruct((block, nx, ny_out * nz), jnp.bfloat16),
        in_specs=[pl.BlockSpec(memory_space=pltpu.VMEM)] * 4,
        out_specs=pl.BlockSpec(memory_space=pltpu.VMEM),
        scratch_shapes=[
            pltpu.VMEM((nx + 2, ny_in, nz, channels), field.dtype),
            pltpu.VMEM((nx * ny, nz + 2, channels), jnp.float32),
            pltpu.VMEM((nx, ny, nz, channels), field.dtype),
            pltpu.VMEM((nx + 2, ny, nz, channels), field.dtype),
            pltpu.VMEM((3, nx + 2, ny, nz, channels), field.dtype),
            pltpu.VMEM(((nx + 2) * ny, nz + 2, channels), jnp.float32),
            pltpu.VMEM((count, block, nx * ny_out * nz), jnp.float32),
            pltpu.VMEM((count, block, nx * ny_out * nz), jnp.float32),
            pltpu.SemaphoreType.DMA((2,)),
            pltpu.SemaphoreType.DMA((2,)),
            pltpu.SemaphoreType.DMA((2,)),
            pltpu.SemaphoreType.DMA((2,)),
            pltpu.SemaphoreType.DMA((count,)),
            pltpu.SemaphoreType.DMA((count,)),
        ],
        compiler_params=pltpu.CompilerParams(collective_id=collective, has_side_effects=True),
    )(field, kernel_in, gains, kernel_out)


def local(skips, deconv_weight, norm_gain, conv_in, conv_out):
    inl_size = lax.axis_size("inl")
    tokens_here = skips[0]
    weight = deconv_weight[0]
    gains = norm_gain[0]
    channels = gains.shape[1]
    cell_x = 2 * PXD
    cell_y = 2 * lax.axis_size("xln")
    cell_z = 2 * GZ
    assert tokens_here.shape[0] == inl_size * PXD * GZ
    brick = gather_bricks(tokens_here, weight, gains)
    lines = brick.shape[0]
    field = (
        brick.reshape(lines, PXD, GZ, 2, 2, 2, channels)
        .transpose(1, 3, 0, 4, 2, 5, 6)
        .reshape(cell_x, 2 * lines, cell_z, channels)
    )
    return decoder_block(field, conv_in[0], gains, conv_out[0], 1)


def solution(mesh):
    return jax.shard_map(
        local,
        mesh=mesh,
        in_specs=(
            P("section", ("inl", "xln"), None),
            P("section", None, None),
            P("section", None, None),
            P("section", None, None, None),
            P("section", None, None, None),
        ),
        out_specs=P("section", "inl", "xln"),
        check_vma=False,
    )
```

```python
import functools

import jax
import jax.numpy as jnp
from jax import lax
from jax.experimental import pallas as pl
from jax.experimental.pallas import tpu as pltpu
from jax.sharding import PartitionSpec as P

MESH = pl.DeviceIdType.MESH
PXD = 2
GZ = 8


epsilon = 1e-05


def gelu_tanh(values):
    return 0.5 * values * (1.0 + jnp.tanh(0.7978845608028654 * (values + 0.044715 * (values * values * values))))


def send_groups(me_x, me_y, count):
    return [
        (me_x, me_y + 1, None),
        (me_x + 1, 0, (me_y == count - 1) & (me_x + 1 < count)),
        (me_x - 1, count + 1, (me_y == 0) & (me_x > 0)),
    ]


def gather_kernel(tokens_ref, weight_hbm, gains_ref, out_ref, weight, field, held, send_sem, recv_sem, weight_sem):
    count = lax.axis_size("inl")
    me_x, me_y = lax.axis_index("inl"), lax.axis_index("xln")
    rows = tokens_ref.shape[0] // count
    width = gains_ref.shape[1]
    one = jnp.int32(1)
    loading = pltpu.make_async_copy(weight_hbm, weight, weight_sem)
    loading.start()
    groups = send_groups(me_x, me_y, count)
    sources = [(me_y - 1, count - 1, me_y >= 1)]
    sources += [(me_y, other, None) for other in range(count)]
    sources += [(me_y + 1, 0, me_y + 1 < count)]

    def is_me(x, y):
        return (x == me_x) & (y == me_y)

    barrier = pltpu.get_barrier_semaphore()
    expected = jnp.int32(0)
    for column, _, exists in groups:
        live = True if exists is None else exists
        expected = expected + jnp.where(live, count, 0)
        for other in range(count):

            @pl.when(jnp.logical_and(live, jnp.logical_not(is_me(other, column))))
            def _():
                pl.semaphore_signal(barrier, inc=1, device_id={"inl": other, "xln": column}, device_id_type=MESH)

            expected = expected - jnp.where(jnp.logical_and(live, is_me(other, column)), one, 0)
    for source_x, source_y, exists in sources:
        live = True if exists is None else exists
        mine = jnp.logical_and(live, is_me(source_x, source_y))
        expected = expected + jnp.where(jnp.logical_and(live, jnp.logical_not(mine)), one, 0)

        @pl.when(jnp.logical_and(live, jnp.logical_not(mine)))
        def _():
            pl.semaphore_signal(barrier, inc=1, device_id={"inl": source_x, "xln": source_y}, device_id_type=MESH)

    loading.wait()
    upsampled = jnp.dot(tokens_ref[...], weight[...], preferred_element_type=jnp.float32)
    for group in range(upsampled.shape[1] // width):
        part = upsampled[:, group * width : (group + 1) * width]
        mean_square = jnp.mean(part * part, axis=-1, keepdims=True)
        normed = part * lax.rsqrt(mean_square + epsilon) * gains_ref[0:1, :]
        field[:, group * width : (group + 1) * width] = gelu_tanh(normed).astype(field.dtype)
    pl.semaphore_wait(barrier, expected)
    copies = []
    for index, (column, slot, exists) in enumerate(groups):
        live = True if exists is None else exists
        for turn in range(count):
            other = lax.rem(me_y + turn, count)
            copy = pltpu.make_async_remote_copy(
                src_ref=field.at[pl.ds(pl.multiple_of(other * rows, rows), rows)],
                dst_ref=held.at[slot],
                send_sem=send_sem.at[index * count + turn],
                recv_sem=recv_sem.at[slot],
                device_id={"inl": other, "xln": column},
                device_id_type=MESH,
            )
            remote = jnp.logical_and(live, jnp.logical_not(is_me(other, column)))

            @pl.when(remote)
            def _():
                copy.start()

            copies.append((copy, remote))
    for slot, (source_x, source_y, exists) in enumerate(sources):
        live = True if exists is None else exists
        mine = jnp.logical_and(live, is_me(source_x, source_y))
        remote = jnp.logical_and(live, jnp.logical_not(mine))
        incoming = pltpu.make_async_remote_copy(
            src_ref=field.at[pl.ds(0, rows)],
            dst_ref=held.at[slot],
            send_sem=send_sem.at[0],
            recv_sem=recv_sem.at[slot],
            device_id={"inl": source_x, "xln": source_y},
            device_id_type=MESH,
        )

        @pl.when(remote)
        def _():
            incoming.wait_recv()
            out_ref[slot] = held[slot]

        @pl.when(mine)
        def _():
            out_ref[slot] = field[pl.ds(pl.multiple_of(me_x * rows, rows), rows)]

        @pl.when(jnp.logical_not(live))
        def _():
            out_ref[slot] = jnp.zeros(out_ref.shape[1:], out_ref.dtype)

    for copy, remote in copies:

        @pl.when(remote)
        def _():
            copy.wait_send()


def gather_bricks(tokens, weight, gains):
    count = lax.axis_size("inl")
    rows = tokens.shape[0] // count
    shape = (lax.axis_size("xln") + 2, rows, weight.shape[1])
    return pl.pallas_call(
        gather_kernel,
        out_shape=jax.ShapeDtypeStruct(shape, jnp.bfloat16),
        in_specs=[
            pl.BlockSpec(memory_space=pltpu.VMEM),
            pl.BlockSpec(memory_space=pl.ANY),
            pl.BlockSpec(memory_space=pltpu.VMEM),
        ],
        out_specs=pl.BlockSpec(memory_space=pltpu.VMEM),
        scratch_shapes=[
            pltpu.VMEM(weight.shape, weight.dtype),
            pltpu.VMEM((tokens.shape[0], weight.shape[1]), jnp.bfloat16),
            pltpu.VMEM(shape, jnp.bfloat16),
            pltpu.SemaphoreType.DMA((3 * count,)),
            pltpu.SemaphoreType.DMA((shape[0],)),
            pltpu.SemaphoreType.DMA(()),
        ],
        compiler_params=pltpu.CompilerParams(collective_id=3, has_side_effects=True),
    )(tokens, weight, gains)


def halo_x(field_ref, held, send_sem, recv_sem, others=0):
    nx = field_ref.shape[0]
    count = lax.axis_size("inl")
    me = lax.axis_index("inl")
    if others is not None:
        barrier = pltpu.get_barrier_semaphore()
        for step in (-1, 1):

            @pl.when((me + step >= 0) & (me + step < count))
            def _():
                pl.semaphore_signal(barrier, inc=1, device_id={"inl": me + step}, device_id_type=MESH)

        present = (me > 0).astype(jnp.int32) + (me < count - 1).astype(jnp.int32)
        pl.semaphore_wait(barrier, present + others)
    copies = []
    for index, step in enumerate((-1, 1)):
        source, target = (0, nx + 1) if step < 0 else (nx - 1, 0)
        copy = pltpu.make_async_remote_copy(
            src_ref=field_ref.at[source : source + 1],
            dst_ref=held.at[target : target + 1],
            send_sem=send_sem.at[index],
            recv_sem=recv_sem.at[index],
            device_id={"inl": me + step},
            device_id_type=MESH,
        )
        sends = (me + step >= 0) & (me + step < count)
        gets = (me - step >= 0) & (me - step < count)

        @pl.when(sends)
        def _():
            copy.start()

        @pl.when(jnp.logical_not(gets))
        def _():
            held[target : target + 1] = jnp.zeros((1,) + held.shape[1:], held.dtype)

        copies.append((copy, sends, gets))
    held[1 : nx + 1] = field_ref[...]
    for copy, sends, gets in copies:

        @pl.when(gets)
        def _():
            copy.wait_recv()

        @pl.when(sends)
        def _():
            copy.wait_send()


def block_kernel(
    field_ref, kernel_in_ref, gains_ref, kernel_out_ref, out_ref,
    held, shifted, mixed, held_out, shifted_out, parts, inbox,
    send_sem, recv_sem, send_out, recv_out, sum_send, sum_recv,
):
    count = lax.axis_size("section")
    me = lax.axis_index("section")
    for step in range(1, count):
        pl.semaphore_signal(
            pltpu.get_barrier_semaphore(),
            inc=1,
            device_id={"section": lax.rem(me + step, count)},
            device_id_type=MESH,
        )
    halo_x(field_ref, held, send_sem, recv_sem, count - 1)
    nx, ny_in, nz, channels = field_ref.shape
    ny = ny_in - 2
    cells = nx * ny * nz
    width = channels
    parts_in = []
    for offset_z in range(3):
        part = jnp.zeros((cells, width), jnp.float32)
        for offset_x in range(3):
            for offset_y in range(3):
                window = held[offset_x : offset_x + nx, offset_y : offset_y + ny].reshape(cells, channels)
                tap = kernel_in_ref[(offset_x * 3 + offset_y) * 3 + offset_z]
                part = part + jnp.dot(window, tap, preferred_element_type=jnp.float32)
        parts_in.append(part.reshape(nx * ny, nz, width))
    edge = jnp.zeros((nx * ny, 1, width), jnp.float32)
    shifted[:, 0:1] = edge
    shifted[:, nz + 1 : nz + 2] = edge
    shifted[:, 1 : nz + 1] = parts_in[0]
    total = parts_in[1] + shifted[:, 0:nz]
    shifted[:, 1 : nz + 1] = parts_in[2]
    total = total + shifted[:, 2 : nz + 2]
    mean_square = jnp.mean(total * total, axis=-1, keepdims=True)
    normed = total * lax.rsqrt(mean_square + epsilon) * gains_ref[1:2, :]
    base = field_ref[:, 1 : ny + 1].reshape(nx * ny, nz, channels).astype(jnp.float32)
    activated = gelu_tanh(normed + base).reshape(nx, ny, nz, channels)
    me_y, count_y = lax.axis_index("xln"), lax.axis_size("xln")
    row = lax.broadcasted_iota(jnp.int32, activated.shape, 1)
    outside = ((row == 0) & (me_y == 0)) | ((row == ny - 1) & (me_y == count_y - 1))
    mixed[...] = jnp.where(outside, 0.0, activated).astype(mixed.dtype)

    halo_x(mixed, held_out, send_out, recv_out, None)
    ny_out = ny - 2
    cells_out = nx * ny_out * nz
    outch = kernel_out_ref.shape[1] // 3
    columns = jnp.concatenate(
        [
            held_out[offset_x : offset_x + nx, offset_y : offset_y + ny_out].reshape(cells_out, channels)
            for offset_x in range(3)
            for offset_y in range(3)
        ],
        axis=1,
    )
    by_depth = jnp.dot(columns, kernel_out_ref[...], preferred_element_type=jnp.float32)
    planes = nx * ny_out
    edge = jnp.zeros((planes, 1, outch), jnp.float32)
    shifted_out[:, 0:1] = edge
    shifted_out[:, nz + 1 : nz + 2] = edge
    shifted_out[:, 1 : nz + 1] = by_depth[:, 0:outch].reshape(planes, nz, outch)
    summed = by_depth[:, outch : 2 * outch].reshape(planes, nz, outch) + shifted_out[:, 0:nz]
    shifted_out[:, 1 : nz + 1] = by_depth[:, 2 * outch : 3 * outch].reshape(planes, nz, outch)
    summed = summed + shifted_out[:, 2 : nz + 2]
    result_t = summed.reshape(cells_out, outch).T
    block = outch // count
    for peer in range(count):
        parts[peer] = result_t[peer * block : (peer + 1) * block]
    sends = []
    for step in range(1, count):
        peer = lax.rem(me + step, count)
        copy = pltpu.make_async_remote_copy(
            src_ref=parts.at[peer],
            dst_ref=inbox.at[step],
            send_sem=sum_send.at[step],
            recv_sem=sum_recv.at[step],
            device_id={"section": peer},
            device_id_type=MESH,
        )
        copy.start()
        sends.append(copy)
    result = parts[me]
    for step in range(1, count):
        sends[step - 1].wait_recv()
        result = result + inbox[step]
    for copy in sends:
        copy.wait_send()
    out_ref[...] = result.reshape(out_ref.shape).astype(out_ref.dtype)


def decoder_block(field, kernel_in, gains, kernel_out, collective):
    nx, ny_in, nz, channels = field.shape
    ny = ny_in - 2
    ny_out = ny - 2
    count = lax.axis_size("section")
    outch = kernel_out.shape[1] // 3
    block = outch // count
    return pl.pallas_call(
        block_kernel,
        out_shape=jax.ShapeDtypeStruct((block, nx, ny_out * nz), jnp.bfloat16),
        in_specs=[pl.BlockSpec(memory_space=pltpu.VMEM)] * 4,
        out_specs=pl.BlockSpec(memory_space=pltpu.VMEM),
        scratch_shapes=[
            pltpu.VMEM((nx + 2, ny_in, nz, channels), field.dtype),
            pltpu.VMEM((nx * ny, nz + 2, channels), jnp.float32),
            pltpu.VMEM((nx, ny, nz, channels), field.dtype),
            pltpu.VMEM((nx + 2, ny, nz, channels), field.dtype),
            pltpu.VMEM((nx * ny_out, nz + 2, outch), jnp.float32),
            pltpu.VMEM((count, block, nx * ny_out * nz), jnp.float32),
            pltpu.VMEM((count, block, nx * ny_out * nz), jnp.float32),
            pltpu.SemaphoreType.DMA((2,)),
            pltpu.SemaphoreType.DMA((2,)),
            pltpu.SemaphoreType.DMA((2,)),
            pltpu.SemaphoreType.DMA((2,)),
            pltpu.SemaphoreType.DMA((count,)),
            pltpu.SemaphoreType.DMA((count,)),
        ],
        compiler_params=pltpu.CompilerParams(collective_id=collective, has_side_effects=True),
    )(field, kernel_in, gains, kernel_out)


def local(skips, deconv_weight, norm_gain, conv_in, conv_out):
    inl_size = lax.axis_size("inl")
    tokens_here = skips[0]
    weight = deconv_weight[0]
    gains = norm_gain[0]
    channels = gains.shape[1]
    cell_x = 2 * PXD
    cell_y = 2 * lax.axis_size("xln")
    cell_z = 2 * GZ
    assert tokens_here.shape[0] == inl_size * PXD * GZ
    brick = gather_bricks(tokens_here, weight, gains)
    lines = brick.shape[0]
    field = (
        brick.reshape(lines, PXD, GZ, 2, 2, 2, channels)
        .transpose(1, 3, 0, 4, 2, 5, 6)
        .reshape(cell_x, 2 * lines, cell_z, channels)
    )
    taps, outch, channels_in = conv_out.shape[1:]
    out_weight = (
        conv_out[0].reshape(taps // 3, 3, outch, channels_in).transpose(0, 3, 1, 2).reshape(-1, 3 * outch)
    )
    return decoder_block(field, conv_in[0], gains, out_weight, 1)


def solution(mesh):
    return jax.shard_map(
        local,
        mesh=mesh,
        in_specs=(
            P("section", ("inl", "xln"), None),
            P("section", None, None),
            P("section", None, None),
            P("section", None, None, None),
            P("section", None, None, None),
        ),
        out_specs=P("section", "inl", "xln"),
        check_vma=False,
    )
```

```python
import functools

import jax
import jax.numpy as jnp
from jax import lax
from jax.experimental import pallas as pl
from jax.experimental.pallas import tpu as pltpu
from jax.sharding import PartitionSpec as P

MESH = pl.DeviceIdType.MESH
PXD = 2
GZ = 8


epsilon = 1e-05


def gelu_tanh(values):
    return 0.5 * values * (1.0 + jnp.tanh(0.7978845608028654 * (values + 0.044715 * (values * values * values))))


def send_groups(me_x, me_y, count):
    return [
        (me_x, me_y + 1, None),
        (me_x + 1, 0, (me_y == count - 1) & (me_x + 1 < count)),
        (me_x - 1, count + 1, (me_y == 0) & (me_x > 0)),
    ]


def gather_kernel(tokens_ref, weight_hbm, gains_ref, out_ref, weight, field, held, send_sem, recv_sem, weight_sem):
    count = lax.axis_size("inl")
    me_x, me_y = lax.axis_index("inl"), lax.axis_index("xln")
    rows = tokens_ref.shape[0] // count
    width = gains_ref.shape[1]
    one = jnp.int32(1)
    loading = pltpu.make_async_copy(weight_hbm, weight, weight_sem)
    loading.start()
    groups = send_groups(me_x, me_y, count)
    sources = [(me_y - 1, count - 1, me_y >= 1)]
    sources += [(me_y, other, None) for other in range(count)]
    sources += [(me_y + 1, 0, me_y + 1 < count)]

    def is_me(x, y):
        return (x == me_x) & (y == me_y)

    barrier = pltpu.get_barrier_semaphore()
    expected = jnp.int32(0)
    for column, _, exists in groups:
        live = True if exists is None else exists
        expected = expected + jnp.where(live, count, 0)
        for other in range(count):

            @pl.when(jnp.logical_and(live, jnp.logical_not(is_me(other, column))))
            def _():
                pl.semaphore_signal(barrier, inc=1, device_id={"inl": other, "xln": column}, device_id_type=MESH)

            expected = expected - jnp.where(jnp.logical_and(live, is_me(other, column)), one, 0)
    for source_x, source_y, exists in sources:
        live = True if exists is None else exists
        mine = jnp.logical_and(live, is_me(source_x, source_y))
        expected = expected + jnp.where(jnp.logical_and(live, jnp.logical_not(mine)), one, 0)

        @pl.when(jnp.logical_and(live, jnp.logical_not(mine)))
        def _():
            pl.semaphore_signal(barrier, inc=1, device_id={"inl": source_x, "xln": source_y}, device_id_type=MESH)

    loading.wait()
    upsampled = jnp.dot(tokens_ref[...], weight[...], preferred_element_type=jnp.float32)
    for group in range(upsampled.shape[1] // width):
        part = upsampled[:, group * width : (group + 1) * width]
        mean_square = jnp.mean(part * part, axis=-1, keepdims=True)
        normed = part * lax.rsqrt(mean_square + epsilon) * gains_ref[0:1, :]
        field[:, group * width : (group + 1) * width] = gelu_tanh(normed).astype(field.dtype)
    pl.semaphore_wait(barrier, expected)
    copies = []
    for index, (column, slot, exists) in enumerate(groups):
        live = True if exists is None else exists
        for turn in range(count):
            other = lax.rem(me_y + turn, count)
            copy = pltpu.make_async_remote_copy(
                src_ref=field.at[pl.ds(pl.multiple_of(other * rows, rows), rows)],
                dst_ref=held.at[slot],
                send_sem=send_sem.at[index * count + turn],
                recv_sem=recv_sem.at[slot],
                device_id={"inl": other, "xln": column},
                device_id_type=MESH,
            )
            remote = jnp.logical_and(live, jnp.logical_not(is_me(other, column)))

            @pl.when(remote)
            def _():
                copy.start()

            copies.append((copy, remote))
    for slot, (source_x, source_y, exists) in enumerate(sources):
        live = True if exists is None else exists
        mine = jnp.logical_and(live, is_me(source_x, source_y))
        remote = jnp.logical_and(live, jnp.logical_not(mine))
        incoming = pltpu.make_async_remote_copy(
            src_ref=field.at[pl.ds(0, rows)],
            dst_ref=held.at[slot],
            send_sem=send_sem.at[0],
            recv_sem=recv_sem.at[slot],
            device_id={"inl": source_x, "xln": source_y},
            device_id_type=MESH,
        )

        @pl.when(remote)
        def _():
            incoming.wait_recv()
            out_ref[slot] = held[slot]

        @pl.when(mine)
        def _():
            out_ref[slot] = field[pl.ds(pl.multiple_of(me_x * rows, rows), rows)]

        @pl.when(jnp.logical_not(live))
        def _():
            out_ref[slot] = jnp.zeros(out_ref.shape[1:], out_ref.dtype)

    for copy, remote in copies:

        @pl.when(remote)
        def _():
            copy.wait_send()


def gather_bricks(tokens, weight, gains):
    count = lax.axis_size("inl")
    rows = tokens.shape[0] // count
    shape = (lax.axis_size("xln") + 2, rows, weight.shape[1])
    return pl.pallas_call(
        gather_kernel,
        out_shape=jax.ShapeDtypeStruct(shape, jnp.bfloat16),
        in_specs=[
            pl.BlockSpec(memory_space=pltpu.VMEM),
            pl.BlockSpec(memory_space=pl.ANY),
            pl.BlockSpec(memory_space=pltpu.VMEM),
        ],
        out_specs=pl.BlockSpec(memory_space=pltpu.VMEM),
        scratch_shapes=[
            pltpu.VMEM(weight.shape, weight.dtype),
            pltpu.VMEM((tokens.shape[0], weight.shape[1]), jnp.bfloat16),
            pltpu.VMEM(shape, jnp.bfloat16),
            pltpu.SemaphoreType.DMA((3 * count,)),
            pltpu.SemaphoreType.DMA((shape[0],)),
            pltpu.SemaphoreType.DMA(()),
        ],
        compiler_params=pltpu.CompilerParams(collective_id=3, has_side_effects=True),
    )(tokens, weight, gains)


def halo_x(field_ref, held, send_sem, recv_sem, others=0):
    nx = field_ref.shape[0]
    count = lax.axis_size("inl")
    me = lax.axis_index("inl")
    if others is not None:
        barrier = pltpu.get_barrier_semaphore()
        for step in (-1, 1):

            @pl.when((me + step >= 0) & (me + step < count))
            def _():
                pl.semaphore_signal(barrier, inc=1, device_id={"inl": me + step}, device_id_type=MESH)

        present = (me > 0).astype(jnp.int32) + (me < count - 1).astype(jnp.int32)
        pl.semaphore_wait(barrier, present + others)
    copies = []
    for index, step in enumerate((-1, 1)):
        source, target = (0, nx + 1) if step < 0 else (nx - 1, 0)
        copy = pltpu.make_async_remote_copy(
            src_ref=field_ref.at[source : source + 1],
            dst_ref=held.at[target : target + 1],
            send_sem=send_sem.at[index],
            recv_sem=recv_sem.at[index],
            device_id={"inl": me + step},
            device_id_type=MESH,
        )
        sends = (me + step >= 0) & (me + step < count)
        gets = (me - step >= 0) & (me - step < count)

        @pl.when(sends)
        def _():
            copy.start()

        @pl.when(jnp.logical_not(gets))
        def _():
            held[target : target + 1] = jnp.zeros((1,) + held.shape[1:], held.dtype)

        copies.append((copy, sends, gets))
    held[1 : nx + 1] = field_ref[...]
    for copy, sends, gets in copies:

        @pl.when(gets)
        def _():
            copy.wait_recv()

        @pl.when(sends)
        def _():
            copy.wait_send()


def block_kernel(
    field_ref, kernel_in_ref, gains_ref, kernel_out_ref, out_ref,
    held, shifted, mixed, held_out, shifted_out, parts, inbox,
    send_sem, recv_sem, send_out, recv_out, sum_send, sum_recv,
):
    count = lax.axis_size("section")
    me = lax.axis_index("section")
    for step in range(1, count):
        pl.semaphore_signal(
            pltpu.get_barrier_semaphore(),
            inc=1,
            device_id={"section": lax.rem(me + step, count)},
            device_id_type=MESH,
        )
    halo_x(field_ref, held, send_sem, recv_sem, count - 1)
    nx, ny_in, nz, channels = field_ref.shape
    ny = ny_in - 2
    cells = nx * ny * nz
    width = channels
    parts_in = []
    for offset_z in range(3):
        part = jnp.zeros((cells, width), jnp.float32)
        for offset_x in range(3):
            for offset_y in range(3):
                window = held[offset_x : offset_x + nx, offset_y : offset_y + ny].reshape(cells, channels)
                tap = kernel_in_ref[(offset_x * 3 + offset_y) * 3 + offset_z]
                part = part + jnp.dot(window, tap, preferred_element_type=jnp.float32)
        parts_in.append(part.reshape(nx * ny, nz, width))
    edge = jnp.zeros((nx * ny, 1, width), jnp.float32)
    shifted[:, 0:1] = edge
    shifted[:, nz + 1 : nz + 2] = edge
    shifted[:, 1 : nz + 1] = parts_in[0]
    total = parts_in[1] + shifted[:, 0:nz]
    shifted[:, 1 : nz + 1] = parts_in[2]
    total = total + shifted[:, 2 : nz + 2]
    mean_square = jnp.mean(total * total, axis=-1, keepdims=True)
    normed = total * lax.rsqrt(mean_square + epsilon) * gains_ref[1:2, :]
    base = field_ref[:, 1 : ny + 1].reshape(nx * ny, nz, channels).astype(jnp.float32)
    activated = gelu_tanh(normed + base).reshape(nx, ny, nz, channels)
    me_y, count_y = lax.axis_index("xln"), lax.axis_size("xln")
    row = lax.broadcasted_iota(jnp.int32, activated.shape, 1)
    outside = ((row == 0) & (me_y == 0)) | ((row == ny - 1) & (me_y == count_y - 1))
    mixed[...] = jnp.where(outside, 0.0, activated).astype(mixed.dtype)

    halo_x(mixed, held_out, send_out, recv_out, None)
    ny_out = ny - 2
    cells_out = nx * ny_out * nz
    outch = kernel_out_ref.shape[1] // 3
    by_depth = jnp.zeros((cells_out, 3 * outch), jnp.float32)
    for offset_x in range(3):
        for offset_y in range(3):
            window = held_out[offset_x : offset_x + nx, offset_y : offset_y + ny_out].reshape(cells_out, channels)
            by_depth = by_depth + lax.dot_general(
                window,
                kernel_out_ref[offset_x * 3 + offset_y],
                (((1,), (1,)), ((), ())),
                preferred_element_type=jnp.float32,
            )
    planes = nx * ny_out
    edge = jnp.zeros((planes, 1, outch), jnp.float32)
    shifted_out[:, 0:1] = edge
    shifted_out[:, nz + 1 : nz + 2] = edge
    shifted_out[:, 1 : nz + 1] = by_depth[:, 0:outch].reshape(planes, nz, outch)
    summed = by_depth[:, outch : 2 * outch].reshape(planes, nz, outch) + shifted_out[:, 0:nz]
    shifted_out[:, 1 : nz + 1] = by_depth[:, 2 * outch : 3 * outch].reshape(planes, nz, outch)
    summed = summed + shifted_out[:, 2 : nz + 2]
    result_t = summed.reshape(cells_out, outch).T
    block = outch // count
    for peer in range(count):
        parts[peer] = result_t[peer * block : (peer + 1) * block]
    sends = []
    for step in range(1, count):
        peer = lax.rem(me + step, count)
        copy = pltpu.make_async_remote_copy(
            src_ref=parts.at[peer],
            dst_ref=inbox.at[step],
            send_sem=sum_send.at[step],
            recv_sem=sum_recv.at[step],
            device_id={"section": peer},
            device_id_type=MESH,
        )
        copy.start()
        sends.append(copy)
    result = parts[me]
    for step in range(1, count):
        sends[step - 1].wait_recv()
        result = result + inbox[step]
    for copy in sends:
        copy.wait_send()
    out_ref[...] = result.reshape(out_ref.shape).astype(out_ref.dtype)


def decoder_block(field, kernel_in, gains, kernel_out, collective):
    nx, ny_in, nz, channels = field.shape
    ny = ny_in - 2
    ny_out = ny - 2
    count = lax.axis_size("section")
    outch = kernel_out.shape[1] // 3
    block = outch // count
    return pl.pallas_call(
        block_kernel,
        out_shape=jax.ShapeDtypeStruct((block, nx, ny_out * nz), jnp.bfloat16),
        in_specs=[pl.BlockSpec(memory_space=pltpu.VMEM)] * 4,
        out_specs=pl.BlockSpec(memory_space=pltpu.VMEM),
        scratch_shapes=[
            pltpu.VMEM((nx + 2, ny_in, nz, channels), field.dtype),
            pltpu.VMEM((nx * ny, nz + 2, channels), jnp.float32),
            pltpu.VMEM((nx, ny, nz, channels), field.dtype),
            pltpu.VMEM((nx + 2, ny, nz, channels), field.dtype),
            pltpu.VMEM((nx * ny_out, nz + 2, outch), jnp.float32),
            pltpu.VMEM((count, block, nx * ny_out * nz), jnp.float32),
            pltpu.VMEM((count, block, nx * ny_out * nz), jnp.float32),
            pltpu.SemaphoreType.DMA((2,)),
            pltpu.SemaphoreType.DMA((2,)),
            pltpu.SemaphoreType.DMA((2,)),
            pltpu.SemaphoreType.DMA((2,)),
            pltpu.SemaphoreType.DMA((count,)),
            pltpu.SemaphoreType.DMA((count,)),
        ],
        compiler_params=pltpu.CompilerParams(collective_id=collective, has_side_effects=True),
    )(field, kernel_in, gains, kernel_out)


def local(skips, deconv_weight, norm_gain, conv_in, conv_out):
    inl_size = lax.axis_size("inl")
    tokens_here = skips[0]
    weight = deconv_weight[0]
    gains = norm_gain[0]
    channels = gains.shape[1]
    cell_x = 2 * PXD
    cell_y = 2 * lax.axis_size("xln")
    cell_z = 2 * GZ
    assert tokens_here.shape[0] == inl_size * PXD * GZ
    brick = gather_bricks(tokens_here, weight, gains)
    lines = brick.shape[0]
    field = (
        brick.reshape(lines, PXD, GZ, 2, 2, 2, channels)
        .transpose(1, 3, 0, 4, 2, 5, 6)
        .reshape(cell_x, 2 * lines, cell_z, channels)
    )
    taps, outch, channels_in = conv_out.shape[1:]
    out_weight = conv_out[0].reshape(taps // 3, 3 * outch, channels_in)
    return decoder_block(field, conv_in[0], gains, out_weight, 1)


def solution(mesh):
    return jax.shard_map(
        local,
        mesh=mesh,
        in_specs=(
            P("section", ("inl", "xln"), None),
            P("section", None, None),
            P("section", None, None),
            P("section", None, None, None),
            P("section", None, None, None),
        ),
        out_specs=P("section", "inl", "xln"),
        check_vma=False,
    )
```

```python
import functools

import jax
import jax.numpy as jnp
from jax import lax
from jax.experimental import pallas as pl
from jax.experimental.pallas import tpu as pltpu
from jax.sharding import PartitionSpec as P

MESH = pl.DeviceIdType.MESH
PXD = 2
GZ = 8


epsilon = 1e-05


def gelu_tanh(values):
    return 0.5 * values * (1.0 + jnp.tanh(0.7978845608028654 * (values + 0.044715 * (values * values * values))))


def send_groups(me_x, me_y, count):
    return [
        (me_x, me_y + 1, None),
        (me_x + 1, 0, (me_y == count - 1) & (me_x + 1 < count)),
        (me_x - 1, count + 1, (me_y == 0) & (me_x > 0)),
    ]


def gather_kernel(tokens_ref, weight_hbm, gains_ref, out_ref, weight, field, held, send_sem, recv_sem, weight_sem):
    count = lax.axis_size("inl")
    me_x, me_y = lax.axis_index("inl"), lax.axis_index("xln")
    rows = tokens_ref.shape[0] // count
    width = gains_ref.shape[1]
    one = jnp.int32(1)
    loading = pltpu.make_async_copy(weight_hbm, weight, weight_sem)
    loading.start()
    groups = send_groups(me_x, me_y, count)
    sources = [(me_y - 1, count - 1, me_y >= 1)]
    sources += [(me_y, other, None) for other in range(count)]
    sources += [(me_y + 1, 0, me_y + 1 < count)]

    def is_me(x, y):
        return (x == me_x) & (y == me_y)

    barrier = pltpu.get_barrier_semaphore()
    expected = jnp.int32(0)
    for column, _, exists in groups:
        live = True if exists is None else exists
        expected = expected + jnp.where(live, count, 0)
        for other in range(count):

            @pl.when(jnp.logical_and(live, jnp.logical_not(is_me(other, column))))
            def _():
                pl.semaphore_signal(barrier, inc=1, device_id={"inl": other, "xln": column}, device_id_type=MESH)

            expected = expected - jnp.where(jnp.logical_and(live, is_me(other, column)), one, 0)
    for source_x, source_y, exists in sources:
        live = True if exists is None else exists
        mine = jnp.logical_and(live, is_me(source_x, source_y))
        expected = expected + jnp.where(jnp.logical_and(live, jnp.logical_not(mine)), one, 0)

        @pl.when(jnp.logical_and(live, jnp.logical_not(mine)))
        def _():
            pl.semaphore_signal(barrier, inc=1, device_id={"inl": source_x, "xln": source_y}, device_id_type=MESH)

    loading.wait()
    upsampled = jnp.dot(tokens_ref[...], weight[...], preferred_element_type=jnp.float32)
    for group in range(upsampled.shape[1] // width):
        part = upsampled[:, group * width : (group + 1) * width]
        mean_square = jnp.mean(part * part, axis=-1, keepdims=True)
        normed = part * lax.rsqrt(mean_square + epsilon) * gains_ref[0:1, :]
        field[:, group * width : (group + 1) * width] = gelu_tanh(normed).astype(field.dtype)
    pl.semaphore_wait(barrier, expected)
    copies = []
    for index, (column, slot, exists) in enumerate(groups):
        live = True if exists is None else exists
        for turn in range(count):
            other = lax.rem(me_y + turn, count)
            copy = pltpu.make_async_remote_copy(
                src_ref=field.at[pl.ds(pl.multiple_of(other * rows, rows), rows)],
                dst_ref=held.at[slot],
                send_sem=send_sem.at[index * count + turn],
                recv_sem=recv_sem.at[slot],
                device_id={"inl": other, "xln": column},
                device_id_type=MESH,
            )
            remote = jnp.logical_and(live, jnp.logical_not(is_me(other, column)))

            @pl.when(remote)
            def _():
                copy.start()

            copies.append((copy, remote))
    for slot, (source_x, source_y, exists) in enumerate(sources):
        live = True if exists is None else exists
        mine = jnp.logical_and(live, is_me(source_x, source_y))
        remote = jnp.logical_and(live, jnp.logical_not(mine))
        incoming = pltpu.make_async_remote_copy(
            src_ref=field.at[pl.ds(0, rows)],
            dst_ref=held.at[slot],
            send_sem=send_sem.at[0],
            recv_sem=recv_sem.at[slot],
            device_id={"inl": source_x, "xln": source_y},
            device_id_type=MESH,
        )

        @pl.when(remote)
        def _():
            incoming.wait_recv()
            out_ref[slot] = held[slot]

        @pl.when(mine)
        def _():
            out_ref[slot] = field[pl.ds(pl.multiple_of(me_x * rows, rows), rows)]

        @pl.when(jnp.logical_not(live))
        def _():
            out_ref[slot] = jnp.zeros(out_ref.shape[1:], out_ref.dtype)

    for copy, remote in copies:

        @pl.when(remote)
        def _():
            copy.wait_send()


def gather_bricks(tokens, weight, gains):
    count = lax.axis_size("inl")
    rows = tokens.shape[0] // count
    shape = (lax.axis_size("xln") + 2, rows, weight.shape[1])
    return pl.pallas_call(
        gather_kernel,
        out_shape=jax.ShapeDtypeStruct(shape, jnp.bfloat16),
        in_specs=[
            pl.BlockSpec(memory_space=pltpu.VMEM),
            pl.BlockSpec(memory_space=pl.ANY),
            pl.BlockSpec(memory_space=pltpu.VMEM),
        ],
        out_specs=pl.BlockSpec(memory_space=pltpu.VMEM),
        scratch_shapes=[
            pltpu.VMEM(weight.shape, weight.dtype),
            pltpu.VMEM((tokens.shape[0], weight.shape[1]), jnp.bfloat16),
            pltpu.VMEM(shape, jnp.bfloat16),
            pltpu.SemaphoreType.DMA((3 * count,)),
            pltpu.SemaphoreType.DMA((shape[0],)),
            pltpu.SemaphoreType.DMA(()),
        ],
        compiler_params=pltpu.CompilerParams(collective_id=3, has_side_effects=True),
    )(tokens, weight, gains)


def halo_signal():
    count = lax.axis_size("inl")
    me = lax.axis_index("inl")
    for step in (-1, 1):

        @pl.when((me + step >= 0) & (me + step < count))
        def _():
            pl.semaphore_signal(
                pltpu.get_barrier_semaphore(), inc=1, device_id={"inl": me + step}, device_id_type=MESH
            )

    return (me > 0).astype(jnp.int32) + (me < count - 1).astype(jnp.int32)


def halo_start(field_ref, held, send_sem, recv_sem):
    nx = field_ref.shape[0]
    count = lax.axis_size("inl")
    me = lax.axis_index("inl")
    copies = []
    for index, step in enumerate((-1, 1)):
        source, target = (0, nx + 1) if step < 0 else (nx - 1, 0)
        copy = pltpu.make_async_remote_copy(
            src_ref=field_ref.at[source : source + 1],
            dst_ref=held.at[target : target + 1],
            send_sem=send_sem.at[index],
            recv_sem=recv_sem.at[index],
            device_id={"inl": me + step},
            device_id_type=MESH,
        )
        sends = (me + step >= 0) & (me + step < count)
        gets = (me - step >= 0) & (me - step < count)

        @pl.when(sends)
        def _():
            copy.start()

        @pl.when(jnp.logical_not(gets))
        def _():
            held[target : target + 1] = jnp.zeros((1,) + held.shape[1:], held.dtype)

        copies.append((copy, sends, gets))
    return copies


def halo_finish(copies):
    for copy, sends, gets in copies:

        @pl.when(gets)
        def _():
            copy.wait_recv()

        @pl.when(sends)
        def _():
            copy.wait_send()


def block_kernel(
    field_ref, kernel_in_ref, gains_ref, kernel_out_ref, out_ref,
    held, shifted, mixed, held_out, shifted_out, parts, inbox,
    send_sem, recv_sem, send_out, recv_out, sum_send, sum_recv,
):
    count = lax.axis_size("section")
    me = lax.axis_index("section")
    barrier = pltpu.get_barrier_semaphore()
    for step in range(1, count):
        pl.semaphore_signal(
            barrier, inc=1, device_id={"section": lax.rem(me + step, count)}, device_id_type=MESH
        )
    present = halo_signal()
    nx, ny_in, nz, channels = field_ref.shape
    ny = ny_in - 2
    ny_out = ny - 2
    outch = kernel_out_ref.shape[1] // 3
    me_y, count_y = lax.axis_index("xln"), lax.axis_size("xln")
    edge = jnp.zeros((nx * ny, 1, channels), jnp.float32)
    shifted[:, 0:1] = edge
    shifted[:, nz + 1 : nz + 2] = edge
    held[1 : nx + 1] = field_ref[...]

    def inner_rows(first, last):
        rows = last - first
        cells = rows * ny * nz
        planes = rows * ny
        parts_in = []
        for offset_z in range(3):
            part = jnp.zeros((cells, channels), jnp.float32)
            for offset_x in range(3):
                for offset_y in range(3):
                    window = held[first + offset_x : last + offset_x, offset_y : offset_y + ny].reshape(cells, channels)
                    tap = kernel_in_ref[(offset_x * 3 + offset_y) * 3 + offset_z]
                    part = part + jnp.dot(window, tap, preferred_element_type=jnp.float32)
            parts_in.append(part.reshape(planes, nz, channels))
        shifted[0:planes, 1 : nz + 1] = parts_in[0]
        total = parts_in[1] + shifted[0:planes, 0:nz]
        shifted[0:planes, 1 : nz + 1] = parts_in[2]
        total = total + shifted[0:planes, 2 : nz + 2]
        mean_square = jnp.mean(total * total, axis=-1, keepdims=True)
        normed = total * lax.rsqrt(mean_square + epsilon) * gains_ref[1:2, :]
        base = field_ref[first:last, 1 : ny + 1].reshape(planes, nz, channels).astype(jnp.float32)
        activated = gelu_tanh(normed + base).reshape(rows, ny, nz, channels)
        row = lax.broadcasted_iota(jnp.int32, activated.shape, 1)
        outside = ((row == 0) & (me_y == 0)) | ((row == ny - 1) & (me_y == count_y - 1))
        mixed[first:last] = jnp.where(outside, 0.0, activated).astype(mixed.dtype)

    def outer_rows(first, last):
        cells = (last - first) * ny_out * nz
        by_depth = jnp.zeros((cells, 3 * outch), jnp.float32)
        for offset_x in range(3):
            for offset_y in range(3):
                window = held_out[first + offset_x : last + offset_x, offset_y : offset_y + ny_out].reshape(
                    cells, channels
                )
                by_depth = by_depth + lax.dot_general(
                    window,
                    kernel_out_ref[offset_x * 3 + offset_y],
                    (((1,), (1,)), ((), ())),
                    preferred_element_type=jnp.float32,
                )
        return by_depth

    inner_rows(1, nx - 1)
    pl.semaphore_wait(barrier, present + count - 1)
    halo_finish(halo_start(field_ref, held, send_sem, recv_sem))
    inner_rows(0, 1)
    inner_rows(nx - 1, nx)

    copies = halo_start(mixed, held_out, send_out, recv_out)
    held_out[1 : nx + 1] = mixed[...]
    middle = outer_rows(1, nx - 1)
    halo_finish(copies)
    by_depth = jnp.concatenate([outer_rows(0, 1), middle, outer_rows(nx - 1, nx)], axis=0)
    cells_out = nx * ny_out * nz
    planes = nx * ny_out
    edge = jnp.zeros((planes, 1, outch), jnp.float32)
    shifted_out[:, 0:1] = edge
    shifted_out[:, nz + 1 : nz + 2] = edge
    shifted_out[:, 1 : nz + 1] = by_depth[:, 0:outch].reshape(planes, nz, outch)
    summed = by_depth[:, outch : 2 * outch].reshape(planes, nz, outch) + shifted_out[:, 0:nz]
    shifted_out[:, 1 : nz + 1] = by_depth[:, 2 * outch : 3 * outch].reshape(planes, nz, outch)
    summed = summed + shifted_out[:, 2 : nz + 2]
    result_t = summed.reshape(cells_out, outch).T
    block = outch // count
    for peer in range(count):
        parts[peer] = result_t[peer * block : (peer + 1) * block]
    sends = []
    for step in range(1, count):
        peer = lax.rem(me + step, count)
        copy = pltpu.make_async_remote_copy(
            src_ref=parts.at[peer],
            dst_ref=inbox.at[step],
            send_sem=sum_send.at[step],
            recv_sem=sum_recv.at[step],
            device_id={"section": peer},
            device_id_type=MESH,
        )
        copy.start()
        sends.append(copy)
    result = parts[me]
    for step in range(1, count):
        sends[step - 1].wait_recv()
        result = result + inbox[step]
    for copy in sends:
        copy.wait_send()
    out_ref[...] = result.reshape(out_ref.shape).astype(out_ref.dtype)


def decoder_block(field, kernel_in, gains, kernel_out, collective):
    nx, ny_in, nz, channels = field.shape
    ny = ny_in - 2
    ny_out = ny - 2
    count = lax.axis_size("section")
    outch = kernel_out.shape[1] // 3
    block = outch // count
    return pl.pallas_call(
        block_kernel,
        out_shape=jax.ShapeDtypeStruct((block, nx, ny_out * nz), jnp.bfloat16),
        in_specs=[pl.BlockSpec(memory_space=pltpu.VMEM)] * 4,
        out_specs=pl.BlockSpec(memory_space=pltpu.VMEM),
        scratch_shapes=[
            pltpu.VMEM((nx + 2, ny_in, nz, channels), field.dtype),
            pltpu.VMEM((nx * ny, nz + 2, channels), jnp.float32),
            pltpu.VMEM((nx, ny, nz, channels), field.dtype),
            pltpu.VMEM((nx + 2, ny, nz, channels), field.dtype),
            pltpu.VMEM((nx * ny_out, nz + 2, outch), jnp.float32),
            pltpu.VMEM((count, block, nx * ny_out * nz), jnp.float32),
            pltpu.VMEM((count, block, nx * ny_out * nz), jnp.float32),
            pltpu.SemaphoreType.DMA((2,)),
            pltpu.SemaphoreType.DMA((2,)),
            pltpu.SemaphoreType.DMA((2,)),
            pltpu.SemaphoreType.DMA((2,)),
            pltpu.SemaphoreType.DMA((count,)),
            pltpu.SemaphoreType.DMA((count,)),
        ],
        compiler_params=pltpu.CompilerParams(collective_id=collective, has_side_effects=True),
    )(field, kernel_in, gains, kernel_out)


def local(skips, deconv_weight, norm_gain, conv_in, conv_out):
    inl_size = lax.axis_size("inl")
    tokens_here = skips[0]
    weight = deconv_weight[0]
    gains = norm_gain[0]
    channels = gains.shape[1]
    cell_x = 2 * PXD
    cell_y = 2 * lax.axis_size("xln")
    cell_z = 2 * GZ
    assert tokens_here.shape[0] == inl_size * PXD * GZ
    brick = gather_bricks(tokens_here, weight, gains)
    lines = brick.shape[0]
    field = (
        brick.reshape(lines, PXD, GZ, 2, 2, 2, channels)
        .transpose(1, 3, 0, 4, 2, 5, 6)
        .reshape(cell_x, 2 * lines, cell_z, channels)
    )
    taps, outch, channels_in = conv_out.shape[1:]
    out_weight = conv_out[0].reshape(taps // 3, 3 * outch, channels_in)
    return decoder_block(field, conv_in[0], gains, out_weight, 1)


def solution(mesh):
    return jax.shard_map(
        local,
        mesh=mesh,
        in_specs=(
            P("section", ("inl", "xln"), None),
            P("section", None, None),
            P("section", None, None),
            P("section", None, None, None),
            P("section", None, None, None),
        ),
        out_specs=P("section", "inl", "xln"),
        check_vma=False,
    )
```

```python
import functools

import jax
import jax.numpy as jnp
from jax import lax
from jax.experimental import pallas as pl
from jax.experimental.pallas import tpu as pltpu
from jax.sharding import PartitionSpec as P

MESH = pl.DeviceIdType.MESH
PXD = 2
GZ = 8


epsilon = 1e-05


def gelu_tanh(values):
    return 0.5 * values * (1.0 + jnp.tanh(0.7978845608028654 * (values + 0.044715 * (values * values * values))))


def send_groups(me_x, me_y, count):
    return [
        (me_x, me_y + 1, None),
        (me_x + 1, 0, (me_y == count - 1) & (me_x + 1 < count)),
        (me_x - 1, count + 1, (me_y == 0) & (me_x > 0)),
    ]


def gather_kernel(tokens_ref, weight_hbm, gains_ref, out_ref, weight, field, held, send_sem, recv_sem, weight_sem):
    count = lax.axis_size("inl")
    me_x, me_y = lax.axis_index("inl"), lax.axis_index("xln")
    rows = tokens_ref.shape[0] // count
    width = gains_ref.shape[1]
    one = jnp.int32(1)
    loading = pltpu.make_async_copy(weight_hbm, weight, weight_sem)
    loading.start()
    groups = send_groups(me_x, me_y, count)
    sources = [(me_y - 1, count - 1, me_y >= 1)]
    sources += [(me_y, other, None) for other in range(count)]
    sources += [(me_y + 1, 0, me_y + 1 < count)]

    def is_me(x, y):
        return (x == me_x) & (y == me_y)

    barrier = pltpu.get_barrier_semaphore()
    expected = jnp.int32(0)
    for column, _, exists in groups:
        live = True if exists is None else exists
        expected = expected + jnp.where(live, count, 0)
        for other in range(count):

            @pl.when(jnp.logical_and(live, jnp.logical_not(is_me(other, column))))
            def _():
                pl.semaphore_signal(barrier, inc=1, device_id={"inl": other, "xln": column}, device_id_type=MESH)

            expected = expected - jnp.where(jnp.logical_and(live, is_me(other, column)), one, 0)
    for source_x, source_y, exists in sources:
        live = True if exists is None else exists
        mine = jnp.logical_and(live, is_me(source_x, source_y))
        expected = expected + jnp.where(jnp.logical_and(live, jnp.logical_not(mine)), one, 0)

        @pl.when(jnp.logical_and(live, jnp.logical_not(mine)))
        def _():
            pl.semaphore_signal(barrier, inc=1, device_id={"inl": source_x, "xln": source_y}, device_id_type=MESH)

    loading.wait()
    upsampled = jnp.dot(tokens_ref[...], weight[...], preferred_element_type=jnp.float32)
    for group in range(upsampled.shape[1] // width):
        part = upsampled[:, group * width : (group + 1) * width]
        mean_square = jnp.mean(part * part, axis=-1, keepdims=True)
        normed = part * lax.rsqrt(mean_square + epsilon) * gains_ref[0:1, :]
        field[:, group * width : (group + 1) * width] = gelu_tanh(normed).astype(field.dtype)
    pl.semaphore_wait(barrier, expected)
    copies = []
    for index, (column, slot, exists) in enumerate(groups):
        live = True if exists is None else exists
        for turn in range(count):
            other = lax.rem(me_y + turn, count)
            copy = pltpu.make_async_remote_copy(
                src_ref=field.at[pl.ds(pl.multiple_of(other * rows, rows), rows)],
                dst_ref=held.at[slot],
                send_sem=send_sem.at[index * count + turn],
                recv_sem=recv_sem.at[slot],
                device_id={"inl": other, "xln": column},
                device_id_type=MESH,
            )
            remote = jnp.logical_and(live, jnp.logical_not(is_me(other, column)))

            @pl.when(remote)
            def _():
                copy.start()

            copies.append((copy, remote))
    for slot, (source_x, source_y, exists) in enumerate(sources):
        live = True if exists is None else exists
        mine = jnp.logical_and(live, is_me(source_x, source_y))
        remote = jnp.logical_and(live, jnp.logical_not(mine))
        incoming = pltpu.make_async_remote_copy(
            src_ref=field.at[pl.ds(0, rows)],
            dst_ref=held.at[slot],
            send_sem=send_sem.at[0],
            recv_sem=recv_sem.at[slot],
            device_id={"inl": source_x, "xln": source_y},
            device_id_type=MESH,
        )

        @pl.when(remote)
        def _():
            incoming.wait_recv()
            out_ref[slot] = held[slot]

        @pl.when(mine)
        def _():
            out_ref[slot] = field[pl.ds(pl.multiple_of(me_x * rows, rows), rows)]

        @pl.when(jnp.logical_not(live))
        def _():
            out_ref[slot] = jnp.zeros(out_ref.shape[1:], out_ref.dtype)

    for copy, remote in copies:

        @pl.when(remote)
        def _():
            copy.wait_send()


def gather_bricks(tokens, weight, gains):
    count = lax.axis_size("inl")
    rows = tokens.shape[0] // count
    shape = (lax.axis_size("xln") + 2, rows, weight.shape[1])
    return pl.pallas_call(
        gather_kernel,
        out_shape=jax.ShapeDtypeStruct(shape, jnp.bfloat16),
        in_specs=[
            pl.BlockSpec(memory_space=pltpu.VMEM),
            pl.BlockSpec(memory_space=pl.ANY),
            pl.BlockSpec(memory_space=pltpu.VMEM),
        ],
        out_specs=pl.BlockSpec(memory_space=pltpu.VMEM),
        scratch_shapes=[
            pltpu.VMEM(weight.shape, weight.dtype),
            pltpu.VMEM((tokens.shape[0], weight.shape[1]), jnp.bfloat16),
            pltpu.VMEM(shape, jnp.bfloat16),
            pltpu.SemaphoreType.DMA((3 * count,)),
            pltpu.SemaphoreType.DMA((shape[0],)),
            pltpu.SemaphoreType.DMA(()),
        ],
        compiler_params=pltpu.CompilerParams(collective_id=3, has_side_effects=True),
    )(tokens, weight, gains)


def halo_signal():
    count = lax.axis_size("inl")
    me = lax.axis_index("inl")
    for step in (-1, 1):

        @pl.when((me + step >= 0) & (me + step < count))
        def _():
            pl.semaphore_signal(
                pltpu.get_barrier_semaphore(), inc=1, device_id={"inl": me + step}, device_id_type=MESH
            )

    return (me > 0).astype(jnp.int32) + (me < count - 1).astype(jnp.int32)


def halo_start(field_ref, held, send_sem, recv_sem):
    nx = field_ref.shape[0]
    count = lax.axis_size("inl")
    me = lax.axis_index("inl")
    copies = []
    for index, step in enumerate((-1, 1)):
        source, target = (0, nx + 1) if step < 0 else (nx - 1, 0)
        copy = pltpu.make_async_remote_copy(
            src_ref=field_ref.at[source : source + 1],
            dst_ref=held.at[target : target + 1],
            send_sem=send_sem.at[index],
            recv_sem=recv_sem.at[index],
            device_id={"inl": me + step},
            device_id_type=MESH,
        )
        sends = (me + step >= 0) & (me + step < count)
        gets = (me - step >= 0) & (me - step < count)

        @pl.when(sends)
        def _():
            copy.start()

        @pl.when(jnp.logical_not(gets))
        def _():
            held[target : target + 1] = jnp.zeros((1,) + held.shape[1:], held.dtype)

        copies.append((copy, sends, gets))
    return copies


def halo_finish(copies):
    for copy, sends, gets in copies:

        @pl.when(gets)
        def _():
            copy.wait_recv()

        @pl.when(sends)
        def _():
            copy.wait_send()


def block_kernel(
    field_ref, kernel_in_ref, gains_ref, kernel_out_ref, out_ref,
    held, shifted, mixed, held_out, shifted_out, parts, inbox,
    send_sem, recv_sem, send_out, recv_out, sum_send, sum_recv,
):
    count = lax.axis_size("section")
    me = lax.axis_index("section")
    barrier = pltpu.get_barrier_semaphore()
    for step in range(1, count):
        pl.semaphore_signal(
            barrier, inc=1, device_id={"section": lax.rem(me + step, count)}, device_id_type=MESH
        )
    present = halo_signal()
    nx, ny_in, nz, channels = field_ref.shape
    ny = ny_in - 2
    ny_out = ny - 2
    outch = kernel_out_ref.shape[1] // 3
    me_y, count_y = lax.axis_index("xln"), lax.axis_size("xln")
    edge = jnp.zeros((nx * ny, 1, channels), jnp.float32)
    shifted[:, 0:1] = edge
    shifted[:, nz + 1 : nz + 2] = edge
    held[1 : nx + 1] = field_ref[...]

    def inner_rows(first, last):
        rows = last - first
        cells = rows * ny * nz
        planes = rows * ny
        parts_in = []
        for offset_z in range(3):
            part = jnp.zeros((cells, channels), jnp.float32)
            for offset_x in range(3):
                for offset_y in range(3):
                    window = held[first + offset_x : last + offset_x, offset_y : offset_y + ny].reshape(cells, channels)
                    tap = kernel_in_ref[(offset_x * 3 + offset_y) * 3 + offset_z]
                    part = part + jnp.dot(window, tap, preferred_element_type=jnp.float32)
            parts_in.append(part.reshape(planes, nz, channels))
        shifted[0:planes, 1 : nz + 1] = parts_in[0]
        total = parts_in[1] + shifted[0:planes, 0:nz]
        shifted[0:planes, 1 : nz + 1] = parts_in[2]
        total = total + shifted[0:planes, 2 : nz + 2]
        mean_square = jnp.mean(total * total, axis=-1, keepdims=True)
        normed = total * lax.rsqrt(mean_square + epsilon) * gains_ref[1:2, :]
        base = field_ref[first:last, 1 : ny + 1].reshape(planes, nz, channels).astype(jnp.float32)
        activated = gelu_tanh(normed + base).reshape(rows, ny, nz, channels)
        row = lax.broadcasted_iota(jnp.int32, activated.shape, 1)
        outside = ((row == 0) & (me_y == 0)) | ((row == ny - 1) & (me_y == count_y - 1))
        mixed[first:last] = jnp.where(outside, 0.0, activated).astype(mixed.dtype)

    def outer_rows(first, last):
        cells = (last - first) * ny_out * nz
        by_depth = jnp.zeros((cells, 3 * outch), jnp.float32)
        for offset_x in range(3):
            for offset_y in range(3):
                window = held_out[first + offset_x : last + offset_x, offset_y : offset_y + ny_out].reshape(
                    cells, channels
                )
                by_depth = by_depth + lax.dot_general(
                    window,
                    kernel_out_ref[offset_x * 3 + offset_y],
                    (((1,), (1,)), ((), ())),
                    preferred_element_type=jnp.float32,
                )
        return by_depth

    inner_rows(1, nx - 1)
    pl.semaphore_wait(barrier, present + count - 1)
    halo_finish(halo_start(field_ref, held, send_sem, recv_sem))
    inner_rows(0, 1)
    inner_rows(nx - 1, nx)

    edge = jnp.zeros((nx * ny_out, 1, outch), jnp.float32)
    shifted_out[:, 0:1] = edge
    shifted_out[:, nz + 1 : nz + 2] = edge

    def by_channel(by_depth, rows):
        planes = rows * ny_out
        shifted_out[0:planes, 1 : nz + 1] = by_depth[:, 0:outch].reshape(planes, nz, outch)
        summed = by_depth[:, outch : 2 * outch].reshape(planes, nz, outch) + shifted_out[0:planes, 0:nz]
        shifted_out[0:planes, 1 : nz + 1] = by_depth[:, 2 * outch : 3 * outch].reshape(planes, nz, outch)
        summed = summed + shifted_out[0:planes, 2 : nz + 2]
        return summed.reshape(planes * nz, outch).T

    block = outch // count

    def share(phase, values):
        for peer in range(count):
            parts[phase, peer] = values[peer * block : (peer + 1) * block]
        sends = []
        for step in range(1, count):
            peer = lax.rem(me + step, count)
            copy = pltpu.make_async_remote_copy(
                src_ref=parts.at[phase, peer],
                dst_ref=inbox.at[phase, step],
                send_sem=sum_send.at[phase, step],
                recv_sem=sum_recv.at[phase, step],
                device_id={"section": peer},
                device_id_type=MESH,
            )
            copy.start()
            sends.append(copy)
        return sends

    def gather(phase, sends):
        result = parts[phase, me]
        for step in range(1, count):
            sends[step - 1].wait_recv()
            result = result + inbox[phase, step]
        for copy in sends:
            copy.wait_send()
        return result

    copies = halo_start(mixed, held_out, send_out, recv_out)
    held_out[1 : nx + 1] = mixed[...]
    middle_sends = share(0, by_channel(outer_rows(1, nx - 1), nx - 2))
    halo_finish(copies)
    row_cells = ny_out * nz
    ends = jnp.concatenate(
        [by_channel(outer_rows(0, 1), 1), by_channel(outer_rows(nx - 1, nx), 1)], axis=1
    )
    end_sends = share(1, ends)
    middle = gather(0, middle_sends)
    ends = gather(1, end_sends)
    result = jnp.concatenate([ends[:, 0:row_cells], middle, ends[:, row_cells:]], axis=1)
    out_ref[...] = result.reshape(out_ref.shape).astype(out_ref.dtype)


def decoder_block(field, kernel_in, gains, kernel_out, collective):
    nx, ny_in, nz, channels = field.shape
    ny = ny_in - 2
    ny_out = ny - 2
    count = lax.axis_size("section")
    outch = kernel_out.shape[1] // 3
    block = outch // count
    return pl.pallas_call(
        block_kernel,
        out_shape=jax.ShapeDtypeStruct((block, nx, ny_out * nz), jnp.bfloat16),
        in_specs=[pl.BlockSpec(memory_space=pltpu.VMEM)] * 4,
        out_specs=pl.BlockSpec(memory_space=pltpu.VMEM),
        scratch_shapes=[
            pltpu.VMEM((nx + 2, ny_in, nz, channels), field.dtype),
            pltpu.VMEM((nx * ny, nz + 2, channels), jnp.float32),
            pltpu.VMEM((nx, ny, nz, channels), field.dtype),
            pltpu.VMEM((nx + 2, ny, nz, channels), field.dtype),
            pltpu.VMEM((nx * ny_out, nz + 2, outch), jnp.float32),
            pltpu.VMEM((2, count, block, (nx - 2) * ny_out * nz), jnp.float32),
            pltpu.VMEM((2, count, block, (nx - 2) * ny_out * nz), jnp.float32),
            pltpu.SemaphoreType.DMA((2,)),
            pltpu.SemaphoreType.DMA((2,)),
            pltpu.SemaphoreType.DMA((2,)),
            pltpu.SemaphoreType.DMA((2,)),
            pltpu.SemaphoreType.DMA((2, count)),
            pltpu.SemaphoreType.DMA((2, count)),
        ],
        compiler_params=pltpu.CompilerParams(collective_id=collective, has_side_effects=True),
    )(field, kernel_in, gains, kernel_out)


def local(skips, deconv_weight, norm_gain, conv_in, conv_out):
    inl_size = lax.axis_size("inl")
    tokens_here = skips[0]
    weight = deconv_weight[0]
    gains = norm_gain[0]
    channels = gains.shape[1]
    cell_x = 2 * PXD
    cell_y = 2 * lax.axis_size("xln")
    cell_z = 2 * GZ
    assert tokens_here.shape[0] == inl_size * PXD * GZ
    brick = gather_bricks(tokens_here, weight, gains)
    lines = brick.shape[0]
    field = (
        brick.reshape(lines, PXD, GZ, 2, 2, 2, channels)
        .transpose(1, 3, 0, 4, 2, 5, 6)
        .reshape(cell_x, 2 * lines, cell_z, channels)
    )
    taps, outch, channels_in = conv_out.shape[1:]
    out_weight = conv_out[0].reshape(taps // 3, 3 * outch, channels_in)
    return decoder_block(field, conv_in[0], gains, out_weight, 1)


def solution(mesh):
    return jax.shard_map(
        local,
        mesh=mesh,
        in_specs=(
            P("section", ("inl", "xln"), None),
            P("section", None, None),
            P("section", None, None),
            P("section", None, None, None),
            P("section", None, None, None),
        ),
        out_specs=P("section", "inl", "xln"),
        check_vma=False,
    )
```

```python
import functools

import jax
import jax.numpy as jnp
from jax import lax
from jax.experimental import pallas as pl
from jax.experimental.pallas import tpu as pltpu
from jax.sharding import PartitionSpec as P

MESH = pl.DeviceIdType.MESH
PXD = 2
GZ = 8


epsilon = 1e-05


def gelu_tanh(values):
    return 0.5 * values * (1.0 + jnp.tanh(0.7978845608028654 * (values + 0.044715 * (values * values * values))))


def send_groups(me_x, me_y, count):
    return [
        (me_x, me_y + 1, None),
        (me_x + 1, 0, (me_y == count - 1) & (me_x + 1 < count)),
        (me_x - 1, count + 1, (me_y == 0) & (me_x > 0)),
    ]


def gather_kernel(tokens_ref, weight_hbm, gains_ref, out_ref, weight, field, held, send_sem, recv_sem, weight_sem):
    count = lax.axis_size("inl")
    me_x, me_y = lax.axis_index("inl"), lax.axis_index("xln")
    rows = tokens_ref.shape[0] // count
    width = gains_ref.shape[1]
    one = jnp.int32(1)
    loading = pltpu.make_async_copy(weight_hbm, weight, weight_sem)
    loading.start()
    groups = send_groups(me_x, me_y, count)
    sources = [(me_y - 1, count - 1, me_y >= 1)]
    sources += [(me_y, other, None) for other in range(count)]
    sources += [(me_y + 1, 0, me_y + 1 < count)]

    def is_me(x, y):
        return (x == me_x) & (y == me_y)

    barrier = pltpu.get_barrier_semaphore()
    expected = jnp.int32(0)
    for column, _, exists in groups:
        live = True if exists is None else exists
        expected = expected + jnp.where(live, count, 0)
        for other in range(count):

            @pl.when(jnp.logical_and(live, jnp.logical_not(is_me(other, column))))
            def _():
                pl.semaphore_signal(barrier, inc=1, device_id={"inl": other, "xln": column}, device_id_type=MESH)

            expected = expected - jnp.where(jnp.logical_and(live, is_me(other, column)), one, 0)
    for source_x, source_y, exists in sources:
        live = True if exists is None else exists
        mine = jnp.logical_and(live, is_me(source_x, source_y))
        expected = expected + jnp.where(jnp.logical_and(live, jnp.logical_not(mine)), one, 0)

        @pl.when(jnp.logical_and(live, jnp.logical_not(mine)))
        def _():
            pl.semaphore_signal(barrier, inc=1, device_id={"inl": source_x, "xln": source_y}, device_id_type=MESH)

    loading.wait()
    upsampled = jnp.dot(tokens_ref[...], weight[...], preferred_element_type=jnp.float32)
    for group in range(upsampled.shape[1] // width):
        part = upsampled[:, group * width : (group + 1) * width]
        mean_square = jnp.mean(part * part, axis=-1, keepdims=True)
        normed = part * lax.rsqrt(mean_square + epsilon) * gains_ref[0:1, :]
        field[:, group * width : (group + 1) * width] = gelu_tanh(normed).astype(field.dtype)
    depth = 2 * (rows // 2)
    target = lax.broadcasted_iota(jnp.int32, (2 * rows, 2 * rows), 0)
    origin = lax.broadcasted_iota(jnp.int32, (2 * rows, 2 * rows), 1)
    half = rows // 2
    same = (
        (target // depth == (origin % rows) // half)
        & ((target % depth) // 2 == origin % half)
        & (target % 2 == origin // rows)
    )
    interleave = jnp.where(same, 1.0, 0.0).astype(jnp.bfloat16)

    def place(slot, block):
        for u in range(2):
            for v in range(2):
                first = ((u * 2 + v) * 2) * width
                pair = jnp.concatenate([block[:, first : first + width], block[:, first + width : first + 2 * width]], axis=0)
                cells = jnp.dot(interleave, pair, preferred_element_type=jnp.float32).astype(out_ref.dtype)
                for ix in range(2):
                    out_ref[2 * ix + u, 2 * slot + v] = cells[ix * depth : (ix + 1) * depth]

    pl.semaphore_wait(barrier, expected)
    copies = []
    for index, (column, slot, exists) in enumerate(groups):
        live = True if exists is None else exists
        for turn in range(count):
            other = lax.rem(me_y + turn, count)
            copy = pltpu.make_async_remote_copy(
                src_ref=field.at[pl.ds(pl.multiple_of(other * rows, rows), rows)],
                dst_ref=held.at[slot],
                send_sem=send_sem.at[index * count + turn],
                recv_sem=recv_sem.at[slot],
                device_id={"inl": other, "xln": column},
                device_id_type=MESH,
            )
            remote = jnp.logical_and(live, jnp.logical_not(is_me(other, column)))

            @pl.when(remote)
            def _():
                copy.start()

            copies.append((copy, remote))
    for slot, (source_x, source_y, exists) in enumerate(sources):
        live = True if exists is None else exists
        mine = jnp.logical_and(live, is_me(source_x, source_y))
        remote = jnp.logical_and(live, jnp.logical_not(mine))
        incoming = pltpu.make_async_remote_copy(
            src_ref=field.at[pl.ds(0, rows)],
            dst_ref=held.at[slot],
            send_sem=send_sem.at[0],
            recv_sem=recv_sem.at[slot],
            device_id={"inl": source_x, "xln": source_y},
            device_id_type=MESH,
        )

        @pl.when(remote)
        def _():
            incoming.wait_recv()
            place(slot, held[slot])

        @pl.when(mine)
        def _():
            place(slot, field[pl.ds(pl.multiple_of(me_x * rows, rows), rows)])

        @pl.when(jnp.logical_not(live))
        def _():
            out_ref[:, 2 * slot : 2 * slot + 2] = jnp.zeros(
                (out_ref.shape[0], 2) + out_ref.shape[2:], out_ref.dtype
            )

    for copy, remote in copies:

        @pl.when(remote)
        def _():
            copy.wait_send()


def gather_bricks(tokens, weight, gains):
    count = lax.axis_size("inl")
    rows = tokens.shape[0] // count
    shape = (lax.axis_size("xln") + 2, rows, weight.shape[1])
    brick = (2 * PXD, 2 * shape[0], 2 * GZ, gains.shape[1])
    return pl.pallas_call(
        gather_kernel,
        out_shape=jax.ShapeDtypeStruct(brick, jnp.bfloat16),
        in_specs=[
            pl.BlockSpec(memory_space=pltpu.VMEM),
            pl.BlockSpec(memory_space=pl.ANY),
            pl.BlockSpec(memory_space=pltpu.VMEM),
        ],
        out_specs=pl.BlockSpec(memory_space=pltpu.VMEM),
        scratch_shapes=[
            pltpu.VMEM(weight.shape, weight.dtype),
            pltpu.VMEM((tokens.shape[0], weight.shape[1]), jnp.bfloat16),
            pltpu.VMEM(shape, jnp.bfloat16),
            pltpu.SemaphoreType.DMA((3 * count,)),
            pltpu.SemaphoreType.DMA((shape[0],)),
            pltpu.SemaphoreType.DMA(()),
        ],
        compiler_params=pltpu.CompilerParams(collective_id=3, has_side_effects=True),
    )(tokens, weight, gains)


def halo_signal():
    count = lax.axis_size("inl")
    me = lax.axis_index("inl")
    for step in (-1, 1):

        @pl.when((me + step >= 0) & (me + step < count))
        def _():
            pl.semaphore_signal(
                pltpu.get_barrier_semaphore(), inc=1, device_id={"inl": me + step}, device_id_type=MESH
            )

    return (me > 0).astype(jnp.int32) + (me < count - 1).astype(jnp.int32)


def halo_start(field_ref, held, send_sem, recv_sem):
    nx = field_ref.shape[0]
    count = lax.axis_size("inl")
    me = lax.axis_index("inl")
    copies = []
    for index, step in enumerate((-1, 1)):
        source, target = (0, nx + 1) if step < 0 else (nx - 1, 0)
        copy = pltpu.make_async_remote_copy(
            src_ref=field_ref.at[source : source + 1],
            dst_ref=held.at[target : target + 1],
            send_sem=send_sem.at[index],
            recv_sem=recv_sem.at[index],
            device_id={"inl": me + step},
            device_id_type=MESH,
        )
        sends = (me + step >= 0) & (me + step < count)
        gets = (me - step >= 0) & (me - step < count)

        @pl.when(sends)
        def _():
            copy.start()

        @pl.when(jnp.logical_not(gets))
        def _():
            held[target : target + 1] = jnp.zeros((1,) + held.shape[1:], held.dtype)

        copies.append((copy, sends, gets))
    return copies


def halo_finish(copies):
    for copy, sends, gets in copies:

        @pl.when(gets)
        def _():
            copy.wait_recv()

        @pl.when(sends)
        def _():
            copy.wait_send()


def block_kernel(
    field_ref, kernel_in_ref, gains_ref, kernel_out_ref, out_ref,
    held, shifted, mixed, held_out, shifted_out, parts, inbox,
    send_sem, recv_sem, send_out, recv_out, sum_send, sum_recv,
):
    count = lax.axis_size("section")
    me = lax.axis_index("section")
    barrier = pltpu.get_barrier_semaphore()
    for step in range(1, count):
        pl.semaphore_signal(
            barrier, inc=1, device_id={"section": lax.rem(me + step, count)}, device_id_type=MESH
        )
    present = halo_signal()
    nx, ny_in, nz, channels = field_ref.shape
    ny = ny_in - 2
    ny_out = ny - 2
    outch = kernel_out_ref.shape[1] // 3
    me_y, count_y = lax.axis_index("xln"), lax.axis_size("xln")
    edge = jnp.zeros((nx * ny, 1, channels), jnp.float32)
    shifted[:, 0:1] = edge
    shifted[:, nz + 1 : nz + 2] = edge
    held[1 : nx + 1] = field_ref[...]

    def inner_rows(first, last):
        rows = last - first
        cells = rows * ny * nz
        planes = rows * ny
        parts_in = []
        for offset_z in range(3):
            part = jnp.zeros((cells, channels), jnp.float32)
            for offset_x in range(3):
                for offset_y in range(3):
                    window = held[first + offset_x : last + offset_x, offset_y : offset_y + ny].reshape(cells, channels)
                    tap = kernel_in_ref[(offset_x * 3 + offset_y) * 3 + offset_z]
                    part = part + jnp.dot(window, tap, preferred_element_type=jnp.float32)
            parts_in.append(part.reshape(planes, nz, channels))
        shifted[0:planes, 1 : nz + 1] = parts_in[0]
        total = parts_in[1] + shifted[0:planes, 0:nz]
        shifted[0:planes, 1 : nz + 1] = parts_in[2]
        total = total + shifted[0:planes, 2 : nz + 2]
        mean_square = jnp.mean(total * total, axis=-1, keepdims=True)
        normed = total * lax.rsqrt(mean_square + epsilon) * gains_ref[1:2, :]
        base = field_ref[first:last, 1 : ny + 1].reshape(planes, nz, channels).astype(jnp.float32)
        activated = gelu_tanh(normed + base).reshape(rows, ny, nz, channels)
        row = lax.broadcasted_iota(jnp.int32, activated.shape, 1)
        outside = ((row == 0) & (me_y == 0)) | ((row == ny - 1) & (me_y == count_y - 1))
        mixed[first:last] = jnp.where(outside, 0.0, activated).astype(mixed.dtype)

    def outer_rows(first, last):
        cells = (last - first) * ny_out * nz
        by_depth = jnp.zeros((cells, 3 * outch), jnp.float32)
        for offset_x in range(3):
            for offset_y in range(3):
                window = held_out[first + offset_x : last + offset_x, offset_y : offset_y + ny_out].reshape(
                    cells, channels
                )
                by_depth = by_depth + lax.dot_general(
                    window,
                    kernel_out_ref[offset_x * 3 + offset_y],
                    (((1,), (1,)), ((), ())),
                    preferred_element_type=jnp.float32,
                )
        return by_depth

    inner_rows(1, nx - 1)
    pl.semaphore_wait(barrier, present + count - 1)
    halo_finish(halo_start(field_ref, held, send_sem, recv_sem))
    inner_rows(0, 1)
    inner_rows(nx - 1, nx)

    edge = jnp.zeros((nx * ny_out, 1, outch), jnp.float32)
    shifted_out[:, 0:1] = edge
    shifted_out[:, nz + 1 : nz + 2] = edge

    def by_channel(by_depth, rows):
        planes = rows * ny_out
        shifted_out[0:planes, 1 : nz + 1] = by_depth[:, 0:outch].reshape(planes, nz, outch)
        summed = by_depth[:, outch : 2 * outch].reshape(planes, nz, outch) + shifted_out[0:planes, 0:nz]
        shifted_out[0:planes, 1 : nz + 1] = by_depth[:, 2 * outch : 3 * outch].reshape(planes, nz, outch)
        summed = summed + shifted_out[0:planes, 2 : nz + 2]
        return summed.reshape(planes * nz, outch).T

    block = outch // count

    def share(phase, values):
        for peer in range(count):
            parts[phase, peer] = values[peer * block : (peer + 1) * block]
        sends = []
        for step in range(1, count):
            peer = lax.rem(me + step, count)
            copy = pltpu.make_async_remote_copy(
                src_ref=parts.at[phase, peer],
                dst_ref=inbox.at[phase, step],
                send_sem=sum_send.at[phase, step],
                recv_sem=sum_recv.at[phase, step],
                device_id={"section": peer},
                device_id_type=MESH,
            )
            copy.start()
            sends.append(copy)
        return sends

    def gather(phase, sends):
        result = parts[phase, me]
        for step in range(1, count):
            sends[step - 1].wait_recv()
            result = result + inbox[phase, step]
        for copy in sends:
            copy.wait_send()
        return result

    copies = halo_start(mixed, held_out, send_out, recv_out)
    held_out[1 : nx + 1] = mixed[...]
    middle_sends = share(0, by_channel(outer_rows(1, nx - 1), nx - 2))
    halo_finish(copies)
    row_cells = ny_out * nz
    ends = jnp.concatenate(
        [by_channel(outer_rows(0, 1), 1), by_channel(outer_rows(nx - 1, nx), 1)], axis=1
    )
    end_sends = share(1, ends)
    middle = gather(0, middle_sends)
    ends = gather(1, end_sends)
    result = jnp.concatenate([ends[:, 0:row_cells], middle, ends[:, row_cells:]], axis=1)
    out_ref[...] = result.reshape(out_ref.shape).astype(out_ref.dtype)


def decoder_block(field, kernel_in, gains, kernel_out, collective):
    nx, ny_in, nz, channels = field.shape
    ny = ny_in - 2
    ny_out = ny - 2
    count = lax.axis_size("section")
    outch = kernel_out.shape[1] // 3
    block = outch // count
    return pl.pallas_call(
        block_kernel,
        out_shape=jax.ShapeDtypeStruct((block, nx, ny_out * nz), jnp.bfloat16),
        in_specs=[pl.BlockSpec(memory_space=pltpu.VMEM)] * 4,
        out_specs=pl.BlockSpec(memory_space=pltpu.VMEM),
        scratch_shapes=[
            pltpu.VMEM((nx + 2, ny_in, nz, channels), field.dtype),
            pltpu.VMEM((nx * ny, nz + 2, channels), jnp.float32),
            pltpu.VMEM((nx, ny, nz, channels), field.dtype),
            pltpu.VMEM((nx + 2, ny, nz, channels), field.dtype),
            pltpu.VMEM((nx * ny_out, nz + 2, outch), jnp.float32),
            pltpu.VMEM((2, count, block, (nx - 2) * ny_out * nz), jnp.float32),
            pltpu.VMEM((2, count, block, (nx - 2) * ny_out * nz), jnp.float32),
            pltpu.SemaphoreType.DMA((2,)),
            pltpu.SemaphoreType.DMA((2,)),
            pltpu.SemaphoreType.DMA((2,)),
            pltpu.SemaphoreType.DMA((2,)),
            pltpu.SemaphoreType.DMA((2, count)),
            pltpu.SemaphoreType.DMA((2, count)),
        ],
        compiler_params=pltpu.CompilerParams(collective_id=collective, has_side_effects=True),
    )(field, kernel_in, gains, kernel_out)


def local(skips, deconv_weight, norm_gain, conv_in, conv_out):
    inl_size = lax.axis_size("inl")
    tokens_here = skips[0]
    weight = deconv_weight[0]
    gains = norm_gain[0]
    channels = gains.shape[1]
    cell_x = 2 * PXD
    cell_y = 2 * lax.axis_size("xln")
    cell_z = 2 * GZ
    assert tokens_here.shape[0] == inl_size * PXD * GZ
    field = gather_bricks(tokens_here, weight, gains)
    taps, outch, channels_in = conv_out.shape[1:]
    out_weight = conv_out[0].reshape(taps // 3, 3 * outch, channels_in)
    return decoder_block(field, conv_in[0], gains, out_weight, 1)


def solution(mesh):
    return jax.shard_map(
        local,
        mesh=mesh,
        in_specs=(
            P("section", ("inl", "xln"), None),
            P("section", None, None),
            P("section", None, None),
            P("section", None, None, None),
            P("section", None, None, None),
        ),
        out_specs=P("section", "inl", "xln"),
        check_vma=False,
    )
```

```python
import functools

import jax
import jax.numpy as jnp
from jax import lax
from jax.experimental import pallas as pl
from jax.experimental.pallas import tpu as pltpu
from jax.sharding import PartitionSpec as P

MESH = pl.DeviceIdType.MESH
PXD = 2
GZ = 8


epsilon = 1e-05


def gelu_tanh(values):
    return 0.5 * values * (1.0 + jnp.tanh(0.7978845608028654 * (values + 0.044715 * (values * values * values))))


def send_groups(me_x, me_y, count):
    return [
        (me_x, me_y + 1, None),
        (me_x + 1, 0, (me_y == count - 1) & (me_x + 1 < count)),
        (me_x - 1, count + 1, (me_y == 0) & (me_x > 0)),
    ]


def gather_kernel(tokens_ref, weight_hbm, gains_ref, out_ref, weight, field, held, send_sem, recv_sem, weight_sem):
    count = lax.axis_size("inl")
    me_x, me_y = lax.axis_index("inl"), lax.axis_index("xln")
    rows = tokens_ref.shape[0] // count
    width = gains_ref.shape[1]
    one = jnp.int32(1)
    loading = pltpu.make_async_copy(weight_hbm, weight, weight_sem)
    loading.start()
    groups = send_groups(me_x, me_y, count)
    sources = [(me_y - 1, count - 1, me_y >= 1)]
    sources += [(me_y, other, None) for other in range(count)]
    sources += [(me_y + 1, 0, me_y + 1 < count)]

    def is_me(x, y):
        return (x == me_x) & (y == me_y)

    barrier = pltpu.get_barrier_semaphore()
    expected = jnp.int32(0)
    for column, _, exists in groups:
        live = True if exists is None else exists
        expected = expected + jnp.where(live, count, 0)
        for other in range(count):

            @pl.when(jnp.logical_and(live, jnp.logical_not(is_me(other, column))))
            def _():
                pl.semaphore_signal(barrier, inc=1, device_id={"inl": other, "xln": column}, device_id_type=MESH)

            expected = expected - jnp.where(jnp.logical_and(live, is_me(other, column)), one, 0)
    for source_x, source_y, exists in sources:
        live = True if exists is None else exists
        mine = jnp.logical_and(live, is_me(source_x, source_y))
        expected = expected + jnp.where(jnp.logical_and(live, jnp.logical_not(mine)), one, 0)

        @pl.when(jnp.logical_and(live, jnp.logical_not(mine)))
        def _():
            pl.semaphore_signal(barrier, inc=1, device_id={"inl": source_x, "xln": source_y}, device_id_type=MESH)

    loading.wait()
    upsampled = jnp.dot(tokens_ref[...], weight[...], preferred_element_type=jnp.float32)
    for group in range(upsampled.shape[1] // width):
        part = upsampled[:, group * width : (group + 1) * width]
        mean_square = jnp.mean(part * part, axis=-1, keepdims=True)
        normed = part * lax.rsqrt(mean_square + epsilon) * gains_ref[0:1, :]
        field[:, group * width : (group + 1) * width] = gelu_tanh(normed).astype(field.dtype)
    depth = 2 * (rows // 2)
    target = lax.broadcasted_iota(jnp.int32, (2 * rows, 2 * rows), 0)
    origin = lax.broadcasted_iota(jnp.int32, (2 * rows, 2 * rows), 1)
    half = rows // 2
    same = (
        (target // depth == (origin % rows) // half)
        & ((target % depth) // 2 == origin % half)
        & (target % 2 == origin // rows)
    )
    interleave = jnp.where(same, 1.0, 0.0).astype(jnp.bfloat16)

    def place(slot, block):
        for u in range(2):
            for v in range(2):
                first = ((u * 2 + v) * 2) * width
                pair = jnp.concatenate([block[:, first : first + width], block[:, first + width : first + 2 * width]], axis=0)
                cells = jnp.dot(interleave, pair, preferred_element_type=jnp.float32).astype(out_ref.dtype)
                for ix in range(2):
                    out_ref[2 * ix + u, 2 * slot + v] = cells[ix * depth : (ix + 1) * depth]

    pl.semaphore_wait(barrier, expected)
    copies = []
    for index, (column, slot, exists) in enumerate(groups):
        live = True if exists is None else exists
        for turn in range(count):
            other = lax.rem(me_y + turn, count)
            copy = pltpu.make_async_remote_copy(
                src_ref=field.at[pl.ds(pl.multiple_of(other * rows, rows), rows)],
                dst_ref=held.at[slot],
                send_sem=send_sem.at[index * count + turn],
                recv_sem=recv_sem.at[slot],
                device_id={"inl": other, "xln": column},
                device_id_type=MESH,
            )
            remote = jnp.logical_and(live, jnp.logical_not(is_me(other, column)))

            @pl.when(remote)
            def _():
                copy.start()

            copies.append((copy, remote))
    for slot, (source_x, source_y, exists) in enumerate(sources):
        live = True if exists is None else exists
        mine = jnp.logical_and(live, is_me(source_x, source_y))
        remote = jnp.logical_and(live, jnp.logical_not(mine))
        incoming = pltpu.make_async_remote_copy(
            src_ref=field.at[pl.ds(0, rows)],
            dst_ref=held.at[slot],
            send_sem=send_sem.at[0],
            recv_sem=recv_sem.at[slot],
            device_id={"inl": source_x, "xln": source_y},
            device_id_type=MESH,
        )

        @pl.when(remote)
        def _():
            incoming.wait_recv()
            place(slot, held[slot])

        @pl.when(mine)
        def _():
            place(slot, field[pl.ds(pl.multiple_of(me_x * rows, rows), rows)])

        @pl.when(jnp.logical_not(live))
        def _():
            out_ref[:, 2 * slot : 2 * slot + 2] = jnp.zeros(
                (out_ref.shape[0], 2) + out_ref.shape[2:], out_ref.dtype
            )

    for copy, remote in copies:

        @pl.when(remote)
        def _():
            copy.wait_send()


def gather_bricks(tokens, weight, gains):
    count = lax.axis_size("inl")
    rows = tokens.shape[0] // count
    shape = (lax.axis_size("xln") + 2, rows, weight.shape[1])
    brick = (2 * PXD, 2 * shape[0], 2 * GZ, gains.shape[1])
    return pl.pallas_call(
        gather_kernel,
        out_shape=jax.ShapeDtypeStruct(brick, jnp.bfloat16),
        in_specs=[
            pl.BlockSpec(memory_space=pltpu.VMEM),
            pl.BlockSpec(memory_space=pl.ANY),
            pl.BlockSpec(memory_space=pltpu.VMEM),
        ],
        out_specs=pl.BlockSpec(memory_space=pltpu.VMEM),
        scratch_shapes=[
            pltpu.VMEM(weight.shape, weight.dtype),
            pltpu.VMEM((tokens.shape[0], weight.shape[1]), jnp.bfloat16),
            pltpu.VMEM(shape, jnp.bfloat16),
            pltpu.SemaphoreType.DMA((3 * count,)),
            pltpu.SemaphoreType.DMA((shape[0],)),
            pltpu.SemaphoreType.DMA(()),
        ],
        compiler_params=pltpu.CompilerParams(collective_id=3, has_side_effects=True),
    )(tokens, weight, gains)


def halo_signal():
    count = lax.axis_size("inl")
    me = lax.axis_index("inl")
    for step in (-1, 1):

        @pl.when((me + step >= 0) & (me + step < count))
        def _():
            pl.semaphore_signal(
                pltpu.get_barrier_semaphore(), inc=1, device_id={"inl": me + step}, device_id_type=MESH
            )

    return (me > 0).astype(jnp.int32) + (me < count - 1).astype(jnp.int32)


def halo_start(field_ref, held, send_sem, recv_sem):
    nx = field_ref.shape[0]
    count = lax.axis_size("inl")
    me = lax.axis_index("inl")
    copies = []
    for index, step in enumerate((-1, 1)):
        source, target = (0, nx + 1) if step < 0 else (nx - 1, 0)
        copy = pltpu.make_async_remote_copy(
            src_ref=field_ref.at[source : source + 1],
            dst_ref=held.at[target : target + 1],
            send_sem=send_sem.at[index],
            recv_sem=recv_sem.at[index],
            device_id={"inl": me + step},
            device_id_type=MESH,
        )
        sends = (me + step >= 0) & (me + step < count)
        gets = (me - step >= 0) & (me - step < count)

        @pl.when(sends)
        def _():
            copy.start()

        @pl.when(jnp.logical_not(gets))
        def _():
            held[target : target + 1] = jnp.zeros((1,) + held.shape[1:], held.dtype)

        copies.append((copy, sends, gets))
    return copies


def halo_finish(copies):
    for copy, sends, gets in copies:

        @pl.when(gets)
        def _():
            copy.wait_recv()

        @pl.when(sends)
        def _():
            copy.wait_send()


def block_kernel(
    field_ref, kernel_in_ref, gains_ref, kernel_out_ref, out_ref,
    held, shifted, mixed, held_out, shifted_out, parts, inbox,
    send_sem, recv_sem, send_out, recv_out, sum_send, sum_recv,
):
    count = lax.axis_size("section")
    me = lax.axis_index("section")
    barrier = pltpu.get_barrier_semaphore()
    for step in range(1, count):
        pl.semaphore_signal(
            barrier, inc=1, device_id={"section": lax.rem(me + step, count)}, device_id_type=MESH
        )
    present = halo_signal()
    nx, ny_in, nz, channels = field_ref.shape
    ny = ny_in - 2
    ny_out = ny - 2
    outch = kernel_out_ref.shape[1] // 3
    me_y, count_y = lax.axis_index("xln"), lax.axis_size("xln")
    edge = jnp.zeros((nx * ny, 1, channels), jnp.float32)
    shifted[:, 0:1] = edge
    shifted[:, nz + 1 : nz + 2] = edge
    held[1 : nx + 1] = field_ref[...]

    def inner_taps(first, last, offsets_x):
        cells = (last - first) * ny * nz
        parts_in = []
        for offset_z in range(3):
            part = jnp.zeros((cells, channels), jnp.float32)
            for offset_x in offsets_x:
                for offset_y in range(3):
                    window = held[first + offset_x : last + offset_x, offset_y : offset_y + ny].reshape(cells, channels)
                    tap = kernel_in_ref[(offset_x * 3 + offset_y) * 3 + offset_z]
                    part = part + jnp.dot(window, tap, preferred_element_type=jnp.float32)
            parts_in.append(part)
        return parts_in

    def inner_rows(first, last, parts_in):
        rows = last - first
        planes = rows * ny
        parts_in = [part.reshape(planes, nz, channels) for part in parts_in]
        shifted[0:planes, 1 : nz + 1] = parts_in[0]
        total = parts_in[1] + shifted[0:planes, 0:nz]
        shifted[0:planes, 1 : nz + 1] = parts_in[2]
        total = total + shifted[0:planes, 2 : nz + 2]
        mean_square = jnp.mean(total * total, axis=-1, keepdims=True)
        normed = total * lax.rsqrt(mean_square + epsilon) * gains_ref[1:2, :]
        base = field_ref[first:last, 1 : ny + 1].reshape(planes, nz, channels).astype(jnp.float32)
        activated = gelu_tanh(normed + base).reshape(rows, ny, nz, channels)
        row = lax.broadcasted_iota(jnp.int32, activated.shape, 1)
        outside = ((row == 0) & (me_y == 0)) | ((row == ny - 1) & (me_y == count_y - 1))
        mixed[first:last] = jnp.where(outside, 0.0, activated).astype(mixed.dtype)

    def outer_rows(first, last):
        cells = (last - first) * ny_out * nz
        by_depth = jnp.zeros((cells, 3 * outch), jnp.float32)
        for offset_x in range(3):
            for offset_y in range(3):
                window = held_out[first + offset_x : last + offset_x, offset_y : offset_y + ny_out].reshape(
                    cells, channels
                )
                by_depth = by_depth + lax.dot_general(
                    window,
                    kernel_out_ref[offset_x * 3 + offset_y],
                    (((1,), (1,)), ((), ())),
                    preferred_element_type=jnp.float32,
                )
        return by_depth

    inner_rows(1, nx - 1, inner_taps(1, nx - 1, (0, 1, 2)))
    low = inner_taps(0, 1, (1, 2))
    high = inner_taps(nx - 1, nx, (0, 1))
    pl.semaphore_wait(barrier, present + count - 1)
    halo_finish(halo_start(field_ref, held, send_sem, recv_sem))
    inner_rows(0, 1, [a + b for a, b in zip(low, inner_taps(0, 1, (0,)))])
    inner_rows(nx - 1, nx, [a + b for a, b in zip(high, inner_taps(nx - 1, nx, (2,)))])

    edge = jnp.zeros((nx * ny_out, 1, outch), jnp.float32)
    shifted_out[:, 0:1] = edge
    shifted_out[:, nz + 1 : nz + 2] = edge

    def by_channel(by_depth, rows):
        planes = rows * ny_out
        shifted_out[0:planes, 1 : nz + 1] = by_depth[:, 0:outch].reshape(planes, nz, outch)
        summed = by_depth[:, outch : 2 * outch].reshape(planes, nz, outch) + shifted_out[0:planes, 0:nz]
        shifted_out[0:planes, 1 : nz + 1] = by_depth[:, 2 * outch : 3 * outch].reshape(planes, nz, outch)
        summed = summed + shifted_out[0:planes, 2 : nz + 2]
        return summed.reshape(planes * nz, outch).T

    block = outch // count

    def share(phase, values):
        for peer in range(count):
            parts[phase, peer] = values[peer * block : (peer + 1) * block]
        sends = []
        for step in range(1, count):
            peer = lax.rem(me + step, count)
            copy = pltpu.make_async_remote_copy(
                src_ref=parts.at[phase, peer],
                dst_ref=inbox.at[phase, step],
                send_sem=sum_send.at[phase, step],
                recv_sem=sum_recv.at[phase, step],
                device_id={"section": peer},
                device_id_type=MESH,
            )
            copy.start()
            sends.append(copy)
        return sends

    def gather(phase, sends):
        result = parts[phase, me]
        for step in range(1, count):
            sends[step - 1].wait_recv()
            result = result + inbox[phase, step]
        for copy in sends:
            copy.wait_send()
        return result

    copies = halo_start(mixed, held_out, send_out, recv_out)
    held_out[1 : nx + 1] = mixed[...]
    middle_sends = share(0, by_channel(outer_rows(1, nx - 1), nx - 2))
    halo_finish(copies)
    row_cells = ny_out * nz
    ends = jnp.concatenate(
        [by_channel(outer_rows(0, 1), 1), by_channel(outer_rows(nx - 1, nx), 1)], axis=1
    )
    end_sends = share(1, ends)
    middle = gather(0, middle_sends)
    ends = gather(1, end_sends)
    result = jnp.concatenate([ends[:, 0:row_cells], middle, ends[:, row_cells:]], axis=1)
    out_ref[...] = result.reshape(out_ref.shape).astype(out_ref.dtype)


def decoder_block(field, kernel_in, gains, kernel_out, collective):
    nx, ny_in, nz, channels = field.shape
    ny = ny_in - 2
    ny_out = ny - 2
    count = lax.axis_size("section")
    outch = kernel_out.shape[1] // 3
    block = outch // count
    return pl.pallas_call(
        block_kernel,
        out_shape=jax.ShapeDtypeStruct((block, nx, ny_out * nz), jnp.bfloat16),
        in_specs=[pl.BlockSpec(memory_space=pltpu.VMEM)] * 4,
        out_specs=pl.BlockSpec(memory_space=pltpu.VMEM),
        scratch_shapes=[
            pltpu.VMEM((nx + 2, ny_in, nz, channels), field.dtype),
            pltpu.VMEM((nx * ny, nz + 2, channels), jnp.float32),
            pltpu.VMEM((nx, ny, nz, channels), field.dtype),
            pltpu.VMEM((nx + 2, ny, nz, channels), field.dtype),
            pltpu.VMEM((nx * ny_out, nz + 2, outch), jnp.float32),
            pltpu.VMEM((2, count, block, (nx - 2) * ny_out * nz), jnp.float32),
            pltpu.VMEM((2, count, block, (nx - 2) * ny_out * nz), jnp.float32),
            pltpu.SemaphoreType.DMA((2,)),
            pltpu.SemaphoreType.DMA((2,)),
            pltpu.SemaphoreType.DMA((2,)),
            pltpu.SemaphoreType.DMA((2,)),
            pltpu.SemaphoreType.DMA((2, count)),
            pltpu.SemaphoreType.DMA((2, count)),
        ],
        compiler_params=pltpu.CompilerParams(collective_id=collective, has_side_effects=True),
    )(field, kernel_in, gains, kernel_out)


def local(skips, deconv_weight, norm_gain, conv_in, conv_out):
    inl_size = lax.axis_size("inl")
    tokens_here = skips[0]
    weight = deconv_weight[0]
    gains = norm_gain[0]
    channels = gains.shape[1]
    cell_x = 2 * PXD
    cell_y = 2 * lax.axis_size("xln")
    cell_z = 2 * GZ
    assert tokens_here.shape[0] == inl_size * PXD * GZ
    field = gather_bricks(tokens_here, weight, gains)
    taps, outch, channels_in = conv_out.shape[1:]
    out_weight = conv_out[0].reshape(taps // 3, 3 * outch, channels_in)
    return decoder_block(field, conv_in[0], gains, out_weight, 1)


def solution(mesh):
    return jax.shard_map(
        local,
        mesh=mesh,
        in_specs=(
            P("section", ("inl", "xln"), None),
            P("section", None, None),
            P("section", None, None),
            P("section", None, None, None),
            P("section", None, None, None),
        ),
        out_specs=P("section", "inl", "xln"),
        check_vma=False,
    )
```

```python
import functools

import jax
import jax.numpy as jnp
from jax import lax
from jax.experimental import pallas as pl
from jax.experimental.pallas import tpu as pltpu
from jax.sharding import PartitionSpec as P

MESH = pl.DeviceIdType.MESH
PXD = 2
GZ = 8


epsilon = 1e-05


def gelu_tanh(values):
    return 0.5 * values * (1.0 + jnp.tanh(0.7978845608028654 * (values + 0.044715 * (values * values * values))))


def send_groups(me_x, me_y, count):
    return [
        (me_x, me_y + 1, None),
        (me_x + 1, 0, (me_y == count - 1) & (me_x + 1 < count)),
        (me_x - 1, count + 1, (me_y == 0) & (me_x > 0)),
    ]


def gather_kernel(
    tokens_ref, weight_hbm, gains_ref, out_ref, weight, field, held, send_sem, recv_sem, weight_sem, extra=0
):
    count = lax.axis_size("inl")
    me_x, me_y = lax.axis_index("inl"), lax.axis_index("xln")
    rows = tokens_ref.shape[0] // count
    width = gains_ref.shape[1]
    one = jnp.int32(1)
    loading = pltpu.make_async_copy(weight_hbm, weight, weight_sem)
    loading.start()
    groups = send_groups(me_x, me_y, count)
    sources = [(me_y - 1, count - 1, me_y >= 1)]
    sources += [(me_y, other, None) for other in range(count)]
    sources += [(me_y + 1, 0, me_y + 1 < count)]

    def is_me(x, y):
        return (x == me_x) & (y == me_y)

    barrier = pltpu.get_barrier_semaphore()
    expected = jnp.int32(0)
    for column, _, exists in groups:
        live = True if exists is None else exists
        expected = expected + jnp.where(live, count, 0)
        for other in range(count):

            @pl.when(jnp.logical_and(live, jnp.logical_not(is_me(other, column))))
            def _():
                pl.semaphore_signal(barrier, inc=1, device_id={"inl": other, "xln": column}, device_id_type=MESH)

            expected = expected - jnp.where(jnp.logical_and(live, is_me(other, column)), one, 0)
    for source_x, source_y, exists in sources:
        live = True if exists is None else exists
        mine = jnp.logical_and(live, is_me(source_x, source_y))
        expected = expected + jnp.where(jnp.logical_and(live, jnp.logical_not(mine)), one, 0)

        @pl.when(jnp.logical_and(live, jnp.logical_not(mine)))
        def _():
            pl.semaphore_signal(barrier, inc=1, device_id={"inl": source_x, "xln": source_y}, device_id_type=MESH)

    loading.wait()
    upsampled = jnp.dot(tokens_ref[...], weight[...], preferred_element_type=jnp.float32)
    for group in range(upsampled.shape[1] // width):
        part = upsampled[:, group * width : (group + 1) * width]
        mean_square = jnp.mean(part * part, axis=-1, keepdims=True)
        normed = part * lax.rsqrt(mean_square + epsilon) * gains_ref[0:1, :]
        field[:, group * width : (group + 1) * width] = gelu_tanh(normed).astype(field.dtype)
    depth = 2 * (rows // 2)
    target = lax.broadcasted_iota(jnp.int32, (2 * rows, 2 * rows), 0)
    origin = lax.broadcasted_iota(jnp.int32, (2 * rows, 2 * rows), 1)
    half = rows // 2
    same = (
        (target // depth == (origin % rows) // half)
        & ((target % depth) // 2 == origin % half)
        & (target % 2 == origin // rows)
    )
    interleave = jnp.where(same, 1.0, 0.0).astype(jnp.bfloat16)

    def place(slot, block):
        for u in range(2):
            for v in range(2):
                first = ((u * 2 + v) * 2) * width
                pair = jnp.concatenate([block[:, first : first + width], block[:, first + width : first + 2 * width]], axis=0)
                cells = jnp.dot(interleave, pair, preferred_element_type=jnp.float32).astype(out_ref.dtype)
                for ix in range(2):
                    out_ref[2 * ix + u, 2 * slot + v] = cells[ix * depth : (ix + 1) * depth]

    pl.semaphore_wait(barrier, expected + extra)
    copies = []
    for index, (column, slot, exists) in enumerate(groups):
        live = True if exists is None else exists
        for turn in range(count):
            other = lax.rem(me_y + turn, count)
            copy = pltpu.make_async_remote_copy(
                src_ref=field.at[pl.ds(pl.multiple_of(other * rows, rows), rows)],
                dst_ref=held.at[slot],
                send_sem=send_sem.at[index * count + turn],
                recv_sem=recv_sem.at[slot],
                device_id={"inl": other, "xln": column},
                device_id_type=MESH,
            )
            remote = jnp.logical_and(live, jnp.logical_not(is_me(other, column)))

            @pl.when(remote)
            def _():
                copy.start()

            copies.append((copy, remote))
    for slot, (source_x, source_y, exists) in enumerate(sources):
        live = True if exists is None else exists
        mine = jnp.logical_and(live, is_me(source_x, source_y))
        remote = jnp.logical_and(live, jnp.logical_not(mine))
        incoming = pltpu.make_async_remote_copy(
            src_ref=field.at[pl.ds(0, rows)],
            dst_ref=held.at[slot],
            send_sem=send_sem.at[0],
            recv_sem=recv_sem.at[slot],
            device_id={"inl": source_x, "xln": source_y},
            device_id_type=MESH,
        )

        @pl.when(remote)
        def _():
            incoming.wait_recv()
            place(slot, held[slot])

        @pl.when(mine)
        def _():
            place(slot, field[pl.ds(pl.multiple_of(me_x * rows, rows), rows)])

        @pl.when(jnp.logical_not(live))
        def _():
            out_ref[:, 2 * slot : 2 * slot + 2] = jnp.zeros(
                (out_ref.shape[0], 2) + out_ref.shape[2:], out_ref.dtype
            )

    for copy, remote in copies:

        @pl.when(remote)
        def _():
            copy.wait_send()


def halo_signal():
    count = lax.axis_size("inl")
    me = lax.axis_index("inl")
    for step in (-1, 1):

        @pl.when((me + step >= 0) & (me + step < count))
        def _():
            pl.semaphore_signal(
                pltpu.get_barrier_semaphore(), inc=1, device_id={"inl": me + step}, device_id_type=MESH
            )

    return (me > 0).astype(jnp.int32) + (me < count - 1).astype(jnp.int32)


def halo_start(field_ref, held, send_sem, recv_sem):
    nx = field_ref.shape[0]
    count = lax.axis_size("inl")
    me = lax.axis_index("inl")
    copies = []
    for index, step in enumerate((-1, 1)):
        source, target = (0, nx + 1) if step < 0 else (nx - 1, 0)
        copy = pltpu.make_async_remote_copy(
            src_ref=field_ref.at[source : source + 1],
            dst_ref=held.at[target : target + 1],
            send_sem=send_sem.at[index],
            recv_sem=recv_sem.at[index],
            device_id={"inl": me + step},
            device_id_type=MESH,
        )
        sends = (me + step >= 0) & (me + step < count)
        gets = (me - step >= 0) & (me - step < count)

        @pl.when(sends)
        def _():
            copy.start()

        @pl.when(jnp.logical_not(gets))
        def _():
            held[target : target + 1] = jnp.zeros((1,) + held.shape[1:], held.dtype)

        copies.append((copy, sends, gets))
    return copies


def halo_finish(copies):
    for copy, sends, gets in copies:

        @pl.when(gets)
        def _():
            copy.wait_recv()

        @pl.when(sends)
        def _():
            copy.wait_send()


def entry_signals():
    count = lax.axis_size("section")
    me = lax.axis_index("section")
    for step in range(1, count):
        pl.semaphore_signal(
            pltpu.get_barrier_semaphore(),
            inc=1,
            device_id={"section": lax.rem(me + step, count)},
            device_id_type=MESH,
        )
    return halo_signal() + count - 1


def block_kernel(
    merged, field_ref, kernel_in_ref, gains_ref, kernel_out_ref, out_ref,
    held, shifted, mixed, held_out, shifted_out, parts, inbox,
    send_sem, recv_sem, send_out, recv_out, sum_send, sum_recv,
):
    count = lax.axis_size("section")
    me = lax.axis_index("section")
    barrier = pltpu.get_barrier_semaphore()
    if not merged:
        expected = entry_signals()
    nx, ny_in, nz, channels = field_ref.shape
    ny = ny_in - 2
    ny_out = ny - 2
    outch = kernel_out_ref.shape[1] // 3
    me_y, count_y = lax.axis_index("xln"), lax.axis_size("xln")
    edge = jnp.zeros((nx * ny, 1, channels), jnp.float32)
    shifted[:, 0:1] = edge
    shifted[:, nz + 1 : nz + 2] = edge
    held[1 : nx + 1] = field_ref[...]

    def inner_taps(first, last, offsets_x):
        cells = (last - first) * ny * nz
        parts_in = []
        for offset_z in range(3):
            part = jnp.zeros((cells, channels), jnp.float32)
            for offset_x in offsets_x:
                for offset_y in range(3):
                    window = held[first + offset_x : last + offset_x, offset_y : offset_y + ny].reshape(cells, channels)
                    tap = kernel_in_ref[(offset_x * 3 + offset_y) * 3 + offset_z]
                    part = part + jnp.dot(window, tap, preferred_element_type=jnp.float32)
            parts_in.append(part)
        return parts_in

    def inner_rows(first, last, parts_in):
        rows = last - first
        planes = rows * ny
        parts_in = [part.reshape(planes, nz, channels) for part in parts_in]
        shifted[0:planes, 1 : nz + 1] = parts_in[0]
        total = parts_in[1] + shifted[0:planes, 0:nz]
        shifted[0:planes, 1 : nz + 1] = parts_in[2]
        total = total + shifted[0:planes, 2 : nz + 2]
        mean_square = jnp.mean(total * total, axis=-1, keepdims=True)
        normed = total * lax.rsqrt(mean_square + epsilon) * gains_ref[1:2, :]
        base = field_ref[first:last, 1 : ny + 1].reshape(planes, nz, channels).astype(jnp.float32)
        activated = gelu_tanh(normed + base).reshape(rows, ny, nz, channels)
        row = lax.broadcasted_iota(jnp.int32, activated.shape, 1)
        outside = ((row == 0) & (me_y == 0)) | ((row == ny - 1) & (me_y == count_y - 1))
        mixed[first:last] = jnp.where(outside, 0.0, activated).astype(mixed.dtype)

    def outer_rows(first, last):
        cells = (last - first) * ny_out * nz
        by_depth = jnp.zeros((cells, 3 * outch), jnp.float32)
        for offset_x in range(3):
            for offset_y in range(3):
                window = held_out[first + offset_x : last + offset_x, offset_y : offset_y + ny_out].reshape(
                    cells, channels
                )
                by_depth = by_depth + lax.dot_general(
                    window,
                    kernel_out_ref[offset_x * 3 + offset_y],
                    (((1,), (1,)), ((), ())),
                    preferred_element_type=jnp.float32,
                )
        return by_depth

    inner_rows(1, nx - 1, inner_taps(1, nx - 1, (0, 1, 2)))
    low = inner_taps(0, 1, (1, 2))
    high = inner_taps(nx - 1, nx, (0, 1))
    if not merged:
        pl.semaphore_wait(barrier, expected)
    halo_finish(halo_start(field_ref, held, send_sem, recv_sem))
    inner_rows(0, 1, [a + b for a, b in zip(low, inner_taps(0, 1, (0,)))])
    inner_rows(nx - 1, nx, [a + b for a, b in zip(high, inner_taps(nx - 1, nx, (2,)))])

    edge = jnp.zeros((nx * ny_out, 1, outch), jnp.float32)
    shifted_out[:, 0:1] = edge
    shifted_out[:, nz + 1 : nz + 2] = edge

    def by_channel(by_depth, rows):
        planes = rows * ny_out
        shifted_out[0:planes, 1 : nz + 1] = by_depth[:, 0:outch].reshape(planes, nz, outch)
        summed = by_depth[:, outch : 2 * outch].reshape(planes, nz, outch) + shifted_out[0:planes, 0:nz]
        shifted_out[0:planes, 1 : nz + 1] = by_depth[:, 2 * outch : 3 * outch].reshape(planes, nz, outch)
        summed = summed + shifted_out[0:planes, 2 : nz + 2]
        return summed.reshape(planes * nz, outch).T

    block = outch // count

    def share(phase, values):
        for peer in range(count):
            parts[phase, peer] = values[peer * block : (peer + 1) * block]
        sends = []
        for step in range(1, count):
            peer = lax.rem(me + step, count)
            copy = pltpu.make_async_remote_copy(
                src_ref=parts.at[phase, peer],
                dst_ref=inbox.at[phase, step],
                send_sem=sum_send.at[phase, step],
                recv_sem=sum_recv.at[phase, step],
                device_id={"section": peer},
                device_id_type=MESH,
            )
            copy.start()
            sends.append(copy)
        return sends

    def gather(phase, sends):
        result = parts[phase, me]
        for step in range(1, count):
            sends[step - 1].wait_recv()
            result = result + inbox[phase, step]
        for copy in sends:
            copy.wait_send()
        return result

    copies = halo_start(mixed, held_out, send_out, recv_out)
    held_out[1 : nx + 1] = mixed[...]
    middle_sends = share(0, by_channel(outer_rows(1, nx - 1), nx - 2))
    halo_finish(copies)
    row_cells = ny_out * nz
    ends = jnp.concatenate(
        [by_channel(outer_rows(0, 1), 1), by_channel(outer_rows(nx - 1, nx), 1)], axis=1
    )
    end_sends = share(1, ends)
    middle = gather(0, middle_sends)
    ends = gather(1, end_sends)
    result = jnp.concatenate([ends[:, 0:row_cells], middle, ends[:, row_cells:]], axis=1)
    out_ref[...] = result.reshape(out_ref.shape).astype(out_ref.dtype)


def whole_kernel(tokens_ref, weight_hbm, gains_ref, kernel_in_hbm, kernel_out_hbm, out_ref, *scratch):
    weight, field, rows_in, send_rows, recv_rows, weight_sem = scratch[:6]
    brick, kernel_in, kernel_out, kernel_sem = scratch[6:10]
    loads = [
        pltpu.make_async_copy(kernel_in_hbm, kernel_in, kernel_sem.at[0]),
        pltpu.make_async_copy(kernel_out_hbm, kernel_out, kernel_sem.at[1]),
    ]
    for load in loads:
        load.start()
    extra = entry_signals()
    gather_kernel(
        tokens_ref, weight_hbm, gains_ref, brick, weight, field, rows_in, send_rows, recv_rows, weight_sem, extra
    )
    for load in loads:
        load.wait()
    block_kernel(True, brick, kernel_in, gains_ref, kernel_out, out_ref, *scratch[10:])


def decoder_block(tokens, weight, gains, kernel_in, kernel_out, collective):
    count_x = lax.axis_size("inl")
    rows = tokens.shape[0] // count_x
    slots = lax.axis_size("xln") + 2
    nx, ny_in, nz, channels = 2 * PXD, 2 * slots, 2 * GZ, gains.shape[1]
    ny = ny_in - 2
    ny_out = ny - 2
    count = lax.axis_size("section")
    outch = kernel_out.shape[1] // 3
    block = outch // count
    return pl.pallas_call(
        whole_kernel,
        out_shape=jax.ShapeDtypeStruct((block, nx, ny_out * nz), jnp.bfloat16),
        in_specs=[
            pl.BlockSpec(memory_space=pltpu.VMEM),
            pl.BlockSpec(memory_space=pl.ANY),
            pl.BlockSpec(memory_space=pltpu.VMEM),
            pl.BlockSpec(memory_space=pl.ANY),
            pl.BlockSpec(memory_space=pl.ANY),
        ],
        out_specs=pl.BlockSpec(memory_space=pltpu.VMEM),
        scratch_shapes=[
            pltpu.VMEM(weight.shape, weight.dtype),
            pltpu.VMEM((tokens.shape[0], weight.shape[1]), jnp.bfloat16),
            pltpu.VMEM((slots, rows, weight.shape[1]), jnp.bfloat16),
            pltpu.SemaphoreType.DMA((3 * count_x,)),
            pltpu.SemaphoreType.DMA((slots,)),
            pltpu.SemaphoreType.DMA(()),
            pltpu.VMEM((nx, ny_in, nz, channels), jnp.bfloat16),
            pltpu.VMEM(kernel_in.shape, kernel_in.dtype),
            pltpu.VMEM(kernel_out.shape, kernel_out.dtype),
            pltpu.SemaphoreType.DMA((2,)),
            pltpu.VMEM((nx + 2, ny_in, nz, channels), jnp.bfloat16),
            pltpu.VMEM((nx * ny, nz + 2, channels), jnp.float32),
            pltpu.VMEM((nx, ny, nz, channels), jnp.bfloat16),
            pltpu.VMEM((nx + 2, ny, nz, channels), jnp.bfloat16),
            pltpu.VMEM((nx * ny_out, nz + 2, outch), jnp.float32),
            pltpu.VMEM((2, count, block, (nx - 2) * ny_out * nz), jnp.float32),
            pltpu.VMEM((2, count, block, (nx - 2) * ny_out * nz), jnp.float32),
            pltpu.SemaphoreType.DMA((2,)),
            pltpu.SemaphoreType.DMA((2,)),
            pltpu.SemaphoreType.DMA((2,)),
            pltpu.SemaphoreType.DMA((2,)),
            pltpu.SemaphoreType.DMA((2, count)),
            pltpu.SemaphoreType.DMA((2, count)),
        ],
        compiler_params=pltpu.CompilerParams(collective_id=collective, has_side_effects=True),
    )(tokens, weight, gains, kernel_in, kernel_out)


def local(skips, deconv_weight, norm_gain, conv_in, conv_out):
    inl_size = lax.axis_size("inl")
    tokens_here = skips[0]
    weight = deconv_weight[0]
    gains = norm_gain[0]
    channels = gains.shape[1]
    cell_x = 2 * PXD
    cell_y = 2 * lax.axis_size("xln")
    cell_z = 2 * GZ
    assert tokens_here.shape[0] == inl_size * PXD * GZ
    taps, outch, channels_in = conv_out.shape[1:]
    out_weight = conv_out[0].reshape(taps // 3, 3 * outch, channels_in)
    return decoder_block(tokens_here, weight, gains, conv_in[0], out_weight, 3)


def solution(mesh):
    return jax.shard_map(
        local,
        mesh=mesh,
        in_specs=(
            P("section", ("inl", "xln"), None),
            P("section", None, None),
            P("section", None, None),
            P("section", None, None, None),
            P("section", None, None, None),
        ),
        out_specs=P("section", "inl", "xln"),
        check_vma=False,
    )
```

```python
import functools

import jax
import jax.numpy as jnp
from jax import lax
from jax.experimental import pallas as pl
from jax.experimental.pallas import tpu as pltpu
from jax.sharding import PartitionSpec as P

MESH = pl.DeviceIdType.MESH
PXD = 2
GZ = 8


epsilon = 1e-05


def gelu_tanh(values):
    return 0.5 * values * (1.0 + jnp.tanh(0.7978845608028654 * (values + 0.044715 * (values * values * values))))


def send_groups(me_x, me_y, count):
    return [
        (me_x, me_y + 1, None),
        (me_x + 1, 0, (me_y == count - 1) & (me_x + 1 < count)),
        (me_x - 1, count + 1, (me_y == 0) & (me_x > 0)),
    ]


def gather_kernel(
    tokens_ref, weight_hbm, gains_ref, out_ref, weight, field, held, send_sem, recv_sem, weight_sem, extra=0,
    hooks=None,
):
    count = lax.axis_size("inl")
    me_x, me_y = lax.axis_index("inl"), lax.axis_index("xln")
    rows = tokens_ref.shape[0] // count
    width = gains_ref.shape[1]
    one = jnp.int32(1)
    loading = pltpu.make_async_copy(weight_hbm, weight, weight_sem)
    loading.start()
    groups = send_groups(me_x, me_y, count)
    sources = [(me_y - 1, count - 1, me_y >= 1)]
    sources += [(me_y, other, None) for other in range(count)]
    sources += [(me_y + 1, 0, me_y + 1 < count)]

    def is_me(x, y):
        return (x == me_x) & (y == me_y)

    barrier = pltpu.get_barrier_semaphore()
    expected = jnp.int32(0)
    for column, _, exists in groups:
        live = True if exists is None else exists
        expected = expected + jnp.where(live, count, 0)
        for other in range(count):

            @pl.when(jnp.logical_and(live, jnp.logical_not(is_me(other, column))))
            def _():
                pl.semaphore_signal(barrier, inc=1, device_id={"inl": other, "xln": column}, device_id_type=MESH)

            expected = expected - jnp.where(jnp.logical_and(live, is_me(other, column)), one, 0)
    for source_x, source_y, exists in sources:
        live = True if exists is None else exists
        mine = jnp.logical_and(live, is_me(source_x, source_y))
        expected = expected + jnp.where(jnp.logical_and(live, jnp.logical_not(mine)), one, 0)

        @pl.when(jnp.logical_and(live, jnp.logical_not(mine)))
        def _():
            pl.semaphore_signal(barrier, inc=1, device_id={"inl": source_x, "xln": source_y}, device_id_type=MESH)

    loading.wait()
    upsampled = jnp.dot(tokens_ref[...], weight[...], preferred_element_type=jnp.float32)
    for group in range(upsampled.shape[1] // width):
        part = upsampled[:, group * width : (group + 1) * width]
        mean_square = jnp.mean(part * part, axis=-1, keepdims=True)
        normed = part * lax.rsqrt(mean_square + epsilon) * gains_ref[0:1, :]
        field[:, group * width : (group + 1) * width] = gelu_tanh(normed).astype(field.dtype)
    depth = 2 * (rows // 2)
    target = lax.broadcasted_iota(jnp.int32, (2 * rows, 2 * rows), 0)
    origin = lax.broadcasted_iota(jnp.int32, (2 * rows, 2 * rows), 1)
    half = rows // 2
    same = (
        (target // depth == (origin % rows) // half)
        & ((target % depth) // 2 == origin % half)
        & (target % 2 == origin // rows)
    )
    interleave = jnp.where(same, 1.0, 0.0).astype(jnp.bfloat16)

    def place(slot, block):
        for u in range(2):
            for v in range(2):
                first = ((u * 2 + v) * 2) * width
                pair = jnp.concatenate([block[:, first : first + width], block[:, first + width : first + 2 * width]], axis=0)
                cells = jnp.dot(interleave, pair, preferred_element_type=jnp.float32).astype(out_ref.dtype)
                for ix in range(2):
                    out_ref[2 * ix + u, 2 * slot + v] = cells[ix * depth : (ix + 1) * depth]

    pl.semaphore_wait(barrier, expected + extra)
    copies = []
    for index, (column, slot, exists) in enumerate(groups):
        live = True if exists is None else exists
        for turn in range(count):
            other = lax.rem(me_y + turn, count)
            copy = pltpu.make_async_remote_copy(
                src_ref=field.at[pl.ds(pl.multiple_of(other * rows, rows), rows)],
                dst_ref=held.at[slot],
                send_sem=send_sem.at[index * count + turn],
                recv_sem=recv_sem.at[slot],
                device_id={"inl": other, "xln": column},
                device_id_type=MESH,
            )
            remote = jnp.logical_and(live, jnp.logical_not(is_me(other, column)))

            @pl.when(remote)
            def _():
                copy.start()

            copies.append((copy, remote))
    for slot, (source_x, source_y, exists) in enumerate(sources):
        live = True if exists is None else exists
        mine = jnp.logical_and(live, is_me(source_x, source_y))
        remote = jnp.logical_and(live, jnp.logical_not(mine))
        incoming = pltpu.make_async_remote_copy(
            src_ref=field.at[pl.ds(0, rows)],
            dst_ref=held.at[slot],
            send_sem=send_sem.at[0],
            recv_sem=recv_sem.at[slot],
            device_id={"inl": source_x, "xln": source_y},
            device_id_type=MESH,
        )

        @pl.when(remote)
        def _():
            incoming.wait_recv()
            place(slot, held[slot])

        @pl.when(mine)
        def _():
            place(slot, field[pl.ds(pl.multiple_of(me_x * rows, rows), rows)])

        @pl.when(jnp.logical_not(live))
        def _():
            out_ref[:, 2 * slot : 2 * slot + 2] = jnp.zeros(
                (out_ref.shape[0], 2) + out_ref.shape[2:], out_ref.dtype
            )

        if hooks and slot in hooks:
            hooks[slot]()

    for copy, remote in copies:

        @pl.when(remote)
        def _():
            copy.wait_send()


def halo_signal():
    count = lax.axis_size("inl")
    me = lax.axis_index("inl")
    for step in (-1, 1):

        @pl.when((me + step >= 0) & (me + step < count))
        def _():
            pl.semaphore_signal(
                pltpu.get_barrier_semaphore(), inc=1, device_id={"inl": me + step}, device_id_type=MESH
            )

    return (me > 0).astype(jnp.int32) + (me < count - 1).astype(jnp.int32)


def halo_start(field_ref, held, send_sem, recv_sem):
    nx = field_ref.shape[0]
    count = lax.axis_size("inl")
    me = lax.axis_index("inl")
    copies = []
    for index, step in enumerate((-1, 1)):
        source, target = (0, nx + 1) if step < 0 else (nx - 1, 0)
        copy = pltpu.make_async_remote_copy(
            src_ref=field_ref.at[source : source + 1],
            dst_ref=held.at[target : target + 1],
            send_sem=send_sem.at[index],
            recv_sem=recv_sem.at[index],
            device_id={"inl": me + step},
            device_id_type=MESH,
        )
        sends = (me + step >= 0) & (me + step < count)
        gets = (me - step >= 0) & (me - step < count)

        @pl.when(sends)
        def _():
            copy.start()

        @pl.when(jnp.logical_not(gets))
        def _():
            held[target : target + 1] = jnp.zeros((1,) + held.shape[1:], held.dtype)

        copies.append((copy, sends, gets))
    return copies


def halo_finish(copies):
    for copy, sends, gets in copies:

        @pl.when(gets)
        def _():
            copy.wait_recv()

        @pl.when(sends)
        def _():
            copy.wait_send()


def conv_in_rows(field_ref, kernel_in_ref, gains_ref, held, shifted, mixed):
    nx, ny_in, nz, channels = field_ref.shape
    ny = ny_in - 2
    me_y, count_y = lax.axis_index("xln"), lax.axis_size("xln")

    def inner_taps(first, last, offsets_x, low=0, high=ny):
        cells = (last - first) * (high - low) * nz
        parts_in = []
        for offset_z in range(3):
            part = jnp.zeros((cells, channels), jnp.float32)
            for offset_x in offsets_x:
                for offset_y in range(3):
                    window = held[first + offset_x : last + offset_x, low + offset_y : high + offset_y].reshape(
                        cells, channels
                    )
                    tap = kernel_in_ref[(offset_x * 3 + offset_y) * 3 + offset_z]
                    part = part + jnp.dot(window, tap, preferred_element_type=jnp.float32)
            parts_in.append(part)
        return parts_in

    def inner_rows(first, last, parts_in, low=0, high=ny):
        rows = last - first
        planes = rows * (high - low)
        parts_in = [part.reshape(planes, nz, channels) for part in parts_in]
        shifted[0:planes, 1 : nz + 1] = parts_in[0]
        total = parts_in[1] + shifted[0:planes, 0:nz]
        shifted[0:planes, 1 : nz + 1] = parts_in[2]
        total = total + shifted[0:planes, 2 : nz + 2]
        mean_square = jnp.mean(total * total, axis=-1, keepdims=True)
        normed = total * lax.rsqrt(mean_square + epsilon) * gains_ref[1:2, :]
        base = field_ref[first:last, 1 + low : 1 + high].reshape(planes, nz, channels).astype(jnp.float32)
        activated = gelu_tanh(normed + base).reshape(rows, high - low, nz, channels)
        row = low + lax.broadcasted_iota(jnp.int32, activated.shape, 1)
        outside = ((row == 0) & (me_y == 0)) | ((row == ny - 1) & (me_y == count_y - 1))
        mixed[first:last, low:high] = jnp.where(outside, 0.0, activated).astype(mixed.dtype)

    return inner_taps, inner_rows


def entry_signals():
    count = lax.axis_size("section")
    me = lax.axis_index("section")
    for step in range(1, count):
        pl.semaphore_signal(
            pltpu.get_barrier_semaphore(),
            inc=1,
            device_id={"section": lax.rem(me + step, count)},
            device_id_type=MESH,
        )
    return halo_signal() + count - 1


def block_kernel(
    merged, done, field_ref, kernel_in_ref, gains_ref, kernel_out_ref, out_ref,
    held, shifted, mixed, held_out, shifted_out, parts, inbox,
    send_sem, recv_sem, send_out, recv_out, sum_send, sum_recv,
):
    count = lax.axis_size("section")
    me = lax.axis_index("section")
    barrier = pltpu.get_barrier_semaphore()
    if not merged:
        expected = entry_signals()
    nx, ny_in, nz, channels = field_ref.shape
    ny = ny_in - 2
    ny_out = ny - 2
    outch = kernel_out_ref.shape[1] // 3
    me_y, count_y = lax.axis_index("xln"), lax.axis_size("xln")
    if not done:
        edge = jnp.zeros((nx * ny, 1, channels), jnp.float32)
        shifted[:, 0:1] = edge
        shifted[:, nz + 1 : nz + 2] = edge
        held[1 : nx + 1] = field_ref[...]
    else:
        held[1 : nx + 1, done + 2 :] = field_ref[:, done + 2 :]

    inner_taps, inner_rows = conv_in_rows(field_ref, kernel_in_ref, gains_ref, held, shifted, mixed)

    def outer_rows(first, last):
        cells = (last - first) * ny_out * nz
        by_depth = jnp.zeros((cells, 3 * outch), jnp.float32)
        for offset_x in range(3):
            for offset_y in range(3):
                window = held_out[first + offset_x : last + offset_x, offset_y : offset_y + ny_out].reshape(
                    cells, channels
                )
                by_depth = by_depth + lax.dot_general(
                    window,
                    kernel_out_ref[offset_x * 3 + offset_y],
                    (((1,), (1,)), ((), ())),
                    preferred_element_type=jnp.float32,
                )
        return by_depth

    inner_rows(1, nx - 1, inner_taps(1, nx - 1, (0, 1, 2), done, ny), done, ny)
    low = inner_taps(0, 1, (1, 2))
    high = inner_taps(nx - 1, nx, (0, 1))
    if not merged:
        pl.semaphore_wait(barrier, expected)
    halo_finish(halo_start(field_ref, held, send_sem, recv_sem))
    inner_rows(0, 1, [a + b for a, b in zip(low, inner_taps(0, 1, (0,)))])
    inner_rows(nx - 1, nx, [a + b for a, b in zip(high, inner_taps(nx - 1, nx, (2,)))])

    edge = jnp.zeros((nx * ny_out, 1, outch), jnp.float32)
    shifted_out[:, 0:1] = edge
    shifted_out[:, nz + 1 : nz + 2] = edge

    def by_channel(by_depth, rows):
        planes = rows * ny_out
        shifted_out[0:planes, 1 : nz + 1] = by_depth[:, 0:outch].reshape(planes, nz, outch)
        summed = by_depth[:, outch : 2 * outch].reshape(planes, nz, outch) + shifted_out[0:planes, 0:nz]
        shifted_out[0:planes, 1 : nz + 1] = by_depth[:, 2 * outch : 3 * outch].reshape(planes, nz, outch)
        summed = summed + shifted_out[0:planes, 2 : nz + 2]
        return summed.reshape(planes * nz, outch).T

    block = outch // count

    def share(phase, values):
        for peer in range(count):
            parts[phase, peer] = values[peer * block : (peer + 1) * block]
        sends = []
        for step in range(1, count):
            peer = lax.rem(me + step, count)
            copy = pltpu.make_async_remote_copy(
                src_ref=parts.at[phase, peer],
                dst_ref=inbox.at[phase, step],
                send_sem=sum_send.at[phase, step],
                recv_sem=sum_recv.at[phase, step],
                device_id={"section": peer},
                device_id_type=MESH,
            )
            copy.start()
            sends.append(copy)
        return sends

    def gather(phase, sends):
        result = parts[phase, me]
        for step in range(1, count):
            sends[step - 1].wait_recv()
            result = result + inbox[phase, step]
        for copy in sends:
            copy.wait_send()
        return result

    copies = halo_start(mixed, held_out, send_out, recv_out)
    held_out[1 : nx + 1] = mixed[...]
    middle_sends = share(0, by_channel(outer_rows(1, nx - 1), nx - 2))
    halo_finish(copies)
    row_cells = ny_out * nz
    ends = jnp.concatenate(
        [by_channel(outer_rows(0, 1), 1), by_channel(outer_rows(nx - 1, nx), 1)], axis=1
    )
    end_sends = share(1, ends)
    middle = gather(0, middle_sends)
    ends = gather(1, end_sends)
    result = jnp.concatenate([ends[:, 0:row_cells], middle, ends[:, row_cells:]], axis=1)
    out_ref[...] = result.reshape(out_ref.shape).astype(out_ref.dtype)


def whole_kernel(tokens_ref, weight_hbm, gains_ref, kernel_in_hbm, kernel_out_hbm, out_ref, *scratch):
    weight, field, rows_in, send_rows, recv_rows, weight_sem = scratch[:6]
    brick, kernel_in, kernel_out, kernel_sem = scratch[6:10]
    loads = [
        pltpu.make_async_copy(kernel_in_hbm, kernel_in, kernel_sem.at[0]),
        pltpu.make_async_copy(kernel_out_hbm, kernel_out, kernel_sem.at[1]),
    ]
    for load in loads:
        load.start()
    extra = entry_signals()
    held, shifted, mixed = scratch[10:13]
    nx, ny_in, nz, channels = brick.shape
    done = ny_in // 2
    inner_taps, inner_rows = conv_in_rows(brick, kernel_in, gains_ref, held, shifted, mixed)

    def early():
        loads[0].wait()
        edge = jnp.zeros((shifted.shape[0], 1, channels), jnp.float32)
        shifted[:, 0:1] = edge
        shifted[:, nz + 1 : nz + 2] = edge
        held[1 : nx + 1, 0 : done + 2] = brick[:, 0 : done + 2]
        inner_rows(1, nx - 1, inner_taps(1, nx - 1, (0, 1, 2), 0, done), 0, done)

    gather_kernel(
        tokens_ref, weight_hbm, gains_ref, brick, weight, field, rows_in, send_rows, recv_rows, weight_sem, extra,
        {done // 2: early},
    )
    loads[1].wait()
    block_kernel(True, done, brick, kernel_in, gains_ref, kernel_out, out_ref, *scratch[10:])


def decoder_block(tokens, weight, gains, kernel_in, kernel_out, collective):
    count_x = lax.axis_size("inl")
    rows = tokens.shape[0] // count_x
    slots = lax.axis_size("xln") + 2
    nx, ny_in, nz, channels = 2 * PXD, 2 * slots, 2 * GZ, gains.shape[1]
    ny = ny_in - 2
    ny_out = ny - 2
    count = lax.axis_size("section")
    outch = kernel_out.shape[1] // 3
    block = outch // count
    return pl.pallas_call(
        whole_kernel,
        out_shape=jax.ShapeDtypeStruct((block, nx, ny_out * nz), jnp.bfloat16),
        in_specs=[
            pl.BlockSpec(memory_space=pltpu.VMEM),
            pl.BlockSpec(memory_space=pl.ANY),
            pl.BlockSpec(memory_space=pltpu.VMEM),
            pl.BlockSpec(memory_space=pl.ANY),
            pl.BlockSpec(memory_space=pl.ANY),
        ],
        out_specs=pl.BlockSpec(memory_space=pltpu.VMEM),
        scratch_shapes=[
            pltpu.VMEM(weight.shape, weight.dtype),
            pltpu.VMEM((tokens.shape[0], weight.shape[1]), jnp.bfloat16),
            pltpu.VMEM((slots, rows, weight.shape[1]), jnp.bfloat16),
            pltpu.SemaphoreType.DMA((3 * count_x,)),
            pltpu.SemaphoreType.DMA((slots,)),
            pltpu.SemaphoreType.DMA(()),
            pltpu.VMEM((nx, ny_in, nz, channels), jnp.bfloat16),
            pltpu.VMEM(kernel_in.shape, kernel_in.dtype),
            pltpu.VMEM(kernel_out.shape, kernel_out.dtype),
            pltpu.SemaphoreType.DMA((2,)),
            pltpu.VMEM((nx + 2, ny_in, nz, channels), jnp.bfloat16),
            pltpu.VMEM((nx * ny, nz + 2, channels), jnp.float32),
            pltpu.VMEM((nx, ny, nz, channels), jnp.bfloat16),
            pltpu.VMEM((nx + 2, ny, nz, channels), jnp.bfloat16),
            pltpu.VMEM((nx * ny_out, nz + 2, outch), jnp.float32),
            pltpu.VMEM((2, count, block, (nx - 2) * ny_out * nz), jnp.float32),
            pltpu.VMEM((2, count, block, (nx - 2) * ny_out * nz), jnp.float32),
            pltpu.SemaphoreType.DMA((2,)),
            pltpu.SemaphoreType.DMA((2,)),
            pltpu.SemaphoreType.DMA((2,)),
            pltpu.SemaphoreType.DMA((2,)),
            pltpu.SemaphoreType.DMA((2, count)),
            pltpu.SemaphoreType.DMA((2, count)),
        ],
        compiler_params=pltpu.CompilerParams(collective_id=collective, has_side_effects=True),
    )(tokens, weight, gains, kernel_in, kernel_out)


def local(skips, deconv_weight, norm_gain, conv_in, conv_out):
    inl_size = lax.axis_size("inl")
    tokens_here = skips[0]
    weight = deconv_weight[0]
    gains = norm_gain[0]
    channels = gains.shape[1]
    cell_x = 2 * PXD
    cell_y = 2 * lax.axis_size("xln")
    cell_z = 2 * GZ
    assert tokens_here.shape[0] == inl_size * PXD * GZ
    taps, outch, channels_in = conv_out.shape[1:]
    out_weight = conv_out[0].reshape(taps // 3, 3 * outch, channels_in)
    return decoder_block(tokens_here, weight, gains, conv_in[0], out_weight, 3)


def solution(mesh):
    return jax.shard_map(
        local,
        mesh=mesh,
        in_specs=(
            P("section", ("inl", "xln"), None),
            P("section", None, None),
            P("section", None, None),
            P("section", None, None, None),
            P("section", None, None, None),
        ),
        out_specs=P("section", "inl", "xln"),
        check_vma=False,
    )
```

```python
import functools

import jax
import jax.numpy as jnp
from jax import lax
from jax.experimental import pallas as pl
from jax.experimental.pallas import tpu as pltpu
from jax.sharding import PartitionSpec as P

MESH = pl.DeviceIdType.MESH
PXD = 2
GZ = 8


epsilon = 1e-05


def gelu_tanh(values):
    return 0.5 * values * (1.0 + jnp.tanh(0.7978845608028654 * (values + 0.044715 * (values * values * values))))


def send_groups(me_x, me_y, count):
    return [
        (me_x, me_y + 1, None),
        (me_x + 1, 0, (me_y == count - 1) & (me_x + 1 < count)),
        (me_x - 1, count + 1, (me_y == 0) & (me_x > 0)),
    ]


def gather_kernel(
    tokens_ref, weight_hbm, gains_ref, out_ref, weight, field, held, send_sem, recv_sem, weight_sem, extra=0,
    hooks=None,
):
    count = lax.axis_size("inl")
    me_x, me_y = lax.axis_index("inl"), lax.axis_index("xln")
    rows = tokens_ref.shape[0] // count
    width = gains_ref.shape[1]
    one = jnp.int32(1)
    loading = pltpu.make_async_copy(weight_hbm, weight, weight_sem)
    loading.start()
    groups = send_groups(me_x, me_y, count)
    sources = [(me_y - 1, count - 1, me_y >= 1)]
    sources += [(me_y, other, None) for other in range(count)]
    sources += [(me_y + 1, 0, me_y + 1 < count)]

    def is_me(x, y):
        return (x == me_x) & (y == me_y)

    barrier = pltpu.get_barrier_semaphore()
    expected = jnp.int32(0)
    for column, _, exists in groups:
        live = True if exists is None else exists
        expected = expected + jnp.where(live, count, 0)
        for other in range(count):

            @pl.when(jnp.logical_and(live, jnp.logical_not(is_me(other, column))))
            def _():
                pl.semaphore_signal(barrier, inc=1, device_id={"inl": other, "xln": column}, device_id_type=MESH)

            expected = expected - jnp.where(jnp.logical_and(live, is_me(other, column)), one, 0)
    for source_x, source_y, exists in sources:
        live = True if exists is None else exists
        mine = jnp.logical_and(live, is_me(source_x, source_y))
        expected = expected + jnp.where(jnp.logical_and(live, jnp.logical_not(mine)), one, 0)

        @pl.when(jnp.logical_and(live, jnp.logical_not(mine)))
        def _():
            pl.semaphore_signal(barrier, inc=1, device_id={"inl": source_x, "xln": source_y}, device_id_type=MESH)

    loading.wait()
    upsampled = jnp.dot(tokens_ref[...], weight[...], preferred_element_type=jnp.float32)
    for group in range(upsampled.shape[1] // width):
        part = upsampled[:, group * width : (group + 1) * width]
        mean_square = jnp.mean(part * part, axis=-1, keepdims=True)
        normed = part * lax.rsqrt(mean_square + epsilon) * gains_ref[0:1, :]
        field[:, group * width : (group + 1) * width] = gelu_tanh(normed).astype(field.dtype)
    depth = 2 * (rows // 2)
    target = lax.broadcasted_iota(jnp.int32, (2 * rows, 2 * rows), 0)
    origin = lax.broadcasted_iota(jnp.int32, (2 * rows, 2 * rows), 1)
    half = rows // 2
    same = (
        (target // depth == (origin % rows) // half)
        & ((target % depth) // 2 == origin % half)
        & (target % 2 == origin // rows)
    )
    interleave = jnp.where(same, 1.0, 0.0).astype(jnp.bfloat16)

    def place(slot, block):
        for u in range(2):
            for v in range(2):
                first = ((u * 2 + v) * 2) * width
                pair = jnp.concatenate([block[:, first : first + width], block[:, first + width : first + 2 * width]], axis=0)
                cells = jnp.dot(interleave, pair, preferred_element_type=jnp.float32).astype(out_ref.dtype)
                for ix in range(2):
                    out_ref[2 * ix + u, 2 * slot + v] = cells[ix * depth : (ix + 1) * depth]

    pl.semaphore_wait(barrier, expected + extra)
    copies = []
    for index, (column, slot, exists) in enumerate(groups):
        live = True if exists is None else exists
        for turn in range(count):
            other = lax.rem(me_y + turn, count)
            copy = pltpu.make_async_remote_copy(
                src_ref=field.at[pl.ds(pl.multiple_of(other * rows, rows), rows)],
                dst_ref=held.at[slot],
                send_sem=send_sem.at[index * count + turn],
                recv_sem=recv_sem.at[slot],
                device_id={"inl": other, "xln": column},
                device_id_type=MESH,
            )
            remote = jnp.logical_and(live, jnp.logical_not(is_me(other, column)))

            @pl.when(remote)
            def _():
                copy.start()

            copies.append((copy, remote))
    for slot, (source_x, source_y, exists) in enumerate(sources):
        live = True if exists is None else exists
        mine = jnp.logical_and(live, is_me(source_x, source_y))
        remote = jnp.logical_and(live, jnp.logical_not(mine))
        incoming = pltpu.make_async_remote_copy(
            src_ref=field.at[pl.ds(0, rows)],
            dst_ref=held.at[slot],
            send_sem=send_sem.at[0],
            recv_sem=recv_sem.at[slot],
            device_id={"inl": source_x, "xln": source_y},
            device_id_type=MESH,
        )

        @pl.when(remote)
        def _():
            incoming.wait_recv()
            place(slot, held[slot])

        @pl.when(mine)
        def _():
            place(slot, field[pl.ds(pl.multiple_of(me_x * rows, rows), rows)])

        @pl.when(jnp.logical_not(live))
        def _():
            out_ref[:, 2 * slot : 2 * slot + 2] = jnp.zeros(
                (out_ref.shape[0], 2) + out_ref.shape[2:], out_ref.dtype
            )

        if hooks and slot in hooks:
            hooks[slot]()

    for copy, remote in copies:

        @pl.when(remote)
        def _():
            copy.wait_send()


def halo_signal():
    count = lax.axis_size("inl")
    me = lax.axis_index("inl")
    for step in (-1, 1):

        @pl.when((me + step >= 0) & (me + step < count))
        def _():
            pl.semaphore_signal(
                pltpu.get_barrier_semaphore(), inc=1, device_id={"inl": me + step}, device_id_type=MESH
            )

    return (me > 0).astype(jnp.int32) + (me < count - 1).astype(jnp.int32)


def halo_start(field_ref, held, send_sem, recv_sem):
    nx = field_ref.shape[0]
    count = lax.axis_size("inl")
    me = lax.axis_index("inl")
    copies = []
    for index, step in enumerate((-1, 1)):
        source, target = (0, nx + 1) if step < 0 else (nx - 1, 0)
        copy = pltpu.make_async_remote_copy(
            src_ref=field_ref.at[source : source + 1],
            dst_ref=held.at[target : target + 1],
            send_sem=send_sem.at[index],
            recv_sem=recv_sem.at[index],
            device_id={"inl": me + step},
            device_id_type=MESH,
        )
        sends = (me + step >= 0) & (me + step < count)
        gets = (me - step >= 0) & (me - step < count)

        @pl.when(sends)
        def _():
            copy.start()

        @pl.when(jnp.logical_not(gets))
        def _():
            held[target : target + 1] = jnp.zeros((1,) + held.shape[1:], held.dtype)

        copies.append((copy, sends, gets))
    return copies


def halo_finish(copies):
    for copy, sends, gets in copies:

        @pl.when(gets)
        def _():
            copy.wait_recv()

        @pl.when(sends)
        def _():
            copy.wait_send()


def conv_in_rows(field_ref, kernel_in_ref, gains_ref, held, shifted, mixed):
    nx, ny_in, nz, channels = field_ref.shape
    ny = ny_in - 2
    me_y, count_y = lax.axis_index("xln"), lax.axis_size("xln")

    def inner_taps(first, last, offsets_x, low=0, high=ny):
        cells = (last - first) * (high - low) * nz
        parts_in = []
        for offset_z in range(3):
            part = jnp.zeros((cells, channels), jnp.float32)
            for offset_x in offsets_x:
                for offset_y in range(3):
                    window = held[first + offset_x : last + offset_x, low + offset_y : high + offset_y].reshape(
                        cells, channels
                    )
                    tap = kernel_in_ref[(offset_x * 3 + offset_y) * 3 + offset_z]
                    part = part + jnp.dot(window, tap, preferred_element_type=jnp.float32)
            parts_in.append(part)
        return parts_in

    def inner_rows(first, last, parts_in, low=0, high=ny):
        rows = last - first
        planes = rows * (high - low)
        parts_in = [part.reshape(planes, nz, channels) for part in parts_in]
        shifted[0:planes, 1 : nz + 1] = parts_in[0]
        total = parts_in[1] + shifted[0:planes, 0:nz]
        shifted[0:planes, 1 : nz + 1] = parts_in[2]
        total = total + shifted[0:planes, 2 : nz + 2]
        mean_square = jnp.mean(total * total, axis=-1, keepdims=True)
        normed = total * lax.rsqrt(mean_square + epsilon) * gains_ref[1:2, :]
        base = field_ref[first:last, 1 + low : 1 + high].reshape(planes, nz, channels).astype(jnp.float32)
        activated = gelu_tanh(normed + base).reshape(rows, high - low, nz, channels)
        row = low + lax.broadcasted_iota(jnp.int32, activated.shape, 1)
        outside = ((row == 0) & (me_y == 0)) | ((row == ny - 1) & (me_y == count_y - 1))
        mixed[first:last, low:high] = jnp.where(outside, 0.0, activated).astype(mixed.dtype)

    return inner_taps, inner_rows


def entry_signals():
    count = lax.axis_size("section")
    me = lax.axis_index("section")
    for step in range(1, count):
        pl.semaphore_signal(
            pltpu.get_barrier_semaphore(),
            inc=1,
            device_id={"section": lax.rem(me + step, count)},
            device_id_type=MESH,
        )
    return halo_signal() + count - 1


def block_kernel(
    merged, done, field_ref, kernel_in_ref, gains_ref, kernel_out_ref, out_ref,
    held, shifted, mixed, held_out, shifted_out, parts, inbox,
    send_sem, recv_sem, send_out, recv_out, sum_send, sum_recv,
):
    count = lax.axis_size("section")
    me = lax.axis_index("section")
    barrier = pltpu.get_barrier_semaphore()
    if not merged:
        expected = entry_signals()
    nx, ny_in, nz, channels = field_ref.shape
    ny = ny_in - 2
    ny_out = ny - 2
    outch = kernel_out_ref.shape[1] // 3
    me_y, count_y = lax.axis_index("xln"), lax.axis_size("xln")
    if not done:
        edge = jnp.zeros((nx * ny, 1, channels), jnp.float32)
        shifted[:, 0:1] = edge
        shifted[:, nz + 1 : nz + 2] = edge
        held[1 : nx + 1] = field_ref[...]
    else:
        held[1 : nx + 1, done + 2 :] = field_ref[:, done + 2 :]

    inner_taps, inner_rows = conv_in_rows(field_ref, kernel_in_ref, gains_ref, held, shifted, mixed)

    def outer_rows(first, last):
        cells = (last - first) * ny_out * nz
        by_depth = jnp.zeros((cells, 3 * outch), jnp.float32)
        for offset_x in range(3):
            for offset_y in range(3):
                window = held_out[first + offset_x : last + offset_x, offset_y : offset_y + ny_out].reshape(
                    cells, channels
                )
                by_depth = by_depth + lax.dot_general(
                    window,
                    kernel_out_ref[offset_x * 3 + offset_y],
                    (((1,), (1,)), ((), ())),
                    preferred_element_type=jnp.float32,
                )
        return by_depth

    if merged:
        first_halo = halo_start(field_ref, held, send_sem, recv_sem)
    inner_rows(1, nx - 1, inner_taps(1, nx - 1, (0, 1, 2), done, ny), done, ny)
    low = inner_taps(0, 1, (1, 2))
    high = inner_taps(nx - 1, nx, (0, 1))
    if not merged:
        pl.semaphore_wait(barrier, expected)
        first_halo = halo_start(field_ref, held, send_sem, recv_sem)
    halo_finish(first_halo)
    inner_rows(0, 1, [a + b for a, b in zip(low, inner_taps(0, 1, (0,)))])
    inner_rows(nx - 1, nx, [a + b for a, b in zip(high, inner_taps(nx - 1, nx, (2,)))])

    edge = jnp.zeros((nx * ny_out, 1, outch), jnp.float32)
    shifted_out[:, 0:1] = edge
    shifted_out[:, nz + 1 : nz + 2] = edge

    def by_channel(by_depth, rows):
        planes = rows * ny_out
        shifted_out[0:planes, 1 : nz + 1] = by_depth[:, 0:outch].reshape(planes, nz, outch)
        summed = by_depth[:, outch : 2 * outch].reshape(planes, nz, outch) + shifted_out[0:planes, 0:nz]
        shifted_out[0:planes, 1 : nz + 1] = by_depth[:, 2 * outch : 3 * outch].reshape(planes, nz, outch)
        summed = summed + shifted_out[0:planes, 2 : nz + 2]
        return summed.reshape(planes * nz, outch).T

    block = outch // count

    def share(phase, values):
        for peer in range(count):
            parts[phase, peer] = values[peer * block : (peer + 1) * block]
        sends = []
        for step in range(1, count):
            peer = lax.rem(me + step, count)
            copy = pltpu.make_async_remote_copy(
                src_ref=parts.at[phase, peer],
                dst_ref=inbox.at[phase, step],
                send_sem=sum_send.at[phase, step],
                recv_sem=sum_recv.at[phase, step],
                device_id={"section": peer},
                device_id_type=MESH,
            )
            copy.start()
            sends.append(copy)
        return sends

    def gather(phase, sends):
        result = parts[phase, me]
        for step in range(1, count):
            sends[step - 1].wait_recv()
            result = result + inbox[phase, step]
        for copy in sends:
            copy.wait_send()
        return result

    copies = halo_start(mixed, held_out, send_out, recv_out)
    held_out[1 : nx + 1] = mixed[...]
    middle_sends = share(0, by_channel(outer_rows(1, nx - 1), nx - 2))
    halo_finish(copies)
    row_cells = ny_out * nz
    ends = jnp.concatenate(
        [by_channel(outer_rows(0, 1), 1), by_channel(outer_rows(nx - 1, nx), 1)], axis=1
    )
    end_sends = share(1, ends)
    middle = gather(0, middle_sends)
    ends = gather(1, end_sends)
    result = jnp.concatenate([ends[:, 0:row_cells], middle, ends[:, row_cells:]], axis=1)
    out_ref[...] = result.reshape(out_ref.shape).astype(out_ref.dtype)


def whole_kernel(tokens_ref, weight_hbm, gains_ref, kernel_in_hbm, kernel_out_hbm, out_ref, *scratch):
    weight, field, rows_in, send_rows, recv_rows, weight_sem = scratch[:6]
    brick, kernel_in, kernel_out, kernel_sem = scratch[6:10]
    loads = [
        pltpu.make_async_copy(kernel_in_hbm, kernel_in, kernel_sem.at[0]),
        pltpu.make_async_copy(kernel_out_hbm, kernel_out, kernel_sem.at[1]),
    ]
    for load in loads:
        load.start()
    extra = entry_signals()
    held, shifted, mixed = scratch[10:13]
    nx, ny_in, nz, channels = brick.shape
    done = ny_in // 2
    inner_taps, inner_rows = conv_in_rows(brick, kernel_in, gains_ref, held, shifted, mixed)

    def early():
        loads[0].wait()
        edge = jnp.zeros((shifted.shape[0], 1, channels), jnp.float32)
        shifted[:, 0:1] = edge
        shifted[:, nz + 1 : nz + 2] = edge
        held[1 : nx + 1, 0 : done + 2] = brick[:, 0 : done + 2]
        inner_rows(1, nx - 1, inner_taps(1, nx - 1, (0, 1, 2), 0, done), 0, done)

    gather_kernel(
        tokens_ref, weight_hbm, gains_ref, brick, weight, field, rows_in, send_rows, recv_rows, weight_sem, extra,
        {done // 2: early},
    )
    loads[1].wait()
    block_kernel(True, done, brick, kernel_in, gains_ref, kernel_out, out_ref, *scratch[10:])


def decoder_block(tokens, weight, gains, kernel_in, kernel_out, collective):
    count_x = lax.axis_size("inl")
    rows = tokens.shape[0] // count_x
    slots = lax.axis_size("xln") + 2
    nx, ny_in, nz, channels = 2 * PXD, 2 * slots, 2 * GZ, gains.shape[1]
    ny = ny_in - 2
    ny_out = ny - 2
    count = lax.axis_size("section")
    outch = kernel_out.shape[1] // 3
    block = outch // count
    return pl.pallas_call(
        whole_kernel,
        out_shape=jax.ShapeDtypeStruct((block, nx, ny_out * nz), jnp.bfloat16),
        in_specs=[
            pl.BlockSpec(memory_space=pltpu.VMEM),
            pl.BlockSpec(memory_space=pl.ANY),
            pl.BlockSpec(memory_space=pltpu.VMEM),
            pl.BlockSpec(memory_space=pl.ANY),
            pl.BlockSpec(memory_space=pl.ANY),
        ],
        out_specs=pl.BlockSpec(memory_space=pltpu.VMEM),
        scratch_shapes=[
            pltpu.VMEM(weight.shape, weight.dtype),
            pltpu.VMEM((tokens.shape[0], weight.shape[1]), jnp.bfloat16),
            pltpu.VMEM((slots, rows, weight.shape[1]), jnp.bfloat16),
            pltpu.SemaphoreType.DMA((3 * count_x,)),
            pltpu.SemaphoreType.DMA((slots,)),
            pltpu.SemaphoreType.DMA(()),
            pltpu.VMEM((nx, ny_in, nz, channels), jnp.bfloat16),
            pltpu.VMEM(kernel_in.shape, kernel_in.dtype),
            pltpu.VMEM(kernel_out.shape, kernel_out.dtype),
            pltpu.SemaphoreType.DMA((2,)),
            pltpu.VMEM((nx + 2, ny_in, nz, channels), jnp.bfloat16),
            pltpu.VMEM((nx * ny, nz + 2, channels), jnp.float32),
            pltpu.VMEM((nx, ny, nz, channels), jnp.bfloat16),
            pltpu.VMEM((nx + 2, ny, nz, channels), jnp.bfloat16),
            pltpu.VMEM((nx * ny_out, nz + 2, outch), jnp.float32),
            pltpu.VMEM((2, count, block, (nx - 2) * ny_out * nz), jnp.float32),
            pltpu.VMEM((2, count, block, (nx - 2) * ny_out * nz), jnp.float32),
            pltpu.SemaphoreType.DMA((2,)),
            pltpu.SemaphoreType.DMA((2,)),
            pltpu.SemaphoreType.DMA((2,)),
            pltpu.SemaphoreType.DMA((2,)),
            pltpu.SemaphoreType.DMA((2, count)),
            pltpu.SemaphoreType.DMA((2, count)),
        ],
        compiler_params=pltpu.CompilerParams(collective_id=collective, has_side_effects=True),
    )(tokens, weight, gains, kernel_in, kernel_out)


def local(skips, deconv_weight, norm_gain, conv_in, conv_out):
    inl_size = lax.axis_size("inl")
    tokens_here = skips[0]
    weight = deconv_weight[0]
    gains = norm_gain[0]
    channels = gains.shape[1]
    cell_x = 2 * PXD
    cell_y = 2 * lax.axis_size("xln")
    cell_z = 2 * GZ
    assert tokens_here.shape[0] == inl_size * PXD * GZ
    taps, outch, channels_in = conv_out.shape[1:]
    out_weight = conv_out[0].reshape(taps // 3, 3 * outch, channels_in)
    return decoder_block(tokens_here, weight, gains, conv_in[0], out_weight, 3)


def solution(mesh):
    return jax.shard_map(
        local,
        mesh=mesh,
        in_specs=(
            P("section", ("inl", "xln"), None),
            P("section", None, None),
            P("section", None, None),
            P("section", None, None, None),
            P("section", None, None, None),
        ),
        out_specs=P("section", "inl", "xln"),
        check_vma=False,
    )
```

```python
import functools

import jax
import jax.numpy as jnp
from jax import lax
from jax.experimental import pallas as pl
from jax.experimental.pallas import tpu as pltpu
from jax.sharding import PartitionSpec as P

MESH = pl.DeviceIdType.MESH
PXD = 2
GZ = 8


epsilon = 1e-05


def gelu_tanh(values):
    return 0.5 * values * (1.0 + jnp.tanh(0.7978845608028654 * (values + 0.044715 * (values * values * values))))


def send_groups(me_x, me_y, count):
    return [
        (me_x, me_y + 1, None),
        (me_x + 1, 0, (me_y == count - 1) & (me_x + 1 < count)),
        (me_x - 1, count + 1, (me_y == 0) & (me_x > 0)),
    ]


def gather_kernel(
    tokens_ref, weight_hbm, gains_ref, out_ref, weight, field, held, send_sem, recv_sem, weight_sem, extra=0,
    hooks=None,
):
    count = lax.axis_size("inl")
    me_x, me_y = lax.axis_index("inl"), lax.axis_index("xln")
    rows = tokens_ref.shape[0] // count
    width = gains_ref.shape[1]
    one = jnp.int32(1)
    loading = pltpu.make_async_copy(weight_hbm, weight, weight_sem)
    loading.start()
    groups = send_groups(me_x, me_y, count)
    sources = [(me_y - 1, count - 1, me_y >= 1)]
    sources += [(me_y, other, None) for other in range(count)]
    sources += [(me_y + 1, 0, me_y + 1 < count)]

    def is_me(x, y):
        return (x == me_x) & (y == me_y)

    barrier = pltpu.get_barrier_semaphore()
    expected = jnp.int32(0)
    for column, _, exists in groups:
        live = True if exists is None else exists
        expected = expected + jnp.where(live, count, 0)
        for other in range(count):

            @pl.when(jnp.logical_and(live, jnp.logical_not(is_me(other, column))))
            def _():
                pl.semaphore_signal(barrier, inc=1, device_id={"inl": other, "xln": column}, device_id_type=MESH)

            expected = expected - jnp.where(jnp.logical_and(live, is_me(other, column)), one, 0)
    for source_x, source_y, exists in sources:
        live = True if exists is None else exists
        mine = jnp.logical_and(live, is_me(source_x, source_y))
        expected = expected + jnp.where(jnp.logical_and(live, jnp.logical_not(mine)), one, 0)

        @pl.when(jnp.logical_and(live, jnp.logical_not(mine)))
        def _():
            pl.semaphore_signal(barrier, inc=1, device_id={"inl": source_x, "xln": source_y}, device_id_type=MESH)

    loading.wait()
    upsampled = jnp.dot(tokens_ref[...], weight[...], preferred_element_type=jnp.float32)
    for group in range(upsampled.shape[1] // width):
        part = upsampled[:, group * width : (group + 1) * width]
        mean_square = jnp.mean(part * part, axis=-1, keepdims=True)
        normed = part * lax.rsqrt(mean_square + epsilon) * gains_ref[0:1, :]
        field[:, group * width : (group + 1) * width] = gelu_tanh(normed).astype(field.dtype)
    depth = 2 * (rows // 2)
    target = lax.broadcasted_iota(jnp.int32, (2 * rows, 2 * rows), 0)
    origin = lax.broadcasted_iota(jnp.int32, (2 * rows, 2 * rows), 1)
    half = rows // 2
    same = (
        (target // depth == (origin % rows) // half)
        & ((target % depth) // 2 == origin % half)
        & (target % 2 == origin // rows)
    )
    interleave = jnp.where(same, 1.0, 0.0).astype(jnp.bfloat16)

    def place(slot, block):
        for u in range(2):
            for v in range(2):
                first = ((u * 2 + v) * 2) * width
                pair = jnp.concatenate([block[:, first : first + width], block[:, first + width : first + 2 * width]], axis=0)
                cells = jnp.dot(interleave, pair, preferred_element_type=jnp.float32).astype(out_ref.dtype)
                for ix in range(2):
                    out_ref[2 * ix + u, 2 * slot + v] = cells[ix * depth : (ix + 1) * depth]

    pl.semaphore_wait(barrier, expected + extra)
    copies = []
    for index, (column, slot, exists) in enumerate(groups):
        live = True if exists is None else exists
        for turn in range(count):
            other = lax.rem(me_y + turn, count)
            copy = pltpu.make_async_remote_copy(
                src_ref=field.at[pl.ds(pl.multiple_of(other * rows, rows), rows)],
                dst_ref=held.at[slot],
                send_sem=send_sem.at[index * count + turn],
                recv_sem=recv_sem.at[slot],
                device_id={"inl": other, "xln": column},
                device_id_type=MESH,
            )
            remote = jnp.logical_and(live, jnp.logical_not(is_me(other, column)))

            @pl.when(remote)
            def _():
                copy.start()

            copies.append((copy, remote))
    for slot, (source_x, source_y, exists) in enumerate(sources):
        live = True if exists is None else exists
        mine = jnp.logical_and(live, is_me(source_x, source_y))
        remote = jnp.logical_and(live, jnp.logical_not(mine))
        incoming = pltpu.make_async_remote_copy(
            src_ref=field.at[pl.ds(0, rows)],
            dst_ref=held.at[slot],
            send_sem=send_sem.at[0],
            recv_sem=recv_sem.at[slot],
            device_id={"inl": source_x, "xln": source_y},
            device_id_type=MESH,
        )

        @pl.when(remote)
        def _():
            incoming.wait_recv()
            place(slot, held[slot])

        @pl.when(mine)
        def _():
            place(slot, field[pl.ds(pl.multiple_of(me_x * rows, rows), rows)])

        @pl.when(jnp.logical_not(live))
        def _():
            out_ref[:, 2 * slot : 2 * slot + 2] = jnp.zeros(
                (out_ref.shape[0], 2) + out_ref.shape[2:], out_ref.dtype
            )

        if hooks and "each" in hooks:
            hooks["each"](slot)
        if hooks and slot in hooks:
            hooks[slot]()

    for copy, remote in copies:

        @pl.when(remote)
        def _():
            copy.wait_send()


def halo_signal():
    count = lax.axis_size("inl")
    me = lax.axis_index("inl")
    for step in (-1, 1):

        @pl.when((me + step >= 0) & (me + step < count))
        def _():
            pl.semaphore_signal(
                pltpu.get_barrier_semaphore(), inc=1, device_id={"inl": me + step}, device_id_type=MESH
            )

    return (me > 0).astype(jnp.int32) + (me < count - 1).astype(jnp.int32)


def halo_start(field_ref, held, send_sem, recv_sem, start=True):
    nx = field_ref.shape[0]
    count = lax.axis_size("inl")
    me = lax.axis_index("inl")
    copies = []
    for index, step in enumerate((-1, 1)):
        source, target = (0, nx + 1) if step < 0 else (nx - 1, 0)
        copy = pltpu.make_async_remote_copy(
            src_ref=field_ref.at[source : source + 1],
            dst_ref=held.at[target : target + 1],
            send_sem=send_sem.at[index],
            recv_sem=recv_sem.at[index],
            device_id={"inl": me + step},
            device_id_type=MESH,
        )
        sends = (me + step >= 0) & (me + step < count)
        gets = (me - step >= 0) & (me - step < count)

        if start:

            @pl.when(sends)
            def _():
                copy.start()

        @pl.when(jnp.logical_not(gets))
        def _():
            held[target : target + 1] = jnp.zeros((1,) + held.shape[1:], held.dtype)

        copies.append((copy, sends, gets))
    return copies


def halo_finish(copies):
    for copy, sends, gets in copies:

        @pl.when(gets)
        def _():
            copy.wait_recv()

        @pl.when(sends)
        def _():
            copy.wait_send()


def conv_in_rows(field_ref, kernel_in_ref, gains_ref, held, shifted, mixed):
    nx, ny_in, nz, channels = field_ref.shape
    ny = ny_in - 2
    me_y, count_y = lax.axis_index("xln"), lax.axis_size("xln")

    def inner_taps(first, last, offsets_x, low=0, high=ny):
        cells = (last - first) * (high - low) * nz
        parts_in = []
        for offset_z in range(3):
            part = jnp.zeros((cells, channels), jnp.float32)
            for offset_x in offsets_x:
                for offset_y in range(3):
                    window = held[first + offset_x : last + offset_x, low + offset_y : high + offset_y].reshape(
                        cells, channels
                    )
                    tap = kernel_in_ref[(offset_x * 3 + offset_y) * 3 + offset_z]
                    part = part + jnp.dot(window, tap, preferred_element_type=jnp.float32)
            parts_in.append(part)
        return parts_in

    def inner_rows(first, last, parts_in, low=0, high=ny):
        rows = last - first
        planes = rows * (high - low)
        parts_in = [part.reshape(planes, nz, channels) for part in parts_in]
        shifted[0:planes, 1 : nz + 1] = parts_in[0]
        total = parts_in[1] + shifted[0:planes, 0:nz]
        shifted[0:planes, 1 : nz + 1] = parts_in[2]
        total = total + shifted[0:planes, 2 : nz + 2]
        mean_square = jnp.mean(total * total, axis=-1, keepdims=True)
        normed = total * lax.rsqrt(mean_square + epsilon) * gains_ref[1:2, :]
        base = field_ref[first:last, 1 + low : 1 + high].reshape(planes, nz, channels).astype(jnp.float32)
        activated = gelu_tanh(normed + base).reshape(rows, high - low, nz, channels)
        row = low + lax.broadcasted_iota(jnp.int32, activated.shape, 1)
        outside = ((row == 0) & (me_y == 0)) | ((row == ny - 1) & (me_y == count_y - 1))
        mixed[first:last, low:high] = jnp.where(outside, 0.0, activated).astype(mixed.dtype)

    return inner_taps, inner_rows


def entry_signals():
    count = lax.axis_size("section")
    me = lax.axis_index("section")
    for step in range(1, count):
        pl.semaphore_signal(
            pltpu.get_barrier_semaphore(),
            inc=1,
            device_id={"section": lax.rem(me + step, count)},
            device_id_type=MESH,
        )
    return halo_signal() + count - 1


def block_kernel(
    merged, done, field_ref, kernel_in_ref, gains_ref, kernel_out_ref, out_ref,
    held, shifted, mixed, held_out, shifted_out, parts, inbox,
    send_sem, recv_sem, send_out, recv_out, sum_send, sum_recv,
):
    count = lax.axis_size("section")
    me = lax.axis_index("section")
    barrier = pltpu.get_barrier_semaphore()
    if not merged:
        expected = entry_signals()
    nx, ny_in, nz, channels = field_ref.shape
    ny = ny_in - 2
    ny_out = ny - 2
    outch = kernel_out_ref.shape[1] // 3
    me_y, count_y = lax.axis_index("xln"), lax.axis_size("xln")
    if not done:
        edge = jnp.zeros((nx * ny, 1, channels), jnp.float32)
        shifted[:, 0:1] = edge
        shifted[:, nz + 1 : nz + 2] = edge
        held[1 : nx + 1] = field_ref[...]
    else:
        held[1 : nx + 1, done + 2 :] = field_ref[:, done + 2 :]

    inner_taps, inner_rows = conv_in_rows(field_ref, kernel_in_ref, gains_ref, held, shifted, mixed)

    def outer_rows(first, last):
        cells = (last - first) * ny_out * nz
        by_depth = jnp.zeros((cells, 3 * outch), jnp.float32)
        for offset_x in range(3):
            for offset_y in range(3):
                window = held_out[first + offset_x : last + offset_x, offset_y : offset_y + ny_out].reshape(
                    cells, channels
                )
                by_depth = by_depth + lax.dot_general(
                    window,
                    kernel_out_ref[offset_x * 3 + offset_y],
                    (((1,), (1,)), ((), ())),
                    preferred_element_type=jnp.float32,
                )
        return by_depth

    if merged:
        first_halo = halo_start(field_ref, held, send_sem, recv_sem, start=False)
    inner_rows(1, nx - 1, inner_taps(1, nx - 1, (0, 1, 2), done, ny), done, ny)
    low = inner_taps(0, 1, (1, 2))
    high = inner_taps(nx - 1, nx, (0, 1))
    if not merged:
        pl.semaphore_wait(barrier, expected)
        first_halo = halo_start(field_ref, held, send_sem, recv_sem)
    halo_finish(first_halo)
    inner_rows(0, 1, [a + b for a, b in zip(low, inner_taps(0, 1, (0,)))])
    inner_rows(nx - 1, nx, [a + b for a, b in zip(high, inner_taps(nx - 1, nx, (2,)))])

    edge = jnp.zeros((nx * ny_out, 1, outch), jnp.float32)
    shifted_out[:, 0:1] = edge
    shifted_out[:, nz + 1 : nz + 2] = edge

    def by_channel(by_depth, rows):
        planes = rows * ny_out
        shifted_out[0:planes, 1 : nz + 1] = by_depth[:, 0:outch].reshape(planes, nz, outch)
        summed = by_depth[:, outch : 2 * outch].reshape(planes, nz, outch) + shifted_out[0:planes, 0:nz]
        shifted_out[0:planes, 1 : nz + 1] = by_depth[:, 2 * outch : 3 * outch].reshape(planes, nz, outch)
        summed = summed + shifted_out[0:planes, 2 : nz + 2]
        return summed.reshape(planes * nz, outch).T

    block = outch // count

    def share(phase, values):
        for peer in range(count):
            parts[phase, peer] = values[peer * block : (peer + 1) * block]
        sends = []
        for step in range(1, count):
            peer = lax.rem(me + step, count)
            copy = pltpu.make_async_remote_copy(
                src_ref=parts.at[phase, peer],
                dst_ref=inbox.at[phase, step],
                send_sem=sum_send.at[phase, step],
                recv_sem=sum_recv.at[phase, step],
                device_id={"section": peer},
                device_id_type=MESH,
            )
            copy.start()
            sends.append(copy)
        return sends

    def gather(phase, sends):
        result = parts[phase, me]
        for step in range(1, count):
            sends[step - 1].wait_recv()
            result = result + inbox[phase, step]
        for copy in sends:
            copy.wait_send()
        return result

    copies = halo_start(mixed, held_out, send_out, recv_out)
    held_out[1 : nx + 1] = mixed[...]
    middle_sends = share(0, by_channel(outer_rows(1, nx - 1), nx - 2))
    halo_finish(copies)
    row_cells = ny_out * nz
    ends = jnp.concatenate(
        [by_channel(outer_rows(0, 1), 1), by_channel(outer_rows(nx - 1, nx), 1)], axis=1
    )
    end_sends = share(1, ends)
    middle = gather(0, middle_sends)
    ends = gather(1, end_sends)
    result = jnp.concatenate([ends[:, 0:row_cells], middle, ends[:, row_cells:]], axis=1)
    out_ref[...] = result.reshape(out_ref.shape).astype(out_ref.dtype)


def whole_kernel(tokens_ref, weight_hbm, gains_ref, kernel_in_hbm, kernel_out_hbm, out_ref, *scratch):
    weight, field, rows_in, send_rows, recv_rows, weight_sem = scratch[:6]
    brick, kernel_in, kernel_out, kernel_sem = scratch[6:10]
    loads = [
        pltpu.make_async_copy(kernel_in_hbm, kernel_in, kernel_sem.at[0]),
        pltpu.make_async_copy(kernel_out_hbm, kernel_out, kernel_sem.at[1]),
    ]
    for load in loads:
        load.start()
    extra = entry_signals()
    held, shifted, mixed = scratch[10:13]
    nx, ny_in, nz, channels = brick.shape
    done = ny_in // 2
    inner_taps, inner_rows = conv_in_rows(brick, kernel_in, gains_ref, held, shifted, mixed)

    def early():
        loads[0].wait()
        edge = jnp.zeros((shifted.shape[0], 1, channels), jnp.float32)
        shifted[:, 0:1] = edge
        shifted[:, nz + 1 : nz + 2] = edge
        held[1 : nx + 1, 0 : done + 2] = brick[:, 0 : done + 2]
        inner_rows(1, nx - 1, inner_taps(1, nx - 1, (0, 1, 2), 0, done), 0, done)

    send_halo, recv_halo = scratch[17], scratch[18]
    count_x = lax.axis_size("inl")
    me_x = lax.axis_index("inl")

    def edge_rows(slot):
        for index, step in enumerate((-1, 1)):
            source, target = (0, nx + 1) if step < 0 else (nx - 1, 0)
            rows = pl.ds(2 * slot, 2)
            copy = pltpu.make_async_remote_copy(
                src_ref=brick.at[source : source + 1, rows],
                dst_ref=held.at[target : target + 1, rows],
                send_sem=send_halo.at[index],
                recv_sem=recv_halo.at[index],
                device_id={"inl": me_x + step},
                device_id_type=MESH,
            )

            @pl.when((me_x + step >= 0) & (me_x + step < count_x))
            def _():
                copy.start()

    gather_kernel(
        tokens_ref, weight_hbm, gains_ref, brick, weight, field, rows_in, send_rows, recv_rows, weight_sem, extra,
        {done // 2: early, "each": edge_rows},
    )
    loads[1].wait()
    block_kernel(True, done, brick, kernel_in, gains_ref, kernel_out, out_ref, *scratch[10:])


def decoder_block(tokens, weight, gains, kernel_in, kernel_out, collective):
    count_x = lax.axis_size("inl")
    rows = tokens.shape[0] // count_x
    slots = lax.axis_size("xln") + 2
    nx, ny_in, nz, channels = 2 * PXD, 2 * slots, 2 * GZ, gains.shape[1]
    ny = ny_in - 2
    ny_out = ny - 2
    count = lax.axis_size("section")
    outch = kernel_out.shape[1] // 3
    block = outch // count
    return pl.pallas_call(
        whole_kernel,
        out_shape=jax.ShapeDtypeStruct((block, nx, ny_out * nz), jnp.bfloat16),
        in_specs=[
            pl.BlockSpec(memory_space=pltpu.VMEM),
            pl.BlockSpec(memory_space=pl.ANY),
            pl.BlockSpec(memory_space=pltpu.VMEM),
            pl.BlockSpec(memory_space=pl.ANY),
            pl.BlockSpec(memory_space=pl.ANY),
        ],
        out_specs=pl.BlockSpec(memory_space=pltpu.VMEM),
        scratch_shapes=[
            pltpu.VMEM(weight.shape, weight.dtype),
            pltpu.VMEM((tokens.shape[0], weight.shape[1]), jnp.bfloat16),
            pltpu.VMEM((slots, rows, weight.shape[1]), jnp.bfloat16),
            pltpu.SemaphoreType.DMA((3 * count_x,)),
            pltpu.SemaphoreType.DMA((slots,)),
            pltpu.SemaphoreType.DMA(()),
            pltpu.VMEM((nx, ny_in, nz, channels), jnp.bfloat16),
            pltpu.VMEM(kernel_in.shape, kernel_in.dtype),
            pltpu.VMEM(kernel_out.shape, kernel_out.dtype),
            pltpu.SemaphoreType.DMA((2,)),
            pltpu.VMEM((nx + 2, ny_in, nz, channels), jnp.bfloat16),
            pltpu.VMEM((nx * ny, nz + 2, channels), jnp.float32),
            pltpu.VMEM((nx, ny, nz, channels), jnp.bfloat16),
            pltpu.VMEM((nx + 2, ny, nz, channels), jnp.bfloat16),
            pltpu.VMEM((nx * ny_out, nz + 2, outch), jnp.float32),
            pltpu.VMEM((2, count, block, (nx - 2) * ny_out * nz), jnp.float32),
            pltpu.VMEM((2, count, block, (nx - 2) * ny_out * nz), jnp.float32),
            pltpu.SemaphoreType.DMA((2,)),
            pltpu.SemaphoreType.DMA((2,)),
            pltpu.SemaphoreType.DMA((2,)),
            pltpu.SemaphoreType.DMA((2,)),
            pltpu.SemaphoreType.DMA((2, count)),
            pltpu.SemaphoreType.DMA((2, count)),
        ],
        compiler_params=pltpu.CompilerParams(collective_id=collective, has_side_effects=True),
    )(tokens, weight, gains, kernel_in, kernel_out)


def local(skips, deconv_weight, norm_gain, conv_in, conv_out):
    inl_size = lax.axis_size("inl")
    tokens_here = skips[0]
    weight = deconv_weight[0]
    gains = norm_gain[0]
    channels = gains.shape[1]
    cell_x = 2 * PXD
    cell_y = 2 * lax.axis_size("xln")
    cell_z = 2 * GZ
    assert tokens_here.shape[0] == inl_size * PXD * GZ
    taps, outch, channels_in = conv_out.shape[1:]
    out_weight = conv_out[0].reshape(taps // 3, 3 * outch, channels_in)
    return decoder_block(tokens_here, weight, gains, conv_in[0], out_weight, 3)


def solution(mesh):
    return jax.shard_map(
        local,
        mesh=mesh,
        in_specs=(
            P("section", ("inl", "xln"), None),
            P("section", None, None),
            P("section", None, None),
            P("section", None, None, None),
            P("section", None, None, None),
        ),
        out_specs=P("section", "inl", "xln"),
        check_vma=False,
    )
```

```python
import functools

import jax
import jax.numpy as jnp
from jax import lax
from jax.experimental import pallas as pl
from jax.experimental.pallas import tpu as pltpu
from jax.sharding import PartitionSpec as P

MESH = pl.DeviceIdType.MESH
PXD = 2
GZ = 8


epsilon = 1e-05


def gelu_tanh(values):
    return 0.5 * values * (1.0 + jnp.tanh(0.7978845608028654 * (values + 0.044715 * (values * values * values))))


def send_groups(me_x, me_y, count):
    return [
        (me_x, me_y + 1, None),
        (me_x + 1, 0, (me_y == count - 1) & (me_x + 1 < count)),
        (me_x - 1, count + 1, (me_y == 0) & (me_x > 0)),
    ]


def gather_kernel(
    tokens_ref, weight_hbm, gains_ref, out_ref, weight, field, held, send_sem, recv_sem, weight_sem, extra=0,
    hooks=None,
):
    count = lax.axis_size("inl")
    me_x, me_y = lax.axis_index("inl"), lax.axis_index("xln")
    rows = tokens_ref.shape[0] // count
    width = gains_ref.shape[1]
    one = jnp.int32(1)
    loading = pltpu.make_async_copy(weight_hbm, weight, weight_sem)
    loading.start()
    groups = send_groups(me_x, me_y, count)
    sources = [(me_y - 1, count - 1, me_y >= 1)]
    sources += [(me_y, other, None) for other in range(count)]
    sources += [(me_y + 1, 0, me_y + 1 < count)]

    def is_me(x, y):
        return (x == me_x) & (y == me_y)

    barrier = pltpu.get_barrier_semaphore()
    expected = jnp.int32(0)
    for column, _, exists in groups:
        live = True if exists is None else exists
        expected = expected + jnp.where(live, count, 0)
        for other in range(count):

            @pl.when(jnp.logical_and(live, jnp.logical_not(is_me(other, column))))
            def _():
                pl.semaphore_signal(barrier, inc=1, device_id={"inl": other, "xln": column}, device_id_type=MESH)

            expected = expected - jnp.where(jnp.logical_and(live, is_me(other, column)), one, 0)
    for source_x, source_y, exists in sources:
        live = True if exists is None else exists
        mine = jnp.logical_and(live, is_me(source_x, source_y))
        expected = expected + jnp.where(jnp.logical_and(live, jnp.logical_not(mine)), one, 0)

        @pl.when(jnp.logical_and(live, jnp.logical_not(mine)))
        def _():
            pl.semaphore_signal(barrier, inc=1, device_id={"inl": source_x, "xln": source_y}, device_id_type=MESH)

    loading.wait()
    upsampled = jnp.dot(tokens_ref[...], weight[...], preferred_element_type=jnp.float32)
    for group in range(upsampled.shape[1] // width):
        part = upsampled[:, group * width : (group + 1) * width]
        mean_square = jnp.mean(part * part, axis=-1, keepdims=True)
        normed = part * lax.rsqrt(mean_square + epsilon) * gains_ref[0:1, :]
        field[:, group * width : (group + 1) * width] = gelu_tanh(normed).astype(field.dtype)
    depth = 2 * (rows // 2)
    target = lax.broadcasted_iota(jnp.int32, (2 * rows, 2 * rows), 0)
    origin = lax.broadcasted_iota(jnp.int32, (2 * rows, 2 * rows), 1)
    half = rows // 2
    same = (
        (target // depth == (origin % rows) // half)
        & ((target % depth) // 2 == origin % half)
        & (target % 2 == origin // rows)
    )
    interleave = jnp.where(same, 1.0, 0.0).astype(jnp.bfloat16)

    def place(slot, block):
        for u in range(2):
            for v in range(2):
                first = ((u * 2 + v) * 2) * width
                pair = jnp.concatenate([block[:, first : first + width], block[:, first + width : first + 2 * width]], axis=0)
                cells = jnp.dot(interleave, pair, preferred_element_type=jnp.float32).astype(out_ref.dtype)
                for ix in range(2):
                    out_ref[2 * ix + u, 2 * slot + v] = cells[ix * depth : (ix + 1) * depth]

    pl.semaphore_wait(barrier, expected + extra)
    copies = []
    for index, (column, slot, exists) in enumerate(groups):
        live = True if exists is None else exists
        for turn in range(count):
            other = lax.rem(me_y + turn, count)
            copy = pltpu.make_async_remote_copy(
                src_ref=field.at[pl.ds(pl.multiple_of(other * rows, rows), rows)],
                dst_ref=held.at[slot],
                send_sem=send_sem.at[index * count + turn],
                recv_sem=recv_sem.at[slot],
                device_id={"inl": other, "xln": column},
                device_id_type=MESH,
            )
            remote = jnp.logical_and(live, jnp.logical_not(is_me(other, column)))

            @pl.when(remote)
            def _():
                copy.start()

            copies.append((copy, remote))
    for slot, (source_x, source_y, exists) in enumerate(sources):
        live = True if exists is None else exists
        mine = jnp.logical_and(live, is_me(source_x, source_y))
        remote = jnp.logical_and(live, jnp.logical_not(mine))
        incoming = pltpu.make_async_remote_copy(
            src_ref=field.at[pl.ds(0, rows)],
            dst_ref=held.at[slot],
            send_sem=send_sem.at[0],
            recv_sem=recv_sem.at[slot],
            device_id={"inl": source_x, "xln": source_y},
            device_id_type=MESH,
        )

        @pl.when(remote)
        def _():
            incoming.wait_recv()
            place(slot, held[slot])

        @pl.when(mine)
        def _():
            place(slot, field[pl.ds(pl.multiple_of(me_x * rows, rows), rows)])

        @pl.when(jnp.logical_not(live))
        def _():
            out_ref[:, 2 * slot : 2 * slot + 2] = jnp.zeros(
                (out_ref.shape[0], 2) + out_ref.shape[2:], out_ref.dtype
            )

        if hooks and "each" in hooks:
            hooks["each"](slot)
        if hooks and slot in hooks:
            hooks[slot]()

    for copy, remote in copies:

        @pl.when(remote)
        def _():
            copy.wait_send()


def halo_signal():
    count = lax.axis_size("inl")
    me = lax.axis_index("inl")
    for step in (-1, 1):

        @pl.when((me + step >= 0) & (me + step < count))
        def _():
            pl.semaphore_signal(
                pltpu.get_barrier_semaphore(), inc=1, device_id={"inl": me + step}, device_id_type=MESH
            )

    return (me > 0).astype(jnp.int32) + (me < count - 1).astype(jnp.int32)


def halo_start(field_ref, held, send_sem, recv_sem, start=True, steps=(-1, 1)):
    nx = field_ref.shape[0]
    count = lax.axis_size("inl")
    me = lax.axis_index("inl")
    copies = []
    for step in steps:
        index = 0 if step < 0 else 1
        source, target = (0, nx + 1) if step < 0 else (nx - 1, 0)
        copy = pltpu.make_async_remote_copy(
            src_ref=field_ref.at[source : source + 1],
            dst_ref=held.at[target : target + 1],
            send_sem=send_sem.at[index],
            recv_sem=recv_sem.at[index],
            device_id={"inl": me + step},
            device_id_type=MESH,
        )
        sends = (me + step >= 0) & (me + step < count)
        gets = (me - step >= 0) & (me - step < count)

        if start:

            @pl.when(sends)
            def _():
                copy.start()

        @pl.when(jnp.logical_not(gets))
        def _():
            held[target : target + 1] = jnp.zeros((1,) + held.shape[1:], held.dtype)

        copies.append((copy, sends, gets))
    return copies


def halo_finish(copies):
    for copy, sends, gets in copies:

        @pl.when(gets)
        def _():
            copy.wait_recv()

        @pl.when(sends)
        def _():
            copy.wait_send()


def conv_in_rows(field_ref, kernel_in_ref, gains_ref, held, shifted, mixed):
    nx, ny_in, nz, channels = field_ref.shape
    ny = ny_in - 2
    me_y, count_y = lax.axis_index("xln"), lax.axis_size("xln")

    def inner_taps(first, last, offsets_x, low=0, high=ny):
        cells = (last - first) * (high - low) * nz
        parts_in = []
        for offset_z in range(3):
            part = jnp.zeros((cells, channels), jnp.float32)
            for offset_x in offsets_x:
                for offset_y in range(3):
                    window = held[first + offset_x : last + offset_x, low + offset_y : high + offset_y].reshape(
                        cells, channels
                    )
                    tap = kernel_in_ref[(offset_x * 3 + offset_y) * 3 + offset_z]
                    part = part + jnp.dot(window, tap, preferred_element_type=jnp.float32)
            parts_in.append(part)
        return parts_in

    def inner_rows(first, last, parts_in, low=0, high=ny):
        rows = last - first
        planes = rows * (high - low)
        parts_in = [part.reshape(planes, nz, channels) for part in parts_in]
        shifted[0:planes, 1 : nz + 1] = parts_in[0]
        total = parts_in[1] + shifted[0:planes, 0:nz]
        shifted[0:planes, 1 : nz + 1] = parts_in[2]
        total = total + shifted[0:planes, 2 : nz + 2]
        mean_square = jnp.mean(total * total, axis=-1, keepdims=True)
        normed = total * lax.rsqrt(mean_square + epsilon) * gains_ref[1:2, :]
        base = field_ref[first:last, 1 + low : 1 + high].reshape(planes, nz, channels).astype(jnp.float32)
        activated = gelu_tanh(normed + base).reshape(rows, high - low, nz, channels)
        row = low + lax.broadcasted_iota(jnp.int32, activated.shape, 1)
        outside = ((row == 0) & (me_y == 0)) | ((row == ny - 1) & (me_y == count_y - 1))
        mixed[first:last, low:high] = jnp.where(outside, 0.0, activated).astype(mixed.dtype)

    return inner_taps, inner_rows


def entry_signals():
    count = lax.axis_size("section")
    me = lax.axis_index("section")
    for step in range(1, count):
        pl.semaphore_signal(
            pltpu.get_barrier_semaphore(),
            inc=1,
            device_id={"section": lax.rem(me + step, count)},
            device_id_type=MESH,
        )
    return halo_signal() + count - 1


def block_kernel(
    merged, done, field_ref, kernel_in_ref, gains_ref, kernel_out_ref, out_ref,
    held, shifted, mixed, held_out, shifted_out, parts, inbox,
    send_sem, recv_sem, send_out, recv_out, sum_send, sum_recv,
):
    count = lax.axis_size("section")
    me = lax.axis_index("section")
    barrier = pltpu.get_barrier_semaphore()
    if not merged:
        expected = entry_signals()
    nx, ny_in, nz, channels = field_ref.shape
    ny = ny_in - 2
    ny_out = ny - 2
    outch = kernel_out_ref.shape[1] // 3
    me_y, count_y = lax.axis_index("xln"), lax.axis_size("xln")
    if not done:
        edge = jnp.zeros((nx * ny, 1, channels), jnp.float32)
        shifted[:, 0:1] = edge
        shifted[:, nz + 1 : nz + 2] = edge
        held[1 : nx + 1] = field_ref[...]
    else:
        held[1 : nx + 1, done + 2 :] = field_ref[:, done + 2 :]

    inner_taps, inner_rows = conv_in_rows(field_ref, kernel_in_ref, gains_ref, held, shifted, mixed)

    def outer_rows(first, last, offsets_x=(0, 1, 2)):
        cells = (last - first) * ny_out * nz
        by_depth = jnp.zeros((cells, 3 * outch), jnp.float32)
        for offset_x in offsets_x:
            for offset_y in range(3):
                window = held_out[first + offset_x : last + offset_x, offset_y : offset_y + ny_out].reshape(
                    cells, channels
                )
                by_depth = by_depth + lax.dot_general(
                    window,
                    kernel_out_ref[offset_x * 3 + offset_y],
                    (((1,), (1,)), ((), ())),
                    preferred_element_type=jnp.float32,
                )
        return by_depth

    if merged:
        first_halo = halo_start(field_ref, held, send_sem, recv_sem, start=False)
    inner_rows(1, nx - 1, inner_taps(1, nx - 1, (0, 1, 2), done, ny), done, ny)
    low = inner_taps(0, 1, (1, 2))
    high = inner_taps(nx - 1, nx, (0, 1))
    if not merged:
        pl.semaphore_wait(barrier, expected)
        first_halo = halo_start(field_ref, held, send_sem, recv_sem)
    halo_finish(first_halo)
    inner_rows(0, 1, [a + b for a, b in zip(low, inner_taps(0, 1, (0,)))])
    second_halo = halo_start(mixed, held_out, send_out, recv_out, steps=(-1,))
    inner_rows(nx - 1, nx, [a + b for a, b in zip(high, inner_taps(nx - 1, nx, (2,)))])
    second_halo += halo_start(mixed, held_out, send_out, recv_out, steps=(1,))

    edge = jnp.zeros((nx * ny_out, 1, outch), jnp.float32)
    shifted_out[:, 0:1] = edge
    shifted_out[:, nz + 1 : nz + 2] = edge

    def by_channel(by_depth, rows):
        planes = rows * ny_out
        shifted_out[0:planes, 1 : nz + 1] = by_depth[:, 0:outch].reshape(planes, nz, outch)
        summed = by_depth[:, outch : 2 * outch].reshape(planes, nz, outch) + shifted_out[0:planes, 0:nz]
        shifted_out[0:planes, 1 : nz + 1] = by_depth[:, 2 * outch : 3 * outch].reshape(planes, nz, outch)
        summed = summed + shifted_out[0:planes, 2 : nz + 2]
        return summed.reshape(planes * nz, outch).T

    block = outch // count

    def share(phase, values):
        for peer in range(count):
            parts[phase, peer] = values[peer * block : (peer + 1) * block]
        sends = []
        for step in range(1, count):
            peer = lax.rem(me + step, count)
            copy = pltpu.make_async_remote_copy(
                src_ref=parts.at[phase, peer],
                dst_ref=inbox.at[phase, step],
                send_sem=sum_send.at[phase, step],
                recv_sem=sum_recv.at[phase, step],
                device_id={"section": peer},
                device_id_type=MESH,
            )
            copy.start()
            sends.append(copy)
        return sends

    def gather(phase, sends):
        result = parts[phase, me]
        for step in range(1, count):
            sends[step - 1].wait_recv()
            result = result + inbox[phase, step]
        for copy in sends:
            copy.wait_send()
        return result

    held_out[1 : nx + 1] = mixed[...]
    middle_sends = share(0, by_channel(outer_rows(1, nx - 1), nx - 2))
    low_out = outer_rows(0, 1, (1, 2))
    high_out = outer_rows(nx - 1, nx, (0, 1))
    halo_finish(second_halo)
    row_cells = ny_out * nz
    ends = jnp.concatenate(
        [
            by_channel(low_out + outer_rows(0, 1, (0,)), 1),
            by_channel(high_out + outer_rows(nx - 1, nx, (2,)), 1),
        ],
        axis=1,
    )
    end_sends = share(1, ends)
    middle = gather(0, middle_sends)
    ends = gather(1, end_sends)
    result = jnp.concatenate([ends[:, 0:row_cells], middle, ends[:, row_cells:]], axis=1)
    out_ref[...] = result.reshape(out_ref.shape).astype(out_ref.dtype)


def whole_kernel(tokens_ref, weight_hbm, gains_ref, kernel_in_hbm, kernel_out_hbm, out_ref, *scratch):
    weight, field, rows_in, send_rows, recv_rows, weight_sem = scratch[:6]
    brick, kernel_in, kernel_out, kernel_sem = scratch[6:10]
    loads = [
        pltpu.make_async_copy(kernel_in_hbm, kernel_in, kernel_sem.at[0]),
        pltpu.make_async_copy(kernel_out_hbm, kernel_out, kernel_sem.at[1]),
    ]
    for load in loads:
        load.start()
    extra = entry_signals()
    held, shifted, mixed = scratch[10:13]
    nx, ny_in, nz, channels = brick.shape
    done = ny_in // 2
    inner_taps, inner_rows = conv_in_rows(brick, kernel_in, gains_ref, held, shifted, mixed)

    def early():
        loads[0].wait()
        edge = jnp.zeros((shifted.shape[0], 1, channels), jnp.float32)
        shifted[:, 0:1] = edge
        shifted[:, nz + 1 : nz + 2] = edge
        held[1 : nx + 1, 0 : done + 2] = brick[:, 0 : done + 2]
        inner_rows(1, nx - 1, inner_taps(1, nx - 1, (0, 1, 2), 0, done), 0, done)

    send_halo, recv_halo = scratch[17], scratch[18]
    count_x = lax.axis_size("inl")
    me_x = lax.axis_index("inl")

    def edge_rows(slot):
        for index, step in enumerate((-1, 1)):
            source, target = (0, nx + 1) if step < 0 else (nx - 1, 0)
            rows = pl.ds(2 * slot, 2)
            copy = pltpu.make_async_remote_copy(
                src_ref=brick.at[source : source + 1, rows],
                dst_ref=held.at[target : target + 1, rows],
                send_sem=send_halo.at[index],
                recv_sem=recv_halo.at[index],
                device_id={"inl": me_x + step},
                device_id_type=MESH,
            )

            @pl.when((me_x + step >= 0) & (me_x + step < count_x))
            def _():
                copy.start()

    gather_kernel(
        tokens_ref, weight_hbm, gains_ref, brick, weight, field, rows_in, send_rows, recv_rows, weight_sem, extra,
        {done // 2: early, "each": edge_rows},
    )
    loads[1].wait()
    block_kernel(True, done, brick, kernel_in, gains_ref, kernel_out, out_ref, *scratch[10:])


def decoder_block(tokens, weight, gains, kernel_in, kernel_out, collective):
    count_x = lax.axis_size("inl")
    rows = tokens.shape[0] // count_x
    slots = lax.axis_size("xln") + 2
    nx, ny_in, nz, channels = 2 * PXD, 2 * slots, 2 * GZ, gains.shape[1]
    ny = ny_in - 2
    ny_out = ny - 2
    count = lax.axis_size("section")
    outch = kernel_out.shape[1] // 3
    block = outch // count
    return pl.pallas_call(
        whole_kernel,
        out_shape=jax.ShapeDtypeStruct((block, nx, ny_out * nz), jnp.bfloat16),
        in_specs=[
            pl.BlockSpec(memory_space=pltpu.VMEM),
            pl.BlockSpec(memory_space=pl.ANY),
            pl.BlockSpec(memory_space=pltpu.VMEM),
            pl.BlockSpec(memory_space=pl.ANY),
            pl.BlockSpec(memory_space=pl.ANY),
        ],
        out_specs=pl.BlockSpec(memory_space=pltpu.VMEM),
        scratch_shapes=[
            pltpu.VMEM(weight.shape, weight.dtype),
            pltpu.VMEM((tokens.shape[0], weight.shape[1]), jnp.bfloat16),
            pltpu.VMEM((slots, rows, weight.shape[1]), jnp.bfloat16),
            pltpu.SemaphoreType.DMA((3 * count_x,)),
            pltpu.SemaphoreType.DMA((slots,)),
            pltpu.SemaphoreType.DMA(()),
            pltpu.VMEM((nx, ny_in, nz, channels), jnp.bfloat16),
            pltpu.VMEM(kernel_in.shape, kernel_in.dtype),
            pltpu.VMEM(kernel_out.shape, kernel_out.dtype),
            pltpu.SemaphoreType.DMA((2,)),
            pltpu.VMEM((nx + 2, ny_in, nz, channels), jnp.bfloat16),
            pltpu.VMEM((nx * ny, nz + 2, channels), jnp.float32),
            pltpu.VMEM((nx, ny, nz, channels), jnp.bfloat16),
            pltpu.VMEM((nx + 2, ny, nz, channels), jnp.bfloat16),
            pltpu.VMEM((nx * ny_out, nz + 2, outch), jnp.float32),
            pltpu.VMEM((2, count, block, (nx - 2) * ny_out * nz), jnp.float32),
            pltpu.VMEM((2, count, block, (nx - 2) * ny_out * nz), jnp.float32),
            pltpu.SemaphoreType.DMA((2,)),
            pltpu.SemaphoreType.DMA((2,)),
            pltpu.SemaphoreType.DMA((2,)),
            pltpu.SemaphoreType.DMA((2,)),
            pltpu.SemaphoreType.DMA((2, count)),
            pltpu.SemaphoreType.DMA((2, count)),
        ],
        compiler_params=pltpu.CompilerParams(collective_id=collective, has_side_effects=True),
    )(tokens, weight, gains, kernel_in, kernel_out)


def local(skips, deconv_weight, norm_gain, conv_in, conv_out):
    inl_size = lax.axis_size("inl")
    tokens_here = skips[0]
    weight = deconv_weight[0]
    gains = norm_gain[0]
    channels = gains.shape[1]
    cell_x = 2 * PXD
    cell_y = 2 * lax.axis_size("xln")
    cell_z = 2 * GZ
    assert tokens_here.shape[0] == inl_size * PXD * GZ
    taps, outch, channels_in = conv_out.shape[1:]
    out_weight = conv_out[0].reshape(taps // 3, 3 * outch, channels_in)
    return decoder_block(tokens_here, weight, gains, conv_in[0], out_weight, 3)


def solution(mesh):
    return jax.shard_map(
        local,
        mesh=mesh,
        in_specs=(
            P("section", ("inl", "xln"), None),
            P("section", None, None),
            P("section", None, None),
            P("section", None, None, None),
            P("section", None, None, None),
        ),
        out_specs=P("section", "inl", "xln"),
        check_vma=False,
    )
```

```python
import functools

import jax
import jax.numpy as jnp
from jax import lax
from jax.experimental import pallas as pl
from jax.experimental.pallas import tpu as pltpu
from jax.sharding import PartitionSpec as P

MESH = pl.DeviceIdType.MESH
PXD = 2
GZ = 8


epsilon = 1e-05


def gelu_tanh(values):
    return 0.5 * values * (1.0 + jnp.tanh(0.7978845608028654 * (values + 0.044715 * (values * values * values))))


def send_groups(me_x, me_y, count):
    return [
        (me_x, me_y + 1, None),
        (me_x + 1, 0, (me_y == count - 1) & (me_x + 1 < count)),
        (me_x - 1, count + 1, (me_y == 0) & (me_x > 0)),
    ]


def gather_kernel(
    tokens_ref, weight_hbm, gains_ref, out_ref, weight, field, held, send_sem, recv_sem, weight_sem, extra=0,
    hooks=None,
):
    count = lax.axis_size("inl")
    me_x, me_y = lax.axis_index("inl"), lax.axis_index("xln")
    rows = tokens_ref.shape[0] // count
    width = gains_ref.shape[1]
    one = jnp.int32(1)
    loading = pltpu.make_async_copy(weight_hbm, weight, weight_sem)
    loading.start()
    groups = send_groups(me_x, me_y, count)
    sources = [(me_y - 1, count - 1, me_y >= 1)]
    sources += [(me_y, other, None) for other in range(count)]
    sources += [(me_y + 1, 0, me_y + 1 < count)]

    def is_me(x, y):
        return (x == me_x) & (y == me_y)

    barrier = pltpu.get_barrier_semaphore()
    expected = jnp.int32(0)
    for column, _, exists in groups:
        live = True if exists is None else exists
        expected = expected + jnp.where(live, count, 0)
        for other in range(count):

            @pl.when(jnp.logical_and(live, jnp.logical_not(is_me(other, column))))
            def _():
                pl.semaphore_signal(barrier, inc=1, device_id={"inl": other, "xln": column}, device_id_type=MESH)

            expected = expected - jnp.where(jnp.logical_and(live, is_me(other, column)), one, 0)
    for source_x, source_y, exists in sources:
        live = True if exists is None else exists
        mine = jnp.logical_and(live, is_me(source_x, source_y))
        expected = expected + jnp.where(jnp.logical_and(live, jnp.logical_not(mine)), one, 0)

        @pl.when(jnp.logical_and(live, jnp.logical_not(mine)))
        def _():
            pl.semaphore_signal(barrier, inc=1, device_id={"inl": source_x, "xln": source_y}, device_id_type=MESH)

    loading.wait()
    upsampled = jnp.dot(tokens_ref[...], weight[...], preferred_element_type=jnp.float32)
    for group in range(upsampled.shape[1] // width):
        part = upsampled[:, group * width : (group + 1) * width]
        mean_square = jnp.mean(part * part, axis=-1, keepdims=True)
        normed = part * lax.rsqrt(mean_square + epsilon) * gains_ref[0:1, :]
        field[:, group * width : (group + 1) * width] = gelu_tanh(normed).astype(field.dtype)
    depth = 2 * (rows // 2)
    target = lax.broadcasted_iota(jnp.int32, (2 * rows, 2 * rows), 0)
    origin = lax.broadcasted_iota(jnp.int32, (2 * rows, 2 * rows), 1)
    half = rows // 2
    same = (
        (target // depth == (origin % rows) // half)
        & ((target % depth) // 2 == origin % half)
        & (target % 2 == origin // rows)
    )
    interleave = jnp.where(same, 1.0, 0.0).astype(jnp.bfloat16)

    def place(slot, block):
        for u in range(2):
            for v in range(2):
                first = ((u * 2 + v) * 2) * width
                pair = jnp.concatenate([block[:, first : first + width], block[:, first + width : first + 2 * width]], axis=0)
                cells = jnp.dot(interleave, pair, preferred_element_type=jnp.float32).astype(out_ref.dtype)
                for ix in range(2):
                    out_ref[2 * ix + u, 2 * slot + v] = cells[ix * depth : (ix + 1) * depth]

    pl.semaphore_wait(barrier, expected + extra)
    copies = []
    for index, (column, slot, exists) in enumerate(groups):
        live = True if exists is None else exists
        for turn in range(count):
            other = lax.rem(me_y + turn, count)
            copy = pltpu.make_async_remote_copy(
                src_ref=field.at[pl.ds(pl.multiple_of(other * rows, rows), rows)],
                dst_ref=held.at[slot],
                send_sem=send_sem.at[index * count + turn],
                recv_sem=recv_sem.at[slot],
                device_id={"inl": other, "xln": column},
                device_id_type=MESH,
            )
            remote = jnp.logical_and(live, jnp.logical_not(is_me(other, column)))

            @pl.when(remote)
            def _():
                copy.start()

            copies.append((copy, remote))
    for slot, (source_x, source_y, exists) in enumerate(sources):
        live = True if exists is None else exists
        mine = jnp.logical_and(live, is_me(source_x, source_y))
        remote = jnp.logical_and(live, jnp.logical_not(mine))
        incoming = pltpu.make_async_remote_copy(
            src_ref=field.at[pl.ds(0, rows)],
            dst_ref=held.at[slot],
            send_sem=send_sem.at[0],
            recv_sem=recv_sem.at[slot],
            device_id={"inl": source_x, "xln": source_y},
            device_id_type=MESH,
        )

        @pl.when(remote)
        def _():
            incoming.wait_recv()
            place(slot, held[slot])

        @pl.when(mine)
        def _():
            place(slot, field[pl.ds(pl.multiple_of(me_x * rows, rows), rows)])

        @pl.when(jnp.logical_not(live))
        def _():
            out_ref[:, 2 * slot : 2 * slot + 2] = jnp.zeros(
                (out_ref.shape[0], 2) + out_ref.shape[2:], out_ref.dtype
            )

        if hooks and "each" in hooks:
            hooks["each"](slot)
        if hooks and slot in hooks:
            hooks[slot]()

    for copy, remote in copies:

        @pl.when(remote)
        def _():
            copy.wait_send()


def halo_signal():
    count = lax.axis_size("inl")
    me = lax.axis_index("inl")
    for step in (-1, 1):

        @pl.when((me + step >= 0) & (me + step < count))
        def _():
            pl.semaphore_signal(
                pltpu.get_barrier_semaphore(), inc=1, device_id={"inl": me + step}, device_id_type=MESH
            )

    return (me > 0).astype(jnp.int32) + (me < count - 1).astype(jnp.int32)


def halo_start(field_ref, held, send_sem, recv_sem, start=True, steps=(-1, 1)):
    nx = field_ref.shape[0]
    count = lax.axis_size("inl")
    me = lax.axis_index("inl")
    copies = []
    for step in steps:
        index = 0 if step < 0 else 1
        source, target = (0, nx + 1) if step < 0 else (nx - 1, 0)
        copy = pltpu.make_async_remote_copy(
            src_ref=field_ref.at[source : source + 1],
            dst_ref=held.at[target : target + 1],
            send_sem=send_sem.at[index],
            recv_sem=recv_sem.at[index],
            device_id={"inl": me + step},
            device_id_type=MESH,
        )
        sends = (me + step >= 0) & (me + step < count)
        gets = (me - step >= 0) & (me - step < count)

        if start:

            @pl.when(sends)
            def _():
                copy.start()

        @pl.when(jnp.logical_not(gets))
        def _():
            held[target : target + 1] = jnp.zeros((1,) + held.shape[1:], held.dtype)

        copies.append((copy, sends, gets))
    return copies


def halo_finish(copies):
    for copy, sends, gets in copies:

        @pl.when(gets)
        def _():
            copy.wait_recv()

        @pl.when(sends)
        def _():
            copy.wait_send()


def conv_in_rows(field_ref, kernel_in_ref, gains_ref, held, shifted, mixed):
    nx, ny_in, nz, channels = field_ref.shape
    ny = ny_in - 2
    me_y, count_y = lax.axis_index("xln"), lax.axis_size("xln")

    def inner_taps(first, last, offsets_x, low=0, high=ny):
        cells = (last - first) * (high - low) * nz
        parts_in = []
        for offset_z in range(3):
            part = jnp.zeros((cells, channels), jnp.float32)
            for offset_x in offsets_x:
                for offset_y in range(3):
                    window = held[first + offset_x : last + offset_x, low + offset_y : high + offset_y].reshape(
                        cells, channels
                    )
                    tap = kernel_in_ref[(offset_x * 3 + offset_y) * 3 + offset_z]
                    part = part + jnp.dot(window, tap, preferred_element_type=jnp.float32)
            parts_in.append(part)
        return parts_in

    def inner_rows(first, last, parts_in, low=0, high=ny):
        rows = last - first
        planes = rows * (high - low)
        parts_in = [part.reshape(planes, nz, channels) for part in parts_in]
        shifted[0:planes, 1 : nz + 1] = parts_in[0]
        total = parts_in[1] + shifted[0:planes, 0:nz]
        shifted[0:planes, 1 : nz + 1] = parts_in[2]
        total = total + shifted[0:planes, 2 : nz + 2]
        mean_square = jnp.mean(total * total, axis=-1, keepdims=True)
        normed = total * lax.rsqrt(mean_square + epsilon) * gains_ref[1:2, :]
        base = field_ref[first:last, 1 + low : 1 + high].reshape(planes, nz, channels).astype(jnp.float32)
        activated = gelu_tanh(normed + base).reshape(rows, high - low, nz, channels)
        row = low + lax.broadcasted_iota(jnp.int32, activated.shape, 1)
        outside = ((row == 0) & (me_y == 0)) | ((row == ny - 1) & (me_y == count_y - 1))
        mixed[first:last, low:high] = jnp.where(outside, 0.0, activated).astype(mixed.dtype)

    return inner_taps, inner_rows


def entry_signals():
    count = lax.axis_size("section")
    me = lax.axis_index("section")
    for step in range(1, count):
        pl.semaphore_signal(
            pltpu.get_barrier_semaphore(),
            inc=1,
            device_id={"section": lax.rem(me + step, count)},
            device_id_type=MESH,
        )
    return halo_signal() + count - 1


def block_kernel(
    merged, done, field_ref, kernel_in_ref, gains_ref, kernel_out_ref, out_ref,
    held, shifted, mixed, held_out, shifted_out, parts, inbox,
    send_sem, recv_sem, send_out, recv_out, sum_send, sum_recv,
):
    count = lax.axis_size("section")
    me = lax.axis_index("section")
    barrier = pltpu.get_barrier_semaphore()
    if not merged:
        expected = entry_signals()
    nx, ny_in, nz, channels = field_ref.shape
    ny = ny_in - 2
    ny_out = ny - 2
    outch = kernel_out_ref.shape[1] // 3
    me_y, count_y = lax.axis_index("xln"), lax.axis_size("xln")
    if not done:
        edge = jnp.zeros((nx * ny, 1, channels), jnp.float32)
        shifted[:, 0:1] = edge
        shifted[:, nz + 1 : nz + 2] = edge
        held[1 : nx + 1] = field_ref[...]
    else:
        held[1 : nx + 1, done + 2 :] = field_ref[:, done + 2 :]

    inner_taps, inner_rows = conv_in_rows(field_ref, kernel_in_ref, gains_ref, held, shifted, mixed)

    def outer_rows(first, last, offsets_x=(0, 1, 2)):
        cells = (last - first) * ny_out * nz
        by_depth = jnp.zeros((cells, 3 * outch), jnp.float32)
        for offset_x in offsets_x:
            for offset_y in range(3):
                window = held_out[first + offset_x : last + offset_x, offset_y : offset_y + ny_out].reshape(
                    cells, channels
                )
                by_depth = by_depth + lax.dot_general(
                    window,
                    kernel_out_ref[offset_x * 3 + offset_y],
                    (((1,), (1,)), ((), ())),
                    preferred_element_type=jnp.float32,
                )
        return by_depth

    if merged:
        first_halo = halo_start(field_ref, held, send_sem, recv_sem, start=False)
    inner_rows(1, nx - 1, inner_taps(1, nx - 1, (0, 1, 2), done, ny), done, ny)
    low = inner_taps(0, 1, (1, 2))
    high = inner_taps(nx - 1, nx, (0, 1))
    if not merged:
        pl.semaphore_wait(barrier, expected)
        first_halo = halo_start(field_ref, held, send_sem, recv_sem)
    halo_finish(first_halo)
    inner_rows(0, 1, [a + b for a, b in zip(low, inner_taps(0, 1, (0,)))])
    second_halo = halo_start(mixed, held_out, send_out, recv_out, steps=(-1,))
    inner_rows(nx - 1, nx, [a + b for a, b in zip(high, inner_taps(nx - 1, nx, (2,)))])
    second_halo += halo_start(mixed, held_out, send_out, recv_out, steps=(1,))

    edge = jnp.zeros((nx * ny_out, 1, outch), jnp.float32)
    shifted_out[:, 0:1] = edge
    shifted_out[:, nz + 1 : nz + 2] = edge

    def by_channel(by_depth, rows):
        planes = rows * ny_out
        shifted_out[0:planes, 1 : nz + 1] = by_depth[:, 0:outch].reshape(planes, nz, outch)
        summed = by_depth[:, outch : 2 * outch].reshape(planes, nz, outch) + shifted_out[0:planes, 0:nz]
        shifted_out[0:planes, 1 : nz + 1] = by_depth[:, 2 * outch : 3 * outch].reshape(planes, nz, outch)
        summed = summed + shifted_out[0:planes, 2 : nz + 2]
        return summed.reshape(planes * nz, outch).T

    block = outch // count

    def share(phase, values):
        for peer in range(count):
            parts[phase, peer] = values[peer * block : (peer + 1) * block]
        sends = []
        for step in range(1, count):
            peer = lax.rem(me + step, count)
            copy = pltpu.make_async_remote_copy(
                src_ref=parts.at[phase, peer],
                dst_ref=inbox.at[phase, step],
                send_sem=sum_send.at[phase, step],
                recv_sem=sum_recv.at[phase, step],
                device_id={"section": peer},
                device_id_type=MESH,
            )
            copy.start()
            sends.append(copy)
        return sends

    def gather(phase, sends):
        result = parts[phase, me]
        for step in range(1, count):
            sends[step - 1].wait_recv()
            result = result + inbox[phase, step]
        for copy in sends:
            copy.wait_send()
        return result

    held_out[1 : nx + 1] = mixed[...]
    middle_sends = share(0, by_channel(outer_rows(1, nx - 1), nx - 2))
    low_out = outer_rows(0, 1, (1, 2))
    high_out = outer_rows(nx - 1, nx, (0, 1))
    halo_finish(second_halo)
    row_cells = ny_out * nz
    ends = jnp.concatenate(
        [
            by_channel(low_out + outer_rows(0, 1, (0,)), 1),
            by_channel(high_out + outer_rows(nx - 1, nx, (2,)), 1),
        ],
        axis=1,
    )
    end_sends = share(1, ends)
    middle = gather(0, middle_sends)
    ends = gather(1, end_sends)
    result = jnp.concatenate([ends[:, 0:row_cells], middle, ends[:, row_cells:]], axis=1)
    out_ref[...] = result.reshape(out_ref.shape).astype(out_ref.dtype)


def whole_kernel(tokens_ref, weight_hbm, gains_ref, kernel_in_hbm, kernel_out_hbm, out_ref, *scratch):
    weight, field, rows_in, send_rows, recv_rows, weight_sem = scratch[:6]
    brick, kernel_in, kernel_out, kernel_sem = scratch[6:10]
    loads = [
        pltpu.make_async_copy(kernel_in_hbm, kernel_in, kernel_sem.at[0]),
        pltpu.make_async_copy(kernel_out_hbm, kernel_out, kernel_sem.at[1]),
    ]
    for load in loads:
        load.start()
    extra = entry_signals()
    held, shifted, mixed = scratch[10:13]
    nx, ny_in, nz, channels = brick.shape
    ny = ny_in - 2
    bounds = [2 * (ny // 6), 2 * (ny // 3)]
    done = bounds[-1]
    inner_taps, inner_rows = conv_in_rows(brick, kernel_in, gains_ref, held, shifted, mixed)

    def chunk(low, high):
        def run():
            if low == 0:
                loads[0].wait()
                edge = jnp.zeros((shifted.shape[0], 1, channels), jnp.float32)
                shifted[:, 0:1] = edge
                shifted[:, nz + 1 : nz + 2] = edge
                held[1 : nx + 1, 0 : high + 2] = brick[:, 0 : high + 2]
            else:
                held[1 : nx + 1, low + 2 : high + 2] = brick[:, low + 2 : high + 2]
            inner_rows(1, nx - 1, inner_taps(1, nx - 1, (0, 1, 2), low, high), low, high)

        return run

    send_halo, recv_halo = scratch[17], scratch[18]
    count_x = lax.axis_size("inl")
    me_x = lax.axis_index("inl")

    def edge_rows(slot):
        for index, step in enumerate((-1, 1)):
            source, target = (0, nx + 1) if step < 0 else (nx - 1, 0)
            rows = pl.ds(2 * slot, 2)
            copy = pltpu.make_async_remote_copy(
                src_ref=brick.at[source : source + 1, rows],
                dst_ref=held.at[target : target + 1, rows],
                send_sem=send_halo.at[index],
                recv_sem=recv_halo.at[index],
                device_id={"inl": me_x + step},
                device_id_type=MESH,
            )

            @pl.when((me_x + step >= 0) & (me_x + step < count_x))
            def _():
                copy.start()

    gather_kernel(
        tokens_ref, weight_hbm, gains_ref, brick, weight, field, rows_in, send_rows, recv_rows, weight_sem, extra,
        {bounds[0] // 2: chunk(0, bounds[0]), bounds[1] // 2: chunk(bounds[0], bounds[1]), "each": edge_rows},
    )
    loads[1].wait()
    block_kernel(True, done, brick, kernel_in, gains_ref, kernel_out, out_ref, *scratch[10:])


def decoder_block(tokens, weight, gains, kernel_in, kernel_out, collective):
    count_x = lax.axis_size("inl")
    rows = tokens.shape[0] // count_x
    slots = lax.axis_size("xln") + 2
    nx, ny_in, nz, channels = 2 * PXD, 2 * slots, 2 * GZ, gains.shape[1]
    ny = ny_in - 2
    ny_out = ny - 2
    count = lax.axis_size("section")
    outch = kernel_out.shape[1] // 3
    block = outch // count
    return pl.pallas_call(
        whole_kernel,
        out_shape=jax.ShapeDtypeStruct((block, nx, ny_out * nz), jnp.bfloat16),
        in_specs=[
            pl.BlockSpec(memory_space=pltpu.VMEM),
            pl.BlockSpec(memory_space=pl.ANY),
            pl.BlockSpec(memory_space=pltpu.VMEM),
            pl.BlockSpec(memory_space=pl.ANY),
            pl.BlockSpec(memory_space=pl.ANY),
        ],
        out_specs=pl.BlockSpec(memory_space=pltpu.VMEM),
        scratch_shapes=[
            pltpu.VMEM(weight.shape, weight.dtype),
            pltpu.VMEM((tokens.shape[0], weight.shape[1]), jnp.bfloat16),
            pltpu.VMEM((slots, rows, weight.shape[1]), jnp.bfloat16),
            pltpu.SemaphoreType.DMA((3 * count_x,)),
            pltpu.SemaphoreType.DMA((slots,)),
            pltpu.SemaphoreType.DMA(()),
            pltpu.VMEM((nx, ny_in, nz, channels), jnp.bfloat16),
            pltpu.VMEM(kernel_in.shape, kernel_in.dtype),
            pltpu.VMEM(kernel_out.shape, kernel_out.dtype),
            pltpu.SemaphoreType.DMA((2,)),
            pltpu.VMEM((nx + 2, ny_in, nz, channels), jnp.bfloat16),
            pltpu.VMEM((nx * ny, nz + 2, channels), jnp.float32),
            pltpu.VMEM((nx, ny, nz, channels), jnp.bfloat16),
            pltpu.VMEM((nx + 2, ny, nz, channels), jnp.bfloat16),
            pltpu.VMEM((nx * ny_out, nz + 2, outch), jnp.float32),
            pltpu.VMEM((2, count, block, (nx - 2) * ny_out * nz), jnp.float32),
            pltpu.VMEM((2, count, block, (nx - 2) * ny_out * nz), jnp.float32),
            pltpu.SemaphoreType.DMA((2,)),
            pltpu.SemaphoreType.DMA((2,)),
            pltpu.SemaphoreType.DMA((2,)),
            pltpu.SemaphoreType.DMA((2,)),
            pltpu.SemaphoreType.DMA((2, count)),
            pltpu.SemaphoreType.DMA((2, count)),
        ],
        compiler_params=pltpu.CompilerParams(collective_id=collective, has_side_effects=True),
    )(tokens, weight, gains, kernel_in, kernel_out)


def local(skips, deconv_weight, norm_gain, conv_in, conv_out):
    inl_size = lax.axis_size("inl")
    tokens_here = skips[0]
    weight = deconv_weight[0]
    gains = norm_gain[0]
    channels = gains.shape[1]
    cell_x = 2 * PXD
    cell_y = 2 * lax.axis_size("xln")
    cell_z = 2 * GZ
    assert tokens_here.shape[0] == inl_size * PXD * GZ
    taps, outch, channels_in = conv_out.shape[1:]
    out_weight = conv_out[0].reshape(taps // 3, 3 * outch, channels_in)
    return decoder_block(tokens_here, weight, gains, conv_in[0], out_weight, 3)


def solution(mesh):
    return jax.shard_map(
        local,
        mesh=mesh,
        in_specs=(
            P("section", ("inl", "xln"), None),
            P("section", None, None),
            P("section", None, None),
            P("section", None, None, None),
            P("section", None, None, None),
        ),
        out_specs=P("section", "inl", "xln"),
        check_vma=False,
    )
```

```python
import functools

import jax
import jax.numpy as jnp
from jax import lax
from jax.experimental import pallas as pl
from jax.experimental.pallas import tpu as pltpu
from jax.sharding import PartitionSpec as P

MESH = pl.DeviceIdType.MESH
PXD = 2
GZ = 8


epsilon = 1e-05


def gelu_tanh(values):
    return 0.5 * values * (1.0 + jnp.tanh(0.7978845608028654 * (values + 0.044715 * (values * values * values))))


def send_groups(me_x, me_y, count):
    return [
        (me_x, me_y + 1, None),
        (me_x + 1, 0, (me_y == count - 1) & (me_x + 1 < count)),
        (me_x - 1, count + 1, (me_y == 0) & (me_x > 0)),
    ]


def gather_kernel(
    tokens_ref, weight_hbm, gains_ref, out_ref, weight, field, held, send_sem, recv_sem, weight_sem, extra=0,
    hooks=None,
):
    count = lax.axis_size("inl")
    me_x, me_y = lax.axis_index("inl"), lax.axis_index("xln")
    rows = tokens_ref.shape[0] // count
    width = gains_ref.shape[1]
    one = jnp.int32(1)
    loading = pltpu.make_async_copy(weight_hbm, weight, weight_sem)
    loading.start()
    groups = send_groups(me_x, me_y, count)
    sources = [(me_y - 1, count - 1, me_y >= 1)]
    sources += [(me_y, other, None) for other in range(count)]
    sources += [(me_y + 1, 0, me_y + 1 < count)]

    def is_me(x, y):
        return (x == me_x) & (y == me_y)

    barrier = pltpu.get_barrier_semaphore()
    expected = jnp.int32(0)
    for column, _, exists in groups:
        live = True if exists is None else exists
        expected = expected + jnp.where(live, count, 0)
        for other in range(count):

            @pl.when(jnp.logical_and(live, jnp.logical_not(is_me(other, column))))
            def _():
                pl.semaphore_signal(barrier, inc=1, device_id={"inl": other, "xln": column}, device_id_type=MESH)

            expected = expected - jnp.where(jnp.logical_and(live, is_me(other, column)), one, 0)
    for source_x, source_y, exists in sources:
        live = True if exists is None else exists
        mine = jnp.logical_and(live, is_me(source_x, source_y))
        expected = expected + jnp.where(jnp.logical_and(live, jnp.logical_not(mine)), one, 0)

        @pl.when(jnp.logical_and(live, jnp.logical_not(mine)))
        def _():
            pl.semaphore_signal(barrier, inc=1, device_id={"inl": source_x, "xln": source_y}, device_id_type=MESH)

    loading.wait()
    upsampled = jnp.dot(tokens_ref[...], weight[...], preferred_element_type=jnp.float32)
    for group in range(upsampled.shape[1] // width):
        part = upsampled[:, group * width : (group + 1) * width]
        mean_square = jnp.mean(part * part, axis=-1, keepdims=True)
        normed = part * lax.rsqrt(mean_square + epsilon) * gains_ref[0:1, :]
        field[:, group * width : (group + 1) * width] = gelu_tanh(normed).astype(field.dtype)
    depth = 2 * (rows // 2)
    target = lax.broadcasted_iota(jnp.int32, (2 * rows, 2 * rows), 0)
    origin = lax.broadcasted_iota(jnp.int32, (2 * rows, 2 * rows), 1)
    half = rows // 2
    same = (
        (target // depth == (origin % rows) // half)
        & ((target % depth) // 2 == origin % half)
        & (target % 2 == origin // rows)
    )
    interleave = jnp.where(same, 1.0, 0.0).astype(jnp.bfloat16)

    def place(slot, block):
        for u in range(2):
            for v in range(2):
                first = ((u * 2 + v) * 2) * width
                pair = jnp.concatenate([block[:, first : first + width], block[:, first + width : first + 2 * width]], axis=0)
                cells = jnp.dot(interleave, pair, preferred_element_type=jnp.float32).astype(out_ref.dtype)
                for ix in range(2):
                    out_ref[2 * ix + u, 2 * slot + v] = cells[ix * depth : (ix + 1) * depth]

    pl.semaphore_wait(barrier, expected + extra)
    copies = []
    for index, (column, slot, exists) in enumerate(groups):
        live = True if exists is None else exists
        for turn in range(count):
            other = lax.rem(me_y + turn, count)
            copy = pltpu.make_async_remote_copy(
                src_ref=field.at[pl.ds(pl.multiple_of(other * rows, rows), rows)],
                dst_ref=held.at[slot],
                send_sem=send_sem.at[index * count + turn],
                recv_sem=recv_sem.at[slot],
                device_id={"inl": other, "xln": column},
                device_id_type=MESH,
            )
            remote = jnp.logical_and(live, jnp.logical_not(is_me(other, column)))

            @pl.when(remote)
            def _():
                copy.start()

            copies.append((copy, remote))
    for slot, (source_x, source_y, exists) in enumerate(sources):
        live = True if exists is None else exists
        mine = jnp.logical_and(live, is_me(source_x, source_y))
        remote = jnp.logical_and(live, jnp.logical_not(mine))
        incoming = pltpu.make_async_remote_copy(
            src_ref=field.at[pl.ds(0, rows)],
            dst_ref=held.at[slot],
            send_sem=send_sem.at[0],
            recv_sem=recv_sem.at[slot],
            device_id={"inl": source_x, "xln": source_y},
            device_id_type=MESH,
        )

        @pl.when(remote)
        def _():
            incoming.wait_recv()
            place(slot, held[slot])

        @pl.when(mine)
        def _():
            place(slot, field[pl.ds(pl.multiple_of(me_x * rows, rows), rows)])

        @pl.when(jnp.logical_not(live))
        def _():
            out_ref[:, 2 * slot : 2 * slot + 2] = jnp.zeros(
                (out_ref.shape[0], 2) + out_ref.shape[2:], out_ref.dtype
            )

        if hooks and "each" in hooks:
            hooks["each"](slot)
        if hooks and slot in hooks:
            hooks[slot]()

    for copy, remote in copies:

        @pl.when(remote)
        def _():
            copy.wait_send()


def halo_signal():
    count = lax.axis_size("inl")
    me = lax.axis_index("inl")
    for step in (-1, 1):

        @pl.when((me + step >= 0) & (me + step < count))
        def _():
            pl.semaphore_signal(
                pltpu.get_barrier_semaphore(), inc=1, device_id={"inl": me + step}, device_id_type=MESH
            )

    return (me > 0).astype(jnp.int32) + (me < count - 1).astype(jnp.int32)


def halo_start(field_ref, held, send_sem, recv_sem, start=True, steps=(-1, 1)):
    nx = field_ref.shape[0]
    count = lax.axis_size("inl")
    me = lax.axis_index("inl")
    copies = []
    for step in steps:
        index = 0 if step < 0 else 1
        source, target = (0, nx + 1) if step < 0 else (nx - 1, 0)
        copy = pltpu.make_async_remote_copy(
            src_ref=field_ref.at[source : source + 1],
            dst_ref=held.at[target : target + 1],
            send_sem=send_sem.at[index],
            recv_sem=recv_sem.at[index],
            device_id={"inl": me + step},
            device_id_type=MESH,
        )
        sends = (me + step >= 0) & (me + step < count)
        gets = (me - step >= 0) & (me - step < count)

        if start:

            @pl.when(sends)
            def _():
                copy.start()

        @pl.when(jnp.logical_not(gets))
        def _():
            held[target : target + 1] = jnp.zeros((1,) + held.shape[1:], held.dtype)

        copies.append((copy, sends, gets))
    return copies


def halo_finish(copies):
    for copy, sends, gets in copies:

        @pl.when(gets)
        def _():
            copy.wait_recv()

        @pl.when(sends)
        def _():
            copy.wait_send()


def conv_in_rows(field_ref, kernel_in_ref, gains_ref, held, shifted, mixed):
    nx, ny_in, nz, channels = field_ref.shape
    ny = ny_in - 2
    me_y, count_y = lax.axis_index("xln"), lax.axis_size("xln")

    def inner_taps(first, last, offsets_x, low=0, high=ny):
        cells = (last - first) * (high - low) * nz
        parts_in = []
        for offset_z in range(3):
            part = jnp.zeros((cells, channels), jnp.float32)
            for offset_x in offsets_x:
                for offset_y in range(3):
                    window = held[first + offset_x : last + offset_x, low + offset_y : high + offset_y].reshape(
                        cells, channels
                    )
                    tap = kernel_in_ref[(offset_x * 3 + offset_y) * 3 + offset_z]
                    part = part + jnp.dot(window, tap, preferred_element_type=jnp.float32)
            parts_in.append(part)
        return parts_in

    def inner_rows(first, last, parts_in, low=0, high=ny):
        rows = last - first
        planes = rows * (high - low)
        parts_in = [part.reshape(planes, nz, channels) for part in parts_in]
        shifted[0:planes, 1 : nz + 1] = parts_in[0]
        total = parts_in[1] + shifted[0:planes, 0:nz]
        shifted[0:planes, 1 : nz + 1] = parts_in[2]
        total = total + shifted[0:planes, 2 : nz + 2]
        mean_square = jnp.mean(total * total, axis=-1, keepdims=True)
        normed = total * lax.rsqrt(mean_square + epsilon) * gains_ref[1:2, :]
        base = field_ref[first:last, 1 + low : 1 + high].reshape(planes, nz, channels).astype(jnp.float32)
        activated = gelu_tanh(normed + base).reshape(rows, high - low, nz, channels)
        row = low + lax.broadcasted_iota(jnp.int32, activated.shape, 1)
        outside = ((row == 0) & (me_y == 0)) | ((row == ny - 1) & (me_y == count_y - 1))
        mixed[first:last, low:high] = jnp.where(outside, 0.0, activated).astype(mixed.dtype)

    return inner_taps, inner_rows


def entry_signals():
    count = lax.axis_size("section")
    me = lax.axis_index("section")
    for step in range(1, count):
        pl.semaphore_signal(
            pltpu.get_barrier_semaphore(),
            inc=1,
            device_id={"section": lax.rem(me + step, count)},
            device_id_type=MESH,
        )
    return halo_signal() + count - 1


def block_kernel(
    merged, done, field_ref, kernel_in_ref, gains_ref, kernel_out_ref, out_ref,
    held, shifted, mixed, held_out, shifted_out, parts, inbox,
    send_sem, recv_sem, send_out, recv_out, sum_send, sum_recv,
):
    count = lax.axis_size("section")
    me = lax.axis_index("section")
    barrier = pltpu.get_barrier_semaphore()
    if not merged:
        expected = entry_signals()
    nx, ny_in, nz, channels = field_ref.shape
    ny = ny_in - 2
    ny_out = ny - 2
    outch = kernel_out_ref.shape[1] // 3
    me_y, count_y = lax.axis_index("xln"), lax.axis_size("xln")
    if not done:
        edge = jnp.zeros((nx * ny, 1, channels), jnp.float32)
        shifted[:, 0:1] = edge
        shifted[:, nz + 1 : nz + 2] = edge
        held[1 : nx + 1] = field_ref[...]
    else:
        held[1 : nx + 1, done + 2 :] = field_ref[:, done + 2 :]

    inner_taps, inner_rows = conv_in_rows(field_ref, kernel_in_ref, gains_ref, held, shifted, mixed)

    def outer_rows(first, last, offsets_x=(0, 1, 2)):
        cells = (last - first) * ny_out * nz
        by_depth = jnp.zeros((cells, 3 * outch), jnp.float32)
        for offset_x in offsets_x:
            for offset_y in range(3):
                window = held_out[first + offset_x : last + offset_x, offset_y : offset_y + ny_out].reshape(
                    cells, channels
                )
                by_depth = by_depth + lax.dot_general(
                    window,
                    kernel_out_ref[offset_x * 3 + offset_y],
                    (((1,), (1,)), ((), ())),
                    preferred_element_type=jnp.float32,
                )
        return by_depth

    if merged:
        first_halo = halo_start(field_ref, held, send_sem, recv_sem, start=False)
    inner_rows(1, nx - 1, inner_taps(1, nx - 1, (0, 1, 2), done, ny), done, ny)
    low = inner_taps(0, 1, (1, 2))
    high = inner_taps(nx - 1, nx, (0, 1))
    if not merged:
        pl.semaphore_wait(barrier, expected)
        first_halo = halo_start(field_ref, held, send_sem, recv_sem)
    halo_finish(first_halo)
    inner_rows(0, 1, [a + b for a, b in zip(low, inner_taps(0, 1, (0,)))])
    second_halo = halo_start(mixed, held_out, send_out, recv_out, steps=(-1,))
    inner_rows(nx - 1, nx, [a + b for a, b in zip(high, inner_taps(nx - 1, nx, (2,)))])
    second_halo += halo_start(mixed, held_out, send_out, recv_out, steps=(1,))

    edge = jnp.zeros((nx * ny_out, 1, outch), jnp.float32)
    shifted_out[:, 0:1] = edge
    shifted_out[:, nz + 1 : nz + 2] = edge

    def by_channel(by_depth, rows):
        planes = rows * ny_out
        shifted_out[0:planes, 1 : nz + 1] = by_depth[:, 0:outch].reshape(planes, nz, outch)
        summed = by_depth[:, outch : 2 * outch].reshape(planes, nz, outch) + shifted_out[0:planes, 0:nz]
        shifted_out[0:planes, 1 : nz + 1] = by_depth[:, 2 * outch : 3 * outch].reshape(planes, nz, outch)
        summed = summed + shifted_out[0:planes, 2 : nz + 2]
        return summed.reshape(planes * nz, outch).T

    block = outch // count

    def share(phase, values):
        for peer in range(count):
            parts[phase, peer] = values[peer * block : (peer + 1) * block]
        sends = []
        for step in range(1, count):
            peer = lax.rem(me + step, count)
            copy = pltpu.make_async_remote_copy(
                src_ref=parts.at[phase, peer],
                dst_ref=inbox.at[phase, step],
                send_sem=sum_send.at[phase, step],
                recv_sem=sum_recv.at[phase, step],
                device_id={"section": peer},
                device_id_type=MESH,
            )
            copy.start()
            sends.append(copy)
        return sends

    def gather(phase, sends):
        result = parts[phase, me]
        for step in range(1, count):
            sends[step - 1].wait_recv()
            result = result + inbox[phase, step]
        for copy in sends:
            copy.wait_send()
        return result

    middle_sends = share(0, by_channel(outer_rows(1, nx - 1), nx - 2))
    low_out = outer_rows(0, 1, (1, 2))
    high_out = outer_rows(nx - 1, nx, (0, 1))
    halo_finish(second_halo)
    row_cells = ny_out * nz
    ends = jnp.concatenate(
        [
            by_channel(low_out + outer_rows(0, 1, (0,)), 1),
            by_channel(high_out + outer_rows(nx - 1, nx, (2,)), 1),
        ],
        axis=1,
    )
    end_sends = share(1, ends)
    middle = gather(0, middle_sends)
    ends = gather(1, end_sends)
    result = jnp.concatenate([ends[:, 0:row_cells], middle, ends[:, row_cells:]], axis=1)
    out_ref[...] = result.reshape(out_ref.shape).astype(out_ref.dtype)


def whole_kernel(tokens_ref, weight_hbm, gains_ref, kernel_in_hbm, kernel_out_hbm, out_ref, *scratch):
    weight, field, rows_in, send_rows, recv_rows, weight_sem = scratch[:6]
    brick, kernel_in, kernel_out, kernel_sem = scratch[6:10]
    loads = [
        pltpu.make_async_copy(kernel_in_hbm, kernel_in, kernel_sem.at[0]),
        pltpu.make_async_copy(kernel_out_hbm, kernel_out, kernel_sem.at[1]),
    ]
    for load in loads:
        load.start()
    extra = entry_signals()
    held, shifted = scratch[10:12]
    mixed = scratch[13].at[1 : brick.shape[0] + 1]
    nx, ny_in, nz, channels = brick.shape
    done = ny_in // 2
    inner_taps, inner_rows = conv_in_rows(brick, kernel_in, gains_ref, held, shifted, mixed)

    def early():
        loads[0].wait()
        edge = jnp.zeros((shifted.shape[0], 1, channels), jnp.float32)
        shifted[:, 0:1] = edge
        shifted[:, nz + 1 : nz + 2] = edge
        held[1 : nx + 1, 0 : done + 2] = brick[:, 0 : done + 2]
        inner_rows(1, nx - 1, inner_taps(1, nx - 1, (0, 1, 2), 0, done), 0, done)

    send_halo, recv_halo = scratch[17], scratch[18]
    count_x = lax.axis_size("inl")
    me_x = lax.axis_index("inl")

    def edge_rows(slot):
        for index, step in enumerate((-1, 1)):
            source, target = (0, nx + 1) if step < 0 else (nx - 1, 0)
            rows = pl.ds(2 * slot, 2)
            copy = pltpu.make_async_remote_copy(
                src_ref=brick.at[source : source + 1, rows],
                dst_ref=held.at[target : target + 1, rows],
                send_sem=send_halo.at[index],
                recv_sem=recv_halo.at[index],
                device_id={"inl": me_x + step},
                device_id_type=MESH,
            )

            @pl.when((me_x + step >= 0) & (me_x + step < count_x))
            def _():
                copy.start()

    gather_kernel(
        tokens_ref, weight_hbm, gains_ref, brick, weight, field, rows_in, send_rows, recv_rows, weight_sem, extra,
        {done // 2: early, "each": edge_rows},
    )
    loads[1].wait()
    block_kernel(True, done, brick, kernel_in, gains_ref, kernel_out, out_ref, held, shifted, mixed, *scratch[13:])


def decoder_block(tokens, weight, gains, kernel_in, kernel_out, collective):
    count_x = lax.axis_size("inl")
    rows = tokens.shape[0] // count_x
    slots = lax.axis_size("xln") + 2
    nx, ny_in, nz, channels = 2 * PXD, 2 * slots, 2 * GZ, gains.shape[1]
    ny = ny_in - 2
    ny_out = ny - 2
    count = lax.axis_size("section")
    outch = kernel_out.shape[1] // 3
    block = outch // count
    return pl.pallas_call(
        whole_kernel,
        out_shape=jax.ShapeDtypeStruct((block, nx, ny_out * nz), jnp.bfloat16),
        in_specs=[
            pl.BlockSpec(memory_space=pltpu.VMEM),
            pl.BlockSpec(memory_space=pl.ANY),
            pl.BlockSpec(memory_space=pltpu.VMEM),
            pl.BlockSpec(memory_space=pl.ANY),
            pl.BlockSpec(memory_space=pl.ANY),
        ],
        out_specs=pl.BlockSpec(memory_space=pltpu.VMEM),
        scratch_shapes=[
            pltpu.VMEM(weight.shape, weight.dtype),
            pltpu.VMEM((tokens.shape[0], weight.shape[1]), jnp.bfloat16),
            pltpu.VMEM((slots, rows, weight.shape[1]), jnp.bfloat16),
            pltpu.SemaphoreType.DMA((3 * count_x,)),
            pltpu.SemaphoreType.DMA((slots,)),
            pltpu.SemaphoreType.DMA(()),
            pltpu.VMEM((nx, ny_in, nz, channels), jnp.bfloat16),
            pltpu.VMEM(kernel_in.shape, kernel_in.dtype),
            pltpu.VMEM(kernel_out.shape, kernel_out.dtype),
            pltpu.SemaphoreType.DMA((2,)),
            pltpu.VMEM((nx + 2, ny_in, nz, channels), jnp.bfloat16),
            pltpu.VMEM((nx * ny, nz + 2, channels), jnp.float32),
            pltpu.VMEM((nx, ny, nz, channels), jnp.bfloat16),
            pltpu.VMEM((nx + 2, ny, nz, channels), jnp.bfloat16),
            pltpu.VMEM((nx * ny_out, nz + 2, outch), jnp.float32),
            pltpu.VMEM((2, count, block, (nx - 2) * ny_out * nz), jnp.float32),
            pltpu.VMEM((2, count, block, (nx - 2) * ny_out * nz), jnp.float32),
            pltpu.SemaphoreType.DMA((2,)),
            pltpu.SemaphoreType.DMA((2,)),
            pltpu.SemaphoreType.DMA((2,)),
            pltpu.SemaphoreType.DMA((2,)),
            pltpu.SemaphoreType.DMA((2, count)),
            pltpu.SemaphoreType.DMA((2, count)),
        ],
        compiler_params=pltpu.CompilerParams(collective_id=collective, has_side_effects=True),
    )(tokens, weight, gains, kernel_in, kernel_out)


def local(skips, deconv_weight, norm_gain, conv_in, conv_out):
    inl_size = lax.axis_size("inl")
    tokens_here = skips[0]
    weight = deconv_weight[0]
    gains = norm_gain[0]
    channels = gains.shape[1]
    cell_x = 2 * PXD
    cell_y = 2 * lax.axis_size("xln")
    cell_z = 2 * GZ
    assert tokens_here.shape[0] == inl_size * PXD * GZ
    taps, outch, channels_in = conv_out.shape[1:]
    out_weight = conv_out[0].reshape(taps // 3, 3 * outch, channels_in)
    return decoder_block(tokens_here, weight, gains, conv_in[0], out_weight, 3)


def solution(mesh):
    return jax.shard_map(
        local,
        mesh=mesh,
        in_specs=(
            P("section", ("inl", "xln"), None),
            P("section", None, None),
            P("section", None, None),
            P("section", None, None, None),
            P("section", None, None, None),
        ),
        out_specs=P("section", "inl", "xln"),
        check_vma=False,
    )
```

```python
import functools

import jax
import jax.numpy as jnp
from jax import lax
from jax.experimental import pallas as pl
from jax.experimental.pallas import tpu as pltpu
from jax.sharding import PartitionSpec as P

MESH = pl.DeviceIdType.MESH
PXD = 2
GZ = 8


epsilon = 1e-05


def gelu_tanh(values):
    return 0.5 * values * (1.0 + jnp.tanh(0.7978845608028654 * (values + 0.044715 * (values * values * values))))


def send_groups(me_x, me_y, count):
    return [
        (me_x, me_y + 1, None),
        (me_x + 1, 0, (me_y == count - 1) & (me_x + 1 < count)),
        (me_x - 1, count + 1, (me_y == 0) & (me_x > 0)),
    ]


def gather_kernel(
    tokens_ref, weight_hbm, gains_ref, out_ref, weight, field, held, send_sem, recv_sem, weight_sem, extra=0,
    hooks=None,
):
    count = lax.axis_size("inl")
    me_x, me_y = lax.axis_index("inl"), lax.axis_index("xln")
    rows = tokens_ref.shape[0] // count
    width = gains_ref.shape[1]
    one = jnp.int32(1)
    loading = pltpu.make_async_copy(weight_hbm, weight, weight_sem)
    loading.start()
    groups = send_groups(me_x, me_y, count)
    sources = [(me_y - 1, count - 1, me_y >= 1)]
    sources += [(me_y, other, None) for other in range(count)]
    sources += [(me_y + 1, 0, me_y + 1 < count)]

    def is_me(x, y):
        return (x == me_x) & (y == me_y)

    barrier = pltpu.get_barrier_semaphore()
    expected = jnp.int32(0)
    for column, _, exists in groups:
        live = True if exists is None else exists
        expected = expected + jnp.where(live, count, 0)
        for other in range(count):

            @pl.when(jnp.logical_and(live, jnp.logical_not(is_me(other, column))))
            def _():
                pl.semaphore_signal(barrier, inc=1, device_id={"inl": other, "xln": column}, device_id_type=MESH)

            expected = expected - jnp.where(jnp.logical_and(live, is_me(other, column)), one, 0)
    for source_x, source_y, exists in sources:
        live = True if exists is None else exists
        mine = jnp.logical_and(live, is_me(source_x, source_y))
        expected = expected + jnp.where(jnp.logical_and(live, jnp.logical_not(mine)), one, 0)

        @pl.when(jnp.logical_and(live, jnp.logical_not(mine)))
        def _():
            pl.semaphore_signal(barrier, inc=1, device_id={"inl": source_x, "xln": source_y}, device_id_type=MESH)

    loading.wait()
    if hooks and "loaded" in hooks:
        hooks["loaded"]()
    upsampled = jnp.dot(tokens_ref[...], weight[...], preferred_element_type=jnp.float32)
    for group in range(upsampled.shape[1] // width):
        part = upsampled[:, group * width : (group + 1) * width]
        mean_square = jnp.mean(part * part, axis=-1, keepdims=True)
        normed = part * lax.rsqrt(mean_square + epsilon) * gains_ref[0:1, :]
        field[:, group * width : (group + 1) * width] = gelu_tanh(normed).astype(field.dtype)
    depth = 2 * (rows // 2)
    target = lax.broadcasted_iota(jnp.int32, (2 * rows, 2 * rows), 0)
    origin = lax.broadcasted_iota(jnp.int32, (2 * rows, 2 * rows), 1)
    half = rows // 2
    same = (
        (target // depth == (origin % rows) // half)
        & ((target % depth) // 2 == origin % half)
        & (target % 2 == origin // rows)
    )
    interleave = jnp.where(same, 1.0, 0.0).astype(jnp.bfloat16)

    def place(slot, block):
        for u in range(2):
            for v in range(2):
                first = ((u * 2 + v) * 2) * width
                pair = jnp.concatenate([block[:, first : first + width], block[:, first + width : first + 2 * width]], axis=0)
                cells = jnp.dot(interleave, pair, preferred_element_type=jnp.float32).astype(out_ref.dtype)
                for ix in range(2):
                    out_ref[2 * ix + u, 2 * slot + v] = cells[ix * depth : (ix + 1) * depth]

    pl.semaphore_wait(barrier, expected + extra)
    copies = []
    for index, (column, slot, exists) in enumerate(groups):
        live = True if exists is None else exists
        for turn in range(count):
            other = lax.rem(me_y + turn, count)
            copy = pltpu.make_async_remote_copy(
                src_ref=field.at[pl.ds(pl.multiple_of(other * rows, rows), rows)],
                dst_ref=held.at[slot],
                send_sem=send_sem.at[index * count + turn],
                recv_sem=recv_sem.at[slot],
                device_id={"inl": other, "xln": column},
                device_id_type=MESH,
            )
            remote = jnp.logical_and(live, jnp.logical_not(is_me(other, column)))

            @pl.when(remote)
            def _():
                copy.start()

            copies.append((copy, remote))
    for slot, (source_x, source_y, exists) in enumerate(sources):
        live = True if exists is None else exists
        mine = jnp.logical_and(live, is_me(source_x, source_y))
        remote = jnp.logical_and(live, jnp.logical_not(mine))
        incoming = pltpu.make_async_remote_copy(
            src_ref=field.at[pl.ds(0, rows)],
            dst_ref=held.at[slot],
            send_sem=send_sem.at[0],
            recv_sem=recv_sem.at[slot],
            device_id={"inl": source_x, "xln": source_y},
            device_id_type=MESH,
        )

        @pl.when(remote)
        def _():
            incoming.wait_recv()
            place(slot, held[slot])

        @pl.when(mine)
        def _():
            place(slot, field[pl.ds(pl.multiple_of(me_x * rows, rows), rows)])

        @pl.when(jnp.logical_not(live))
        def _():
            out_ref[:, 2 * slot : 2 * slot + 2] = jnp.zeros(
                (out_ref.shape[0], 2) + out_ref.shape[2:], out_ref.dtype
            )

        if hooks and "each" in hooks:
            hooks["each"](slot)
        if hooks and slot in hooks:
            hooks[slot]()

    for copy, remote in copies:

        @pl.when(remote)
        def _():
            copy.wait_send()


def halo_signal():
    count = lax.axis_size("inl")
    me = lax.axis_index("inl")
    for step in (-1, 1):

        @pl.when((me + step >= 0) & (me + step < count))
        def _():
            pl.semaphore_signal(
                pltpu.get_barrier_semaphore(), inc=1, device_id={"inl": me + step}, device_id_type=MESH
            )

    return (me > 0).astype(jnp.int32) + (me < count - 1).astype(jnp.int32)


def halo_start(field_ref, held, send_sem, recv_sem, start=True, steps=(-1, 1)):
    nx = field_ref.shape[0]
    count = lax.axis_size("inl")
    me = lax.axis_index("inl")
    copies = []
    for step in steps:
        index = 0 if step < 0 else 1
        source, target = (0, nx + 1) if step < 0 else (nx - 1, 0)
        copy = pltpu.make_async_remote_copy(
            src_ref=field_ref.at[source : source + 1],
            dst_ref=held.at[target : target + 1],
            send_sem=send_sem.at[index],
            recv_sem=recv_sem.at[index],
            device_id={"inl": me + step},
            device_id_type=MESH,
        )
        sends = (me + step >= 0) & (me + step < count)
        gets = (me - step >= 0) & (me - step < count)

        if start:

            @pl.when(sends)
            def _():
                copy.start()

        @pl.when(jnp.logical_not(gets))
        def _():
            held[target : target + 1] = jnp.zeros((1,) + held.shape[1:], held.dtype)

        copies.append((copy, sends, gets))
    return copies


def halo_finish(copies):
    for copy, sends, gets in copies:

        @pl.when(gets)
        def _():
            copy.wait_recv()

        @pl.when(sends)
        def _():
            copy.wait_send()


def conv_in_rows(field_ref, kernel_in_ref, gains_ref, held, shifted, mixed):
    nx, ny_in, nz, channels = field_ref.shape
    ny = ny_in - 2
    me_y, count_y = lax.axis_index("xln"), lax.axis_size("xln")

    def inner_taps(first, last, offsets_x, low=0, high=ny):
        cells = (last - first) * (high - low) * nz
        parts_in = []
        for offset_z in range(3):
            part = jnp.zeros((cells, channels), jnp.float32)
            for offset_x in offsets_x:
                for offset_y in range(3):
                    window = held[first + offset_x : last + offset_x, low + offset_y : high + offset_y].reshape(
                        cells, channels
                    )
                    tap = kernel_in_ref[(offset_x * 3 + offset_y) * 3 + offset_z]
                    part = part + jnp.dot(window, tap, preferred_element_type=jnp.float32)
            parts_in.append(part)
        return parts_in

    def inner_rows(first, last, parts_in, low=0, high=ny):
        rows = last - first
        planes = rows * (high - low)
        parts_in = [part.reshape(planes, nz, channels) for part in parts_in]
        shifted[0:planes, 1 : nz + 1] = parts_in[0]
        total = parts_in[1] + shifted[0:planes, 0:nz]
        shifted[0:planes, 1 : nz + 1] = parts_in[2]
        total = total + shifted[0:planes, 2 : nz + 2]
        mean_square = jnp.mean(total * total, axis=-1, keepdims=True)
        normed = total * lax.rsqrt(mean_square + epsilon) * gains_ref[1:2, :]
        base = field_ref[first:last, 1 + low : 1 + high].reshape(planes, nz, channels).astype(jnp.float32)
        activated = gelu_tanh(normed + base).reshape(rows, high - low, nz, channels)
        row = low + lax.broadcasted_iota(jnp.int32, activated.shape, 1)
        outside = ((row == 0) & (me_y == 0)) | ((row == ny - 1) & (me_y == count_y - 1))
        mixed[first:last, low:high] = jnp.where(outside, 0.0, activated).astype(mixed.dtype)

    return inner_taps, inner_rows


def entry_signals():
    count = lax.axis_size("section")
    me = lax.axis_index("section")
    for step in range(1, count):
        pl.semaphore_signal(
            pltpu.get_barrier_semaphore(),
            inc=1,
            device_id={"section": lax.rem(me + step, count)},
            device_id_type=MESH,
        )
    return halo_signal() + count - 1


def block_kernel(
    merged, done, field_ref, kernel_in_ref, gains_ref, kernel_out_ref, out_ref,
    held, shifted, mixed, held_out, shifted_out, parts, inbox,
    send_sem, recv_sem, send_out, recv_out, sum_send, sum_recv,
):
    count = lax.axis_size("section")
    me = lax.axis_index("section")
    barrier = pltpu.get_barrier_semaphore()
    if not merged:
        expected = entry_signals()
    nx, ny_in, nz, channels = field_ref.shape
    ny = ny_in - 2
    ny_out = ny - 2
    outch = kernel_out_ref.shape[1] // 3
    me_y, count_y = lax.axis_index("xln"), lax.axis_size("xln")
    if not done:
        edge = jnp.zeros((nx * ny, 1, channels), jnp.float32)
        shifted[:, 0:1] = edge
        shifted[:, nz + 1 : nz + 2] = edge
        held[1 : nx + 1] = field_ref[...]
    else:
        held[1 : nx + 1, done + 2 :] = field_ref[:, done + 2 :]

    inner_taps, inner_rows = conv_in_rows(field_ref, kernel_in_ref, gains_ref, held, shifted, mixed)

    def outer_rows(first, last, offsets_x=(0, 1, 2)):
        cells = (last - first) * ny_out * nz
        by_depth = jnp.zeros((cells, 3 * outch), jnp.float32)
        for offset_x in offsets_x:
            for offset_y in range(3):
                window = held_out[first + offset_x : last + offset_x, offset_y : offset_y + ny_out].reshape(
                    cells, channels
                )
                by_depth = by_depth + lax.dot_general(
                    window,
                    kernel_out_ref[offset_x * 3 + offset_y],
                    (((1,), (1,)), ((), ())),
                    preferred_element_type=jnp.float32,
                )
        return by_depth

    if merged:
        first_halo = halo_start(field_ref, held, send_sem, recv_sem, start=False)
    inner_rows(1, nx - 1, inner_taps(1, nx - 1, (0, 1, 2), done, ny), done, ny)
    low = inner_taps(0, 1, (1, 2))
    high = inner_taps(nx - 1, nx, (0, 1))
    if not merged:
        pl.semaphore_wait(barrier, expected)
        first_halo = halo_start(field_ref, held, send_sem, recv_sem)
    halo_finish(first_halo)
    inner_rows(0, 1, [a + b for a, b in zip(low, inner_taps(0, 1, (0,)))])
    second_halo = halo_start(mixed, held_out, send_out, recv_out, steps=(-1,))
    inner_rows(nx - 1, nx, [a + b for a, b in zip(high, inner_taps(nx - 1, nx, (2,)))])
    second_halo += halo_start(mixed, held_out, send_out, recv_out, steps=(1,))

    edge = jnp.zeros((nx * ny_out, 1, outch), jnp.float32)
    shifted_out[:, 0:1] = edge
    shifted_out[:, nz + 1 : nz + 2] = edge

    def by_channel(by_depth, rows):
        planes = rows * ny_out
        shifted_out[0:planes, 1 : nz + 1] = by_depth[:, 0:outch].reshape(planes, nz, outch)
        summed = by_depth[:, outch : 2 * outch].reshape(planes, nz, outch) + shifted_out[0:planes, 0:nz]
        shifted_out[0:planes, 1 : nz + 1] = by_depth[:, 2 * outch : 3 * outch].reshape(planes, nz, outch)
        summed = summed + shifted_out[0:planes, 2 : nz + 2]
        return summed.reshape(planes * nz, outch).T

    block = outch // count

    def share(phase, values):
        for peer in range(count):
            parts[phase, peer] = values[peer * block : (peer + 1) * block]
        sends = []
        for step in range(1, count):
            peer = lax.rem(me + step, count)
            copy = pltpu.make_async_remote_copy(
                src_ref=parts.at[phase, peer],
                dst_ref=inbox.at[phase, step],
                send_sem=sum_send.at[phase, step],
                recv_sem=sum_recv.at[phase, step],
                device_id={"section": peer},
                device_id_type=MESH,
            )
            copy.start()
            sends.append(copy)
        return sends

    def gather(phase, sends):
        result = parts[phase, me]
        for step in range(1, count):
            sends[step - 1].wait_recv()
            result = result + inbox[phase, step]
        for copy in sends:
            copy.wait_send()
        return result

    held_out[1 : nx + 1] = mixed[...]
    middle_sends = share(0, by_channel(outer_rows(1, nx - 1), nx - 2))
    low_out = outer_rows(0, 1, (1, 2))
    high_out = outer_rows(nx - 1, nx, (0, 1))
    halo_finish(second_halo)
    row_cells = ny_out * nz
    ends = jnp.concatenate(
        [
            by_channel(low_out + outer_rows(0, 1, (0,)), 1),
            by_channel(high_out + outer_rows(nx - 1, nx, (2,)), 1),
        ],
        axis=1,
    )
    end_sends = share(1, ends)
    middle = gather(0, middle_sends)
    ends = gather(1, end_sends)
    result = jnp.concatenate([ends[:, 0:row_cells], middle, ends[:, row_cells:]], axis=1)
    out_ref[...] = result.reshape(out_ref.shape).astype(out_ref.dtype)


def whole_kernel(tokens_ref, weight_hbm, gains_ref, kernel_in_hbm, kernel_out_hbm, out_ref, *scratch):
    weight, field, rows_in, send_rows, recv_rows, weight_sem = scratch[:6]
    brick, kernel_in, kernel_out, kernel_sem = scratch[6:10]
    loads = [
        pltpu.make_async_copy(kernel_in_hbm, kernel_in, kernel_sem.at[0]),
        pltpu.make_async_copy(kernel_out_hbm, kernel_out, kernel_sem.at[1]),
    ]
    extra = entry_signals()

    def start_loads():
        for load in loads:
            load.start()

    held, shifted, mixed = scratch[10:13]
    nx, ny_in, nz, channels = brick.shape
    done = ny_in // 2
    inner_taps, inner_rows = conv_in_rows(brick, kernel_in, gains_ref, held, shifted, mixed)

    def early():
        loads[0].wait()
        edge = jnp.zeros((shifted.shape[0], 1, channels), jnp.float32)
        shifted[:, 0:1] = edge
        shifted[:, nz + 1 : nz + 2] = edge
        held[1 : nx + 1, 0 : done + 2] = brick[:, 0 : done + 2]
        inner_rows(1, nx - 1, inner_taps(1, nx - 1, (0, 1, 2), 0, done), 0, done)

    send_halo, recv_halo = scratch[17], scratch[18]
    count_x = lax.axis_size("inl")
    me_x = lax.axis_index("inl")

    def edge_rows(slot):
        for index, step in enumerate((-1, 1)):
            source, target = (0, nx + 1) if step < 0 else (nx - 1, 0)
            rows = pl.ds(2 * slot, 2)
            copy = pltpu.make_async_remote_copy(
                src_ref=brick.at[source : source + 1, rows],
                dst_ref=held.at[target : target + 1, rows],
                send_sem=send_halo.at[index],
                recv_sem=recv_halo.at[index],
                device_id={"inl": me_x + step},
                device_id_type=MESH,
            )

            @pl.when((me_x + step >= 0) & (me_x + step < count_x))
            def _():
                copy.start()

    gather_kernel(
        tokens_ref, weight_hbm, gains_ref, brick, weight, field, rows_in, send_rows, recv_rows, weight_sem, extra,
        {done // 2: early, "each": edge_rows, "loaded": start_loads},
    )
    loads[1].wait()
    block_kernel(True, done, brick, kernel_in, gains_ref, kernel_out, out_ref, *scratch[10:])


def decoder_block(tokens, weight, gains, kernel_in, kernel_out, collective):
    count_x = lax.axis_size("inl")
    rows = tokens.shape[0] // count_x
    slots = lax.axis_size("xln") + 2
    nx, ny_in, nz, channels = 2 * PXD, 2 * slots, 2 * GZ, gains.shape[1]
    ny = ny_in - 2
    ny_out = ny - 2
    count = lax.axis_size("section")
    outch = kernel_out.shape[1] // 3
    block = outch // count
    return pl.pallas_call(
        whole_kernel,
        out_shape=jax.ShapeDtypeStruct((block, nx, ny_out * nz), jnp.bfloat16),
        in_specs=[
            pl.BlockSpec(memory_space=pltpu.VMEM),
            pl.BlockSpec(memory_space=pl.ANY),
            pl.BlockSpec(memory_space=pltpu.VMEM),
            pl.BlockSpec(memory_space=pl.ANY),
            pl.BlockSpec(memory_space=pl.ANY),
        ],
        out_specs=pl.BlockSpec(memory_space=pltpu.VMEM),
        scratch_shapes=[
            pltpu.VMEM(weight.shape, weight.dtype),
            pltpu.VMEM((tokens.shape[0], weight.shape[1]), jnp.bfloat16),
            pltpu.VMEM((slots, rows, weight.shape[1]), jnp.bfloat16),
            pltpu.SemaphoreType.DMA((3 * count_x,)),
            pltpu.SemaphoreType.DMA((slots,)),
            pltpu.SemaphoreType.DMA(()),
            pltpu.VMEM((nx, ny_in, nz, channels), jnp.bfloat16),
            pltpu.VMEM(kernel_in.shape, kernel_in.dtype),
            pltpu.VMEM(kernel_out.shape, kernel_out.dtype),
            pltpu.SemaphoreType.DMA((2,)),
            pltpu.VMEM((nx + 2, ny_in, nz, channels), jnp.bfloat16),
            pltpu.VMEM((nx * ny, nz + 2, channels), jnp.float32),
            pltpu.VMEM((nx, ny, nz, channels), jnp.bfloat16),
            pltpu.VMEM((nx + 2, ny, nz, channels), jnp.bfloat16),
            pltpu.VMEM((nx * ny_out, nz + 2, outch), jnp.float32),
            pltpu.VMEM((2, count, block, (nx - 2) * ny_out * nz), jnp.float32),
            pltpu.VMEM((2, count, block, (nx - 2) * ny_out * nz), jnp.float32),
            pltpu.SemaphoreType.DMA((2,)),
            pltpu.SemaphoreType.DMA((2,)),
            pltpu.SemaphoreType.DMA((2,)),
            pltpu.SemaphoreType.DMA((2,)),
            pltpu.SemaphoreType.DMA((2, count)),
            pltpu.SemaphoreType.DMA((2, count)),
        ],
        compiler_params=pltpu.CompilerParams(collective_id=collective, has_side_effects=True),
    )(tokens, weight, gains, kernel_in, kernel_out)


def local(skips, deconv_weight, norm_gain, conv_in, conv_out):
    inl_size = lax.axis_size("inl")
    tokens_here = skips[0]
    weight = deconv_weight[0]
    gains = norm_gain[0]
    channels = gains.shape[1]
    cell_x = 2 * PXD
    cell_y = 2 * lax.axis_size("xln")
    cell_z = 2 * GZ
    assert tokens_here.shape[0] == inl_size * PXD * GZ
    taps, outch, channels_in = conv_out.shape[1:]
    out_weight = conv_out[0].reshape(taps // 3, 3 * outch, channels_in)
    return decoder_block(tokens_here, weight, gains, conv_in[0], out_weight, 3)


def solution(mesh):
    return jax.shard_map(
        local,
        mesh=mesh,
        in_specs=(
            P("section", ("inl", "xln"), None),
            P("section", None, None),
            P("section", None, None),
            P("section", None, None, None),
            P("section", None, None, None),
        ),
        out_specs=P("section", "inl", "xln"),
        check_vma=False,
    )
```

```python
import functools

import jax
import jax.numpy as jnp
from jax import lax
from jax.experimental import pallas as pl
from jax.experimental.pallas import tpu as pltpu
from jax.sharding import PartitionSpec as P

MESH = pl.DeviceIdType.MESH
PXD = 2
GZ = 8


epsilon = 1e-05


def gelu_tanh(values):
    return 0.5 * values * (1.0 + jnp.tanh(0.7978845608028654 * (values + 0.044715 * (values * values * values))))


def send_groups(me_x, me_y, count):
    return [
        (me_x, me_y + 1, None),
        (me_x + 1, 0, (me_y == count - 1) & (me_x + 1 < count)),
        (me_x - 1, count + 1, (me_y == 0) & (me_x > 0)),
    ]


def gather_kernel(
    tokens_ref, weight_hbm, gains_ref, out_ref, weight, field, held, send_sem, recv_sem, weight_sem, extra=0,
    hooks=None,
):
    count = lax.axis_size("inl")
    me_x, me_y = lax.axis_index("inl"), lax.axis_index("xln")
    rows = tokens_ref.shape[0] // count
    width = gains_ref.shape[1]
    one = jnp.int32(1)
    loading = pltpu.make_async_copy(weight_hbm, weight, weight_sem)
    loading.start()
    groups = send_groups(me_x, me_y, count)
    sources = [(me_y - 1, count - 1, me_y >= 1)]
    sources += [(me_y, other, None) for other in range(count)]
    sources += [(me_y + 1, 0, me_y + 1 < count)]

    def is_me(x, y):
        return (x == me_x) & (y == me_y)

    barrier = pltpu.get_barrier_semaphore()
    expected = jnp.int32(0)
    for column, _, exists in groups:
        live = True if exists is None else exists
        expected = expected + jnp.where(live, count, 0)
        for other in range(count):

            @pl.when(jnp.logical_and(live, jnp.logical_not(is_me(other, column))))
            def _():
                pl.semaphore_signal(barrier, inc=1, device_id={"inl": other, "xln": column}, device_id_type=MESH)

            expected = expected - jnp.where(jnp.logical_and(live, is_me(other, column)), one, 0)
    for source_x, source_y, exists in sources:
        live = True if exists is None else exists
        mine = jnp.logical_and(live, is_me(source_x, source_y))
        expected = expected + jnp.where(jnp.logical_and(live, jnp.logical_not(mine)), one, 0)

        @pl.when(jnp.logical_and(live, jnp.logical_not(mine)))
        def _():
            pl.semaphore_signal(barrier, inc=1, device_id={"inl": source_x, "xln": source_y}, device_id_type=MESH)

    loading.wait()
    upsampled = jnp.dot(tokens_ref[...], weight[...], preferred_element_type=jnp.float32)
    for group in range(upsampled.shape[1] // width):
        part = upsampled[:, group * width : (group + 1) * width]
        mean_square = jnp.mean(part * part, axis=-1, keepdims=True)
        normed = part * lax.rsqrt(mean_square + epsilon) * gains_ref[0:1, :]
        field[:, group * width : (group + 1) * width] = gelu_tanh(normed).astype(field.dtype)
    depth = 2 * (rows // 2)
    target = lax.broadcasted_iota(jnp.int32, (2 * rows, 2 * rows), 0)
    origin = lax.broadcasted_iota(jnp.int32, (2 * rows, 2 * rows), 1)
    half = rows // 2
    same = (
        (target // depth == (origin % rows) // half)
        & ((target % depth) // 2 == origin % half)
        & (target % 2 == origin // rows)
    )
    interleave = jnp.where(same, 1.0, 0.0).astype(jnp.bfloat16)

    def place(slot, block):
        for u in range(2):
            for v in range(2):
                first = ((u * 2 + v) * 2) * width
                pair = jnp.concatenate([block[:, first : first + width], block[:, first + width : first + 2 * width]], axis=0)
                cells = jnp.dot(interleave, pair, preferred_element_type=jnp.float32).astype(out_ref.dtype)
                for ix in range(2):
                    out_ref[2 * ix + u, 2 * slot + v] = cells[ix * depth : (ix + 1) * depth]

    pl.semaphore_wait(barrier, expected + extra)
    copies = []
    for index, (column, slot, exists) in enumerate(groups):
        live = True if exists is None else exists
        for turn in range(count):
            other = lax.rem(me_y + turn, count)
            copy = pltpu.make_async_remote_copy(
                src_ref=field.at[pl.ds(pl.multiple_of(other * rows, rows), rows)],
                dst_ref=held.at[slot],
                send_sem=send_sem.at[index * count + turn],
                recv_sem=recv_sem.at[slot],
                device_id={"inl": other, "xln": column},
                device_id_type=MESH,
            )
            remote = jnp.logical_and(live, jnp.logical_not(is_me(other, column)))

            @pl.when(remote)
            def _():
                copy.start()

            copies.append((copy, remote))
    for slot, (source_x, source_y, exists) in enumerate(sources):
        live = True if exists is None else exists
        mine = jnp.logical_and(live, is_me(source_x, source_y))
        remote = jnp.logical_and(live, jnp.logical_not(mine))
        incoming = pltpu.make_async_remote_copy(
            src_ref=field.at[pl.ds(0, rows)],
            dst_ref=held.at[slot],
            send_sem=send_sem.at[0],
            recv_sem=recv_sem.at[slot],
            device_id={"inl": source_x, "xln": source_y},
            device_id_type=MESH,
        )

        @pl.when(remote)
        def _():
            incoming.wait_recv()
            place(slot, held[slot])

        @pl.when(mine)
        def _():
            place(slot, field[pl.ds(pl.multiple_of(me_x * rows, rows), rows)])

        @pl.when(jnp.logical_not(live))
        def _():
            out_ref[:, 2 * slot : 2 * slot + 2] = jnp.zeros(
                (out_ref.shape[0], 2) + out_ref.shape[2:], out_ref.dtype
            )

        if hooks and "each" in hooks:
            hooks["each"](slot)
        if hooks and slot in hooks:
            hooks[slot]()

    for copy, remote in copies:

        @pl.when(remote)
        def _():
            copy.wait_send()


def halo_signal():
    count = lax.axis_size("inl")
    me = lax.axis_index("inl")
    for step in (-1, 1):

        @pl.when((me + step >= 0) & (me + step < count))
        def _():
            pl.semaphore_signal(
                pltpu.get_barrier_semaphore(), inc=1, device_id={"inl": me + step}, device_id_type=MESH
            )

    return (me > 0).astype(jnp.int32) + (me < count - 1).astype(jnp.int32)


def halo_start(field_ref, held, send_sem, recv_sem, start=True, steps=(-1, 1)):
    nx = field_ref.shape[0]
    count = lax.axis_size("inl")
    me = lax.axis_index("inl")
    copies = []
    for step in steps:
        index = 0 if step < 0 else 1
        source, target = (0, nx + 1) if step < 0 else (nx - 1, 0)
        copy = pltpu.make_async_remote_copy(
            src_ref=field_ref.at[source : source + 1],
            dst_ref=held.at[target : target + 1],
            send_sem=send_sem.at[index],
            recv_sem=recv_sem.at[index],
            device_id={"inl": me + step},
            device_id_type=MESH,
        )
        sends = (me + step >= 0) & (me + step < count)
        gets = (me - step >= 0) & (me - step < count)

        if start:

            @pl.when(sends)
            def _():
                copy.start()

        @pl.when(jnp.logical_not(gets))
        def _():
            held[target : target + 1] = jnp.zeros((1,) + held.shape[1:], held.dtype)

        copies.append((copy, sends, gets))
    return copies


def halo_finish(copies):
    for copy, sends, gets in copies:

        @pl.when(gets)
        def _():
            copy.wait_recv()

        @pl.when(sends)
        def _():
            copy.wait_send()


def conv_in_rows(field_ref, kernel_in_ref, gains_ref, held, shifted, mixed):
    nx, ny_in, nz, channels = field_ref.shape
    ny = ny_in - 2
    me_y, count_y = lax.axis_index("xln"), lax.axis_size("xln")

    def inner_taps(first, last, offsets_x, low=0, high=ny):
        cells = (last - first) * (high - low) * nz
        parts_in = []
        for offset_z in range(3):
            part = jnp.zeros((cells, channels), jnp.float32)
            for offset_x in offsets_x:
                for offset_y in range(3):
                    window = held[first + offset_x : last + offset_x, low + offset_y : high + offset_y].reshape(
                        cells, channels
                    )
                    tap = kernel_in_ref[(offset_x * 3 + offset_y) * 3 + offset_z]
                    part = part + jnp.dot(window, tap, preferred_element_type=jnp.float32)
            parts_in.append(part)
        return parts_in

    def inner_rows(first, last, parts_in, low=0, high=ny):
        rows = last - first
        planes = rows * (high - low)
        parts_in = [part.reshape(planes, nz, channels) for part in parts_in]
        shifted[0:planes, 1 : nz + 1] = parts_in[0]
        total = parts_in[1] + shifted[0:planes, 0:nz]
        shifted[0:planes, 1 : nz + 1] = parts_in[2]
        total = total + shifted[0:planes, 2 : nz + 2]
        mean_square = jnp.mean(total * total, axis=-1, keepdims=True)
        normed = total * lax.rsqrt(mean_square + epsilon) * gains_ref[1:2, :]
        base = field_ref[first:last, 1 + low : 1 + high].reshape(planes, nz, channels).astype(jnp.float32)
        activated = gelu_tanh(normed + base).reshape(rows, high - low, nz, channels)
        row = low + lax.broadcasted_iota(jnp.int32, activated.shape, 1)
        outside = ((row == 0) & (me_y == 0)) | ((row == ny - 1) & (me_y == count_y - 1))
        mixed[first:last, low:high] = jnp.where(outside, 0.0, activated).astype(mixed.dtype)

    return inner_taps, inner_rows


def entry_signals():
    count = lax.axis_size("section")
    me = lax.axis_index("section")
    for step in range(1, count):
        pl.semaphore_signal(
            pltpu.get_barrier_semaphore(),
            inc=1,
            device_id={"section": lax.rem(me + step, count)},
            device_id_type=MESH,
        )
    return halo_signal() + count - 1


def block_kernel(
    merged, done, field_ref, kernel_in_ref, gains_ref, kernel_out_ref, out_ref,
    held, shifted, mixed, held_out, shifted_out, parts, inbox,
    send_sem, recv_sem, send_out, recv_out, sum_send, sum_recv,
):
    count = lax.axis_size("section")
    me = lax.axis_index("section")
    barrier = pltpu.get_barrier_semaphore()
    if not merged:
        expected = entry_signals()
    nx, ny_in, nz, channels = field_ref.shape
    ny = ny_in - 2
    ny_out = ny - 2
    outch = kernel_out_ref.shape[1] // 3
    me_y, count_y = lax.axis_index("xln"), lax.axis_size("xln")
    if not done:
        edge = jnp.zeros((nx * ny, 1, channels), jnp.float32)
        shifted[:, 0:1] = edge
        shifted[:, nz + 1 : nz + 2] = edge
        held[1 : nx + 1] = field_ref[...]
    else:
        held[1 : nx + 1, done + 2 :] = field_ref[:, done + 2 :]

    inner_taps, inner_rows = conv_in_rows(field_ref, kernel_in_ref, gains_ref, held, shifted, mixed)

    def outer_rows(first, last, offsets_x=(0, 1, 2)):
        cells = (last - first) * ny_out * nz
        by_depth = jnp.zeros((cells, 3 * outch), jnp.float32)
        for offset_x in offsets_x:
            for offset_y in range(3):
                window = held_out[first + offset_x : last + offset_x, offset_y : offset_y + ny_out].reshape(
                    cells, channels
                )
                by_depth = by_depth + lax.dot_general(
                    window,
                    kernel_out_ref[offset_x * 3 + offset_y],
                    (((1,), (1,)), ((), ())),
                    preferred_element_type=jnp.float32,
                )
        return by_depth

    if merged:
        first_halo = halo_start(field_ref, held, send_sem, recv_sem, start=False)
    inner_rows(1, nx - 1, inner_taps(1, nx - 1, (0, 1, 2), done, ny), done, ny)
    low = inner_taps(0, 1, (1, 2))
    high = inner_taps(nx - 1, nx, (0, 1))
    if not merged:
        pl.semaphore_wait(barrier, expected)
        first_halo = halo_start(field_ref, held, send_sem, recv_sem)
    halo_finish(first_halo)
    inner_rows(0, 1, [a + b for a, b in zip(low, inner_taps(0, 1, (0,)))])
    second_halo = halo_start(mixed, held_out, send_out, recv_out, steps=(-1,))
    inner_rows(nx - 1, nx, [a + b for a, b in zip(high, inner_taps(nx - 1, nx, (2,)))])
    second_halo += halo_start(mixed, held_out, send_out, recv_out, steps=(1,))

    edge = jnp.zeros((nx * ny_out, 1, outch), jnp.float32)
    shifted_out[:, 0:1] = edge
    shifted_out[:, nz + 1 : nz + 2] = edge

    def by_channel(by_depth, rows):
        planes = rows * ny_out
        shifted_out[0:planes, 1 : nz + 1] = by_depth[:, 0:outch].reshape(planes, nz, outch)
        summed = by_depth[:, outch : 2 * outch].reshape(planes, nz, outch) + shifted_out[0:planes, 0:nz]
        shifted_out[0:planes, 1 : nz + 1] = by_depth[:, 2 * outch : 3 * outch].reshape(planes, nz, outch)
        summed = summed + shifted_out[0:planes, 2 : nz + 2]
        return summed.reshape(planes * nz, outch).T

    block = outch // count

    def share(phase, values):
        for peer in range(count):
            parts[phase, peer] = values[peer * block : (peer + 1) * block]
        sends = []
        for step in range(1, count):
            peer = lax.rem(me + step, count)
            copy = pltpu.make_async_remote_copy(
                src_ref=parts.at[phase, peer],
                dst_ref=inbox.at[phase, step],
                send_sem=sum_send.at[phase, step],
                recv_sem=sum_recv.at[phase, step],
                device_id={"section": peer},
                device_id_type=MESH,
            )
            copy.start()
            sends.append(copy)
        return sends

    def gather(phase, sends):
        result = parts[phase, me]
        for step in range(1, count):
            sends[step - 1].wait_recv()
            result = result + inbox[phase, step]
        for copy in sends:
            copy.wait_send()
        return result

    held_out[1 : nx + 1] = mixed[...]
    middle_sends = share(0, by_channel(outer_rows(1, nx - 1), nx - 2))
    low_out = outer_rows(0, 1, (1, 2))
    high_out = outer_rows(nx - 1, nx, (0, 1))
    halo_finish(second_halo)
    row_cells = ny_out * nz
    ends = jnp.concatenate(
        [
            by_channel(low_out + outer_rows(0, 1, (0,)), 1),
            by_channel(high_out + outer_rows(nx - 1, nx, (2,)), 1),
        ],
        axis=1,
    )
    end_sends = share(1, ends)
    middle = gather(0, middle_sends)
    ends = gather(1, end_sends)
    result = jnp.concatenate([ends[:, 0:row_cells], middle, ends[:, row_cells:]], axis=1)
    out_ref[...] = result.reshape(out_ref.shape).astype(out_ref.dtype)


def whole_kernel(tokens_ref, weight_hbm, gains_ref, kernel_in_hbm, kernel_out_hbm, out_ref, *scratch):
    weight, field, rows_in, send_rows, recv_rows, weight_sem = scratch[:6]
    brick, kernel_in, kernel_out, kernel_sem = scratch[6:10]
    loads = [
        pltpu.make_async_copy(kernel_in_hbm, kernel_in, kernel_sem.at[0]),
        pltpu.make_async_copy(kernel_out_hbm, kernel_out, kernel_sem.at[1]),
    ]
    for load in loads:
        load.start()
    extra = entry_signals()
    held, shifted, mixed = scratch[10:13]
    nx, ny_in, nz, channels = brick.shape
    done = ny_in // 2
    inner_taps, inner_rows = conv_in_rows(brick, kernel_in, gains_ref, held, shifted, mixed)

    def early():
        loads[0].wait()
        edge = jnp.zeros((shifted.shape[0], 1, channels), jnp.float32)
        shifted[:, 0:1] = edge
        shifted[:, nz + 1 : nz + 2] = edge
        held[1 : nx + 1, 0 : done + 2] = brick[:, 0 : done + 2]
        inner_rows(1, nx - 1, inner_taps(1, nx - 1, (0, 1, 2), 0, done), 0, done)

    send_halo, recv_halo = scratch[17], scratch[18]
    count_x = lax.axis_size("inl")
    me_x = lax.axis_index("inl")

    def edge_rows(slot):
        for index, step in enumerate((-1, 1)):
            source, target = (0, nx + 1) if step < 0 else (nx - 1, 0)
            rows = pl.ds(2 * slot, 2)
            copy = pltpu.make_async_remote_copy(
                src_ref=brick.at[source : source + 1, rows],
                dst_ref=held.at[target : target + 1, rows],
                send_sem=send_halo.at[index],
                recv_sem=recv_halo.at[index],
                device_id={"inl": me_x + step},
                device_id_type=MESH,
            )

            @pl.when((me_x + step >= 0) & (me_x + step < count_x))
            def _():
                copy.start()

    gather_kernel(
        tokens_ref, weight_hbm, gains_ref, brick, weight, field, rows_in, send_rows, recv_rows, weight_sem, extra,
        {done // 2: early, "each": edge_rows},
    )
    loads[1].wait()
    block_kernel(True, done, brick, kernel_in, gains_ref, kernel_out, out_ref, *scratch[10:])


def decoder_block(tokens, weight, gains, kernel_in, kernel_out, collective):
    count_x = lax.axis_size("inl")
    rows = tokens.shape[0] // count_x
    slots = lax.axis_size("xln") + 2
    nx, ny_in, nz, channels = 2 * PXD, 2 * slots, 2 * GZ, gains.shape[1]
    ny = ny_in - 2
    ny_out = ny - 2
    count = lax.axis_size("section")
    outch = kernel_out.shape[1] // 3
    block = outch // count
    return pl.pallas_call(
        whole_kernel,
        out_shape=jax.ShapeDtypeStruct((block, nx, ny_out * nz), jnp.float32),
        in_specs=[
            pl.BlockSpec(memory_space=pltpu.VMEM),
            pl.BlockSpec(memory_space=pl.ANY),
            pl.BlockSpec(memory_space=pltpu.VMEM),
            pl.BlockSpec(memory_space=pl.ANY),
            pl.BlockSpec(memory_space=pl.ANY),
        ],
        out_specs=pl.BlockSpec(memory_space=pltpu.VMEM),
        scratch_shapes=[
            pltpu.VMEM(weight.shape, weight.dtype),
            pltpu.VMEM((tokens.shape[0], weight.shape[1]), jnp.bfloat16),
            pltpu.VMEM((slots, rows, weight.shape[1]), jnp.bfloat16),
            pltpu.SemaphoreType.DMA((3 * count_x,)),
            pltpu.SemaphoreType.DMA((slots,)),
            pltpu.SemaphoreType.DMA(()),
            pltpu.VMEM((nx, ny_in, nz, channels), jnp.bfloat16),
            pltpu.VMEM(kernel_in.shape, kernel_in.dtype),
            pltpu.VMEM(kernel_out.shape, kernel_out.dtype),
            pltpu.SemaphoreType.DMA((2,)),
            pltpu.VMEM((nx + 2, ny_in, nz, channels), jnp.bfloat16),
            pltpu.VMEM((nx * ny, nz + 2, channels), jnp.float32),
            pltpu.VMEM((nx, ny, nz, channels), jnp.bfloat16),
            pltpu.VMEM((nx + 2, ny, nz, channels), jnp.bfloat16),
            pltpu.VMEM((nx * ny_out, nz + 2, outch), jnp.float32),
            pltpu.VMEM((2, count, block, (nx - 2) * ny_out * nz), jnp.float32),
            pltpu.VMEM((2, count, block, (nx - 2) * ny_out * nz), jnp.float32),
            pltpu.SemaphoreType.DMA((2,)),
            pltpu.SemaphoreType.DMA((2,)),
            pltpu.SemaphoreType.DMA((2,)),
            pltpu.SemaphoreType.DMA((2,)),
            pltpu.SemaphoreType.DMA((2, count)),
            pltpu.SemaphoreType.DMA((2, count)),
        ],
        compiler_params=pltpu.CompilerParams(collective_id=collective, has_side_effects=True),
    )(tokens, weight, gains, kernel_in, kernel_out)


def local(skips, deconv_weight, norm_gain, conv_in, conv_out):
    inl_size = lax.axis_size("inl")
    tokens_here = skips[0]
    weight = deconv_weight[0]
    gains = norm_gain[0]
    channels = gains.shape[1]
    cell_x = 2 * PXD
    cell_y = 2 * lax.axis_size("xln")
    cell_z = 2 * GZ
    assert tokens_here.shape[0] == inl_size * PXD * GZ
    taps, outch, channels_in = conv_out.shape[1:]
    out_weight = conv_out[0].reshape(taps // 3, 3 * outch, channels_in)
    return decoder_block(tokens_here, weight, gains, conv_in[0], out_weight, 3).astype(jnp.bfloat16)


def solution(mesh):
    return jax.shard_map(
        local,
        mesh=mesh,
        in_specs=(
            P("section", ("inl", "xln"), None),
            P("section", None, None),
            P("section", None, None),
            P("section", None, None, None),
            P("section", None, None, None),
        ),
        out_specs=P("section", "inl", "xln"),
        check_vma=False,
    )
```

```python
import functools

import jax
import jax.numpy as jnp
from jax import lax
from jax.experimental import pallas as pl
from jax.experimental.pallas import tpu as pltpu
from jax.sharding import PartitionSpec as P

MESH = pl.DeviceIdType.MESH
PXD = 2
GZ = 8


epsilon = 1e-05


def gelu_tanh(values):
    return 0.5 * values * (1.0 + jnp.tanh(0.7978845608028654 * (values + 0.044715 * (values * values * values))))


def send_groups(me_x, me_y, count):
    return [
        (me_x, me_y + 1, None),
        (me_x + 1, 0, (me_y == count - 1) & (me_x + 1 < count)),
        (me_x - 1, count + 1, (me_y == 0) & (me_x > 0)),
    ]


def gather_kernel(
    tokens_ref, weight_hbm, gains_ref, out_ref, weight, field, held, send_sem, recv_sem, weight_sem, extra=0,
    hooks=None,
):
    count = lax.axis_size("inl")
    me_x, me_y = lax.axis_index("inl"), lax.axis_index("xln")
    rows = tokens_ref.shape[0] // count
    width = gains_ref.shape[1]
    one = jnp.int32(1)
    loading = pltpu.make_async_copy(weight_hbm, weight, weight_sem)
    loading.start()
    groups = send_groups(me_x, me_y, count)
    sources = [(me_y - 1, count - 1, me_y >= 1)]
    sources += [(me_y, other, None) for other in range(count)]
    sources += [(me_y + 1, 0, me_y + 1 < count)]

    def is_me(x, y):
        return (x == me_x) & (y == me_y)

    barrier = pltpu.get_barrier_semaphore()
    expected = jnp.int32(0)
    for column, _, exists in groups:
        live = True if exists is None else exists
        expected = expected + jnp.where(live, count, 0)
        for other in range(count):

            @pl.when(jnp.logical_and(live, jnp.logical_not(is_me(other, column))))
            def _():
                pl.semaphore_signal(barrier, inc=1, device_id={"inl": other, "xln": column}, device_id_type=MESH)

            expected = expected - jnp.where(jnp.logical_and(live, is_me(other, column)), one, 0)
    for source_x, source_y, exists in sources:
        live = True if exists is None else exists
        mine = jnp.logical_and(live, is_me(source_x, source_y))
        expected = expected + jnp.where(jnp.logical_and(live, jnp.logical_not(mine)), one, 0)

        @pl.when(jnp.logical_and(live, jnp.logical_not(mine)))
        def _():
            pl.semaphore_signal(barrier, inc=1, device_id={"inl": source_x, "xln": source_y}, device_id_type=MESH)

    loading.wait()
    upsampled = jnp.dot(tokens_ref[...], weight[...], preferred_element_type=jnp.float32)
    for group in range(upsampled.shape[1] // width):
        part = upsampled[:, group * width : (group + 1) * width]
        mean_square = jnp.mean(part * part, axis=-1, keepdims=True)
        normed = part * lax.rsqrt(mean_square + epsilon) * gains_ref[0:1, :]
        field[:, group * width : (group + 1) * width] = gelu_tanh(normed).astype(field.dtype)
    depth = 2 * (rows // 2)
    target = lax.broadcasted_iota(jnp.int32, (2 * rows, 2 * rows), 0)
    origin = lax.broadcasted_iota(jnp.int32, (2 * rows, 2 * rows), 1)
    half = rows // 2
    same = (
        (target // depth == (origin % rows) // half)
        & ((target % depth) // 2 == origin % half)
        & (target % 2 == origin // rows)
    )
    interleave = jnp.where(same, 1.0, 0.0).astype(jnp.bfloat16)

    def place(slot, block):
        pairs = jnp.concatenate(
            [
                jnp.concatenate(
                    [block[:, ((u * 2 + v) * 2 + w) * width : ((u * 2 + v) * 2 + w + 1) * width] for u in range(2) for v in range(2)],
                    axis=1,
                )
                for w in range(2)
            ],
            axis=0,
        )
        cells = jnp.dot(interleave, pairs, preferred_element_type=jnp.float32).astype(out_ref.dtype)
        for u in range(2):
            for v in range(2):
                column = (u * 2 + v) * width
                for ix in range(2):
                    out_ref[2 * ix + u, 2 * slot + v] = cells[ix * depth : (ix + 1) * depth, column : column + width]

    pl.semaphore_wait(barrier, expected + extra)
    copies = []
    for index, (column, slot, exists) in enumerate(groups):
        live = True if exists is None else exists
        for turn in range(count):
            other = lax.rem(me_y + turn, count)
            copy = pltpu.make_async_remote_copy(
                src_ref=field.at[pl.ds(pl.multiple_of(other * rows, rows), rows)],
                dst_ref=held.at[slot],
                send_sem=send_sem.at[index * count + turn],
                recv_sem=recv_sem.at[slot],
                device_id={"inl": other, "xln": column},
                device_id_type=MESH,
            )
            remote = jnp.logical_and(live, jnp.logical_not(is_me(other, column)))

            @pl.when(remote)
            def _():
                copy.start()

            copies.append((copy, remote))
    for slot, (source_x, source_y, exists) in enumerate(sources):
        live = True if exists is None else exists
        mine = jnp.logical_and(live, is_me(source_x, source_y))
        remote = jnp.logical_and(live, jnp.logical_not(mine))
        incoming = pltpu.make_async_remote_copy(
            src_ref=field.at[pl.ds(0, rows)],
            dst_ref=held.at[slot],
            send_sem=send_sem.at[0],
            recv_sem=recv_sem.at[slot],
            device_id={"inl": source_x, "xln": source_y},
            device_id_type=MESH,
        )

        @pl.when(remote)
        def _():
            incoming.wait_recv()
            place(slot, held[slot])

        @pl.when(mine)
        def _():
            place(slot, field[pl.ds(pl.multiple_of(me_x * rows, rows), rows)])

        @pl.when(jnp.logical_not(live))
        def _():
            out_ref[:, 2 * slot : 2 * slot + 2] = jnp.zeros(
                (out_ref.shape[0], 2) + out_ref.shape[2:], out_ref.dtype
            )

        if hooks and "each" in hooks:
            hooks["each"](slot)
        if hooks and slot in hooks:
            hooks[slot]()

    for copy, remote in copies:

        @pl.when(remote)
        def _():
            copy.wait_send()


def halo_signal():
    count = lax.axis_size("inl")
    me = lax.axis_index("inl")
    for step in (-1, 1):

        @pl.when((me + step >= 0) & (me + step < count))
        def _():
            pl.semaphore_signal(
                pltpu.get_barrier_semaphore(), inc=1, device_id={"inl": me + step}, device_id_type=MESH
            )

    return (me > 0).astype(jnp.int32) + (me < count - 1).astype(jnp.int32)


def halo_start(field_ref, held, send_sem, recv_sem, start=True, steps=(-1, 1)):
    nx = field_ref.shape[0]
    count = lax.axis_size("inl")
    me = lax.axis_index("inl")
    copies = []
    for step in steps:
        index = 0 if step < 0 else 1
        source, target = (0, nx + 1) if step < 0 else (nx - 1, 0)
        copy = pltpu.make_async_remote_copy(
            src_ref=field_ref.at[source : source + 1],
            dst_ref=held.at[target : target + 1],
            send_sem=send_sem.at[index],
            recv_sem=recv_sem.at[index],
            device_id={"inl": me + step},
            device_id_type=MESH,
        )
        sends = (me + step >= 0) & (me + step < count)
        gets = (me - step >= 0) & (me - step < count)

        if start:

            @pl.when(sends)
            def _():
                copy.start()

        @pl.when(jnp.logical_not(gets))
        def _():
            held[target : target + 1] = jnp.zeros((1,) + held.shape[1:], held.dtype)

        copies.append((copy, sends, gets))
    return copies


def halo_finish(copies):
    for copy, sends, gets in copies:

        @pl.when(gets)
        def _():
            copy.wait_recv()

        @pl.when(sends)
        def _():
            copy.wait_send()


def conv_in_rows(field_ref, kernel_in_ref, gains_ref, held, shifted, mixed):
    nx, ny_in, nz, channels = field_ref.shape
    ny = ny_in - 2
    me_y, count_y = lax.axis_index("xln"), lax.axis_size("xln")

    def inner_taps(first, last, offsets_x, low=0, high=ny):
        cells = (last - first) * (high - low) * nz
        parts_in = []
        for offset_z in range(3):
            part = jnp.zeros((cells, channels), jnp.float32)
            for offset_x in offsets_x:
                for offset_y in range(3):
                    window = held[first + offset_x : last + offset_x, low + offset_y : high + offset_y].reshape(
                        cells, channels
                    )
                    tap = kernel_in_ref[(offset_x * 3 + offset_y) * 3 + offset_z]
                    part = part + jnp.dot(window, tap, preferred_element_type=jnp.float32)
            parts_in.append(part)
        return parts_in

    def inner_rows(first, last, parts_in, low=0, high=ny):
        rows = last - first
        planes = rows * (high - low)
        parts_in = [part.reshape(planes, nz, channels) for part in parts_in]
        shifted[0:planes, 1 : nz + 1] = parts_in[0]
        total = parts_in[1] + shifted[0:planes, 0:nz]
        shifted[0:planes, 1 : nz + 1] = parts_in[2]
        total = total + shifted[0:planes, 2 : nz + 2]
        mean_square = jnp.mean(total * total, axis=-1, keepdims=True)
        normed = total * lax.rsqrt(mean_square + epsilon) * gains_ref[1:2, :]
        base = field_ref[first:last, 1 + low : 1 + high].reshape(planes, nz, channels).astype(jnp.float32)
        activated = gelu_tanh(normed + base).reshape(rows, high - low, nz, channels)
        row = low + lax.broadcasted_iota(jnp.int32, activated.shape, 1)
        outside = ((row == 0) & (me_y == 0)) | ((row == ny - 1) & (me_y == count_y - 1))
        mixed[first:last, low:high] = jnp.where(outside, 0.0, activated).astype(mixed.dtype)

    return inner_taps, inner_rows


def entry_signals():
    count = lax.axis_size("section")
    me = lax.axis_index("section")
    for step in range(1, count):
        pl.semaphore_signal(
            pltpu.get_barrier_semaphore(),
            inc=1,
            device_id={"section": lax.rem(me + step, count)},
            device_id_type=MESH,
        )
    return halo_signal() + count - 1


def block_kernel(
    merged, done, field_ref, kernel_in_ref, gains_ref, kernel_out_ref, out_ref,
    held, shifted, mixed, held_out, shifted_out, parts, inbox,
    send_sem, recv_sem, send_out, recv_out, sum_send, sum_recv,
):
    count = lax.axis_size("section")
    me = lax.axis_index("section")
    barrier = pltpu.get_barrier_semaphore()
    if not merged:
        expected = entry_signals()
    nx, ny_in, nz, channels = field_ref.shape
    ny = ny_in - 2
    ny_out = ny - 2
    outch = kernel_out_ref.shape[1] // 3
    me_y, count_y = lax.axis_index("xln"), lax.axis_size("xln")
    if not done:
        edge = jnp.zeros((nx * ny, 1, channels), jnp.float32)
        shifted[:, 0:1] = edge
        shifted[:, nz + 1 : nz + 2] = edge
        held[1 : nx + 1] = field_ref[...]
    else:
        held[1 : nx + 1, done + 2 :] = field_ref[:, done + 2 :]

    inner_taps, inner_rows = conv_in_rows(field_ref, kernel_in_ref, gains_ref, held, shifted, mixed)

    def outer_rows(first, last, offsets_x=(0, 1, 2)):
        cells = (last - first) * ny_out * nz
        by_depth = jnp.zeros((cells, 3 * outch), jnp.float32)
        for offset_x in offsets_x:
            for offset_y in range(3):
                window = held_out[first + offset_x : last + offset_x, offset_y : offset_y + ny_out].reshape(
                    cells, channels
                )
                by_depth = by_depth + lax.dot_general(
                    window,
                    kernel_out_ref[offset_x * 3 + offset_y],
                    (((1,), (1,)), ((), ())),
                    preferred_element_type=jnp.float32,
                )
        return by_depth

    if merged:
        first_halo = halo_start(field_ref, held, send_sem, recv_sem, start=False)
    inner_rows(1, nx - 1, inner_taps(1, nx - 1, (0, 1, 2), done, ny), done, ny)
    low = inner_taps(0, 1, (1, 2))
    high = inner_taps(nx - 1, nx, (0, 1))
    if not merged:
        pl.semaphore_wait(barrier, expected)
        first_halo = halo_start(field_ref, held, send_sem, recv_sem)
    halo_finish(first_halo)
    inner_rows(0, 1, [a + b for a, b in zip(low, inner_taps(0, 1, (0,)))])
    second_halo = halo_start(mixed, held_out, send_out, recv_out, steps=(-1,))
    inner_rows(nx - 1, nx, [a + b for a, b in zip(high, inner_taps(nx - 1, nx, (2,)))])
    second_halo += halo_start(mixed, held_out, send_out, recv_out, steps=(1,))

    edge = jnp.zeros((nx * ny_out, 1, outch), jnp.float32)
    shifted_out[:, 0:1] = edge
    shifted_out[:, nz + 1 : nz + 2] = edge

    def by_channel(by_depth, rows):
        planes = rows * ny_out
        shifted_out[0:planes, 1 : nz + 1] = by_depth[:, 0:outch].reshape(planes, nz, outch)
        summed = by_depth[:, outch : 2 * outch].reshape(planes, nz, outch) + shifted_out[0:planes, 0:nz]
        shifted_out[0:planes, 1 : nz + 1] = by_depth[:, 2 * outch : 3 * outch].reshape(planes, nz, outch)
        summed = summed + shifted_out[0:planes, 2 : nz + 2]
        return summed.reshape(planes * nz, outch).T

    block = outch // count

    def share(phase, values):
        for peer in range(count):
            parts[phase, peer] = values[peer * block : (peer + 1) * block]
        sends = []
        for step in range(1, count):
            peer = lax.rem(me + step, count)
            copy = pltpu.make_async_remote_copy(
                src_ref=parts.at[phase, peer],
                dst_ref=inbox.at[phase, step],
                send_sem=sum_send.at[phase, step],
                recv_sem=sum_recv.at[phase, step],
                device_id={"section": peer},
                device_id_type=MESH,
            )
            copy.start()
            sends.append(copy)
        return sends

    def gather(phase, sends):
        result = parts[phase, me]
        for step in range(1, count):
            sends[step - 1].wait_recv()
            result = result + inbox[phase, step]
        for copy in sends:
            copy.wait_send()
        return result

    held_out[1 : nx + 1] = mixed[...]
    middle_sends = share(0, by_channel(outer_rows(1, nx - 1), nx - 2))
    low_out = outer_rows(0, 1, (1, 2))
    high_out = outer_rows(nx - 1, nx, (0, 1))
    halo_finish(second_halo)
    row_cells = ny_out * nz
    ends = jnp.concatenate(
        [
            by_channel(low_out + outer_rows(0, 1, (0,)), 1),
            by_channel(high_out + outer_rows(nx - 1, nx, (2,)), 1),
        ],
        axis=1,
    )
    end_sends = share(1, ends)
    middle = gather(0, middle_sends)
    ends = gather(1, end_sends)
    result = jnp.concatenate([ends[:, 0:row_cells], middle, ends[:, row_cells:]], axis=1)
    out_ref[...] = result.reshape(out_ref.shape).astype(out_ref.dtype)


def whole_kernel(tokens_ref, weight_hbm, gains_ref, kernel_in_hbm, kernel_out_hbm, out_ref, *scratch):
    weight, field, rows_in, send_rows, recv_rows, weight_sem = scratch[:6]
    brick, kernel_in, kernel_out, kernel_sem = scratch[6:10]
    loads = [
        pltpu.make_async_copy(kernel_in_hbm, kernel_in, kernel_sem.at[0]),
        pltpu.make_async_copy(kernel_out_hbm, kernel_out, kernel_sem.at[1]),
    ]
    for load in loads:
        load.start()
    extra = entry_signals()
    held, shifted, mixed = scratch[10:13]
    nx, ny_in, nz, channels = brick.shape
    done = ny_in // 2
    inner_taps, inner_rows = conv_in_rows(brick, kernel_in, gains_ref, held, shifted, mixed)

    def early():
        loads[0].wait()
        edge = jnp.zeros((shifted.shape[0], 1, channels), jnp.float32)
        shifted[:, 0:1] = edge
        shifted[:, nz + 1 : nz + 2] = edge
        held[1 : nx + 1, 0 : done + 2] = brick[:, 0 : done + 2]
        inner_rows(1, nx - 1, inner_taps(1, nx - 1, (0, 1, 2), 0, done), 0, done)

    send_halo, recv_halo = scratch[17], scratch[18]
    count_x = lax.axis_size("inl")
    me_x = lax.axis_index("inl")

    def edge_rows(slot):
        for index, step in enumerate((-1, 1)):
            source, target = (0, nx + 1) if step < 0 else (nx - 1, 0)
            rows = pl.ds(2 * slot, 2)
            copy = pltpu.make_async_remote_copy(
                src_ref=brick.at[source : source + 1, rows],
                dst_ref=held.at[target : target + 1, rows],
                send_sem=send_halo.at[index],
                recv_sem=recv_halo.at[index],
                device_id={"inl": me_x + step},
                device_id_type=MESH,
            )

            @pl.when((me_x + step >= 0) & (me_x + step < count_x))
            def _():
                copy.start()

    gather_kernel(
        tokens_ref, weight_hbm, gains_ref, brick, weight, field, rows_in, send_rows, recv_rows, weight_sem, extra,
        {done // 2: early, "each": edge_rows},
    )
    loads[1].wait()
    block_kernel(True, done, brick, kernel_in, gains_ref, kernel_out, out_ref, *scratch[10:])


def decoder_block(tokens, weight, gains, kernel_in, kernel_out, collective):
    count_x = lax.axis_size("inl")
    rows = tokens.shape[0] // count_x
    slots = lax.axis_size("xln") + 2
    nx, ny_in, nz, channels = 2 * PXD, 2 * slots, 2 * GZ, gains.shape[1]
    ny = ny_in - 2
    ny_out = ny - 2
    count = lax.axis_size("section")
    outch = kernel_out.shape[1] // 3
    block = outch // count
    return pl.pallas_call(
        whole_kernel,
        out_shape=jax.ShapeDtypeStruct((block, nx, ny_out * nz), jnp.bfloat16),
        in_specs=[
            pl.BlockSpec(memory_space=pltpu.VMEM),
            pl.BlockSpec(memory_space=pl.ANY),
            pl.BlockSpec(memory_space=pltpu.VMEM),
            pl.BlockSpec(memory_space=pl.ANY),
            pl.BlockSpec(memory_space=pl.ANY),
        ],
        out_specs=pl.BlockSpec(memory_space=pltpu.VMEM),
        scratch_shapes=[
            pltpu.VMEM(weight.shape, weight.dtype),
            pltpu.VMEM((tokens.shape[0], weight.shape[1]), jnp.bfloat16),
            pltpu.VMEM((slots, rows, weight.shape[1]), jnp.bfloat16),
            pltpu.SemaphoreType.DMA((3 * count_x,)),
            pltpu.SemaphoreType.DMA((slots,)),
            pltpu.SemaphoreType.DMA(()),
            pltpu.VMEM((nx, ny_in, nz, channels), jnp.bfloat16),
            pltpu.VMEM(kernel_in.shape, kernel_in.dtype),
            pltpu.VMEM(kernel_out.shape, kernel_out.dtype),
            pltpu.SemaphoreType.DMA((2,)),
            pltpu.VMEM((nx + 2, ny_in, nz, channels), jnp.bfloat16),
            pltpu.VMEM((nx * ny, nz + 2, channels), jnp.float32),
            pltpu.VMEM((nx, ny, nz, channels), jnp.bfloat16),
            pltpu.VMEM((nx + 2, ny, nz, channels), jnp.bfloat16),
            pltpu.VMEM((nx * ny_out, nz + 2, outch), jnp.float32),
            pltpu.VMEM((2, count, block, (nx - 2) * ny_out * nz), jnp.float32),
            pltpu.VMEM((2, count, block, (nx - 2) * ny_out * nz), jnp.float32),
            pltpu.SemaphoreType.DMA((2,)),
            pltpu.SemaphoreType.DMA((2,)),
            pltpu.SemaphoreType.DMA((2,)),
            pltpu.SemaphoreType.DMA((2,)),
            pltpu.SemaphoreType.DMA((2, count)),
            pltpu.SemaphoreType.DMA((2, count)),
        ],
        compiler_params=pltpu.CompilerParams(collective_id=collective, has_side_effects=True),
    )(tokens, weight, gains, kernel_in, kernel_out)


def local(skips, deconv_weight, norm_gain, conv_in, conv_out):
    inl_size = lax.axis_size("inl")
    tokens_here = skips[0]
    weight = deconv_weight[0]
    gains = norm_gain[0]
    channels = gains.shape[1]
    cell_x = 2 * PXD
    cell_y = 2 * lax.axis_size("xln")
    cell_z = 2 * GZ
    assert tokens_here.shape[0] == inl_size * PXD * GZ
    taps, outch, channels_in = conv_out.shape[1:]
    out_weight = conv_out[0].reshape(taps // 3, 3 * outch, channels_in)
    return decoder_block(tokens_here, weight, gains, conv_in[0], out_weight, 3)


def solution(mesh):
    return jax.shard_map(
        local,
        mesh=mesh,
        in_specs=(
            P("section", ("inl", "xln"), None),
            P("section", None, None),
            P("section", None, None),
            P("section", None, None, None),
            P("section", None, None, None),
        ),
        out_specs=P("section", "inl", "xln"),
        check_vma=False,
    )
```
